32 devices in a mesh: dp: 8 (over y, x, core), tensor: 4 (over z).
Axes of the slice: x: 2, y: 2, z: 4, core: 2. Of those that a mesh axis runs over, the one named last changes fastest.
Arguments:
- tokens: bfloat16 [32768, 1024], P('dp'), may hold values from -126 to 126
- route_offset: int32 [8, 512], P('dp'), may hold values from 0 to 7
- unit_sequence: int32 [8, 512], P('dp'), may hold values from 0 to 511, as said below
- cotangent: bfloat16 [32768, 1024], P('dp'), may hold values from -6 to 6
- router_weight: bfloat16 [1024], replicated, may hold values from -0.09375 to 0.09375
- first_gain: bfloat16 [1024], replicated, may hold values from 0.5 to 1.5
- second_gain: bfloat16 [1024], replicated, may hold values from 0.5 to 1.5
- qkv_weight: bfloat16 [3, 1024, 1024], P(None, None, 'tensor'), may hold values from -0.1875 to 0.1875
- out_weight: bfloat16 [1024, 1024], P('tensor'), may hold values from -0.5 to 0.5
- up_weight: bfloat16 [1024, 4096], P(None, 'tensor'), may hold values from -0.1875 to 0.1875
- down_weight: bfloat16 [4096, 1024], P('tensor'), may hold values from -0.09375 to 0.09375
Outputs:
- output: bfloat16 [32768, 1024], P('dp')
- input_grad: bfloat16 [32768, 1024], P('dp')
- router_grad: float32 [1024], replicated
- first_gain_grad: float32 [1024], replicated
- second_gain_grad: float32 [1024], replicated
- qkv_grad: float32 [3, 1024, 1024], P(None, None, 'tensor')
- out_grad: float32 [1024, 1024], P('tensor')
- up_grad: float32 [1024, 4096], P(None, 'tensor')
- down_grad: float32 [4096, 1024], P('tensor')
- score_stats: float32 [2], replicated
The draws below stay inside these ranges and needn't reach their ends.
Inputs may be any that keep to these rules, and one draw needn't show every extreme that they name: `unit_sequence`: along each row it starts at 0 and rises by 0 or 1 from one group to the next; some row holds a single sequence of 4096 tokens and some row 512 sequences.
All inputs are finite; a program needn't handle non-finite values.
Results may differ from the reference program's by a relative error of at most 0.015.
Values may be sent and summed in bfloat16 or wider, within the bound.
No kernel may reach another device: no remote copies, remote signals or barrier semaphores. Data moves between devices by JAX's collectives and lax.ppermute only.
A program may use at most 128 MiB of HBM per device.

```python
import math
import jax
import jax.numpy as jnp
from jax import lax

D = 1024
HEADS = 16
HEAD_DIM = 64
FF = 4096
TOK_DEV = 4096
CAP = 512
TOKENS = 32768
ROUTED = 4096
N_DP = 8
N_TENSOR = 4


def draw_tokens(key, part):
    key_base, key_row, key_col, key_big = jax.random.split(key, 4)
    devices = TOKENS // TOK_DEV
    steps_up = jnp.arange(devices, dtype=jnp.float32) / max(devices - 1, 1)
    base = jnp.clip(jax.random.normal(key_base, (devices, TOK_DEV, D), jnp.float32), -6.0, 6.0)
    rising = 0.5 * (1.0 + 2.0 * steps_up)
    row_factor = jnp.exp(jax.random.uniform(key_row, (devices, TOK_DEV, 1), jnp.float32, math.log(0.7), math.log(1.4)))
    col_factor = jnp.exp(jax.random.uniform(key_col, (D,), jnp.float32, math.log(0.5), math.log(2.0)))
    ranks = jax.random.permutation(key_big, jnp.arange(D, dtype=jnp.int32))
    col_factor = jnp.where(ranks < 4, 12.0, col_factor)
    values = 0.75 * base * rising[:, None, None] * row_factor * col_factor
    return values.reshape(TOKENS, D).astype(jnp.bfloat16)


def draw_unit_sequence(key, part):
    key_rate, key_cut, key_pick = jax.random.split(key, 3)
    devices = TOKENS // TOK_DEV
    groups = TOK_DEV // 8
    rate_index = jax.random.randint(key_rate, (devices, 1), 0, 4)
    periods = jnp.array([1, 3, 8, 64], jnp.int32)[rate_index]
    chosen = jax.random.randint(key_pick, (), 0, devices)
    device_ids = jnp.arange(devices, dtype=jnp.int32)[:, None]
    column = jnp.arange(groups, dtype=jnp.int32)[None, :]
    draws = jax.random.randint(key_cut, (devices, groups), 0, 1 << 20)
    cut = draws % periods == 0
    cut = cut & (device_ids != chosen)
    cut = cut | (device_ids == (chosen + 1) % devices)
    cut = cut & (column > 0)
    return jnp.cumsum(cut.astype(jnp.int32), axis=1).astype(jnp.int32)


def plant(values, rng, low, high):
    longest = values.shape.index(max(values.shape))
    spots = []
    for shift in (0, 1):
        where = [jax.random.randint(jax.random.fold_in(rng, axis), (), 0, length) for axis, length in enumerate(values.shape)]
        where[longest] = (where[longest] + shift) % values.shape[longest]
        spots.append(tuple(where))
    return values.at[spots[0]].set(low).at[spots[1]].set(high)


def shard_levels(own_key, shape, pieces, smallest, largest):
    level, own = 1.0, jax.random.fold_in(own_key, 6)
    for dim, blocks in pieces:
        steps = jnp.exp(jax.random.uniform(jax.random.fold_in(own, dim), (blocks,), jnp.float32, smallest / len(pieces), largest / len(pieces)))
        level = level * jnp.repeat(steps, shape[dim] // blocks).reshape([-1 if axis == dim else 1 for axis in range(len(shape))])
    return level


def centred(key, shape, spread, bound, cuts=(), kind=jnp.bfloat16):
    loudness = shard_levels(key, shape, cuts, -0.22, 0.18) if cuts else 1.0
    values = jax.random.normal(key, shape, jnp.float32) * spread * loudness
    return jnp.minimum(jnp.maximum(values, -bound), bound).astype(kind)


def setup_inputs(seed: int = 0) -> dict:
    key_of = jax.random.split(jax.random.key(seed), 12)
    tokens = draw_tokens(jax.random.fold_in(key_of[11], 71), 0)
    route_offset = plant(jax.random.randint(key_of[1], (N_DP, CAP), 0, 8), jax.random.fold_in(key_of[1], 1), 0, 7).astype(jnp.int32)
    unit_sequence = draw_unit_sequence(jax.random.fold_in(key_of[11], 71), 0)
    cotangent = centred(key_of[3], (TOKENS, D), 1.0, 6.0, ((0, 8),))
    router_weight = centred(key_of[4], (D,), (4 * D) ** -0.5, 0.09375)
    first_gain = jnp.clip(1.0 + 0.1 * jax.random.normal(key_of[5], (D,), jnp.float32), 0.5, 1.5).astype(jnp.bfloat16)
    second_gain = jnp.clip(1.0 + 0.1 * jax.random.normal(key_of[6], (D,), jnp.float32), 0.5, 1.5).astype(jnp.bfloat16)
    qkv_weight = centred(key_of[7], (3, D, HEADS * HEAD_DIM), D ** -0.5, 0.1875, ((2, 4),))
    out_weight = centred(key_of[8], (HEADS * HEAD_DIM, D), (D // 8) ** -0.5, 0.5, ((0, 4),))
    up_weight = centred(key_of[9], (D, FF), D ** -0.5, 0.1875, ((1, 4),))
    down_weight = centred(key_of[10], (FF, D), FF ** -0.5, 0.09375, ((0, 4),))
    return dict(tokens=tokens, route_offset=route_offset, unit_sequence=unit_sequence, cotangent=cotangent, router_weight=router_weight, first_gain=first_gain, second_gain=second_gain, qkv_weight=qkv_weight, out_weight=out_weight, up_weight=up_weight, down_weight=down_weight)


@jax.custom_vjp
def low(v):
    return lax.optimization_barrier(v.astype(jnp.bfloat16)).astype(jnp.float32)

@jax.custom_vjp
def low_back(v):
    return v

def low_keep(v):
    return (low(v), None)

def low_pass(kept, grad):
    return (grad,)

def back_keep(v):
    return (v, None)

def back_low(kept, grad):
    return (low(grad),)
low.defvjp(low_keep, low_pass)
low_back.defvjp(back_keep, back_low)
eps = 1e-06
mask_fill = -1000000000.0

def matmul_high(left, right):
    return jnp.dot(left, right, precision=lax.Precision.HIGHEST)

def normalize(row_block, gain_row):
    return row_block * lax.rsqrt(lax.optimization_barrier(jnp.mean(row_block * row_block, axis=-1, keepdims=True)) + eps) * gain_row

def block_forward(token_block, offsets, seq_ids, weights):
    router_weight, first_gain, second_gain, qkv_weight, out_weight, up_weight, down_weight = weights
    row_order = jnp.arange(CAP, dtype=jnp.int32)
    positions = 8 * row_order + offsets.astype(jnp.int32)
    picked = token_block[positions]
    score_rows = matmul_high(picked, router_weight)
    gating = jax.nn.sigmoid(score_rows)
    first_low = low(normalize(picked, first_gain))
    projected = jnp.einsum('cd,kdh->kch', first_low, qkv_weight, precision=lax.Precision.HIGHEST)
    projected = low_back(low(projected))
    query_rows = projected[0].reshape(CAP, HEADS, HEAD_DIM)
    key_rows = projected[1].reshape(CAP, HEADS, HEAD_DIM)
    value_rows = projected[2].reshape(CAP, HEADS, HEAD_DIM)
    logits = jnp.einsum('qhe,khe->hqk', query_rows, key_rows, precision=lax.Precision.HIGHEST) * HEAD_DIM ** (-0.5)
    logits = low_back(logits)
    allowed = (seq_ids[:, None] == seq_ids[None, :]) & (row_order[:, None] >= row_order[None, :])
    logits = jnp.where(allowed[None], logits, mask_fill)
    attention_probs = low(jax.nn.softmax(logits, axis=-1))
    head_out = jnp.einsum('hqk,khe->qhe', attention_probs, value_rows, precision=lax.Precision.HIGHEST)
    head_out = low_back(low(head_out)).reshape(CAP, N_TENSOR, HEADS * HEAD_DIM // N_TENSOR)
    out_groups = out_weight.reshape(N_TENSOR, HEADS * HEAD_DIM // N_TENSOR, D)
    partial_attn = jnp.einsum('cgj,gjd->gcd', head_out, out_groups, precision=lax.Precision.HIGHEST)
    attended = low_back(lax.optimization_barrier(jnp.sum(low(partial_attn), axis=0)))
    hidden_in = picked + attended
    second_low = low(normalize(hidden_in, second_gain))
    pre_act = low_back(matmul_high(second_low, up_weight))
    activated = low(jax.nn.gelu(pre_act, approximate=True)).reshape(CAP, N_TENSOR, FF // N_TENSOR)
    down_groups = down_weight.reshape(N_TENSOR, FF // N_TENSOR, D)
    partial_mlp = jnp.einsum('cgf,gfd->gcd', activated, down_groups, precision=lax.Precision.HIGHEST)
    mixer_out = low_back(lax.optimization_barrier(jnp.sum(low(partial_mlp), axis=0)))
    new_rows = picked + gating[:, None] * (attended + mixer_out)
    return token_block.at[positions].set(new_rows)

def reference(tokens, route_offset, unit_sequence, cotangent, router_weight, first_gain, second_gain, qkv_weight, out_weight, up_weight, down_weight):
    blocks = tokens.astype(jnp.float32).reshape(N_DP, TOK_DEV, D)
    weights = tuple((weight_item.astype(jnp.float32) for weight_item in (router_weight, first_gain, second_gain, qkv_weight, out_weight, up_weight, down_weight)))

    def forward(block_all, weight_all):

        def device_step(device_item):
            return jax.checkpoint(block_forward)(device_item[0], device_item[1], device_item[2], weight_all)
        return lax.map(device_step, (block_all, route_offset, unit_sequence))
    output_blocks, pullback = jax.vjp(forward, blocks, weights)
    grad_blocks, grad_weights = pullback(cotangent.astype(jnp.float32).reshape(N_DP, TOK_DEV, D))
    scores = matmul_high(blocks.reshape(TOKENS, D), weights[0])
    routed_at = 8 * jnp.arange(ROUTED, dtype=jnp.int32) + route_offset.reshape(ROUTED).astype(jnp.int32)
    routed_scores = scores[routed_at]
    score_stats = jnp.stack([jnp.mean(scores * scores), jnp.mean(routed_scores * routed_scores)])
    output = output_blocks.reshape(TOKENS, D).astype(jnp.bfloat16)
    input_grad = grad_blocks.reshape(TOKENS, D).astype(jnp.bfloat16)
    return (output, input_grad, grad_weights[0], grad_weights[1], grad_weights[2], grad_weights[3], grad_weights[4], grad_weights[5], grad_weights[6], score_stats)
```

```python
import jax
import jax.numpy as jnp
from jax import lax
from jax.sharding import PartitionSpec as P

HEAD_DIM = 64
eps = 1e-06
mask_fill = -1000000000.0
BF = jnp.bfloat16
F32 = jnp.float32


def swap(values, axis, bits):
    size = lax.axis_size(axis)
    return lax.ppermute(values, axis, [(i, i ^ bits) for i in range(size)])


def dot(left, right, dims):
    return lax.dot_general(left, right, (dims, ((), ())), preferred_element_type=F32)


NN = ((1,), (0,))
NT = ((1,), (1,))
TN = ((0,), (0,))


def inverse_rms(rows):
    return lax.rsqrt(jnp.mean(rows * rows, axis=-1, keepdims=True) + eps)


def norm_back(grad, rows, inverse, gain):
    scaled = grad * gain
    along = jnp.mean(scaled * rows, axis=-1, keepdims=True)
    return inverse * scaled - rows * (inverse * inverse * inverse * along)


def relative_blocks(whole, index, count):
    rows = whole.shape[0] // count
    return [
        lax.dynamic_slice_in_dim(whole, (index ^ k) * rows, rows, 0) for k in range(count)
    ]


def reduce_blocks(blocks, order):
    kept = list(range(len(blocks)))
    held = jnp.stack(blocks)
    for bit in order:
        stay = [n for n, k in enumerate(kept) if not k & bit]
        leave = [kept.index(kept[n] | bit) for n in stay]
        sent = swap(jnp.stack([held[n] for n in leave]), "dp", bit)
        mine = jnp.stack([held[n] for n in stay])
        held = (mine.astype(F32) + sent.astype(F32)).astype(BF)
        kept = [kept[n] for n in stay]
    return held[0]


def gather_blocks(own, order):
    held = own[None]
    keys = [0]
    for bit in order:
        other = swap(held, "dp", bit)
        held = jnp.concatenate([held, other])
        keys = keys + [k ^ bit for k in keys]
    return {k: held[n] for n, k in enumerate(keys)}


def per_device(
    tokens,
    route_offset,
    unit_sequence,
    cotangent,
    router_weight,
    first_gain,
    second_gain,
    qkv_weight,
    out_weight,
    up_weight,
    down_weight,
):
    rows_local, width = tokens.shape
    routed = route_offset.shape[1]
    ways = lax.axis_size("tensor")
    copies = lax.axis_size("dp")
    mine = lax.axis_index("tensor")
    part = lax.axis_index("dp")
    peers = range(1, ways)
    score_scale = HEAD_DIM ** (-0.5)

    quarter = part & 3
    piece_rows = out_weight.shape[0] // 4
    piece = lax.dynamic_slice_in_dim(out_weight, quarter * piece_rows, piece_rows, 0)
    here = jnp.stack([swap(piece, "tensor", k) for k in peers])
    beside = swap(here, "dp", 2)
    across = swap(jnp.stack([here, beside]), "dp", 1)
    pair_even = jnp.where(part & 1 == 0, jnp.stack([here, across[0]]), jnp.stack([across[0], here]))
    pair_odd = jnp.where(part & 1 == 0, jnp.stack([beside, across[1]]), jnp.stack([across[1], beside]))
    quads = jnp.where(
        part & 2 == 0,
        jnp.concatenate([pair_even, pair_odd]),
        jnp.concatenate([pair_odd, pair_even]),
    )
    out_groups = [out_weight] + [
        quads[:, k - 1].reshape(out_weight.shape) for k in peers
    ]

    row_order = jnp.arange(routed, dtype=jnp.int32)
    positions = 8 * row_order + route_offset[0]
    seq_ids = unit_sequence[0]
    allowed = (seq_ids[:, None] == seq_ids[None, :]) & (row_order[:, None] >= row_order[None, :])
    scores = jnp.dot(tokens, router_weight, preferred_element_type=F32)
    picked_low = tokens[positions]
    picked = picked_low.astype(F32)
    routed_scores = scores[positions]
    gating = jax.nn.sigmoid(routed_scores)[:, None]
    router_float = router_weight.astype(F32)
    gain_one = first_gain.astype(F32)
    gain_two = second_gain.astype(F32)

    inverse_one = inverse_rms(picked)
    first_low = (picked * inverse_one * gain_one).astype(BF)
    weight_wide = jnp.concatenate([qkv_weight[0], qkv_weight[1], qkv_weight[2]], axis=1)
    projected = dot(first_low, weight_wide, NN).astype(BF)
    heads_width = qkv_weight.shape[2]
    heads_local = heads_width // HEAD_DIM

    def split(rows):
        return rows.reshape(routed, heads_local, HEAD_DIM)

    query_rows = split(projected[:, :heads_width])
    key_rows = split(projected[:, heads_width : 2 * heads_width])
    value_rows = split(projected[:, 2 * heads_width :])
    raw = jnp.einsum("qhe,khe->hqk", query_rows, key_rows, preferred_element_type=F32) * score_scale
    logits = jnp.where(allowed[None], raw, mask_fill)
    row_max = jnp.max(logits, axis=-1, keepdims=True)
    raised = jnp.exp(logits - row_max)
    probs = raised / jnp.sum(raised, axis=-1, keepdims=True)
    probs_low = probs.astype(BF)
    head_out = jnp.einsum("hqk,khe->qhe", probs_low, value_rows, preferred_element_type=F32)
    head_out = head_out.astype(BF).reshape(routed, heads_width)

    head_groups = [head_out] + [swap(head_out, "tensor", k) for k in peers]
    attended = sum(dot(rows, weight, NN) for rows, weight in zip(head_groups, out_groups))
    hidden_in = picked + attended
    inverse_two = inverse_rms(hidden_in)
    second_low = (hidden_in * inverse_two * gain_two).astype(BF)
    pre_act = dot(second_low, up_weight, NN)
    activated, gelu_back = jax.vjp(lambda v: jax.nn.gelu(v, approximate=True), pre_act)
    activated_low = activated.astype(BF)
    grad_rows = cotangent[positions].astype(F32)
    grad_branch = gating * grad_rows
    grad_mixer = grad_branch.astype(BF)
    grad_act = dot(grad_mixer, down_weight, NT)
    grad_pre = gelu_back(grad_act)[0].astype(BF)
    second_part = dot(grad_pre, up_weight, NT)
    hidden_part = norm_back(second_part, hidden_in, inverse_two, gain_two)
    second_gain_part = jnp.sum(second_part * hidden_in * inverse_two, axis=0)
    attended_part = (hidden_part + grad_branch * (1.0 / ways)).astype(BF)

    head_sent = [dot(attended_part, weight, NT).astype(BF) for weight in out_groups]
    head_terms = [head_sent[0]] + [swap(head_sent[k], "tensor", k) for k in peers]
    grad_head = split(sum(term.astype(F32) for term in head_terms).astype(BF))

    mixer_part = dot(activated_low, down_weight, NN).astype(BF)
    mixer_blocks = relative_blocks(mixer_part, mine, ways)
    mixer_own = sum(
        term.astype(F32)
        for term in [mixer_blocks[0]] + [swap(mixer_blocks[k], "tensor", k) for k in peers]
    )
    own_rows = routed // ways

    def own(rows):
        return lax.dynamic_slice_in_dim(rows, mine * own_rows, own_rows, 0)

    picked_own, gating_own, attended_own, grad_own = own(picked), own(gating), own(attended), own(grad_rows)
    branch_own = attended_own + mixer_own
    new_own = (picked_own + gating_own * branch_own).astype(BF)
    grad_gating = jnp.sum(grad_own * branch_own, axis=-1, keepdims=True)
    grad_score = grad_gating * gating_own * (1.0 - gating_own)
    router_part = jnp.sum(grad_score * picked_own, axis=0)

    down_part = dot(activated_low, grad_mixer, TN).astype(BF)
    up_part = dot(second_low, grad_pre, TN).astype(BF)
    ladder = [1 << b for b in range(1, copies.bit_length() - 1)]
    order_a = [1] + ladder
    order_b = [1] + ladder[::-1]
    down_own = reduce_blocks(relative_blocks(down_part, part, copies), order_a)
    up_own = reduce_blocks(relative_blocks(up_part, part, copies), order_b)

    grad_probs = jnp.einsum("qhe,khe->hqk", grad_head, value_rows, preferred_element_type=F32)
    grad_values = jnp.einsum("hqk,qhe->khe", probs_low, grad_head, preferred_element_type=F32)
    grad_logits = probs * (grad_probs - jnp.sum(probs * grad_probs, axis=-1, keepdims=True))
    grad_logits = grad_logits.astype(BF)
    grad_query = jnp.einsum("hqk,khe->qhe", grad_logits, key_rows, preferred_element_type=F32) * score_scale
    grad_keys = jnp.einsum("hqk,qhe->khe", grad_logits, query_rows, preferred_element_type=F32) * score_scale
    grad_projected = jnp.concatenate(
        [g.reshape(routed, heads_width) for g in (grad_query, grad_keys, grad_values)], axis=1
    ).astype(BF)
    first_part = dot(grad_projected, weight_wide, NT)
    norm_part = norm_back(first_part, picked, inverse_one, gain_one)
    first_gain_part = jnp.sum(first_part * picked * inverse_one, axis=0)
    input_part = (hidden_part + norm_part).astype(BF)
    input_blocks = relative_blocks(input_part, mine, ways)
    input_terms = [input_blocks[0]] + [swap(input_blocks[k], "tensor", k) for k in peers]
    input_own = sum(term.astype(F32) for term in input_terms) + grad_own + grad_score * router_float
    input_own = input_own.astype(BF)

    qkv_part = dot(first_low, grad_projected, TN).astype(BF)
    qkv_own = reduce_blocks(relative_blocks(qkv_part, part, copies), order_b)
    out_parts = [dot(rows, attended_part, TN).astype(BF) for rows in head_groups]
    out_blocks = [relative_blocks(block, part, copies) for block in out_parts]
    out_own = reduce_blocks(
        [jnp.stack([out_blocks[k][j] for k in range(ways)]) for j in range(copies)], order_a
    )
    out_own = sum(
        term.astype(F32) for term in [out_own[0]] + [swap(out_own[k], "tensor", k) for k in peers]
    ).astype(BF)

    score_sum = jnp.sum(scores * scores) * (1.0 / ways)
    routed_sum = jnp.sum(routed_scores * routed_scores) * (1.0 / ways)
    stats = jnp.zeros((width,), F32).at[0].set(score_sum).at[1].set(routed_sum)
    small = jnp.stack([router_part, first_gain_part, second_gain_part, stats])
    for bit in [1] + ladder:
        small = small + swap(small, "dp", bit)
    step = 1
    while step < ways:
        small = small + swap(small, "tensor", step)
        step *= 2

    def place(base, blocks, index, rows):
        for k, block in blocks.items():
            base = lax.dynamic_update_slice_in_dim(base, block, (index ^ k) * rows, 0)
        return base

    new_rows = place(
        jnp.zeros((routed, width), BF),
        {k: (new_own if k == 0 else swap(new_own, "tensor", k)) for k in range(ways)},
        mine,
        own_rows,
    )
    input_rows = place(
        jnp.zeros((routed, width), BF),
        {k: (input_own if k == 0 else swap(input_own, "tensor", k)) for k in range(ways)},
        mine,
        own_rows,
    )
    output = tokens.at[positions].set(new_rows)
    input_grad = cotangent.at[positions].set(input_rows)

    def spread(block, order, rows):
        pieces = gather_blocks(block, order[::-1])
        pieces = {k: v.astype(F32) for k, v in pieces.items()}
        return place(jnp.zeros((rows, block.shape[1]), F32), pieces, part, rows // copies)

    down_grad = spread(down_own, order_a, down_weight.shape[0])
    up_grad = spread(up_own, order_b, up_weight.shape[0])
    qkv_wide = spread(qkv_own, order_b, width)
    out_grad = spread(out_own, order_a, out_weight.shape[0])
    qkv_grad = jnp.stack(jnp.split(qkv_wide, 3, axis=1))
    score_stats = jnp.stack(
        [small[3, 0] / (rows_local * copies), small[3, 1] / (routed * copies)]
    )
    return (
        output,
        input_grad,
        small[0],
        small[1],
        small[2],
        qkv_grad,
        out_grad,
        up_grad,
        down_grad,
        score_stats,
    )


def solution(mesh):
    placed = (
        P("dp", None),
        P("dp", None),
        P("dp", None),
        P("dp", None),
        P(),
        P(),
        P(),
        P(None, None, "tensor"),
        P("tensor", None),
        P(None, "tensor"),
        P("tensor", None),
    )
    return jax.shard_map(
        per_device,
        mesh=mesh,
        in_specs=placed,
        out_specs=(
            P("dp", None),
            P("dp", None),
            P(),
            P(),
            P(),
            P(None, None, "tensor"),
            P("tensor", None),
            P(None, "tensor"),
            P("tensor", None),
            P(),
        ),
        check_vma=False,
    )
```

```python
import jax
import jax.numpy as jnp
from jax import lax
from jax.experimental import pallas as pl
from jax.experimental.pallas import tpu as pltpu
from jax.sharding import PartitionSpec as P

BF = jnp.bfloat16
F32 = jnp.float32

NN = ((1,), (0,))
NT = ((1,), (1,))
TN = ((0,), (0,))


def dot(left, right, dims):
    return lax.dot_general(left, right, (dims, ((), ())), preferred_element_type=F32)


def swap(values, axis, bits):
    size = lax.axis_size(axis)
    return lax.ppermute(values, axis, [(i, i ^ bits) for i in range(size)])


def to_all(blocks):
    return lax.all_to_all(blocks, "tensor", 0, 0, tiled=True)


def inverse_rms(rows):
    return lax.rsqrt(jnp.mean(rows * rows, axis=-1, keepdims=True) + eps)


HEAD_DIM = 64
GROUP = 8
TERMS = 4
GAP = 16
eps = 1e-06
mask_fill = -1000000000.0


def small_cost():
    return pl.CostEstimate(flops=1024, bytes_accessed=1024, transcendentals=0)


def cost_of(microseconds):
    return pl.CostEstimate(flops=1024, bytes_accessed=int(microseconds * 3.0e6), transcendentals=0)


def pick_rows(base, offsets, weight, mine, ways, cost, limit):
    rows, width = base.shape
    chunks = 2 * ways
    block = rows // chunks
    sub = 256
    sub_groups = sub // GROUP

    def kernel(mine_ref, base_ref, offset_ref, weight_ref, picked_ref, square_ref, held, sems):
        def load(n):
            part = pl.ds(n * block, block)
            return pltpu.make_async_copy(base_ref.at[part], held.at[part], sems.at[n])

        for n in range(chunks):
            load(n).start()
        row = lax.broadcasted_iota(jnp.int32, (sub, sub_groups), 0)
        group = lax.broadcasted_iota(jnp.int32, (sub, sub_groups), 1)
        local = row - GROUP * group
        for n in range(chunks):
            load(n).wait()
            for s in range(n * block // sub, (n + 1) * block // sub):
                to = slice(s * sub_groups, (s + 1) * sub_groups)
                chosen = (local == offset_ref[:, to]).astype(F32).astype(BF)
                picked_ref[to, :] = dot(chosen, held[s * sub : (s + 1) * sub, :], TN).astype(BF)
        if square_ref is not None:
            weights = weight_ref[...].astype(F32)
            total = jnp.zeros((1, 1), F32)
            for n in range(2):
                start = pl.multiple_of((2 * mine_ref[0] + n) * block, block)
                mult = held[pl.ds(start, block), :].astype(F32) * weights
                score = jnp.sum(mult, axis=1, keepdims=True)
                total = total + jnp.sum(score * score, axis=0, keepdims=True)
            square_ref[...] = jnp.broadcast_to(total, square_ref.shape)

    with_squares = weight is not None
    if with_squares:
        body = kernel
    else:

        def body(mine_ref, base_ref, offset_ref, picked_ref, held, sems):
            kernel(mine_ref, base_ref, offset_ref, None, picked_ref, None, held, sems)

    whole = pl.BlockSpec(memory_space=pltpu.VMEM)
    out_shape = [jax.ShapeDtypeStruct((rows // GROUP, width), BF)]
    operands = [mine, base, offsets]
    in_specs = [pl.BlockSpec(memory_space=pltpu.SMEM), pl.BlockSpec(memory_space=pltpu.HBM), whole]
    if with_squares:
        out_shape.append(jax.ShapeDtypeStruct((1, 128), F32))
        operands.append(weight)
        in_specs.append(whole)
    return pl.pallas_call(
        body,
        in_specs=in_specs,
        out_specs=[whole] * len(out_shape),
        out_shape=out_shape,
        scratch_shapes=[pltpu.VMEM((rows, width), BF), pltpu.SemaphoreType.DMA((chunks,))],
        cost_estimate=cost,
        compiler_params=pltpu.CompilerParams(vmem_limit_bytes=limit << 20),
        name="pick_rows",
    )(*operands)


def merge_rows(base, offsets, pieces, parts, held_out=None):
    rows, width = base.shape
    ways, depth, _ = pieces.shape
    count = rows // ways
    groups = count // GROUP
    kept = [] if held_out is None else [held_out]
    sub = 256
    sub_groups = sub // GROUP

    def kernel(part_ref, base_ref, offset_ref, piece_ref, *rest):
        out_ref = rest[-1]
        local = lax.broadcasted_iota(jnp.int32, (sub, sub_groups), 0) - GROUP * lax.broadcasted_iota(
            jnp.int32, (sub, sub_groups), 1
        )
        for s in range(count // sub):
            here = slice(s * sub, (s + 1) * sub)
            to = slice(s * sub_groups, (s + 1) * sub_groups)
            chosen = (local == offset_ref[:, to]).astype(F32)
            hit = jnp.sum(chosen, axis=1, keepdims=True) > 0.5
            spread = dot(chosen.astype(BF), piece_ref[0, to, :], NN)
            out_ref[here, :] = jnp.where(hit, spread, base_ref[here, :].astype(F32)).astype(BF)

    grid_spec = pltpu.PrefetchScalarGridSpec(
        num_scalar_prefetch=1,
        grid=(parts.shape[0],),
        in_specs=[
            pl.BlockSpec((count, width), lambda i, p: (p[i], 0)),
            pl.BlockSpec((1, groups), lambda i, p: (0, p[i])),
            pl.BlockSpec((1, depth, width), lambda i, p: (p[i], 0, 0)),
        ]
        + [pl.BlockSpec(memory_space=pl.ANY)] * len(kept),
        out_specs=pl.BlockSpec((count, width), lambda i, p: (p[i], 0)),
    )
    return pl.pallas_call(
        kernel,
        grid_spec=grid_spec,
        out_shape=jax.ShapeDtypeStruct((rows, width), BF),
        input_output_aliases={4: 0} if kept else {},
        cost_estimate=small_cost(),
        name="merge_rows",
    )(parts, base, offsets, pieces, *kept)


def attend(picked, gain, weight, seq_row, seq_column, router, ways):
    rows, width = picked.shape
    heads_width = weight.shape[2]
    heads = heads_width // HEAD_DIM
    block = min(256, rows)

    def kernel(
        picked_ref, gain_ref, weight_ref, row_ref, column_ref, router_ref, low_ref, qkv_ref, probs_ref, out_ref, gating_ref, square_ref
    ):
        values = picked_ref[...].astype(F32)
        score = jnp.sum(values * router_ref[...].astype(F32), axis=-1, keepdims=True)
        gating_ref[...] = jax.nn.sigmoid(score)
        square_ref[...] = jnp.broadcast_to(jnp.sum(score * score, axis=0, keepdims=True), square_ref.shape)
        low_ref[...] = (values * inverse_rms(values) * gain_ref[...].astype(F32)).astype(BF)
        for n in range(3):
            qkv_ref[n] = dot(low_ref[...], weight_ref[n], NN).astype(BF)
        lane_head = lax.broadcasted_iota(jnp.int32, (1, heads_width), 1) // HEAD_DIM
        for start in range(0, rows, block):
            stop = start + block
            query = qkv_ref[0, start:stop, :] * BF(HEAD_DIM ** (-0.5))
            order = lax.broadcasted_iota(jnp.int32, (block, stop), 0) + start
            keys = lax.broadcasted_iota(jnp.int32, (block, stop), 1)
            allowed = (column_ref[start:stop, :] == row_ref[:, :stop]) & (order >= keys)
            total = jnp.zeros((block, heads_width), F32)
            for head in range(heads):
                here = lane_head == head
                key = jnp.where(here, qkv_ref[1, :stop, :], BF(0))
                logits = jnp.where(allowed, dot(query, key, NT), mask_fill)
                raised = jnp.exp(logits - jnp.max(logits, axis=-1, keepdims=True))
                probs = (raised * (1.0 / jnp.sum(raised, axis=-1, keepdims=True))).astype(BF)
                probs_ref[head, start:stop, :stop] = probs
                if stop < rows:
                    probs_ref[head, start:stop, stop:] = jnp.zeros((block, rows - stop), BF)
                value = jnp.where(here, qkv_ref[2, :stop, :], BF(0))
                total = total + dot(probs, value, NN)
            for k in range(ways):
                out_ref[k, start:stop, :] = total.astype(BF)

    whole = pl.BlockSpec(memory_space=pltpu.VMEM)
    return pl.pallas_call(
        kernel,
        in_specs=[whole] * 6,
        out_specs=[whole] * 6,
        out_shape=[
            jax.ShapeDtypeStruct((rows, width), BF),
            jax.ShapeDtypeStruct((3, rows, heads_width), BF),
            jax.ShapeDtypeStruct((heads, rows, rows), BF),
            jax.ShapeDtypeStruct((ways, rows, heads_width), BF),
            jax.ShapeDtypeStruct((rows, 1), F32),
            jax.ShapeDtypeStruct((1, 128), F32),
        ],
        cost_estimate=cost_of(5.0),
        compiler_params=pltpu.CompilerParams(vmem_limit_bytes=40 << 20),
        name="attend",
    )(picked, gain, weight, seq_row, seq_column, router)


def feed_forward(heads, here, beside, across, picked, gain, up, grad_act, grad_mixer, part):
    tile = up.shape[1]
    sub = min(256, tile)
    rows, width = picked.shape
    hidden = up.shape[1]
    steps = hidden // tile
    count, _, heads_width = heads.shape
    piece = heads_width // 4
    slope = 0.7978845608028654
    cubic = 0.044715

    def kernel(
        part_ref,
        heads_ref,
        here_ref,
        beside_ref,
        across_ref,
        picked_ref,
        gain_ref,
        up_ref,
        act_grad_ref,
        mixer_ref,
        attended_ref,
        low_ref,
        act_ref,
        pre_ref,
        hidden_ref,
        part_out_ref,
        gain_part_ref,
        sent_ref,
        total,
        state,
        weights,
    ):
        step = pl.program_id(0)

        @pl.when(step == 0)
        def _():
            quarter = part_ref[0] & 3
            for n, source in enumerate((here_ref, across_ref.at[0], beside_ref, across_ref.at[1])):
                start = pl.multiple_of((quarter ^ n) * piece, piece)
                for k in range(count):
                    weights[k, pl.ds(start, piece), :] = source[k]
            attended = dot(heads_ref[0], weights[0], NN)
            for k in range(1, count):
                attended = attended + dot(heads_ref[k], weights[k], NN)
            attended_ref[...] = attended
            state_in = picked_ref[...].astype(F32) + attended
            state[...] = state_in
            low_ref[...] = (state_in * inverse_rms(state_in) * gain_ref[...].astype(F32)).astype(BF)
            total[...] = jnp.zeros_like(total)

        for s in range(tile // sub):
            lanes = slice(s * sub, (s + 1) * sub)
            value = dot(low_ref[...], up_ref[:, lanes], NN)
            square = value * value
            bent = jnp.tanh(value * (slope + (slope * cubic) * square))
            half = 0.5 * (1.0 + bent)
            act_ref[:, lanes] = (value * half).astype(BF)
            rise = half + (0.5 * value) * (1.0 - bent * bent) * (slope + (3.0 * slope * cubic) * square)
            pre = (act_grad_ref[:, lanes] * rise).astype(BF)
            pre_ref[:, lanes] = pre
            total[...] += dot(pre, up_ref[:, lanes], NT)

        @pl.when(step == steps - 1)
        def _():
            state_in = state[...]
            grad = total[...]
            inverse = inverse_rms(state_in)
            normal = state_in * inverse
            gain_part_ref[...] = jnp.sum(grad * normal, axis=0, keepdims=True)
            scaled = grad * gain_ref[...].astype(F32)
            along = jnp.mean(scaled * normal, axis=-1, keepdims=True)
            back = inverse * (scaled - normal * along)
            hidden_ref[...] = back.astype(BF)
            part_out_ref[...] = (back + mixer_ref[...].astype(F32) * (1.0 / count)).astype(BF)
            for k in range(count):
                sent_ref[k] = dot(part_out_ref[...], weights[k], NT).astype(BF)

    def fixed(shape):
        return pl.BlockSpec(shape, lambda i: (0,) * len(shape))

    return pl.pallas_call(
        kernel,
        grid=(steps,),
        in_specs=[
            pl.BlockSpec(memory_space=pltpu.SMEM),
            fixed(heads.shape),
            fixed(here.shape),
            fixed(beside.shape),
            fixed(across.shape),
            fixed((rows, width)),
            fixed((1, width)),
            pl.BlockSpec((width, tile), lambda i: (0, i)),
            pl.BlockSpec((rows, tile), lambda i: (0, i)),
            fixed((rows, width)),
        ],
        out_specs=[
            fixed((rows, width)),
            fixed((rows, width)),
            pl.BlockSpec((rows, tile), lambda i: (0, i)),
            pl.BlockSpec((rows, tile), lambda i: (0, i)),
            fixed((rows, width)),
            fixed((rows, width)),
            fixed((1, width)),
            fixed(heads.shape),
        ],
        out_shape=[
            jax.ShapeDtypeStruct((rows, width), F32),
            jax.ShapeDtypeStruct((rows, width), BF),
            jax.ShapeDtypeStruct((rows, hidden), BF),
            jax.ShapeDtypeStruct((rows, hidden), BF),
            jax.ShapeDtypeStruct((rows, width), BF),
            jax.ShapeDtypeStruct((rows, width), BF),
            jax.ShapeDtypeStruct((1, width), F32),
            jax.ShapeDtypeStruct(heads.shape, BF),
        ],
        scratch_shapes=[
            pltpu.VMEM((rows, width), F32),
            pltpu.VMEM((rows, width), F32),
            pltpu.VMEM((count, heads_width, width), BF),
        ],
        cost_estimate=small_cost(),
        compiler_params=pltpu.CompilerParams(vmem_limit_bytes=48 << 20),
        name="feed_forward",
    )(part, heads, here, beside, across, picked, gain, up, grad_act, grad_mixer)


def act_grads(grad_rows, gating, down):
    rows, width = grad_rows.shape

    def kernel(rows_ref, gating_ref, down_ref, mixer_ref, grad_ref):
        mixer_ref[...] = (gating_ref[...] * rows_ref[...].astype(F32)).astype(BF)
        grad_ref[...] = dot(mixer_ref[...], down_ref[...], NT)

    whole = pl.BlockSpec(memory_space=pltpu.VMEM)
    return pl.pallas_call(
        kernel,
        in_specs=[whole] * 3,
        out_specs=[whole] * 2,
        out_shape=[jax.ShapeDtypeStruct((rows, width), BF), jax.ShapeDtypeStruct((rows, down.shape[0]), F32)],
        cost_estimate=small_cost(),
        name="act_grads",
    )(grad_rows, gating, down)


def attend_back(grad_head_in, qkv, probs, weight, picked, gain, hidden_part):
    rows, width = picked.shape
    heads_width = weight.shape[2]
    heads = heads_width // HEAD_DIM
    block = min(256, rows)
    scale = HEAD_DIM ** (-0.5)

    def kernel(
        head_ref,
        qkv_ref,
        probs_ref,
        weight_ref,
        picked_ref,
        gain_ref,
        hidden_ref,
        grads_ref,
        gain_part_ref,
        result,
        grad_key,
        grad_value,
    ):
        lane_head = lax.broadcasted_iota(jnp.int32, (1, heads_width), 1) // HEAD_DIM
        for start in reversed(range(0, rows, block)):
            stop = start + block
            here_rows = slice(start, stop)
            grad_head = head_ref[here_rows, :]
            query = qkv_ref[0, here_rows, :] * BF(scale)
            grad_query = jnp.zeros((block, heads_width), F32)
            add_key = jnp.zeros((stop, heads_width), F32)
            add_value = jnp.zeros((stop, heads_width), F32)
            for head in range(heads):
                here = lane_head == head
                value = jnp.where(here, qkv_ref[2, :stop, :], BF(0))
                key = jnp.where(here, qkv_ref[1, :stop, :], BF(0))
                low = probs_ref[head, here_rows, :stop]
                weighted = low.astype(F32) * dot(grad_head, value, NT)
                row_sum = jnp.sum(weighted, axis=-1, keepdims=True)
                slopes = (weighted - low.astype(F32) * row_sum).astype(BF)
                grad_query = grad_query + dot(slopes, key, NN)
                add_key = add_key + dot(slopes, jnp.where(here, query, BF(0)), TN)
                add_value = add_value + dot(low, jnp.where(here, grad_head, BF(0)), TN)
            grads_ref[0, here_rows, :] = (grad_query * scale).astype(BF)
            if stop == rows:
                grad_key[...] = add_key
                grad_value[...] = add_value
            else:
                grad_key[:stop, :] += add_key
                grad_value[:stop, :] += add_value
        grads_ref[1] = grad_key[...].astype(BF)
        grads_ref[2] = grad_value[...].astype(BF)
        first = dot(grads_ref[0], weight_ref[0], NT)
        for n in range(1, 3):
            first = first + dot(grads_ref[n], weight_ref[n], NT)
        values = picked_ref[...].astype(F32)
        inverse = inverse_rms(values)
        normal = values * inverse
        gain_part_ref[...] = jnp.sum(first * normal, axis=0, keepdims=True)
        scaled = first * gain_ref[...].astype(F32)
        along = jnp.mean(scaled * normal, axis=-1, keepdims=True)
        result[...] = (hidden_ref[...].astype(F32) + inverse * (scaled - normal * along)).astype(BF)

    whole = pl.BlockSpec(memory_space=pltpu.VMEM)
    return pl.pallas_call(
        kernel,
        in_specs=[whole] * 7,
        out_specs=[whole] * 3,
        out_shape=[
            jax.ShapeDtypeStruct((3, rows, heads_width), BF),
            jax.ShapeDtypeStruct((1, width), F32),
            jax.ShapeDtypeStruct((rows, width), BF),
        ],
        scratch_shapes=[
            pltpu.VMEM((rows, heads_width), F32),
            pltpu.VMEM((rows, heads_width), F32),
        ],
        cost_estimate=small_cost(),
        compiler_params=pltpu.CompilerParams(vmem_limit_bytes=48 << 20),
        name="attend_back",
    )(grad_head_in, qkv, probs, weight, picked, gain, hidden_part)


def spread_rows(down_near, down_far, up_near, up_far, index_down, index_up):
    half, rows, width = down_near.shape

    def kernel(down_index, up_index, down_ref, far_ref, up_ref, up_far_ref, down_out, up_out):
        near = pl.program_id(0) < half

        @pl.when(near)
        def _():
            down_out[...] = down_ref[0].astype(F32)
            up_out[...] = up_ref[0].astype(F32)

        @pl.when(jnp.logical_not(near))
        def _():
            down_out[...] = far_ref[0].astype(F32)
            up_out[...] = up_far_ref[0].astype(F32)

    first = pl.BlockSpec((1, rows, width), lambda i, d, u: (jnp.minimum(i, half - 1), 0, 0))
    second = pl.BlockSpec((1, rows, width), lambda i, d, u: (jnp.maximum(i - half, 0), 0, 0))
    return pl.pallas_call(
        kernel,
        grid_spec=pltpu.PrefetchScalarGridSpec(
            num_scalar_prefetch=2,
            grid=(2 * half,),
            in_specs=[first, second, first, second],
            out_specs=[
                pl.BlockSpec((rows, width), lambda i, d, u: (d[i], 0)),
                pl.BlockSpec((rows, width), lambda i, d, u: (u[i], 0)),
            ],
        ),
        out_shape=[jax.ShapeDtypeStruct((2 * half * rows, width), F32)] * 2,
        cost_estimate=small_cost(),
        name="spread_rows",
    )(index_down, index_up, down_near, down_far, up_near, up_far)


def qkv_part_of(first_low, grads):
    rows, width = first_low.shape
    part_width = grads.shape[2]

    def kernel(low_ref, grads_ref, out_ref):
        for n in range(3):
            product = dot(grads_ref[n], low_ref[...], TN)
            out_ref[n * part_width : (n + 1) * part_width, :] = product.astype(BF)

    whole = pl.BlockSpec(memory_space=pltpu.VMEM)
    return pl.pallas_call(
        kernel,
        in_specs=[whole] * 2,
        out_specs=whole,
        out_shape=jax.ShapeDtypeStruct((3 * part_width, width), BF),
        cost_estimate=small_cost(),
        name="qkv_part",
    )(first_low, grads)


def spread_qkv(lane_a, got_a, lane_b, got_b, first, part_width):
    width = lane_a.shape[1]
    rows = lane_a.shape[0] - first
    tile = 128

    def kernel(a_ref, a_got, b_ref, b_got, out_ref):
        for n in range(2 * rows // tile):
            start = first + n * tile % rows
            ref, got = (a_ref, a_got) if n * tile < rows else (b_ref, b_got)
            lane, column = divmod(n * tile, part_width)
            piece = ref[start : start + tile, :].astype(F32) + got[start : start + tile, :].astype(F32)
            out_ref[lane, :, column : column + tile] = piece.T

    whole = pl.BlockSpec(memory_space=pltpu.VMEM)
    return pl.pallas_call(
        kernel,
        in_specs=[whole] * 4,
        out_specs=whole,
        out_shape=jax.ShapeDtypeStruct((2 * rows // part_width, width, part_width), F32),
        cost_estimate=small_cost(),
        compiler_params=pltpu.CompilerParams(vmem_limit_bytes=16 << 20),
        name="spread_qkv",
    )(lane_a, got_a, lane_b, got_b)


def core_grads(activated, grad_mixer, second_low, grad_pre, heads, attended_part, part, keys_a, keys_b):
    rows, hidden = activated.shape
    width = grad_mixer.shape[1]
    copies = len(keys_a)
    half = copies // 2
    count, _, heads_width = heads.shape
    block = hidden // copies
    small = heads_width // copies
    many = count // 2
    depth = half * (block + many * small)

    def kernel(part_ref, act_ref, mixer_ref, low_ref, pre_ref, heads_ref, term_ref, keep_ref, a_ref, b_ref, full, narrow):
        def place(source, each, lane, keys, first, stride):
            for n, key in enumerate(keys):
                start = pl.multiple_of((part_ref[0] ^ key) * each, each)
                at = first + (n % half) * stride
                piece = source[pl.ds(start, each), :]
                if n < half:
                    keep_ref[lane, at : at + each, :] = piece
                else:
                    (b_ref if lane else a_ref)[at : at + each, :] = piece

        full[...] = dot(act_ref[...], mixer_ref[...], TN).astype(BF)
        place(full, block, 0, keys_a, 0, block)
        full[...] = dot(low_ref[...], pre_ref[...], TN).astype(BF)
        place(full, block, 1, keys_b, 0, block)
        for k in range(count):
            narrow[...] = dot(heads_ref[k], term_ref[...], TN).astype(BF)
            lane, spot = divmod(k, many)
            place(narrow, small, lane, keys_b if lane else keys_a, half * block + spot * small, many * small)

    whole = pl.BlockSpec(memory_space=pltpu.VMEM)
    lane_shape = jax.ShapeDtypeStruct((depth, width), BF)
    return pl.pallas_call(
        kernel,
        in_specs=[pl.BlockSpec(memory_space=pltpu.SMEM)] + [whole] * 6,
        out_specs=[whole] * 3,
        out_shape=[jax.ShapeDtypeStruct((2, depth, width), BF), lane_shape, lane_shape],
        scratch_shapes=[pltpu.VMEM((hidden, width), BF), pltpu.VMEM((heads_width, width), BF)],
        cost_estimate=small_cost(),
        compiler_params=pltpu.CompilerParams(vmem_limit_bytes=24 << 20),
        name="core_grads",
    )(part, activated, grad_mixer, second_low, grad_pre, heads, attended_part)


def plus(left, right):
    return (left.astype(F32) + right.astype(F32)).astype(BF)


def halving_sums(keep, got_a, got_b, wide, narrow):
    width = keep.shape[2]

    def kernel(keep_ref, a_got, b_got, stay_ref, a_out, b_out):
        for lane, got, out in ((0, a_got, a_out), (1, b_got, b_out)):
            for first, size, at in ((0, wide // 2, 0), (wide, narrow // 2, wide // 2)):
                stays, leaves = slice(first, first + size), slice(first + size, first + 2 * size)
                to = slice(at, at + size)
                stay_ref[lane, to, :] = plus(keep_ref[lane, stays, :], got[stays, :])
                out[to, :] = plus(keep_ref[lane, leaves, :], got[leaves, :])

    whole = pl.BlockSpec(memory_space=pltpu.VMEM)
    depth = (wide + narrow) // 2
    lane_shape = jax.ShapeDtypeStruct((depth, width), BF)
    return pl.pallas_call(
        kernel,
        in_specs=[whole] * 3,
        out_specs=[whole] * 3,
        out_shape=[jax.ShapeDtypeStruct((2, depth, width), BF), lane_shape, lane_shape],
        cost_estimate=small_cost(),
        compiler_params=pltpu.CompilerParams(vmem_limit_bytes=16 << 20),
        name="halving_sums",
    )(keep, got_a, got_b)


def owned_sums(keep, got_a, got_b, qkv, qkv_got, fresh, small, wide, ways):
    width = keep.shape[2]
    narrow = keep.shape[1] - wide
    third = qkv.shape[0] // 2
    own = fresh.shape[0]
    terms = small.shape[0]
    many = ways // 2
    each = narrow // many
    depth = own + GAP + each

    def kernel(keep_ref, a_got, b_got, qkv_ref, qkv_got_ref, fresh_ref, small_ref, a_out, b_out, sent_ref):
        high = small_ref[...].astype(BF)
        low = (small_ref[...] - high.astype(F32)).astype(BF)
        sums = jnp.concatenate([high, low, jnp.zeros((GAP - 2 * terms, width), BF)], axis=0)
        for lane, got, out in ((0, a_got, a_out), (1, b_got, b_out)):
            out[:wide, :] = plus(keep_ref[lane, :wide, :], got[:wide, :])
            here = slice(lane * third, (lane + 1) * third)
            out[wide:, :] = plus(qkv_ref[here, :], qkv_got_ref[here, :])
            done = plus(keep_ref[lane, wide:, :], got[wide:, :])
            for spot in range(many):
                k = lane * many + spot
                sent_ref[k, :own, :] = fresh_ref[...]
                sent_ref[k, own : own + GAP, :] = sums
                sent_ref[k, own + GAP :, :] = done[spot * each : (spot + 1) * each, :]

    whole = pl.BlockSpec(memory_space=pltpu.VMEM)
    lane_shape = jax.ShapeDtypeStruct((wide + third, width), BF)
    return pl.pallas_call(
        kernel,
        in_specs=[whole] * 7,
        out_specs=[whole] * 3,
        out_shape=[lane_shape, lane_shape, jax.ShapeDtypeStruct((ways, depth, width), BF)],
        cost_estimate=small_cost(),
        compiler_params=pltpu.CompilerParams(vmem_limit_bytes=20 << 20),
        name="owned_sums",
    )(keep, got_a, got_b, qkv, qkv_got, fresh, small)


def gather_sums(lane_a, got_a, lane_b, got_b, wide):
    depth, width = lane_a.shape

    def kernel(a_ref, a_got, b_ref, b_got, a_out, b_out):
        for ref, got, out in ((a_ref, a_got, a_out), (b_ref, b_got, b_out)):
            out[:wide, :] = ref[:wide, :]
            out[wide : 2 * wide, :] = got[:wide, :]
            out[2 * wide :, :] = plus(ref[wide:, :], got[wide:, :])

    whole = pl.BlockSpec(memory_space=pltpu.VMEM)
    lane_shape = jax.ShapeDtypeStruct((depth + wide, width), BF)
    return pl.pallas_call(
        kernel,
        in_specs=[whole] * 4,
        out_specs=[whole] * 2,
        out_shape=[lane_shape, lane_shape],
        cost_estimate=small_cost(),
        compiler_params=pltpu.CompilerParams(vmem_limit_bytes=16 << 20),
        name="gather_sums",
    )(lane_a, got_a, lane_b, got_b)


def gather_blocks(lane_a, got_a, lane_b, got_b, wide):
    width = lane_a.shape[1]

    def kernel(a_ref, a_got, b_ref, b_got, a_out, b_out):
        for ref, got, out in ((a_ref, a_got, a_out), (b_ref, b_got, b_out)):
            out[:wide, :] = ref[...]
            out[wide:, :] = got[...]

    def top(array):
        return pl.BlockSpec((wide, width), lambda i: (0, 0))

    shape = jax.ShapeDtypeStruct((2 * wide, width), BF)
    return pl.pallas_call(
        kernel,
        grid=(1,),
        in_specs=[top(a) for a in (lane_a, got_a, lane_b, got_b)],
        out_specs=[pl.BlockSpec((2 * wide, width), lambda i: (0, 0))] * 2,
        out_shape=[shape, shape],
        cost_estimate=small_cost(),
        name="gather_blocks",
    )(lane_a, got_a, lane_b, got_b)


def split_sums(values):
    high = values.astype(BF)
    low = (values - high.astype(F32)).astype(BF)
    return jnp.concatenate([high, low, jnp.zeros((GAP - 2 * TERMS, values.shape[1]), BF)], axis=0)


def joined_sums(rows):
    return rows[:TERMS].astype(F32) + rows[TERMS : 2 * TERMS].astype(F32)


def first_small(received, own):
    ways, depth, width = received.shape
    each = depth - own - GAP

    def kernel(got_ref, out_ref):
        total = got_ref[0, own + GAP :, :].astype(F32)
        sums = joined_sums(got_ref[0, own : own + GAP, :])
        for k in range(1, ways):
            total = total + got_ref[k, own + GAP :, :].astype(F32)
            sums = sums + joined_sums(got_ref[k, own : own + GAP, :])
        out_ref[:each, :] = total.astype(BF)
        out_ref[each:, :] = split_sums(sums)

    whole = pl.BlockSpec(memory_space=pltpu.VMEM)
    return pl.pallas_call(
        kernel,
        in_specs=[whole],
        out_specs=whole,
        out_shape=jax.ShapeDtypeStruct((each + GAP, width), BF),
        cost_estimate=small_cost(),
        name="first_small",
    )(received)


def join_small(mine_rows, other_rows):
    depth, width = mine_rows.shape
    each = depth - GAP

    def kernel(mine_ref, other_ref, out_ref):
        out_ref[:each, :] = mine_ref[:each, :]
        out_ref[each : 2 * each, :] = other_ref[:each, :]
        out_ref[2 * each :, :] = split_sums(joined_sums(mine_ref[each:, :]) + joined_sums(other_ref[each:, :]))

    whole = pl.BlockSpec(memory_space=pltpu.VMEM)
    return pl.pallas_call(
        kernel,
        in_specs=[whole] * 2,
        out_specs=whole,
        out_shape=jax.ShapeDtypeStruct((2 * each + GAP, width), BF),
        cost_estimate=small_cost(),
        name="join_small",
    )(mine_rows, other_rows)


def last_small(mine_rows, other_rows, index):
    depth, width = mine_rows.shape
    blocks = index.shape[0]
    total = 2 * (depth - GAP)
    each = total // blocks

    def kernel(index_ref, mine_ref, other_ref, out_ref, small_ref):
        for n in range(blocks):
            source, at = (mine_ref, n) if n < blocks // 2 else (other_ref, n - blocks // 2)
            start = pl.multiple_of(index_ref[n] * each, each)
            out_ref[pl.ds(start, each), :] = source[at * each : (at + 1) * each, :].astype(F32)
        small_ref[...] = joined_sums(mine_ref[depth - GAP :, :]) + joined_sums(other_ref[depth - GAP :, :])

    whole = pl.BlockSpec(memory_space=pltpu.VMEM)
    return pl.pallas_call(
        kernel,
        in_specs=[pl.BlockSpec(memory_space=pltpu.SMEM), whole, whole],
        out_specs=[whole] * 2,
        out_shape=[jax.ShapeDtypeStruct((total, width), F32), jax.ShapeDtypeStruct((TERMS, width), F32)],
        cost_estimate=small_cost(),
        name="last_small",
    )(index, mine_rows, other_rows)


def sum_heads(terms):
    def kernel(terms_ref, out_ref):
        total = terms_ref[0].astype(F32)
        for k in range(1, terms.shape[0]):
            total = total + terms_ref[k].astype(F32)
        out_ref[...] = total.astype(BF)

    whole = pl.BlockSpec(memory_space=pltpu.VMEM)
    return pl.pallas_call(
        kernel,
        in_specs=[whole],
        out_specs=whole,
        out_shape=jax.ShapeDtypeStruct(terms.shape[1:], BF),
        cost_estimate=small_cost(),
        name="sum_heads",
    )(terms)


def finish_rows(mixer_terms, picked, gating, attended, grad_rows, gain_one, gain_two, square, routed_square, mine, ways):
    rows, width = picked.shape
    own = rows // ways

    def kernel(
        mine_ref,
        terms_ref,
        picked_ref,
        gating_ref,
        attended_ref,
        rows_ref,
        one_ref,
        two_ref,
        square_ref,
        routed_ref,
        new_ref,
        score_ref,
        small_ref,
    ):
        branch = attended_ref[...]
        for k in range(ways):
            branch = branch + terms_ref[k].astype(F32)
        values = picked_ref[...].astype(F32)
        gate = gating_ref[...]
        new_ref[...] = (values + gate * branch).astype(BF)
        along = jnp.sum(rows_ref[...].astype(F32) * branch, axis=-1, keepdims=True)
        score = along * gate * (1.0 - gate)
        score_ref[...] = score
        small_ref[0:1, :] = jnp.sum(score * values, axis=0, keepdims=True)
        small_ref[1:2, :] = one_ref[...]
        small_ref[2:3, :] = two_ref[...]
        lane = lax.broadcasted_iota(jnp.int32, (1, width), 1)
        both = jnp.where(lane == 0, square_ref[:, 0:1], routed_ref[:, 0:1] * (1.0 / ways))
        small_ref[3:4, :] = jnp.where(lane < 2, both, 0.0)

    def block(shape):
        return pl.BlockSpec(shape, lambda i, m: (m[0], 0))

    def fixed(shape):
        return pl.BlockSpec(shape, lambda i, m: (0, 0))

    return pl.pallas_call(
        kernel,
        grid_spec=pltpu.PrefetchScalarGridSpec(
            num_scalar_prefetch=1,
            grid=(1,),
            in_specs=[pl.BlockSpec(mixer_terms.shape, lambda i, m: (0, 0, 0))]
            + [block((own, width)), block((own, 1)), block((own, width)), block((own, width))]
            + [fixed((1, width))] * 2
            + [fixed((1, 128))] * 2,
            out_specs=[fixed((own, width)), fixed((own, 1)), fixed((4, width))],
        ),
        out_shape=[
            jax.ShapeDtypeStruct((own, width), BF),
            jax.ShapeDtypeStruct((own, 1), F32),
            jax.ShapeDtypeStruct((4, width), F32),
        ],
        cost_estimate=cost_of(10),
        name="finish_rows",
    )(mine, mixer_terms, picked, gating, attended, grad_rows, gain_one, gain_two, square, routed_square)


def finish_input(terms, grad_rows, score, router, mine, ways):
    rows, width = grad_rows.shape
    own = rows // ways

    def kernel(mine_ref, terms_ref, rows_ref, score_ref, router_ref, out_ref):
        total = rows_ref[...].astype(F32) + score_ref[...] * router_ref[...].astype(F32)
        for k in range(ways):
            total = total + terms_ref[k].astype(F32)
        for k in range(ways):
            out_ref[k] = total.astype(BF)

    def fixed(shape):
        return pl.BlockSpec(shape, lambda i, m: (0,) * len(shape))

    return pl.pallas_call(
        kernel,
        grid_spec=pltpu.PrefetchScalarGridSpec(
            num_scalar_prefetch=1,
            grid=(1,),
            in_specs=[
                fixed((ways, own, width)),
                pl.BlockSpec((own, width), lambda i, m: (m[0], 0)),
                fixed((own, 1)),
                fixed((1, width)),
            ],
            out_specs=fixed((ways, own, width)),
        ),
        out_shape=jax.ShapeDtypeStruct((ways, own, width), BF),
        cost_estimate=small_cost(),
        name="finish_input",
    )(mine, terms, grad_rows, score, router)


def split_kept(count, order):
    keys = [0]
    for bit in reversed(order):
        keys = keys + [k ^ bit for k in keys]
    return keys


def per_device(
    tokens,
    route_offset,
    unit_sequence,
    cotangent,
    router_weight,
    first_gain,
    second_gain,
    qkv_weight,
    out_weight,
    up_weight,
    down_weight,
):
    rows_local, width = tokens.shape
    routed = route_offset.shape[1]
    ways = lax.axis_size("tensor")
    copies = lax.axis_size("dp")
    mine = lax.axis_index("tensor")
    part = lax.axis_index("dp")
    mine_array = jnp.reshape(mine, (1,)).astype(jnp.int32)
    part_array = jnp.reshape(part, (1,)).astype(jnp.int32)
    ladder = [1 << b for b in range(1, copies.bit_length() - 1)]
    order_a = [1] + ladder
    order_b = [1] + ladder[::-1]
    keys_a = split_kept(copies, order_a)
    keys_b = split_kept(copies, order_b)

    tie = lax.optimization_barrier
    own_rows = routed // ways
    heads_width = out_weight.shape[0]
    hidden = up_weight.shape[1]
    by_swaps = copies == 8
    bit_x, bit_y = 2, 4

    quarter = part & 3
    piece_rows = heads_width // 4
    piece = lax.dynamic_slice_in_dim(out_weight, quarter * piece_rows, piece_rows, 0)
    here = to_all(jnp.broadcast_to(piece[None], (ways,) + piece.shape))

    weight_row = router_weight[None]
    picked, square = pick_rows(tokens, route_offset, weight_row, mine_array, ways, small_cost(), 60)
    seq_column = unit_sequence.reshape(routed, 1)
    here, picked, square, seq_column = tie((here, picked, square, seq_column))
    beside = swap(here, "dp", bit_x)
    first_low, qkv, probs, head_out, gating, routed_square = attend(
        picked, first_gain[None], qkv_weight, unit_sequence, seq_column, weight_row, ways
    )
    beside, here, head_out = tie((beside, here, head_out))

    heads = to_all(head_out)
    across = swap(jnp.stack([here, beside]), "dp", 1)
    cotangent, head_out = tie((cotangent, head_out))
    grad_rows = pick_rows(cotangent, route_offset, None, mine_array, ways, small_cost(), 24)[0]
    grad_mixer, grad_act = act_grads(grad_rows, gating, down_weight)
    heads, across, grad_act, grad_mixer = tie((heads, across, grad_act, grad_mixer))
    attended, second_low, activated, grad_pre, hidden_part, attended_part, second_gain_part, head_sent = feed_forward(
        heads, here, beside, across, picked, second_gain[None], up_weight, grad_act, grad_mixer, part_array
    )

    head_terms = to_all(head_sent)
    if by_swaps:
        kept, leave_a, leave_b = core_grads(
            activated, grad_mixer, second_low, grad_pre, heads, attended_part, part_array, keys_a, keys_b
        )
        got_a, got_b = swap(leave_a, "dp", 1), swap(leave_b, "dp", 1)
        activated, kept = tie((activated, kept))
    else:
        down_part = dot(activated, grad_mixer, TN).astype(BF)
        up_part = dot(second_low, grad_pre, TN).astype(BF)
        out_parts = jnp.stack([dot(heads[k], attended_part, TN).astype(BF) for k in range(ways)])
    mixer_part = dot(activated, down_weight, NN).astype(BF).reshape(ways, own_rows, width)
    head_terms, mixer_part = tie((head_terms, mixer_part))

    mixer_terms = to_all(mixer_part)
    grad_head = sum_heads(head_terms)
    wide = hidden // 2
    narrow = heads_width * ways // 4
    if by_swaps:
        got_a, got_b, grad_head = tie((got_a, got_b, grad_head))
        kept, leave_a, leave_b = halving_sums(kept, got_a, got_b, wide, narrow)
        got_a, got_b = swap(leave_a, "dp", bit_x), swap(leave_b, "dp", bit_y)
        grad_head, kept = tie((grad_head, kept))
    grad_projected, first_gain_part, input_part = attend_back(
        grad_head, qkv, probs, qkv_weight, picked, first_gain[None], hidden_part
    )
    qkv_part = qkv_part_of(first_low, grad_projected)
    input_part = input_part.reshape(ways, own_rows, width)
    if by_swaps:
        qkv_got = swap(qkv_part, "dp", 1)
        got_a, got_b, qkv_part, input_part = tie((got_a, got_b, qkv_part, input_part))
        kept, leave_a, leave_b = halving_sums(kept, got_a, got_b, wide // 2, narrow // 2)
        got_a, got_b = swap(leave_a, "dp", bit_y), swap(leave_b, "dp", bit_x)
        mixer_terms, input_part, kept = tie((mixer_terms, input_part, kept))
    else:
        mixer_terms, input_part = tie((mixer_terms, input_part))

    input_terms = to_all(input_part)
    new_own, grad_score, small = finish_rows(
        mixer_terms,
        picked,
        gating,
        attended,
        grad_rows,
        first_gain_part,
        second_gain_part,
        square,
        routed_square,
        mine_array,
        ways,
    )
    if by_swaps:
        got_a, got_b, qkv_got, new_own, grad_score, small = tie((got_a, got_b, qkv_got, new_own, grad_score, small))
        lane_a, lane_b, sent = owned_sums(
            kept, got_a, got_b, qkv_part, qkv_got, new_own, small, wide // 4, ways
        )
        got_a, got_b = swap(lane_a, "dp", bit_y), swap(lane_b, "dp", bit_x)
    else:
        sent = jnp.concatenate([new_own, split_sums(small)])
        sent = jnp.broadcast_to(sent[None], (ways,) + sent.shape)
    input_terms, sent = tie((input_terms, sent))

    fresh = to_all(sent)
    last = finish_input(input_terms, grad_rows, grad_score, weight_row, mine_array, ways)
    if by_swaps:
        got_a, got_b, last = tie((got_a, got_b, last))
        lane_a, lane_b = gather_sums(lane_a, got_a, lane_b, got_b, wide // 4)
        got_a, got_b = swap(lane_a, "dp", bit_x), swap(lane_b, "dp", bit_y)
        fresh, last, lane_a = tie((fresh, last, lane_a))
    else:
        fresh, last = tie((fresh, last))

    input_rows = to_all(last)
    spots = jnp.stack([mine ^ k for k in range(ways)]).astype(jnp.int32)
    if by_swaps:
        blocks = first_small(fresh, own_rows)
        other = swap(blocks, "dp", bit_x)
        fresh, blocks = tie((fresh, blocks))
    output = merge_rows(tokens, route_offset, fresh, spots)
    if by_swaps:

        def gathered(order):
            keys = [0]
            for bit in order:
                keys = keys + [k ^ bit for k in keys]
            return jnp.stack([part ^ k for k in keys]).astype(jnp.int32)

        got_a, got_b, other, output = tie((got_a, got_b, other, output))
        half_blocks = wide // 2
        down_near, up_near = gather_blocks(lane_a, got_a, lane_b, got_b, half_blocks)
        down_far, up_far = swap(down_near, "dp", 1), swap(up_near, "dp", 1)
        blocks = join_small(blocks, other)
        other = swap(blocks, "dp", bit_y)
        lane_a, down_near, up_near, blocks = tie((lane_a, down_near, up_near, blocks))
        qkv_grad = spread_qkv(lane_a, got_a, lane_b, got_b, 2 * (wide // 4), qkv_weight.shape[2])
        other, qkv_grad = tie((other, qkv_grad))
        blocks = join_small(blocks, other)
        other = swap(blocks, "dp", 1)
        cotangent, blocks = tie((cotangent, blocks))
    early = merge_rows(cotangent, route_offset, last, spots[:1])
    if by_swaps:
        other, down_far, up_far, early = tie((other, down_far, up_far, early))
        out_grad, small = last_small(blocks, other, gathered([bit_x, bit_y, 1]))
        each = hidden // copies

        def by_block(array):
            return array.reshape(-1, each, width)

        down_grad, up_grad = spread_rows(
            by_block(down_near),
            by_block(down_far),
            by_block(up_near),
            by_block(up_far),
            gathered([bit_y, bit_x, 1]),
            gathered([bit_x, bit_y, 1]),
        )
        input_rows, early, down_grad, up_grad, out_grad = tie((input_rows, early, down_grad, up_grad, out_grad))
    input_grad = merge_rows(cotangent, route_offset, input_rows, spots[1:], early)
    if not by_swaps:
        small = sum(joined_sums(fresh[k, own_rows:]) for k in range(ways))
        small = lax.psum(small, "dp")
        down_grad, up_grad, qkv_sum, out_sum = (
            lax.psum(v, "dp").astype(F32) for v in (down_part, up_part, qkv_part, out_parts)
        )
        out_grad = jnp.sum(to_all(out_sum.astype(BF)).astype(F32), axis=0)
        qkv_grad = qkv_sum.reshape(3, -1, width).transpose(0, 2, 1)
    score_stats = jnp.stack([small[3, 0] / (rows_local * copies), small[3, 1] / (routed * copies)])
    return (
        output,
        input_grad,
        small[0],
        small[1],
        small[2],
        qkv_grad,
        out_grad,
        up_grad,
        down_grad,
        score_stats,
    )


def solution(mesh):
    placed = (
        P("dp", None),
        P("dp", None),
        P("dp", None),
        P("dp", None),
        P(),
        P(),
        P(),
        P(None, None, "tensor"),
        P("tensor", None),
        P(None, "tensor"),
        P("tensor", None),
    )
    return jax.shard_map(
        per_device,
        mesh=mesh,
        in_specs=placed,
        out_specs=(
            P("dp", None),
            P("dp", None),
            P(),
            P(),
            P(),
            P(None, None, "tensor"),
            P("tensor", None),
            P(None, "tensor"),
            P("tensor", None),
            P(),
        ),
        check_vma=False,
    )
```

```python
import jax
import jax.numpy as jnp
from jax import lax
from jax.experimental import pallas as pl
from jax.experimental.pallas import tpu as pltpu
from jax.sharding import PartitionSpec as P

BF = jnp.bfloat16
F32 = jnp.float32

NN = ((1,), (0,))
NT = ((1,), (1,))
TN = ((0,), (0,))


def dot(left, right, dims):
    return lax.dot_general(left, right, (dims, ((), ())), preferred_element_type=F32)


def swap(values, axis, bits):
    size = lax.axis_size(axis)
    return lax.ppermute(values, axis, [(i, i ^ bits) for i in range(size)])


def to_all(blocks):
    return lax.all_to_all(blocks, "tensor", 0, 0, tiled=True)


def inverse_rms(rows):
    return lax.rsqrt(jnp.mean(rows * rows, axis=-1, keepdims=True) + eps)


HEAD_DIM = 64
GROUP = 8
TERMS = 4
GAP = 2 * TERMS
eps = 1e-06
mask_fill = -1000000000.0


def small_cost():
    return pl.CostEstimate(flops=1024, bytes_accessed=1024, transcendentals=0)


def cost_of(microseconds):
    return pl.CostEstimate(flops=1024, bytes_accessed=int(microseconds * 3.0e6), transcendentals=0)


def staged(name, body, scalars, arrays, out_shapes, scratch, limit, cost):
    count, outs, extra = len(arrays), len(out_shapes), len(scalars)

    def kernel(*refs):
        scalar_refs, refs = refs[:extra], refs[extra:]
        in_refs, refs = refs[:count], refs[count:]
        out_refs, refs = refs[:outs], refs[outs:]
        held, refs = refs[:count], refs[count:]
        made, refs = refs[:outs], refs[outs:]
        load_sems, store_sems = refs[:2]
        loads = [pltpu.make_async_copy(s, h, load_sems.at[n]) for n, (s, h) in enumerate(zip(in_refs, held))]
        stores = [pltpu.make_async_copy(m, o, store_sems.at[n]) for n, (m, o) in enumerate(zip(made, out_refs))]
        for copy in loads:
            copy.start()
        here, gone = set(), set()

        def load(n):
            if n not in here:
                here.add(n)
                loads[n].wait()
            return held[n]

        def store(*which):
            for n in which:
                gone.add(n)
                stores[n].start()

        body(load, store, made, scalar_refs, refs[2:])
        for n in range(count):
            load(n)
        for n in range(outs):
            if n not in gone:
                store(n)
        for copy in stores:
            copy.wait()

    anywhere = pl.BlockSpec(memory_space=pl.ANY)
    return pl.pallas_call(
        kernel,
        in_specs=[pl.BlockSpec(memory_space=pltpu.SMEM)] * extra + [anywhere] * count,
        out_specs=[anywhere] * outs,
        out_shape=[jax.ShapeDtypeStruct(shape, kind) for shape, kind in out_shapes],
        scratch_shapes=[pltpu.VMEM(a.shape, a.dtype) for a in arrays]
        + [pltpu.VMEM(shape, kind) for shape, kind in out_shapes]
        + [pltpu.SemaphoreType.DMA((count,)), pltpu.SemaphoreType.DMA((outs,))]
        + scratch,
        cost_estimate=cost,
        compiler_params=pltpu.CompilerParams(vmem_limit_bytes=limit << 20),
        name=name,
    )(*scalars, *arrays)


def pick_rows(base, offsets, ways):
    rows, width = base.shape
    chunks = 2 * ways
    block = rows // chunks
    sub = 256
    sub_groups = sub // GROUP

    def kernel(base_ref, offset_ref, picked_ref, held, sems):
        def load(n):
            part = pl.ds(n * block, block)
            return pltpu.make_async_copy(base_ref.at[part], held.at[part], sems.at[n])

        for n in range(chunks):
            load(n).start()
        local = lax.broadcasted_iota(jnp.int32, (sub, sub_groups), 0) - GROUP * lax.broadcasted_iota(
            jnp.int32, (sub, sub_groups), 1
        )
        for n in range(chunks):
            load(n).wait()
            for s in range(n * block // sub, (n + 1) * block // sub):
                to = slice(s * sub_groups, (s + 1) * sub_groups)
                chosen = (local == offset_ref[:, to]).astype(F32).astype(BF)
                picked_ref[to, :] = dot(chosen, held[s * sub : (s + 1) * sub, :], TN).astype(BF)

    whole = pl.BlockSpec(memory_space=pltpu.VMEM)
    return pl.pallas_call(
        kernel,
        in_specs=[pl.BlockSpec(memory_space=pl.ANY), whole],
        out_specs=whole,
        out_shape=jax.ShapeDtypeStruct((rows // GROUP, width), BF),
        scratch_shapes=[pltpu.VMEM((rows, width), BF), pltpu.SemaphoreType.DMA((chunks,))],
        cost_estimate=small_cost(),
        compiler_params=pltpu.CompilerParams(vmem_limit_bytes=60 << 20),
        name="pick_rows",
    )(base, offsets)


def score_sums(base, router, mine, ways):
    rows, width = base.shape
    block = rows // ways

    def kernel(mine_ref, base_ref, router_ref, square_ref):
        score = jnp.sum(base_ref[...].astype(F32) * router_ref[...].astype(F32), axis=1, keepdims=True)
        square_ref[...] = jnp.broadcast_to(jnp.sum(score * score, axis=0, keepdims=True), square_ref.shape)

    return pl.pallas_call(
        kernel,
        grid_spec=pltpu.PrefetchScalarGridSpec(
            num_scalar_prefetch=1,
            grid=(1,),
            in_specs=[
                pl.BlockSpec((block, width), lambda i, m: (m[0], 0)),
                pl.BlockSpec((1, width), lambda i, m: (0, 0)),
            ],
            out_specs=pl.BlockSpec((1, 128), lambda i, m: (0, 0)),
        ),
        out_shape=jax.ShapeDtypeStruct((1, 128), F32),
        cost_estimate=small_cost(),
        name="score_sums",
    )(mine, base, router)


def pick_only(base, offsets, ways):
    rows, width = base.shape
    block = rows // ways
    groups = block // GROUP
    sub = 256
    sub_groups = sub // GROUP

    def kernel(base_ref, offset_ref, picked_ref):
        local = lax.broadcasted_iota(jnp.int32, (sub, sub_groups), 0) - GROUP * lax.broadcasted_iota(
            jnp.int32, (sub, sub_groups), 1
        )
        for s in range(block // sub):
            to = slice(s * sub_groups, (s + 1) * sub_groups)
            chosen = (local == offset_ref[:, to]).astype(F32).astype(BF)
            picked_ref[to, :] = dot(chosen, base_ref[s * sub : (s + 1) * sub, :], TN).astype(BF)

    return pl.pallas_call(
        kernel,
        grid=(ways,),
        in_specs=[pl.BlockSpec((block, width), lambda i: (i, 0)), pl.BlockSpec((1, groups), lambda i: (0, i))],
        out_specs=pl.BlockSpec((groups, width), lambda i: (i, 0)),
        out_shape=jax.ShapeDtypeStruct((rows // GROUP, width), BF),
        cost_estimate=small_cost(),
        name="pick_only",
    )(base, offsets)


def merge_rows(base, offsets, pieces, parts, held_out=None):
    rows, width = base.shape
    ways, depth, _ = pieces.shape
    count = rows // ways
    groups = count // GROUP
    kept = [] if held_out is None else [held_out]
    sub = 256
    sub_groups = sub // GROUP

    def kernel(part_ref, base_ref, offset_ref, piece_ref, *rest):
        out_ref = rest[-1]
        local = lax.broadcasted_iota(jnp.int32, (sub, sub_groups), 0) - GROUP * lax.broadcasted_iota(
            jnp.int32, (sub, sub_groups), 1
        )
        for s in range(count // sub):
            here = slice(s * sub, (s + 1) * sub)
            to = slice(s * sub_groups, (s + 1) * sub_groups)
            chosen = (local == offset_ref[:, to]).astype(F32)
            hit = jnp.sum(chosen, axis=1, keepdims=True) > 0.5
            spread = dot(chosen.astype(BF), piece_ref[0, to, :], NN)
            out_ref[here, :] = jnp.where(hit, spread, base_ref[here, :].astype(F32)).astype(BF)

    grid_spec = pltpu.PrefetchScalarGridSpec(
        num_scalar_prefetch=1,
        grid=(parts.shape[0],),
        in_specs=[
            pl.BlockSpec((count, width), lambda i, p: (p[i], 0)),
            pl.BlockSpec((1, groups), lambda i, p: (0, p[i])),
            pl.BlockSpec((1, depth, width), lambda i, p: (p[i], 0, 0)),
        ]
        + [pl.BlockSpec(memory_space=pl.ANY)] * len(kept),
        out_specs=pl.BlockSpec((count, width), lambda i, p: (p[i], 0)),
    )
    return pl.pallas_call(
        kernel,
        grid_spec=grid_spec,
        out_shape=jax.ShapeDtypeStruct((rows, width), BF),
        input_output_aliases={4: 0} if kept else {},
        cost_estimate=small_cost(),
        name="merge_rows",
    )(parts, base, offsets, pieces, *kept)


def attend(picked, gain, weight, seq_row, ways):
    rows, width = picked.shape
    heads_width = weight.shape[2]
    heads = heads_width // HEAD_DIM
    block = min(256, rows)

    def body(load, store, outs, scalars, scratch):
        low_ref, qkv_ref, probs_ref, out_ref = outs
        values = load(0)[...].astype(F32)
        low_ref[...] = (values * inverse_rms(values) * load(1)[...].astype(F32)).astype(BF)
        store(0)
        weight_ref = load(2)
        for n in range(3):
            qkv_ref[n] = dot(low_ref[...], weight_ref[n], NN).astype(BF)
        store(1)
        sequence = load(3)[...].astype(F32)
        column = jnp.broadcast_to(sequence, (128, rows)).T[:, :1]
        lane_head = lax.broadcasted_iota(jnp.int32, (1, heads_width), 1) // HEAD_DIM
        for start in range(0, rows, block):
            stop = start + block
            query = qkv_ref[0, start:stop, :] * BF(HEAD_DIM ** (-0.5))
            order = lax.broadcasted_iota(jnp.int32, (block, stop), 0) + start
            keys = lax.broadcasted_iota(jnp.int32, (block, stop), 1)
            allowed = (column[start:stop, :] == sequence[:, :stop]) & (order >= keys)
            total = jnp.zeros((block, heads_width), F32)
            for head in range(heads):
                here = lane_head == head
                key = jnp.where(here, qkv_ref[1, :stop, :], BF(0))
                logits = jnp.where(allowed, dot(query, key, NT), mask_fill)
                raised = jnp.exp(logits - jnp.max(logits, axis=-1, keepdims=True))
                probs = (raised * (1.0 / jnp.sum(raised, axis=-1, keepdims=True))).astype(BF)
                probs_ref[head, start:stop, :stop] = probs
                if stop < rows:
                    probs_ref[head, start:stop, stop:] = jnp.zeros((block, rows - stop), BF)
                value = jnp.where(here, qkv_ref[2, :stop, :], BF(0))
                total = total + dot(probs, value, NN)
            for k in range(ways):
                out_ref[k, start:stop, :] = total.astype(BF)

    return staged(
        "attend",
        body,
        [],
        [picked, gain, weight, seq_row],
        [
            ((rows, width), BF),
            ((3, rows, heads_width), BF),
            ((heads, rows, rows), BF),
            ((ways, rows, heads_width), BF),
        ],
        [],
        60,
        small_cost(),
    )


def feed_forward(heads, here, beside, across, picked, gain, up, grad_act, grad_mixer, part, mine, ways):
    rows, width = picked.shape
    hidden = up.shape[1]
    sub = min(256, hidden)
    count, _, heads_width = heads.shape
    piece = heads_width // 4
    own = rows // ways
    slope = 0.7978845608028654
    cubic = 0.044715

    def body(load, store, outs, scalars, scratch):
        part_ref, mine_ref = scalars
        attended_ref, low_ref, act_ref, pre_ref, hidden_ref, part_out_ref, gain_part_ref, sent_ref = outs
        total, state, weights = scratch
        quarter = part_ref[0] & 3
        heads_ref = load(0)
        here_ref, beside_ref, across_ref = load(1), load(2), load(3)
        for n, source in enumerate((here_ref, across_ref.at[0], beside_ref, across_ref.at[1])):
            start = pl.multiple_of((quarter ^ n) * piece, piece)
            for k in range(count):
                weights[k, pl.ds(start, piece), :] = source[k]
        attended = dot(heads_ref[0], weights[0], NN)
        for k in range(1, count):
            attended = attended + dot(heads_ref[k], weights[k], NN)
        total[...] = attended
        attended_ref[...] = total[pl.ds(pl.multiple_of(mine_ref[0] * own, own), own), :]
        state_in = load(4)[...].astype(F32) + attended
        state[...] = state_in
        gain_row = load(5)[...].astype(F32)
        low_ref[...] = (state_in * inverse_rms(state_in) * gain_row).astype(BF)
        store(0, 1)
        up_ref, act_grad_ref = load(6), load(7)
        for s in range(hidden // sub):
            lanes = slice(s * sub, (s + 1) * sub)
            value = dot(low_ref[...], up_ref[:, lanes], NN)
            square = value * value
            bent = jnp.tanh(value * (slope + (slope * cubic) * square))
            half = 0.5 * (1.0 + bent)
            act_ref[:, lanes] = (value * half).astype(BF)
            rise = half + (0.5 * value) * (1.0 - bent * bent) * (slope + (3.0 * slope * cubic) * square)
            pre = (act_grad_ref[:, lanes] * rise).astype(BF)
            pre_ref[:, lanes] = pre
            term = dot(pre, up_ref[:, lanes], NT)
            if s == 0:
                total[...] = term
            else:
                total[...] += term
        store(2, 3)
        state_in = state[...]
        grad = total[...]
        inverse = inverse_rms(state_in)
        normal = state_in * inverse
        gain_part_ref[...] = jnp.sum(grad * normal, axis=0, keepdims=True)
        scaled = grad * gain_row
        along = jnp.mean(scaled * normal, axis=-1, keepdims=True)
        back = inverse * (scaled - normal * along)
        hidden_ref[...] = back.astype(BF)
        part_out_ref[...] = (back + load(8)[...].astype(F32) * (1.0 / count)).astype(BF)
        store(4, 5, 6)
        for k in range(count):
            sent_ref[k] = dot(part_out_ref[...], weights[k], NT).astype(BF)

    return staged(
        "feed_forward",
        body,
        [part, mine],
        [heads, here, beside, across, picked, gain, up, grad_act, grad_mixer],
        [
            ((own, width), F32),
            ((rows, width), BF),
            ((rows, hidden), BF),
            ((rows, hidden), BF),
            ((rows, width), BF),
            ((rows, width), BF),
            ((1, width), F32),
            (heads.shape, BF),
        ],
        [
            pltpu.VMEM((rows, width), F32),
            pltpu.VMEM((rows, width), F32),
            pltpu.VMEM((count, heads_width, width), BF),
        ],
        60,
        small_cost(),
    )


def act_grads(picked, router, grad_rows, down):
    rows, width = grad_rows.shape

    def kernel(picked_ref, router_ref, rows_ref, down_ref, gating_ref, square_ref, mixer_ref, grad_ref):
        score = jnp.sum(picked_ref[...].astype(F32) * router_ref[...].astype(F32), axis=-1, keepdims=True)
        gating = jax.nn.sigmoid(score)
        gating_ref[...] = gating
        square_ref[...] = jnp.broadcast_to(jnp.sum(score * score, axis=0, keepdims=True), square_ref.shape)
        mixer_ref[...] = (gating * rows_ref[...].astype(F32)).astype(BF)
        grad_ref[...] = dot(mixer_ref[...], down_ref[...], NT)

    whole = pl.BlockSpec(memory_space=pltpu.VMEM)
    return pl.pallas_call(
        kernel,
        in_specs=[whole] * 4,
        out_specs=[whole] * 4,
        out_shape=[
            jax.ShapeDtypeStruct((rows, 1), F32),
            jax.ShapeDtypeStruct((1, 128), F32),
            jax.ShapeDtypeStruct((rows, width), BF),
            jax.ShapeDtypeStruct((rows, down.shape[0]), F32),
        ],
        cost_estimate=small_cost(),
        name="act_grads",
    )(picked, router, grad_rows, down)


def attend_back(head_terms, qkv, probs, weight, picked, gain, hidden_part):
    rows, width = picked.shape
    heads_width = weight.shape[2]
    heads = heads_width // HEAD_DIM
    block = min(256, rows)
    scale = HEAD_DIM ** (-0.5)

    def kernel(
        head_ref,
        qkv_ref,
        probs_ref,
        weight_ref,
        picked_ref,
        gain_ref,
        hidden_ref,
        grads_ref,
        gain_part_ref,
        result,
        grad_key,
        grad_value,
    ):
        lane_head = lax.broadcasted_iota(jnp.int32, (1, heads_width), 1) // HEAD_DIM
        for start in reversed(range(0, rows, block)):
            stop = start + block
            here_rows = slice(start, stop)
            grad_head = head_ref[0, here_rows, :].astype(F32)
            for k in range(1, head_ref.shape[0]):
                grad_head = grad_head + head_ref[k, here_rows, :].astype(F32)
            grad_head = grad_head.astype(BF)
            query = qkv_ref[0, here_rows, :] * BF(scale)
            grad_query = jnp.zeros((block, heads_width), F32)
            add_key = jnp.zeros((stop, heads_width), F32)
            add_value = jnp.zeros((stop, heads_width), F32)
            for head in range(heads):
                here = lane_head == head
                value = jnp.where(here, qkv_ref[2, :stop, :], BF(0))
                key = jnp.where(here, qkv_ref[1, :stop, :], BF(0))
                low = probs_ref[head, here_rows, :stop]
                weighted = low.astype(F32) * dot(grad_head, value, NT)
                row_sum = jnp.sum(weighted, axis=-1, keepdims=True)
                slopes = (weighted - low.astype(F32) * row_sum).astype(BF)
                grad_query = grad_query + dot(slopes, key, NN)
                add_key = add_key + dot(slopes, jnp.where(here, query, BF(0)), TN)
                add_value = add_value + dot(low, jnp.where(here, grad_head, BF(0)), TN)
            grads_ref[0, here_rows, :] = (grad_query * scale).astype(BF)
            if stop == rows:
                grad_key[...] = add_key
                grad_value[...] = add_value
            else:
                grad_key[:stop, :] += add_key
                grad_value[:stop, :] += add_value
        grads_ref[1] = grad_key[...].astype(BF)
        grads_ref[2] = grad_value[...].astype(BF)
        first = dot(grads_ref[0], weight_ref[0], NT)
        for n in range(1, 3):
            first = first + dot(grads_ref[n], weight_ref[n], NT)
        values = picked_ref[...].astype(F32)
        inverse = inverse_rms(values)
        normal = values * inverse
        gain_part_ref[...] = jnp.sum(first * normal, axis=0, keepdims=True)
        scaled = first * gain_ref[...].astype(F32)
        along = jnp.mean(scaled * normal, axis=-1, keepdims=True)
        result[...] = (hidden_ref[...].astype(F32) + inverse * (scaled - normal * along)).astype(BF)

    whole = pl.BlockSpec(memory_space=pltpu.VMEM)
    return pl.pallas_call(
        kernel,
        in_specs=[whole] * 7,
        out_specs=[whole] * 3,
        out_shape=[
            jax.ShapeDtypeStruct((3, rows, heads_width), BF),
            jax.ShapeDtypeStruct((1, width), F32),
            jax.ShapeDtypeStruct((rows, width), BF),
        ],
        scratch_shapes=[
            pltpu.VMEM((rows, heads_width), F32),
            pltpu.VMEM((rows, heads_width), F32),
        ],
        cost_estimate=small_cost(),
        compiler_params=pltpu.CompilerParams(vmem_limit_bytes=20 << 20),
        name="attend_back",
    )(head_terms, qkv, probs, weight, picked, gain, hidden_part)


def spread_rows(down_near, down_far, up_near, up_far, index_down, index_up):
    half, rows, width = down_near.shape

    def kernel(down_index, up_index, down_ref, far_ref, up_ref, up_far_ref, down_out, up_out):
        near = pl.program_id(0) < half

        @pl.when(near)
        def _():
            down_out[...] = down_ref[0].astype(F32)
            up_out[...] = up_ref[0].astype(F32)

        @pl.when(jnp.logical_not(near))
        def _():
            down_out[...] = far_ref[0].astype(F32)
            up_out[...] = up_far_ref[0].astype(F32)

    first = pl.BlockSpec((1, rows, width), lambda i, d, u: (jnp.minimum(i, half - 1), 0, 0))
    second = pl.BlockSpec((1, rows, width), lambda i, d, u: (jnp.maximum(i - half, 0), 0, 0))
    return pl.pallas_call(
        kernel,
        grid_spec=pltpu.PrefetchScalarGridSpec(
            num_scalar_prefetch=2,
            grid=(2 * half,),
            in_specs=[first, second, first, second],
            out_specs=[
                pl.BlockSpec((rows, width), lambda i, d, u: (d[i], 0)),
                pl.BlockSpec((rows, width), lambda i, d, u: (u[i], 0)),
            ],
        ),
        out_shape=[jax.ShapeDtypeStruct((2 * half * rows, width), F32)] * 2,
        cost_estimate=small_cost(),
        name="spread_rows",
    )(index_down, index_up, down_near, down_far, up_near, up_far)


def qkv_part_of(first_low, grads):
    rows, width = first_low.shape
    part_width = grads.shape[2]

    def kernel(low_ref, grads_ref, out_ref):
        for n in range(3):
            product = dot(grads_ref[n], low_ref[...], TN)
            out_ref[n * part_width : (n + 1) * part_width, :] = product.astype(BF)

    whole = pl.BlockSpec(memory_space=pltpu.VMEM)
    return pl.pallas_call(
        kernel,
        in_specs=[whole] * 2,
        out_specs=whole,
        out_shape=jax.ShapeDtypeStruct((3 * part_width, width), BF),
        cost_estimate=small_cost(),
        name="qkv_part",
    )(first_low, grads)


def spread_qkv(lane_a, got_a, lane_b, got_b, part_width):
    rows, width = lane_a.shape
    tile = 128

    def kernel(a_ref, a_got, b_ref, b_got, out_ref):
        for n in range(2 * rows // tile):
            start = n * tile % rows
            ref, got = (a_ref, a_got) if n * tile < rows else (b_ref, b_got)
            lane, column = divmod(n * tile, part_width)
            piece = ref[start : start + tile, :].astype(F32) + got[start : start + tile, :].astype(F32)
            out_ref[lane, :, column : column + tile] = piece.T

    whole = pl.BlockSpec(memory_space=pltpu.VMEM)
    return pl.pallas_call(
        kernel,
        in_specs=[whole] * 4,
        out_specs=whole,
        out_shape=jax.ShapeDtypeStruct((2 * rows // part_width, width, part_width), F32),
        cost_estimate=small_cost(),
        compiler_params=pltpu.CompilerParams(vmem_limit_bytes=16 << 20),
        name="spread_qkv",
    )(lane_a, got_a, lane_b, got_b)


def core_grads(activated, grad_mixer, second_low, grad_pre, heads, attended_part, part, keys_a, keys_b):
    rows, hidden = activated.shape
    width = grad_mixer.shape[1]
    copies = len(keys_a)
    half = copies // 2
    count, _, heads_width = heads.shape
    block = hidden // copies
    small = heads_width // copies
    many = count // 2
    depth = half * (block + many * small)

    def kernel(part_ref, act_ref, mixer_ref, low_ref, pre_ref, heads_ref, term_ref, keep_ref, *rest):
        wide_refs, narrow_refs, (full, narrow) = rest[0:2], rest[2:4], rest[4:]

        def place(source, each, lane, keys, first, stride):
            for n, key in enumerate(keys):
                start = pl.multiple_of((part_ref[0] ^ key) * each, each)
                at = first + (n % half) * stride
                piece = source[pl.ds(start, each), :]
                if n < half:
                    keep_ref[lane, at : at + each, :] = piece
                elif first == 0:
                    wide_refs[lane][at : at + each, :] = piece
                else:
                    narrow_refs[lane][at - half * block : at - half * block + each, :] = piece

        full[...] = dot(act_ref[...], mixer_ref[...], TN).astype(BF)
        place(full, block, 0, keys_a, 0, block)
        full[...] = dot(low_ref[...], pre_ref[...], TN).astype(BF)
        place(full, block, 1, keys_b, 0, block)
        for k in range(count):
            narrow[...] = dot(heads_ref[k], term_ref[...], TN).astype(BF)
            lane, spot = divmod(k, many)
            place(narrow, small, lane, keys_b if lane else keys_a, half * block + spot * small, many * small)

    whole = pl.BlockSpec(memory_space=pltpu.VMEM)
    wide_shape = jax.ShapeDtypeStruct((half * block, width), BF)
    narrow_shape = jax.ShapeDtypeStruct((half * many * small, width), BF)
    return pl.pallas_call(
        kernel,
        in_specs=[pl.BlockSpec(memory_space=pltpu.SMEM)] + [whole] * 6,
        out_specs=[whole] * 5,
        out_shape=[jax.ShapeDtypeStruct((2, depth, width), BF)] + [wide_shape] * 2 + [narrow_shape] * 2,
        scratch_shapes=[pltpu.VMEM((hidden, width), BF), pltpu.VMEM((heads_width, width), BF)],
        cost_estimate=small_cost(),
        compiler_params=pltpu.CompilerParams(vmem_limit_bytes=14 << 20),
        name="core_grads",
    )(part, activated, grad_mixer, second_low, grad_pre, heads, attended_part)


def plus(left, right):
    return (left.astype(F32) + right.astype(F32)).astype(BF)


def halving_sums(keep, got_a, got_b, wide, narrow):
    width = keep.shape[2]
    count = len(got_a)

    def kernel(keep_ref, *refs):
        a_got, b_got, (stay_ref, a_out, b_out) = refs[:count], refs[count : 2 * count], refs[2 * count :]
        for lane, got, out in ((0, a_got, a_out), (1, b_got, b_out)):
            for first, size, at in ((0, wide // 2, 0), (wide, narrow // 2, wide // 2)):
                source, shift = (got[1], wide) if count == 2 and first else (got[0], 0)
                to = slice(at, at + size)
                for start, target in ((first, stay_ref.at[lane]), (first + size, out)):
                    here = slice(start - shift, start - shift + size)
                    target[to, :] = plus(keep_ref[lane, start : start + size, :], source[here, :])

    whole = pl.BlockSpec(memory_space=pltpu.VMEM)
    depth = (wide + narrow) // 2
    lane_shape = jax.ShapeDtypeStruct((depth, width), BF)
    return pl.pallas_call(
        kernel,
        in_specs=[whole] * (1 + 2 * count),
        out_specs=[whole] * 3,
        out_shape=[jax.ShapeDtypeStruct((2, depth, width), BF), lane_shape, lane_shape],
        cost_estimate=small_cost(),
        compiler_params=pltpu.CompilerParams(vmem_limit_bytes=14 << 20),
        name="halving_sums",
    )(keep, *got_a, *got_b)


def owned_sums(keep, got_a, got_b, fresh, small, wide, ways):
    width = keep.shape[2]
    narrow = keep.shape[1] - wide
    own = fresh.shape[0]
    many = ways // 2
    each = narrow // many
    depth = own + GAP + each

    def kernel(keep_ref, a_got, b_got, fresh_ref, small_ref, a_out, b_out, sent_ref):
        sums = split_sums(small_ref[...])
        for lane, got, out in ((0, a_got, a_out), (1, b_got, b_out)):
            out[...] = plus(keep_ref[lane, :wide, :], got[:wide, :])
            done = plus(keep_ref[lane, wide:, :], got[wide:, :])
            for spot in range(many):
                k = lane * many + spot
                sent_ref[k, :own, :] = fresh_ref[...]
                sent_ref[k, own : own + GAP, :] = sums
                sent_ref[k, own + GAP :, :] = done[spot * each : (spot + 1) * each, :]

    whole = pl.BlockSpec(memory_space=pltpu.VMEM)
    lane_shape = jax.ShapeDtypeStruct((wide, width), BF)
    return pl.pallas_call(
        kernel,
        in_specs=[whole] * 5,
        out_specs=[whole] * 3,
        out_shape=[lane_shape, lane_shape, jax.ShapeDtypeStruct((ways, depth, width), BF)],
        cost_estimate=small_cost(),
        name="owned_sums",
    )(keep, got_a, got_b, fresh, small)


def core_sums(rows, other):
    depth, width = rows.shape
    third = depth // 2

    def kernel(rows_ref, other_ref, a_out, b_out):
        a_out[...] = plus(rows_ref[:third, :], other_ref[:third, :])
        b_out[...] = plus(rows_ref[third:, :], other_ref[third:, :])

    whole = pl.BlockSpec(memory_space=pltpu.VMEM)
    return pl.pallas_call(
        kernel,
        in_specs=[whole] * 2,
        out_specs=[whole] * 2,
        out_shape=[jax.ShapeDtypeStruct((third, width), BF)] * 2,
        cost_estimate=small_cost(),
        name="core_sums",
    )(rows, other)


def lane_sums(lane_a, got_a, lane_b, got_b):
    def kernel(a_ref, a_got, b_ref, b_got, a_out, b_out):
        a_out[...] = plus(a_ref[...], a_got[...])
        b_out[...] = plus(b_ref[...], b_got[...])

    whole = pl.BlockSpec(memory_space=pltpu.VMEM)
    return pl.pallas_call(
        kernel,
        in_specs=[whole] * 4,
        out_specs=[whole] * 2,
        out_shape=[jax.ShapeDtypeStruct(lane_a.shape, BF)] * 2,
        cost_estimate=small_cost(),
        name="lane_sums",
    )(lane_a, got_a, lane_b, got_b)


def gather_blocks(blocks_a, blocks_b):
    wide, width = blocks_a[0].shape
    count = len(blocks_a)

    def kernel(*refs):
        for lane in range(2):
            for n in range(count):
                refs[2 * count + lane][n * wide : (n + 1) * wide, :] = refs[lane * count + n][...]

    whole = pl.BlockSpec(memory_space=pltpu.VMEM)
    return pl.pallas_call(
        kernel,
        in_specs=[whole] * (2 * count),
        out_specs=[whole] * 2,
        out_shape=[jax.ShapeDtypeStruct((count * wide, width), BF)] * 2,
        cost_estimate=small_cost(),
        name="gather_blocks",
    )(*blocks_a, *blocks_b)


def split_sums(values):
    high = values.astype(BF)
    low = (values - high.astype(F32)).astype(BF)
    return jnp.concatenate([high, low], axis=0)


def joined_sums(rows):
    return rows[:TERMS].astype(F32) + rows[TERMS : 2 * TERMS].astype(F32)


def first_small(received, own):
    ways, depth, width = received.shape
    each = depth - own - GAP

    def kernel(got_ref, out_ref):
        total = got_ref[0, own + GAP :, :].astype(F32)
        sums = joined_sums(got_ref[0, own : own + GAP, :])
        for k in range(1, ways):
            total = total + got_ref[k, own + GAP :, :].astype(F32)
            sums = sums + joined_sums(got_ref[k, own : own + GAP, :])
        out_ref[:each, :] = total.astype(BF)
        out_ref[each:, :] = split_sums(sums)

    whole = pl.BlockSpec(memory_space=pltpu.VMEM)
    return pl.pallas_call(
        kernel,
        in_specs=[whole],
        out_specs=whole,
        out_shape=jax.ShapeDtypeStruct((each + GAP, width), BF),
        cost_estimate=small_cost(),
        name="first_small",
    )(received)


def last_small(blocks, index, shares):
    depth, width = blocks[0].shape
    each = depth - GAP
    count = len(blocks)

    def kernel(index_ref, *refs):
        out_ref, small_refs = refs[count], refs[count + 1 :]
        total = joined_sums(refs[0][each:, :])
        for n in range(1, count):
            total = total + joined_sums(refs[n][each:, :])
        for n in range(TERMS - 1):
            small_refs[n][...] = total[n : n + 1, :]
        lane = lax.broadcasted_iota(jnp.int32, (1, 128), 1)
        small_refs[TERMS - 1][...] = total[TERMS - 1 :, :128] * jnp.where(lane == 0, shares[0], shares[1])
        for n in range(count):
            start = pl.multiple_of(index_ref[n] * each, each)
            out_ref[pl.ds(start, each), :] = refs[n][:each, :].astype(F32)

    whole = pl.BlockSpec(memory_space=pltpu.VMEM)
    return pl.pallas_call(
        kernel,
        in_specs=[pl.BlockSpec(memory_space=pltpu.SMEM)] + [whole] * count,
        out_specs=[whole] * (1 + TERMS),
        out_shape=[jax.ShapeDtypeStruct((count * each, width), F32)] + [jax.ShapeDtypeStruct((1, width), F32)] * (TERMS - 1)
        + [jax.ShapeDtypeStruct((1, 128), F32)],
        cost_estimate=small_cost(),
        name="last_small",
    )(index, *blocks)


def finish_rows(mixer_terms, picked, gating, attended, grad_rows, gain_one, gain_two, square, routed_square, mine, ways):
    rows, width = picked.shape
    own = rows // ways

    def kernel(
        mine_ref,
        terms_ref,
        picked_ref,
        gating_ref,
        attended_ref,
        rows_ref,
        one_ref,
        two_ref,
        square_ref,
        routed_ref,
        new_ref,
        score_ref,
        small_ref,
    ):
        branch = attended_ref[...]
        for k in range(ways):
            branch = branch + terms_ref[k].astype(F32)
        values = picked_ref[...].astype(F32)
        gate = gating_ref[...]
        new_ref[...] = (values + gate * branch).astype(BF)
        along = jnp.sum(rows_ref[...].astype(F32) * branch, axis=-1, keepdims=True)
        score = along * gate * (1.0 - gate)
        score_ref[...] = score
        small_ref[0:1, :] = jnp.sum(score * values, axis=0, keepdims=True)
        small_ref[1:2, :] = one_ref[...]
        small_ref[2:3, :] = two_ref[...]
        lane = lax.broadcasted_iota(jnp.int32, (1, width), 1)
        both = jnp.where(lane == 0, square_ref[:, 0:1], routed_ref[:, 0:1] * (1.0 / ways))
        small_ref[3:4, :] = jnp.where(lane < 2, both, 0.0)

    def block(shape):
        return pl.BlockSpec(shape, lambda i, m: (m[0], 0))

    def fixed(shape):
        return pl.BlockSpec(shape, lambda i, m: (0, 0))

    return pl.pallas_call(
        kernel,
        grid_spec=pltpu.PrefetchScalarGridSpec(
            num_scalar_prefetch=1,
            grid=(1,),
            in_specs=[pl.BlockSpec(mixer_terms.shape, lambda i, m: (0, 0, 0))]
            + [block((own, width)), block((own, 1)), fixed((own, width)), block((own, width))]
            + [fixed((1, width))] * 2
            + [fixed((1, 128))] * 2,
            out_specs=[fixed((own, width)), fixed((own, 1)), fixed((4, width))],
        ),
        out_shape=[
            jax.ShapeDtypeStruct((own, width), BF),
            jax.ShapeDtypeStruct((own, 1), F32),
            jax.ShapeDtypeStruct((4, width), F32),
        ],
        cost_estimate=cost_of(10),
        name="finish_rows",
    )(mine, mixer_terms, picked, gating, attended, grad_rows, gain_one, gain_two, square, routed_square)


def finish_input(terms, grad_rows, score, router, mine, ways):
    rows, width = grad_rows.shape
    own = rows // ways

    def kernel(mine_ref, terms_ref, rows_ref, score_ref, router_ref, out_ref):
        total = rows_ref[...].astype(F32) + score_ref[...] * router_ref[...].astype(F32)
        for k in range(ways):
            total = total + terms_ref[k].astype(F32)
        for k in range(ways):
            out_ref[k] = total.astype(BF)

    def fixed(shape):
        return pl.BlockSpec(shape, lambda i, m: (0,) * len(shape))

    return pl.pallas_call(
        kernel,
        grid_spec=pltpu.PrefetchScalarGridSpec(
            num_scalar_prefetch=1,
            grid=(1,),
            in_specs=[
                fixed((ways, own, width)),
                pl.BlockSpec((own, width), lambda i, m: (m[0], 0)),
                fixed((own, 1)),
                fixed((1, width)),
            ],
            out_specs=fixed((ways, own, width)),
        ),
        out_shape=jax.ShapeDtypeStruct((ways, own, width), BF),
        cost_estimate=small_cost(),
        name="finish_input",
    )(mine, terms, grad_rows, score, router)


def split_kept(count, order):
    keys = [0]
    for bit in reversed(order):
        keys = keys + [k ^ bit for k in keys]
    return keys


def per_device(
    tokens,
    route_offset,
    unit_sequence,
    cotangent,
    router_weight,
    first_gain,
    second_gain,
    qkv_weight,
    out_weight,
    up_weight,
    down_weight,
):
    rows_local, width = tokens.shape
    routed = route_offset.shape[1]
    ways = lax.axis_size("tensor")
    copies = lax.axis_size("dp")
    mine = lax.axis_index("tensor")
    part = lax.axis_index("dp")
    mine_array = jnp.reshape(mine, (1,)).astype(jnp.int32)
    part_array = jnp.reshape(part, (1,)).astype(jnp.int32)
    ladder = [1 << b for b in range(1, copies.bit_length() - 1)]
    order_a = [1] + ladder
    order_b = [1] + ladder[::-1]
    keys_a = split_kept(copies, order_a)
    keys_b = split_kept(copies, order_b)

    tie = lax.optimization_barrier
    own_rows = routed // ways
    heads_width = out_weight.shape[0]
    hidden = up_weight.shape[1]
    by_swaps = copies == 8
    bit_x, bit_y = 2, 4
    shares = (1.0 / (rows_local * copies), 1.0 / (routed * copies))

    quarter = part & 3
    piece_rows = heads_width // 4
    piece = lax.dynamic_slice_in_dim(out_weight, quarter * piece_rows, piece_rows, 0)
    here = to_all(jnp.broadcast_to(piece[None], (ways,) + piece.shape))

    picked = pick_rows(tokens, route_offset, ways)
    first_low, qkv, probs, head_out = attend(picked, first_gain[None], qkv_weight, unit_sequence, ways)
    here, head_out = tie((here, head_out))

    heads = to_all(head_out)
    beside = swap(here, "dp", bit_x)
    cotangent, router_weight, second_gain, here, head_out = tie(
        (cotangent, router_weight, second_gain, here, head_out)
    )
    weight_row = router_weight[None]
    grad_rows = pick_only(cotangent, route_offset, ways)
    beside, here, grad_rows = tie((beside, here, grad_rows))
    across = swap(jnp.stack([here, beside]), "dp", 1)
    gating, routed_square, grad_mixer, grad_act = act_grads(picked, weight_row, grad_rows, down_weight)
    square = score_sums(tokens, weight_row, mine_array, ways)
    heads, across, grad_act, grad_mixer, square = tie((heads, across, grad_act, grad_mixer, square))
    attended, second_low, activated, grad_pre, hidden_part, attended_part, second_gain_part, head_sent = feed_forward(
        heads,
        here,
        beside,
        across,
        picked,
        second_gain[None],
        up_weight,
        grad_act,
        grad_mixer,
        part_array,
        mine_array,
        ways,
    )

    head_terms = to_all(head_sent)
    wide = hidden // 2
    narrow = heads_width * ways // 4
    if by_swaps:
        kept, *leaving = core_grads(
            activated, grad_mixer, second_low, grad_pre, heads, attended_part, part_array, keys_a, keys_b
        )
        wide_a, wide_b, narrow_a, narrow_b = (swap(array, "dp", 1) for array in leaving)
        activated, kept = tie((activated, kept))
    else:
        down_part = dot(activated, grad_mixer, TN).astype(BF)
        up_part = dot(second_low, grad_pre, TN).astype(BF)
        out_parts = jnp.stack([dot(heads[k], attended_part, TN).astype(BF) for k in range(ways)])
    mixer_part = dot(activated, down_weight, NN).astype(BF).reshape(ways, own_rows, width)
    if by_swaps:
        wide_a, wide_b, narrow_a, narrow_b, mixer_part = tie((wide_a, wide_b, narrow_a, narrow_b, mixer_part))
        kept, leave_a, leave_b = halving_sums(kept, (wide_a, narrow_a), (wide_b, narrow_b), wide, narrow)
        got_a, got_b = swap(leave_a, "dp", bit_x), swap(leave_b, "dp", bit_y)
        head_terms, mixer_part, kept = tie((head_terms, mixer_part, kept))
    else:
        head_terms, mixer_part = tie((head_terms, mixer_part))

    mixer_terms = to_all(mixer_part)
    grad_projected, first_gain_part, input_part = attend_back(
        head_terms, qkv, probs, qkv_weight, picked, first_gain[None], hidden_part
    )
    qkv_part = qkv_part_of(first_low, grad_projected)
    input_part = input_part.reshape(ways, own_rows, width)
    if by_swaps:
        got_a, got_b, qkv_part, input_part = tie((got_a, got_b, qkv_part, input_part))
        kept, leave_a, leave_b = halving_sums(kept, (got_a,), (got_b,), wide // 2, narrow // 2)
        mixer_terms, input_part, qkv_part, kept, leave_a, leave_b = tie(
            (mixer_terms, input_part, qkv_part, kept, leave_a, leave_b)
        )
    else:
        mixer_terms, input_part, qkv_part = tie((mixer_terms, input_part, qkv_part))

    input_terms = to_all(input_part)
    if by_swaps:
        got_a, got_b = swap(leave_a, "dp", bit_y), swap(leave_b, "dp", bit_x)
        qkv_got = swap(qkv_part, "dp", 1)
    new_own, grad_score, small = finish_rows(
        mixer_terms,
        picked,
        gating,
        attended,
        grad_rows,
        first_gain_part,
        second_gain_part,
        square,
        routed_square,
        mine_array,
        ways,
    )
    if by_swaps:
        got_a, got_b, new_own = tie((got_a, got_b, new_own))
        lane_a, lane_b, sent = owned_sums(kept, got_a, got_b, new_own, small, wide // 4, ways)
        got_a, got_b = swap(lane_a, "dp", bit_y), swap(lane_b, "dp", bit_x)
        qkv_part, qkv_got, lane_a, lane_b, sent = tie((qkv_part, qkv_got, lane_a, lane_b, sent))
        qkv_a, qkv_b = core_sums(qkv_part, qkv_got)
        input_terms, sent, got_a, got_b, qkv_a, qkv_b = tie((input_terms, sent, got_a, got_b, qkv_a, qkv_b))
    else:
        sent = jnp.concatenate([new_own, split_sums(small)])
        sent = jnp.broadcast_to(sent[None], (ways,) + sent.shape)
        input_terms, sent = tie((input_terms, sent))

    fresh = to_all(sent)
    if by_swaps:
        more_a = [swap(array, "dp", bit_x) for array in (lane_a, got_a)]
        more_b = [swap(array, "dp", bit_y) for array in (lane_b, got_b)]
    last = finish_input(input_terms, grad_rows, grad_score, weight_row, mine_array, ways)
    spots = jnp.stack([mine ^ k for k in range(ways)]).astype(jnp.int32)
    cotangent, last = tie((cotangent, last))
    early = merge_rows(cotangent, route_offset, last, spots[:1])
    if by_swaps:
        more_a, more_b, early, qkv_a, qkv_b = tie((more_a, more_b, early, qkv_a, qkv_b))
        qkv_a_got, qkv_b_got = swap(qkv_a, "dp", bit_y), swap(qkv_b, "dp", bit_x)
        down_near, up_near = gather_blocks([lane_a, got_a] + more_a, [lane_b, got_b] + more_b)
        down_far, up_far = swap(down_near, "dp", 1), swap(up_near, "dp", 1)

        def gathered(order):
            keys = [0]
            for bit in order:
                keys = keys + [k ^ bit for k in keys]
            return jnp.stack([part ^ k for k in keys]).astype(jnp.int32)

        each = hidden // copies

        def by_block(array):
            return array.reshape(-1, each, width)

        down_grad, up_grad = spread_rows(
            by_block(down_near),
            by_block(down_far),
            by_block(up_near),
            by_block(up_far),
            gathered([bit_y, bit_x, 1]),
            gathered([bit_x, bit_y, 1]),
        )
        fresh, last, down_grad, up_grad = tie((fresh, last, down_grad, up_grad))
    else:
        fresh, last = tie((fresh, last))

    input_rows = to_all(last)
    if by_swaps:
        blocks = [first_small(fresh, own_rows)]
        more = [swap(array, "dp", bit_x) for array in blocks]
        qkv_a_got, qkv_b_got, blocks = tie((qkv_a_got, qkv_b_got, blocks))
        qkv_a, qkv_b = lane_sums(qkv_a, qkv_a_got, qkv_b, qkv_b_got)
        more, qkv_a, qkv_b = tie((more, qkv_a, qkv_b))
        blocks = blocks + more
        more = [swap(array, "dp", bit_y) for array in blocks]
        more, qkv_a, qkv_b = tie((more, qkv_a, qkv_b))
        qkv_a_got, qkv_b_got = swap(qkv_a, "dp", bit_x), swap(qkv_b, "dp", bit_y)
        blocks = blocks + more
        more = [swap(array, "dp", 1) for array in blocks]
        fresh, qkv_a, qkv_b, blocks = tie((fresh, qkv_a, qkv_b, blocks))
    output = merge_rows(tokens, route_offset, fresh, spots)
    if by_swaps:
        more, output = tie((more, output))
        out_grad, *small = last_small(blocks + more, gathered([bit_x, bit_y, 1]), shares)
        qkv_a_got, qkv_b_got, out_grad = tie((qkv_a_got, qkv_b_got, out_grad))
        qkv_grad = spread_qkv(qkv_a, qkv_a_got, qkv_b, qkv_b_got, qkv_weight.shape[2])
        input_rows, early, out_grad, small, output, qkv_grad = tie(
            (input_rows, early, out_grad, small, output, qkv_grad)
        )
    input_grad = merge_rows(cotangent, route_offset, input_rows, spots[1:], early)
    if not by_swaps:
        small = sum(joined_sums(fresh[k, own_rows:]) for k in range(ways))
        small = lax.psum(small, "dp")
        small = [small[n : n + 1] for n in range(TERMS)]
        small[3] = small[3][:, :128] * jnp.array((shares + (0.0,) * 126,), F32)
        down_grad, up_grad, qkv_sum, out_sum = (
            lax.psum(v, "dp").astype(F32) for v in (down_part, up_part, qkv_part, out_parts)
        )
        out_grad = jnp.sum(to_all(out_sum.astype(BF)).astype(F32), axis=0)
        qkv_grad = qkv_sum.reshape(3, -1, width).transpose(0, 2, 1)
    router_grad, first_gain_grad, second_gain_grad = (small[n].reshape(width) for n in range(3))
    score_stats = small[3][0, :2]
    return (
        output,
        input_grad,
        router_grad,
        first_gain_grad,
        second_gain_grad,
        qkv_grad,
        out_grad,
        up_grad,
        down_grad,
        score_stats,
    )


def solution(mesh):
    placed = (
        P("dp", None),
        P("dp", None),
        P("dp", None),
        P("dp", None),
        P(),
        P(),
        P(),
        P(None, None, "tensor"),
        P("tensor", None),
        P(None, "tensor"),
        P("tensor", None),
    )
    return jax.shard_map(
        per_device,
        mesh=mesh,
        in_specs=placed,
        out_specs=(
            P("dp", None),
            P("dp", None),
            P(),
            P(),
            P(),
            P(None, None, "tensor"),
            P("tensor", None),
            P(None, "tensor"),
            P("tensor", None),
            P(),
        ),
        check_vma=False,
    )
```

```python
import jax
import jax.numpy as jnp
from jax import lax
from jax.experimental import pallas as pl
from jax.experimental.pallas import tpu as pltpu
from jax.sharding import PartitionSpec as P

BF = jnp.bfloat16
F32 = jnp.float32

NN = ((1,), (0,))
NT = ((1,), (1,))
TN = ((0,), (0,))


def dot(left, right, dims):
    return lax.dot_general(left, right, (dims, ((), ())), preferred_element_type=F32)


def swap(values, axis, bits):
    size = lax.axis_size(axis)
    return lax.ppermute(values, axis, [(i, i ^ bits) for i in range(size)])


def to_all(blocks):
    return lax.all_to_all(blocks, "tensor", 0, 0, tiled=True)


def inverse_rms(rows):
    return lax.rsqrt(jnp.mean(rows * rows, axis=-1, keepdims=True) + eps)


HEAD_DIM = 64
GROUP = 8
TERMS = 4
GAP = 2 * TERMS
eps = 1e-06
mask_fill = -1000000000.0


def small_cost():
    return pl.CostEstimate(flops=1024, bytes_accessed=1024, transcendentals=0)


def cost_of(microseconds):
    return pl.CostEstimate(flops=1024, bytes_accessed=int(microseconds * 3.0e6), transcendentals=0)


def staged(name, body, scalars, arrays, out_shapes, scratch, limit, cost):
    count, outs, extra = len(arrays), len(out_shapes), len(scalars)

    def kernel(*refs):
        scalar_refs, refs = refs[:extra], refs[extra:]
        in_refs, refs = refs[:count], refs[count:]
        out_refs, refs = refs[:outs], refs[outs:]
        held, refs = refs[:count], refs[count:]
        made, refs = refs[:outs], refs[outs:]
        load_sems, store_sems = refs[:2]
        loads = [pltpu.make_async_copy(s, h, load_sems.at[n]) for n, (s, h) in enumerate(zip(in_refs, held))]
        stores = [pltpu.make_async_copy(m, o, store_sems.at[n]) for n, (m, o) in enumerate(zip(made, out_refs))]
        for copy in loads:
            copy.start()
        here, gone = set(), set()

        def load(n):
            if n not in here:
                here.add(n)
                loads[n].wait()
            return held[n]

        def store(*which):
            for n in which:
                gone.add(n)
                stores[n].start()

        body(load, store, made, scalar_refs, refs[2:])
        for n in range(count):
            load(n)
        for n in range(outs):
            if n not in gone:
                store(n)
        for copy in stores:
            copy.wait()

    anywhere = pl.BlockSpec(memory_space=pl.ANY)
    return pl.pallas_call(
        kernel,
        in_specs=[pl.BlockSpec(memory_space=pltpu.SMEM)] * extra + [anywhere] * count,
        out_specs=[anywhere] * outs,
        out_shape=[jax.ShapeDtypeStruct(shape, kind) for shape, kind in out_shapes],
        scratch_shapes=[pltpu.VMEM(a.shape, a.dtype) for a in arrays]
        + [pltpu.VMEM(shape, kind) for shape, kind in out_shapes]
        + [pltpu.SemaphoreType.DMA((count,)), pltpu.SemaphoreType.DMA((outs,))]
        + scratch,
        cost_estimate=cost,
        compiler_params=pltpu.CompilerParams(vmem_limit_bytes=limit << 20),
        name=name,
    )(*scalars, *arrays)


def pick_rows(base, offsets, ways):
    rows, width = base.shape
    chunks = ways
    block = rows // chunks
    groups = block // GROUP
    sub = 256
    sub_groups = sub // GROUP

    def kernel(base_ref, offset_ref, picked_ref, held, sems):
        def load(n):
            part = pl.ds(pl.multiple_of(n * block, block), block)
            return pltpu.make_async_copy(base_ref.at[part], held.at[part], sems.at[n])

        for n in range(chunks):
            load(n).start()
        local = lax.broadcasted_iota(jnp.int32, (sub, sub_groups), 0) - GROUP * lax.broadcasted_iota(
            jnp.int32, (sub, sub_groups), 1
        )

        def step(n, carry):
            load(n).wait()
            offsets = offset_ref[:, pl.ds(pl.multiple_of(n * groups, groups), groups)]
            for s in range(block // sub):
                chosen = (local == offsets[:, s * sub_groups : (s + 1) * sub_groups]).astype(F32).astype(BF)
                rows_in = held[pl.ds(pl.multiple_of(n * block + s * sub, sub), sub), :]
                to = pl.ds(pl.multiple_of(n * groups + s * sub_groups, sub_groups), sub_groups)
                picked_ref[to, :] = dot(chosen, rows_in, TN).astype(BF)
            return carry

        lax.fori_loop(0, chunks, step, 0)

    whole = pl.BlockSpec(memory_space=pltpu.VMEM)
    return pl.pallas_call(
        kernel,
        in_specs=[pl.BlockSpec(memory_space=pl.ANY), whole],
        out_specs=whole,
        out_shape=jax.ShapeDtypeStruct((rows // GROUP, width), BF),
        scratch_shapes=[pltpu.VMEM((rows, width), BF), pltpu.SemaphoreType.DMA((chunks,))],
        cost_estimate=small_cost(),
        compiler_params=pltpu.CompilerParams(vmem_limit_bytes=60 << 20),
        name="pick_rows",
    )(base, offsets)


def score_sums(base, router, mine, ways):
    rows, width = base.shape
    block = rows // ways

    def kernel(mine_ref, base_ref, router_ref, square_ref):
        score = jnp.sum(base_ref[...].astype(F32) * router_ref[...].astype(F32), axis=1, keepdims=True)
        square_ref[...] = jnp.broadcast_to(jnp.sum(score * score, axis=0, keepdims=True), square_ref.shape)

    return pl.pallas_call(
        kernel,
        grid_spec=pltpu.PrefetchScalarGridSpec(
            num_scalar_prefetch=1,
            grid=(1,),
            in_specs=[
                pl.BlockSpec((block, width), lambda i, m: (m[0], 0)),
                pl.BlockSpec((1, width), lambda i, m: (0, 0)),
            ],
            out_specs=pl.BlockSpec((1, 128), lambda i, m: (0, 0)),
        ),
        out_shape=jax.ShapeDtypeStruct((1, 128), F32),
        cost_estimate=small_cost(),
        name="score_sums",
    )(mine, base, router)


def pick_only(base, offsets, ways):
    rows, width = base.shape
    block = rows // ways
    groups = block // GROUP
    sub = 256
    sub_groups = sub // GROUP

    def kernel(base_ref, offset_ref, picked_ref):
        local = lax.broadcasted_iota(jnp.int32, (sub, sub_groups), 0) - GROUP * lax.broadcasted_iota(
            jnp.int32, (sub, sub_groups), 1
        )
        for s in range(block // sub):
            to = slice(s * sub_groups, (s + 1) * sub_groups)
            chosen = (local == offset_ref[:, to]).astype(F32).astype(BF)
            picked_ref[to, :] = dot(chosen, base_ref[s * sub : (s + 1) * sub, :], TN).astype(BF)

    return pl.pallas_call(
        kernel,
        grid=(ways,),
        in_specs=[pl.BlockSpec((block, width), lambda i: (i, 0)), pl.BlockSpec((1, groups), lambda i: (0, i))],
        out_specs=pl.BlockSpec((groups, width), lambda i: (i, 0)),
        out_shape=jax.ShapeDtypeStruct((rows // GROUP, width), BF),
        cost_estimate=small_cost(),
        name="pick_only",
    )(base, offsets)


def merge_rows(base, offsets, pieces, parts, held_out=None):
    rows, width = base.shape
    ways, depth, _ = pieces.shape
    count = rows // ways
    groups = count // GROUP
    kept = [] if held_out is None else [held_out]
    sub = 256
    sub_groups = sub // GROUP

    def kernel(part_ref, base_ref, offset_ref, piece_ref, *rest):
        out_ref = rest[-1]
        local = lax.broadcasted_iota(jnp.int32, (sub, sub_groups), 0) - GROUP * lax.broadcasted_iota(
            jnp.int32, (sub, sub_groups), 1
        )
        for s in range(count // sub):
            here = slice(s * sub, (s + 1) * sub)
            to = slice(s * sub_groups, (s + 1) * sub_groups)
            chosen = (local == offset_ref[:, to]).astype(F32)
            hit = jnp.sum(chosen, axis=1, keepdims=True) > 0.5
            spread = dot(chosen.astype(BF), piece_ref[0, to, :], NN)
            out_ref[here, :] = jnp.where(hit, spread, base_ref[here, :].astype(F32)).astype(BF)

    grid_spec = pltpu.PrefetchScalarGridSpec(
        num_scalar_prefetch=1,
        grid=(parts.shape[0],),
        in_specs=[
            pl.BlockSpec((count, width), lambda i, p: (p[i], 0)),
            pl.BlockSpec((1, groups), lambda i, p: (0, p[i])),
            pl.BlockSpec((1, depth, width), lambda i, p: (p[i], 0, 0)),
        ]
        + [pl.BlockSpec(memory_space=pl.ANY)] * len(kept),
        out_specs=pl.BlockSpec((count, width), lambda i, p: (p[i], 0)),
    )
    return pl.pallas_call(
        kernel,
        grid_spec=grid_spec,
        out_shape=jax.ShapeDtypeStruct((rows, width), BF),
        input_output_aliases={4: 0} if kept else {},
        cost_estimate=small_cost(),
        name="merge_rows",
    )(parts, base, offsets, pieces, *kept)


def attend(picked, gain, weight, seq_row, ways):
    rows, width = picked.shape
    heads_width = weight.shape[2]
    heads = heads_width // HEAD_DIM
    block = min(256, rows)

    def body(load, store, outs, scalars, scratch):
        low_ref, qkv_ref, probs_ref, out_ref = outs
        values = load(0)[...].astype(F32)
        low_ref[...] = (values * inverse_rms(values) * load(1)[...].astype(F32)).astype(BF)
        store(0)
        weight_ref = load(2)
        for n in range(3):
            qkv_ref[n] = dot(low_ref[...], weight_ref[n], NN).astype(BF)
        store(1)
        sequence = load(3)[...].astype(F32)
        column = jnp.broadcast_to(sequence, (128, rows)).T[:, :1]
        lane_head = lax.broadcasted_iota(jnp.int32, (1, heads_width), 1) // HEAD_DIM
        for start in range(0, rows, block):
            stop = start + block
            query = qkv_ref[0, start:stop, :] * BF(HEAD_DIM ** (-0.5))
            order = lax.broadcasted_iota(jnp.int32, (block, stop), 0) + start
            keys = lax.broadcasted_iota(jnp.int32, (block, stop), 1)
            allowed = (column[start:stop, :] == sequence[:, :stop]) & (order >= keys)
            total = jnp.zeros((block, heads_width), F32)
            for head in range(heads):
                here = lane_head == head
                key = jnp.where(here, qkv_ref[1, :stop, :], BF(0))
                logits = jnp.where(allowed, dot(query, key, NT), mask_fill)
                raised = jnp.exp(logits - jnp.max(logits, axis=-1, keepdims=True))
                probs = (raised * (1.0 / jnp.sum(raised, axis=-1, keepdims=True))).astype(BF)
                probs_ref[head, start:stop, :stop] = probs
                if stop < rows:
                    probs_ref[head, start:stop, stop:] = jnp.zeros((block, rows - stop), BF)
                value = jnp.where(here, qkv_ref[2, :stop, :], BF(0))
                total = total + dot(probs, value, NN)
            for k in range(ways):
                out_ref[k, start:stop, :] = total.astype(BF)

    return staged(
        "attend",
        body,
        [],
        [picked, gain, weight, seq_row],
        [
            ((rows, width), BF),
            ((3, rows, heads_width), BF),
            ((heads, rows, rows), BF),
            ((ways, rows, heads_width), BF),
        ],
        [],
        60,
        small_cost(),
    )


def feed_forward(heads, here, beside, across, picked, gain, up, grad_act, grad_mixer, part, mine, ways):
    rows, width = picked.shape
    hidden = up.shape[1]
    sub = min(256, hidden)
    count, _, heads_width = heads.shape
    piece = heads_width // 4
    own = rows // ways
    slope = 0.7978845608028654
    cubic = 0.044715

    def body(load, store, outs, scalars, scratch):
        part_ref, mine_ref = scalars
        attended_ref, low_ref, act_ref, pre_ref, hidden_ref, part_out_ref, gain_part_ref, sent_ref = outs
        total, state, weights = scratch
        quarter = part_ref[0] & 3
        heads_ref = load(0)
        here_ref, beside_ref, across_ref = load(1), load(2), load(3)
        for n, source in enumerate((here_ref, across_ref.at[0], beside_ref, across_ref.at[1])):
            start = pl.multiple_of((quarter ^ n) * piece, piece)
            for k in range(count):
                weights[k, pl.ds(start, piece), :] = source[k]
        attended = dot(heads_ref[0], weights[0], NN)
        for k in range(1, count):
            attended = attended + dot(heads_ref[k], weights[k], NN)
        total[...] = attended
        attended_ref[...] = total[pl.ds(pl.multiple_of(mine_ref[0] * own, own), own), :]
        state_in = load(4)[...].astype(F32) + attended
        state[...] = state_in
        gain_row = load(5)[...].astype(F32)
        low_ref[...] = (state_in * inverse_rms(state_in) * gain_row).astype(BF)
        store(0, 1)
        up_ref, act_grad_ref = load(6), load(7)
        for s in range(hidden // sub):
            lanes = slice(s * sub, (s + 1) * sub)
            value = dot(low_ref[...], up_ref[:, lanes], NN)
            square = value * value
            bent = jnp.tanh(value * (slope + (slope * cubic) * square))
            half = 0.5 * (1.0 + bent)
            act_ref[:, lanes] = (value * half).astype(BF)
            rise = half + (0.5 * value) * (1.0 - bent * bent) * (slope + (3.0 * slope * cubic) * square)
            pre = (act_grad_ref[:, lanes] * rise).astype(BF)
            pre_ref[:, lanes] = pre
            term = dot(pre, up_ref[:, lanes], NT)
            if s == 0:
                total[...] = term
            else:
                total[...] += term
        store(2, 3)
        state_in = state[...]
        grad = total[...]
        inverse = inverse_rms(state_in)
        normal = state_in * inverse
        gain_part_ref[...] = jnp.sum(grad * normal, axis=0, keepdims=True)
        scaled = grad * gain_row
        along = jnp.mean(scaled * normal, axis=-1, keepdims=True)
        back = inverse * (scaled - normal * along)
        hidden_ref[...] = back.astype(BF)
        part_out_ref[...] = (back + load(8)[...].astype(F32) * (1.0 / count)).astype(BF)
        store(4, 5, 6)
        for k in range(count):
            sent_ref[k] = dot(part_out_ref[...], weights[k], NT).astype(BF)

    return staged(
        "feed_forward",
        body,
        [part, mine],
        [heads, here, beside, across, picked, gain, up, grad_act, grad_mixer],
        [
            ((own, width), F32),
            ((rows, width), BF),
            ((rows, hidden), BF),
            ((rows, hidden), BF),
            ((rows, width), BF),
            ((rows, width), BF),
            ((1, width), F32),
            (heads.shape, BF),
        ],
        [
            pltpu.VMEM((rows, width), F32),
            pltpu.VMEM((rows, width), F32),
            pltpu.VMEM((count, heads_width, width), BF),
        ],
        60,
        small_cost(),
    )


def act_grads(picked, router, grad_rows, down):
    rows, width = grad_rows.shape

    def kernel(picked_ref, router_ref, rows_ref, down_ref, gating_ref, square_ref, mixer_ref, grad_ref):
        score = jnp.sum(picked_ref[...].astype(F32) * router_ref[...].astype(F32), axis=-1, keepdims=True)
        gating = jax.nn.sigmoid(score)
        gating_ref[...] = gating
        square_ref[...] = jnp.broadcast_to(jnp.sum(score * score, axis=0, keepdims=True), square_ref.shape)
        mixer_ref[...] = (gating * rows_ref[...].astype(F32)).astype(BF)
        grad_ref[...] = dot(mixer_ref[...], down_ref[...], NT)

    whole = pl.BlockSpec(memory_space=pltpu.VMEM)
    return pl.pallas_call(
        kernel,
        in_specs=[whole] * 4,
        out_specs=[whole] * 4,
        out_shape=[
            jax.ShapeDtypeStruct((rows, 1), F32),
            jax.ShapeDtypeStruct((1, 128), F32),
            jax.ShapeDtypeStruct((rows, width), BF),
            jax.ShapeDtypeStruct((rows, down.shape[0]), F32),
        ],
        cost_estimate=small_cost(),
        name="act_grads",
    )(picked, router, grad_rows, down)


def attend_back(head_terms, qkv, probs, weight, picked, gain, hidden_part):
    rows, width = picked.shape
    heads_width = weight.shape[2]
    heads = heads_width // HEAD_DIM
    block = min(256, rows)
    scale = HEAD_DIM ** (-0.5)

    def kernel(
        head_ref,
        qkv_ref,
        probs_ref,
        weight_ref,
        picked_ref,
        gain_ref,
        hidden_ref,
        grads_ref,
        gain_part_ref,
        result,
        grad_key,
        grad_value,
    ):
        lane_head = lax.broadcasted_iota(jnp.int32, (1, heads_width), 1) // HEAD_DIM
        for start in reversed(range(0, rows, block)):
            stop = start + block
            here_rows = slice(start, stop)
            grad_head = head_ref[0, here_rows, :].astype(F32)
            for k in range(1, head_ref.shape[0]):
                grad_head = grad_head + head_ref[k, here_rows, :].astype(F32)
            grad_head = grad_head.astype(BF)
            query = qkv_ref[0, here_rows, :] * BF(scale)
            grad_query = jnp.zeros((block, heads_width), F32)
            add_key = jnp.zeros((stop, heads_width), F32)
            add_value = jnp.zeros((stop, heads_width), F32)
            for head in range(heads):
                here = lane_head == head
                value = jnp.where(here, qkv_ref[2, :stop, :], BF(0))
                key = jnp.where(here, qkv_ref[1, :stop, :], BF(0))
                low = probs_ref[head, here_rows, :stop]
                weighted = low.astype(F32) * dot(grad_head, value, NT)
                row_sum = jnp.sum(weighted, axis=-1, keepdims=True)
                slopes = (weighted - low.astype(F32) * row_sum).astype(BF)
                grad_query = grad_query + dot(slopes, key, NN)
                add_key = add_key + dot(slopes, jnp.where(here, query, BF(0)), TN)
                add_value = add_value + dot(low, jnp.where(here, grad_head, BF(0)), TN)
            grads_ref[0, here_rows, :] = (grad_query * scale).astype(BF)
            if stop == rows:
                grad_key[...] = add_key
                grad_value[...] = add_value
            else:
                grad_key[:stop, :] += add_key
                grad_value[:stop, :] += add_value
        grads_ref[1] = grad_key[...].astype(BF)
        grads_ref[2] = grad_value[...].astype(BF)
        first = dot(grads_ref[0], weight_ref[0], NT)
        for n in range(1, 3):
            first = first + dot(grads_ref[n], weight_ref[n], NT)
        values = picked_ref[...].astype(F32)
        inverse = inverse_rms(values)
        normal = values * inverse
        gain_part_ref[...] = jnp.sum(first * normal, axis=0, keepdims=True)
        scaled = first * gain_ref[...].astype(F32)
        along = jnp.mean(scaled * normal, axis=-1, keepdims=True)
        result[...] = (hidden_ref[...].astype(F32) + inverse * (scaled - normal * along)).astype(BF)

    whole = pl.BlockSpec(memory_space=pltpu.VMEM)
    return pl.pallas_call(
        kernel,
        in_specs=[whole] * 7,
        out_specs=[whole] * 3,
        out_shape=[
            jax.ShapeDtypeStruct((3, rows, heads_width), BF),
            jax.ShapeDtypeStruct((1, width), F32),
            jax.ShapeDtypeStruct((rows, width), BF),
        ],
        scratch_shapes=[
            pltpu.VMEM((rows, heads_width), F32),
            pltpu.VMEM((rows, heads_width), F32),
        ],
        cost_estimate=small_cost(),
        compiler_params=pltpu.CompilerParams(vmem_limit_bytes=20 << 20),
        name="attend_back",
    )(head_terms, qkv, probs, weight, picked, gain, hidden_part)


def spread_rows(down_near, down_far, up_near, up_far, index_down, index_up):
    half, rows, width = down_near.shape

    def kernel(down_index, up_index, down_ref, far_ref, up_ref, up_far_ref, down_out, up_out):
        near = pl.program_id(0) < half

        @pl.when(near)
        def _():
            down_out[...] = down_ref[0].astype(F32)
            up_out[...] = up_ref[0].astype(F32)

        @pl.when(jnp.logical_not(near))
        def _():
            down_out[...] = far_ref[0].astype(F32)
            up_out[...] = up_far_ref[0].astype(F32)

    first = pl.BlockSpec((1, rows, width), lambda i, d, u: (jnp.minimum(i, half - 1), 0, 0))
    second = pl.BlockSpec((1, rows, width), lambda i, d, u: (jnp.maximum(i - half, 0), 0, 0))
    return pl.pallas_call(
        kernel,
        grid_spec=pltpu.PrefetchScalarGridSpec(
            num_scalar_prefetch=2,
            grid=(2 * half,),
            in_specs=[first, second, first, second],
            out_specs=[
                pl.BlockSpec((rows, width), lambda i, d, u: (d[i], 0)),
                pl.BlockSpec((rows, width), lambda i, d, u: (u[i], 0)),
            ],
        ),
        out_shape=[jax.ShapeDtypeStruct((2 * half * rows, width), F32)] * 2,
        cost_estimate=small_cost(),
        name="spread_rows",
    )(index_down, index_up, down_near, down_far, up_near, up_far)


def qkv_part_of(first_low, grads):
    rows, width = first_low.shape
    part_width = grads.shape[2]

    def kernel(low_ref, grads_ref, out_ref):
        for n in range(3):
            product = dot(grads_ref[n], low_ref[...], TN)
            out_ref[n * part_width : (n + 1) * part_width, :] = product.astype(BF)

    whole = pl.BlockSpec(memory_space=pltpu.VMEM)
    return pl.pallas_call(
        kernel,
        in_specs=[whole] * 2,
        out_specs=whole,
        out_shape=jax.ShapeDtypeStruct((3 * part_width, width), BF),
        cost_estimate=small_cost(),
        compiler_params=pltpu.CompilerParams(vmem_limit_bytes=12 << 20),
        name="qkv_part",
    )(first_low, grads)


def spread_qkv(lane_a, got_a, lane_b, got_b, part_width):
    rows, width = lane_a.shape
    tile = 128

    def kernel(a_ref, a_got, b_ref, b_got, out_ref):
        for n in range(2 * rows // tile):
            start = n * tile % rows
            ref, got = (a_ref, a_got) if n * tile < rows else (b_ref, b_got)
            lane, column = divmod(n * tile, part_width)
            piece = ref[start : start + tile, :].astype(F32) + got[start : start + tile, :].astype(F32)
            out_ref[lane, :, column : column + tile] = piece.T

    whole = pl.BlockSpec(memory_space=pltpu.VMEM)
    return pl.pallas_call(
        kernel,
        in_specs=[whole] * 4,
        out_specs=whole,
        out_shape=jax.ShapeDtypeStruct((2 * rows // part_width, width, part_width), F32),
        cost_estimate=small_cost(),
        compiler_params=pltpu.CompilerParams(vmem_limit_bytes=16 << 20),
        name="spread_qkv",
    )(lane_a, got_a, lane_b, got_b)


def core_grads(activated, grad_mixer, second_low, grad_pre, heads, attended_part, part, keys_a, keys_b):
    rows, hidden = activated.shape
    width = grad_mixer.shape[1]
    copies = len(keys_a)
    half = copies // 2
    count, _, heads_width = heads.shape
    block = hidden // copies
    small = heads_width // copies
    many = count // 2
    depth = half * (block + many * small)

    def kernel(part_ref, act_ref, mixer_ref, low_ref, pre_ref, heads_ref, term_ref, keep_ref, *rest):
        wide_refs, narrow_refs, (full, narrow) = rest[0:2], rest[2:4], rest[4:]

        def place(source, each, lane, keys, first, stride):
            for n, key in enumerate(keys):
                start = pl.multiple_of((part_ref[0] ^ key) * each, each)
                at = first + (n % half) * stride
                piece = source[pl.ds(start, each), :]
                if n < half:
                    keep_ref[lane, at : at + each, :] = piece
                elif first == 0:
                    wide_refs[lane][at : at + each, :] = piece
                else:
                    narrow_refs[lane][at - half * block : at - half * block + each, :] = piece

        full[...] = dot(act_ref[...], mixer_ref[...], TN).astype(BF)
        place(full, block, 0, keys_a, 0, block)
        full[...] = dot(low_ref[...], pre_ref[...], TN).astype(BF)
        place(full, block, 1, keys_b, 0, block)
        for k in range(count):
            narrow[...] = dot(heads_ref[k], term_ref[...], TN).astype(BF)
            lane, spot = divmod(k, many)
            place(narrow, small, lane, keys_b if lane else keys_a, half * block + spot * small, many * small)

    whole = pl.BlockSpec(memory_space=pltpu.VMEM)
    wide_shape = jax.ShapeDtypeStruct((half * block, width), BF)
    narrow_shape = jax.ShapeDtypeStruct((half * many * small, width), BF)
    return pl.pallas_call(
        kernel,
        in_specs=[pl.BlockSpec(memory_space=pltpu.SMEM)] + [whole] * 6,
        out_specs=[whole] * 5,
        out_shape=[jax.ShapeDtypeStruct((2, depth, width), BF)] + [wide_shape] * 2 + [narrow_shape] * 2,
        scratch_shapes=[pltpu.VMEM((hidden, width), BF), pltpu.VMEM((heads_width, width), BF)],
        cost_estimate=small_cost(),
        compiler_params=pltpu.CompilerParams(vmem_limit_bytes=14 << 20),
        name="core_grads",
    )(part, activated, grad_mixer, second_low, grad_pre, heads, attended_part)


def plus(left, right):
    return (left.astype(F32) + right.astype(F32)).astype(BF)


def halving_sums(keep, got_a, got_b, wide, narrow):
    width = keep.shape[2]
    count = len(got_a)

    def kernel(keep_ref, *refs):
        a_got, b_got, (stay_ref, a_out, b_out) = refs[:count], refs[count : 2 * count], refs[2 * count :]
        for lane, got, out in ((0, a_got, a_out), (1, b_got, b_out)):
            for first, size, at in ((0, wide // 2, 0), (wide, narrow // 2, wide // 2)):
                source, shift = (got[1], wide) if count == 2 and first else (got[0], 0)
                to = slice(at, at + size)
                for start, target in ((first, stay_ref.at[lane]), (first + size, out)):
                    here = slice(start - shift, start - shift + size)
                    target[to, :] = plus(keep_ref[lane, start : start + size, :], source[here, :])

    whole = pl.BlockSpec(memory_space=pltpu.VMEM)
    depth = (wide + narrow) // 2
    lane_shape = jax.ShapeDtypeStruct((depth, width), BF)
    return pl.pallas_call(
        kernel,
        in_specs=[whole] * (1 + 2 * count),
        out_specs=[whole] * 3,
        out_shape=[jax.ShapeDtypeStruct((2, depth, width), BF), lane_shape, lane_shape],
        cost_estimate=small_cost(),
        compiler_params=pltpu.CompilerParams(vmem_limit_bytes=14 << 20),
        name="halving_sums",
    )(keep, *got_a, *got_b)


def owned_sums(keep, got_a, got_b, fresh, small, wide, ways):
    width = keep.shape[2]
    narrow = keep.shape[1] - wide
    own = fresh.shape[0]
    many = ways // 2
    each = narrow // many
    depth = own + GAP + each

    def kernel(keep_ref, a_got, b_got, fresh_ref, small_ref, a_out, b_out, sent_ref):
        sums = split_sums(small_ref[...])
        for lane, got, out in ((0, a_got, a_out), (1, b_got, b_out)):
            out[...] = plus(keep_ref[lane, :wide, :], got[:wide, :])
            done = plus(keep_ref[lane, wide:, :], got[wide:, :])
            for spot in range(many):
                k = lane * many + spot
                sent_ref[k, :own, :] = fresh_ref[...]
                sent_ref[k, own : own + GAP, :] = sums
                sent_ref[k, own + GAP :, :] = done[spot * each : (spot + 1) * each, :]

    whole = pl.BlockSpec(memory_space=pltpu.VMEM)
    lane_shape = jax.ShapeDtypeStruct((wide, width), BF)
    return pl.pallas_call(
        kernel,
        in_specs=[whole] * 5,
        out_specs=[whole] * 3,
        out_shape=[lane_shape, lane_shape, jax.ShapeDtypeStruct((ways, depth, width), BF)],
        cost_estimate=small_cost(),
        compiler_params=pltpu.CompilerParams(vmem_limit_bytes=10 << 20),
        name="owned_sums",
    )(keep, got_a, got_b, fresh, small)


def core_sums(rows, other):
    depth, width = rows.shape
    third = depth // 2

    def kernel(rows_ref, other_ref, a_out, b_out):
        a_out[...] = plus(rows_ref[:third, :], other_ref[:third, :])
        b_out[...] = plus(rows_ref[third:, :], other_ref[third:, :])

    whole = pl.BlockSpec(memory_space=pltpu.VMEM)
    return pl.pallas_call(
        kernel,
        in_specs=[whole] * 2,
        out_specs=[whole] * 2,
        out_shape=[jax.ShapeDtypeStruct((third, width), BF)] * 2,
        cost_estimate=small_cost(),
        compiler_params=pltpu.CompilerParams(vmem_limit_bytes=10 << 20),
        name="core_sums",
    )(rows, other)


def lane_sums(lane_a, got_a, lane_b, got_b):
    def kernel(a_ref, a_got, b_ref, b_got, a_out, b_out):
        a_out[...] = plus(a_ref[...], a_got[...])
        b_out[...] = plus(b_ref[...], b_got[...])

    whole = pl.BlockSpec(memory_space=pltpu.VMEM)
    return pl.pallas_call(
        kernel,
        in_specs=[whole] * 4,
        out_specs=[whole] * 2,
        out_shape=[jax.ShapeDtypeStruct(lane_a.shape, BF)] * 2,
        cost_estimate=small_cost(),
        compiler_params=pltpu.CompilerParams(vmem_limit_bytes=12 << 20),
        name="lane_sums",
    )(lane_a, got_a, lane_b, got_b)


def gather_blocks(blocks_a, blocks_b):
    wide, width = blocks_a[0].shape
    count = len(blocks_a)

    def kernel(*refs):
        for lane in range(2):
            for n in range(count):
                refs[2 * count + lane][n * wide : (n + 1) * wide, :] = refs[lane * count + n][...]

    whole = pl.BlockSpec(memory_space=pltpu.VMEM)
    return pl.pallas_call(
        kernel,
        in_specs=[whole] * (2 * count),
        out_specs=[whole] * 2,
        out_shape=[jax.ShapeDtypeStruct((count * wide, width), BF)] * 2,
        cost_estimate=small_cost(),
        compiler_params=pltpu.CompilerParams(vmem_limit_bytes=10 << 20),
        name="gather_blocks",
    )(*blocks_a, *blocks_b)


def split_sums(values):
    high = values.astype(BF)
    low = (values - high.astype(F32)).astype(BF)
    return jnp.concatenate([high, low], axis=0)


def joined_sums(rows):
    return rows[:TERMS].astype(F32) + rows[TERMS : 2 * TERMS].astype(F32)


def first_small(received, own):
    ways, depth, width = received.shape
    each = depth - own - GAP

    def kernel(got_ref, out_ref):
        total = got_ref[0, own + GAP :, :].astype(F32)
        sums = joined_sums(got_ref[0, own : own + GAP, :])
        for k in range(1, ways):
            total = total + got_ref[k, own + GAP :, :].astype(F32)
            sums = sums + joined_sums(got_ref[k, own : own + GAP, :])
        out_ref[:each, :] = total.astype(BF)
        out_ref[each:, :] = split_sums(sums)

    whole = pl.BlockSpec(memory_space=pltpu.VMEM)
    return pl.pallas_call(
        kernel,
        in_specs=[whole],
        out_specs=whole,
        out_shape=jax.ShapeDtypeStruct((each + GAP, width), BF),
        cost_estimate=small_cost(),
        compiler_params=pltpu.CompilerParams(vmem_limit_bytes=8 << 20),
        name="first_small",
    )(received)


def last_small(blocks, index, shares):
    depth, width = blocks[0].shape
    each = depth - GAP
    count = len(blocks)

    def kernel(index_ref, *refs):
        out_ref, small_refs = refs[count], refs[count + 1 :]
        total = joined_sums(refs[0][each:, :])
        for n in range(1, count):
            total = total + joined_sums(refs[n][each:, :])
        for n in range(TERMS - 1):
            small_refs[n][...] = total[n : n + 1, :]
        lane = lax.broadcasted_iota(jnp.int32, (1, 128), 1)
        small_refs[TERMS - 1][...] = total[TERMS - 1 :, :128] * jnp.where(lane == 0, shares[0], shares[1])
        for n in range(count):
            start = pl.multiple_of(index_ref[n] * each, each)
            out_ref[pl.ds(start, each), :] = refs[n][:each, :].astype(F32)

    whole = pl.BlockSpec(memory_space=pltpu.VMEM)
    return pl.pallas_call(
        kernel,
        in_specs=[pl.BlockSpec(memory_space=pltpu.SMEM)] + [whole] * count,
        out_specs=[whole] * (1 + TERMS),
        out_shape=[jax.ShapeDtypeStruct((count * each, width), F32)] + [jax.ShapeDtypeStruct((1, width), F32)] * (TERMS - 1)
        + [jax.ShapeDtypeStruct((1, 128), F32)],
        cost_estimate=small_cost(),
        compiler_params=pltpu.CompilerParams(vmem_limit_bytes=10 << 20),
        name="last_small",
    )(index, *blocks)


def finish_rows(mixer_terms, picked, gating, attended, grad_rows, gain_one, gain_two, square, routed_square, mine, ways):
    rows, width = picked.shape
    own = rows // ways

    def kernel(
        mine_ref,
        terms_ref,
        picked_ref,
        gating_ref,
        attended_ref,
        rows_ref,
        one_ref,
        two_ref,
        square_ref,
        routed_ref,
        new_ref,
        score_ref,
        small_ref,
    ):
        branch = attended_ref[...]
        for k in range(ways):
            branch = branch + terms_ref[k].astype(F32)
        values = picked_ref[...].astype(F32)
        gate = gating_ref[...]
        new_ref[...] = (values + gate * branch).astype(BF)
        along = jnp.sum(rows_ref[...].astype(F32) * branch, axis=-1, keepdims=True)
        score = along * gate * (1.0 - gate)
        score_ref[...] = score
        small_ref[0:1, :] = jnp.sum(score * values, axis=0, keepdims=True)
        small_ref[1:2, :] = one_ref[...]
        small_ref[2:3, :] = two_ref[...]
        lane = lax.broadcasted_iota(jnp.int32, (1, width), 1)
        both = jnp.where(lane == 0, square_ref[:, 0:1], routed_ref[:, 0:1] * (1.0 / ways))
        small_ref[3:4, :] = jnp.where(lane < 2, both, 0.0)

    def block(shape):
        return pl.BlockSpec(shape, lambda i, m: (m[0], 0))

    def fixed(shape):
        return pl.BlockSpec(shape, lambda i, m: (0, 0))

    return pl.pallas_call(
        kernel,
        grid_spec=pltpu.PrefetchScalarGridSpec(
            num_scalar_prefetch=1,
            grid=(1,),
            in_specs=[pl.BlockSpec(mixer_terms.shape, lambda i, m: (0, 0, 0))]
            + [block((own, width)), block((own, 1)), fixed((own, width)), block((own, width))]
            + [fixed((1, width))] * 2
            + [fixed((1, 128))] * 2,
            out_specs=[fixed((own, width)), fixed((own, 1)), fixed((4, width))],
        ),
        out_shape=[
            jax.ShapeDtypeStruct((own, width), BF),
            jax.ShapeDtypeStruct((own, 1), F32),
            jax.ShapeDtypeStruct((4, width), F32),
        ],
        cost_estimate=cost_of(10),
        name="finish_rows",
    )(mine, mixer_terms, picked, gating, attended, grad_rows, gain_one, gain_two, square, routed_square)


def finish_input(terms, grad_rows, score, router, mine, ways):
    rows, width = grad_rows.shape
    own = rows // ways

    def kernel(mine_ref, terms_ref, rows_ref, score_ref, router_ref, out_ref):
        total = rows_ref[...].astype(F32) + score_ref[...] * router_ref[...].astype(F32)
        for k in range(ways):
            total = total + terms_ref[k].astype(F32)
        for k in range(ways):
            out_ref[k] = total.astype(BF)

    def fixed(shape):
        return pl.BlockSpec(shape, lambda i, m: (0,) * len(shape))

    return pl.pallas_call(
        kernel,
        grid_spec=pltpu.PrefetchScalarGridSpec(
            num_scalar_prefetch=1,
            grid=(1,),
            in_specs=[
                fixed((ways, own, width)),
                pl.BlockSpec((own, width), lambda i, m: (m[0], 0)),
                fixed((own, 1)),
                fixed((1, width)),
            ],
            out_specs=fixed((ways, own, width)),
        ),
        out_shape=jax.ShapeDtypeStruct((ways, own, width), BF),
        cost_estimate=small_cost(),
        compiler_params=pltpu.CompilerParams(vmem_limit_bytes=8 << 20),
        name="finish_input",
    )(mine, terms, grad_rows, score, router)


def split_kept(count, order):
    keys = [0]
    for bit in reversed(order):
        keys = keys + [k ^ bit for k in keys]
    return keys


def per_device(
    tokens,
    route_offset,
    unit_sequence,
    cotangent,
    router_weight,
    first_gain,
    second_gain,
    qkv_weight,
    out_weight,
    up_weight,
    down_weight,
):
    rows_local, width = tokens.shape
    routed = route_offset.shape[1]
    ways = lax.axis_size("tensor")
    copies = lax.axis_size("dp")
    mine = lax.axis_index("tensor")
    part = lax.axis_index("dp")
    mine_array = jnp.reshape(mine, (1,)).astype(jnp.int32)
    part_array = jnp.reshape(part, (1,)).astype(jnp.int32)
    ladder = [1 << b for b in range(1, copies.bit_length() - 1)]
    order_a = [1] + ladder
    order_b = [1] + ladder[::-1]
    keys_a = split_kept(copies, order_a)
    keys_b = split_kept(copies, order_b)

    tie = lax.optimization_barrier
    own_rows = routed // ways
    heads_width = out_weight.shape[0]
    hidden = up_weight.shape[1]
    by_swaps = copies == 8
    bit_x, bit_y = 2, 4
    shares = (1.0 / (rows_local * copies), 1.0 / (routed * copies))

    quarter = part & 3
    piece_rows = heads_width // 4
    piece = lax.dynamic_slice_in_dim(out_weight, quarter * piece_rows, piece_rows, 0)
    here = to_all(jnp.broadcast_to(piece[None], (ways,) + piece.shape))

    picked = pick_rows(tokens, route_offset, ways)
    first_low, qkv, probs, head_out = attend(picked, first_gain[None], qkv_weight, unit_sequence, ways)
    here, head_out = tie((here, head_out))

    heads = to_all(head_out)
    beside = swap(here, "dp", bit_x)
    cotangent, router_weight, second_gain, here, head_out = tie(
        (cotangent, router_weight, second_gain, here, head_out)
    )
    weight_row = router_weight[None]
    grad_rows = pick_only(cotangent, route_offset, ways)
    beside, here, grad_rows = tie((beside, here, grad_rows))
    across = swap(jnp.stack([here, beside]), "dp", 1)
    gating, routed_square, grad_mixer, grad_act = act_grads(picked, weight_row, grad_rows, down_weight)
    square = score_sums(tokens, weight_row, mine_array, ways)
    heads, across, grad_act, grad_mixer, square = tie((heads, across, grad_act, grad_mixer, square))
    attended, second_low, activated, grad_pre, hidden_part, attended_part, second_gain_part, head_sent = feed_forward(
        heads,
        here,
        beside,
        across,
        picked,
        second_gain[None],
        up_weight,
        grad_act,
        grad_mixer,
        part_array,
        mine_array,
        ways,
    )

    head_terms = to_all(head_sent)
    wide = hidden // 2
    narrow = heads_width * ways // 4
    if by_swaps:
        kept, *leaving = core_grads(
            activated, grad_mixer, second_low, grad_pre, heads, attended_part, part_array, keys_a, keys_b
        )
        wide_a, wide_b, narrow_a, narrow_b = (swap(array, "dp", 1) for array in leaving)
        activated, kept = tie((activated, kept))
    else:
        down_part = dot(activated, grad_mixer, TN).astype(BF)
        up_part = dot(second_low, grad_pre, TN).astype(BF)
        out_parts = jnp.stack([dot(heads[k], attended_part, TN).astype(BF) for k in range(ways)])
    mixer_part = dot(activated, down_weight, NN).astype(BF).reshape(ways, own_rows, width)
    if by_swaps:
        wide_a, wide_b, narrow_a, narrow_b, mixer_part = tie((wide_a, wide_b, narrow_a, narrow_b, mixer_part))
        kept, leave_a, leave_b = halving_sums(kept, (wide_a, narrow_a), (wide_b, narrow_b), wide, narrow)
        got_a, got_b = swap(leave_a, "dp", bit_x), swap(leave_b, "dp", bit_y)
        head_terms, mixer_part, kept = tie((head_terms, mixer_part, kept))
    else:
        head_terms, mixer_part = tie((head_terms, mixer_part))

    mixer_terms = to_all(mixer_part)
    grad_projected, first_gain_part, input_part = attend_back(
        head_terms, qkv, probs, qkv_weight, picked, first_gain[None], hidden_part
    )
    qkv_part = qkv_part_of(first_low, grad_projected)
    input_part = input_part.reshape(ways, own_rows, width)
    if by_swaps:
        got_a, got_b, qkv_part, input_part = tie((got_a, got_b, qkv_part, input_part))
        kept, leave_a, leave_b = halving_sums(kept, (got_a,), (got_b,), wide // 2, narrow // 2)
        mixer_terms, input_part, qkv_part, kept, leave_a, leave_b = tie(
            (mixer_terms, input_part, qkv_part, kept, leave_a, leave_b)
        )
    else:
        mixer_terms, input_part, qkv_part = tie((mixer_terms, input_part, qkv_part))

    input_terms = to_all(input_part)
    if by_swaps:
        got_a, got_b = swap(leave_a, "dp", bit_y), swap(leave_b, "dp", bit_x)
        qkv_got = swap(qkv_part, "dp", 1)
    new_own, grad_score, small = finish_rows(
        mixer_terms,
        picked,
        gating,
        attended,
        grad_rows,
        first_gain_part,
        second_gain_part,
        square,
        routed_square,
        mine_array,
        ways,
    )
    if by_swaps:
        got_a, got_b, new_own = tie((got_a, got_b, new_own))
        lane_a, lane_b, sent = owned_sums(kept, got_a, got_b, new_own, small, wide // 4, ways)
        got_a, got_b = swap(lane_a, "dp", bit_y), swap(lane_b, "dp", bit_x)
        qkv_part, qkv_got, lane_a, lane_b, sent = tie((qkv_part, qkv_got, lane_a, lane_b, sent))
        qkv_a, qkv_b = core_sums(qkv_part, qkv_got)
        input_terms, sent, got_a, got_b, qkv_a, qkv_b = tie((input_terms, sent, got_a, got_b, qkv_a, qkv_b))
    else:
        sent = jnp.concatenate([new_own, split_sums(small)])
        sent = jnp.broadcast_to(sent[None], (ways,) + sent.shape)
        input_terms, sent = tie((input_terms, sent))

    fresh = to_all(sent)
    if by_swaps:
        more_a = [swap(array, "dp", bit_x) for array in (lane_a, got_a)]
        more_b = [swap(array, "dp", bit_y) for array in (lane_b, got_b)]
    last = finish_input(input_terms, grad_rows, grad_score, weight_row, mine_array, ways)
    spots = jnp.stack([mine ^ k for k in range(ways)]).astype(jnp.int32)
    cotangent, last = tie((cotangent, last))
    early = merge_rows(cotangent, route_offset, last, spots[:1])
    if by_swaps:
        more_a, more_b, early, qkv_a, qkv_b = tie((more_a, more_b, early, qkv_a, qkv_b))
        qkv_a_got, qkv_b_got = swap(qkv_a, "dp", bit_y), swap(qkv_b, "dp", bit_x)
        down_near, up_near = gather_blocks([lane_a, got_a] + more_a, [lane_b, got_b] + more_b)
        down_far, up_far = swap(down_near, "dp", 1), swap(up_near, "dp", 1)

        def gathered(order):
            keys = [0]
            for bit in order:
                keys = keys + [k ^ bit for k in keys]
            return jnp.stack([part ^ k for k in keys]).astype(jnp.int32)

        each = hidden // copies

        def by_block(array):
            return array.reshape(-1, each, width)

        down_grad, up_grad = spread_rows(
            by_block(down_near),
            by_block(down_far),
            by_block(up_near),
            by_block(up_far),
            gathered([bit_y, bit_x, 1]),
            gathered([bit_x, bit_y, 1]),
        )
        fresh, last, down_grad, up_grad = tie((fresh, last, down_grad, up_grad))
    else:
        fresh, last = tie((fresh, last))

    input_rows = to_all(last)
    if by_swaps:
        blocks = [first_small(fresh, own_rows)]
        more = [swap(array, "dp", bit_x) for array in blocks]
        qkv_a_got, qkv_b_got, blocks = tie((qkv_a_got, qkv_b_got, blocks))
        qkv_a, qkv_b = lane_sums(qkv_a, qkv_a_got, qkv_b, qkv_b_got)
        more, qkv_a, qkv_b = tie((more, qkv_a, qkv_b))
        blocks = blocks + more
        more = [swap(array, "dp", bit_y) for array in blocks]
        fresh, blocks = tie((fresh, blocks))
    output = merge_rows(tokens, route_offset, fresh, spots[: ways // 2])
    if by_swaps:
        more, output, qkv_a, qkv_b = tie((more, output, qkv_a, qkv_b))
        qkv_a_got, qkv_b_got = swap(qkv_a, "dp", bit_x), swap(qkv_b, "dp", bit_y)
        blocks = blocks + more
        more = [swap(array, "dp", 1) for array in blocks]
        fresh, blocks, qkv_a = tie((fresh, blocks, qkv_a))
    output = merge_rows(tokens, route_offset, fresh, spots[ways // 2 :], output)
    if by_swaps:
        more, output = tie((more, output))
        out_grad, *small = last_small(blocks + more, gathered([bit_x, bit_y, 1]), shares)
        input_rows, early, output, out_grad, small = tie((input_rows, early, output, out_grad, small))
    input_grad = merge_rows(cotangent, route_offset, input_rows, spots[1:], early)
    if by_swaps:
        qkv_a_got, qkv_b_got, input_grad = tie((qkv_a_got, qkv_b_got, input_grad))
        qkv_grad = spread_qkv(qkv_a, qkv_a_got, qkv_b, qkv_b_got, qkv_weight.shape[2])
    if not by_swaps:
        small = sum(joined_sums(fresh[k, own_rows:]) for k in range(ways))
        small = lax.psum(small, "dp")
        small = [small[n : n + 1] for n in range(TERMS)]
        small[3] = small[3][:, :128] * jnp.array((shares + (0.0,) * 126,), F32)
        down_grad, up_grad, qkv_sum, out_sum = (
            lax.psum(v, "dp").astype(F32) for v in (down_part, up_part, qkv_part, out_parts)
        )
        out_grad = jnp.sum(to_all(out_sum.astype(BF)).astype(F32), axis=0)
        qkv_grad = qkv_sum.reshape(3, -1, width).transpose(0, 2, 1)
    router_grad, first_gain_grad, second_gain_grad = (small[n].reshape(width) for n in range(3))
    score_stats = small[3][0, :2]
    return (
        output,
        input_grad,
        router_grad,
        first_gain_grad,
        second_gain_grad,
        qkv_grad,
        out_grad,
        up_grad,
        down_grad,
        score_stats,
    )


def solution(mesh):
    placed = (
        P("dp", None),
        P("dp", None),
        P("dp", None),
        P("dp", None),
        P(),
        P(),
        P(),
        P(None, None, "tensor"),
        P("tensor", None),
        P(None, "tensor"),
        P("tensor", None),
    )
    return jax.shard_map(
        per_device,
        mesh=mesh,
        in_specs=placed,
        out_specs=(
            P("dp", None),
            P("dp", None),
            P(),
            P(),
            P(),
            P(None, None, "tensor"),
            P("tensor", None),
            P(None, "tensor"),
            P("tensor", None),
            P(),
        ),
        check_vma=False,
    )
```

```python
import jax
import jax.numpy as jnp
from jax import lax
from jax.experimental import pallas as pl
from jax.experimental.pallas import tpu as pltpu
from jax.sharding import PartitionSpec as P

BF = jnp.bfloat16
F32 = jnp.float32

NN = ((1,), (0,))
NT = ((1,), (1,))
TN = ((0,), (0,))


def dot(left, right, dims):
    return lax.dot_general(left, right, (dims, ((), ())), preferred_element_type=F32)


def swap(values, axis, bits):
    size = lax.axis_size(axis)
    return lax.ppermute(values, axis, [(i, i ^ bits) for i in range(size)])


def to_all(blocks):
    return lax.all_to_all(blocks, "tensor", 0, 0, tiled=True)


def inverse_rms(rows):
    return lax.rsqrt(jnp.mean(rows * rows, axis=-1, keepdims=True) + eps)


HEAD_DIM = 64
GROUP = 8
TERMS = 4
GAP = 2 * TERMS
eps = 1e-06
mask_fill = -1000000000.0


def small_cost():
    return pl.CostEstimate(flops=1024, bytes_accessed=1024, transcendentals=0)


def cost_of(microseconds):
    return pl.CostEstimate(flops=1024, bytes_accessed=int(microseconds * 3.0e6), transcendentals=0)


def staged(name, body, scalars, arrays, out_shapes, scratch, limit, cost):
    count, outs, extra = len(arrays), len(out_shapes), len(scalars)

    def kernel(*refs):
        scalar_refs, refs = refs[:extra], refs[extra:]
        in_refs, refs = refs[:count], refs[count:]
        out_refs, refs = refs[:outs], refs[outs:]
        held, refs = refs[:count], refs[count:]
        made, refs = refs[:outs], refs[outs:]
        load_sems, store_sems = refs[:2]
        loads = [pltpu.make_async_copy(s, h, load_sems.at[n]) for n, (s, h) in enumerate(zip(in_refs, held))]
        stores = [pltpu.make_async_copy(m, o, store_sems.at[n]) for n, (m, o) in enumerate(zip(made, out_refs))]
        for copy in loads:
            copy.start()
        here, gone = set(), set()

        def load(n):
            if n not in here:
                here.add(n)
                loads[n].wait()
            return held[n]

        def store(*which):
            for n in which:
                gone.add(n)
                stores[n].start()

        body(load, store, made, scalar_refs, refs[2:])
        for n in range(count):
            load(n)
        for n in range(outs):
            if n not in gone:
                store(n)
        for copy in stores:
            copy.wait()

    anywhere = pl.BlockSpec(memory_space=pl.ANY)
    return pl.pallas_call(
        kernel,
        in_specs=[pl.BlockSpec(memory_space=pltpu.SMEM)] * extra + [anywhere] * count,
        out_specs=[anywhere] * outs,
        out_shape=[jax.ShapeDtypeStruct(shape, kind) for shape, kind in out_shapes],
        scratch_shapes=[pltpu.VMEM(a.shape, a.dtype) for a in arrays]
        + [pltpu.VMEM(shape, kind) for shape, kind in out_shapes]
        + [pltpu.SemaphoreType.DMA((count,)), pltpu.SemaphoreType.DMA((outs,))]
        + scratch,
        cost_estimate=cost,
        compiler_params=pltpu.CompilerParams(vmem_limit_bytes=limit << 20),
        name=name,
    )(*scalars, *arrays)


def pick_rows(base, offsets, ways):
    rows, width = base.shape
    chunks = ways
    block = rows // chunks
    groups = block // GROUP
    sub = 256
    sub_groups = sub // GROUP

    def kernel(base_ref, offset_ref, picked_ref, held, sems):
        def load(n):
            part = pl.ds(pl.multiple_of(n * block, block), block)
            return pltpu.make_async_copy(base_ref.at[part], held.at[part], sems.at[n])

        for n in range(chunks):
            load(n).start()
        local = lax.broadcasted_iota(jnp.int32, (sub, sub_groups), 0) - GROUP * lax.broadcasted_iota(
            jnp.int32, (sub, sub_groups), 1
        )

        def step(n, carry):
            load(n).wait()
            offsets = offset_ref[:, pl.ds(pl.multiple_of(n * groups, groups), groups)]
            for s in range(block // sub):
                chosen = (local == offsets[:, s * sub_groups : (s + 1) * sub_groups]).astype(F32).astype(BF)
                rows_in = held[pl.ds(pl.multiple_of(n * block + s * sub, sub), sub), :]
                to = pl.ds(pl.multiple_of(n * groups + s * sub_groups, sub_groups), sub_groups)
                picked_ref[to, :] = dot(chosen, rows_in, TN).astype(BF)
            return carry

        lax.fori_loop(0, chunks, step, 0)

    whole = pl.BlockSpec(memory_space=pltpu.VMEM)
    return pl.pallas_call(
        kernel,
        in_specs=[pl.BlockSpec(memory_space=pl.ANY), whole],
        out_specs=whole,
        out_shape=jax.ShapeDtypeStruct((rows // GROUP, width), BF),
        scratch_shapes=[pltpu.VMEM((rows, width), BF), pltpu.SemaphoreType.DMA((chunks,))],
        cost_estimate=small_cost(),
        compiler_params=pltpu.CompilerParams(vmem_limit_bytes=60 << 20),
        name="pick_rows",
    )(base, offsets)


def score_sums(base, router, mine, ways):
    rows, width = base.shape
    block = rows // ways

    def kernel(mine_ref, base_ref, router_ref, square_ref):
        score = jnp.sum(base_ref[...].astype(F32) * router_ref[...].astype(F32), axis=1, keepdims=True)
        square_ref[...] = jnp.broadcast_to(jnp.sum(score * score, axis=0, keepdims=True), square_ref.shape)

    return pl.pallas_call(
        kernel,
        grid_spec=pltpu.PrefetchScalarGridSpec(
            num_scalar_prefetch=1,
            grid=(1,),
            in_specs=[
                pl.BlockSpec((block, width), lambda i, m: (m[0], 0)),
                pl.BlockSpec((1, width), lambda i, m: (0, 0)),
            ],
            out_specs=pl.BlockSpec((1, 128), lambda i, m: (0, 0)),
        ),
        out_shape=jax.ShapeDtypeStruct((1, 128), F32),
        cost_estimate=small_cost(),
        name="score_sums",
    )(mine, base, router)


def pick_only(base, offsets, ways):
    rows, width = base.shape
    block = rows // ways
    groups = block // GROUP
    sub = 256
    sub_groups = sub // GROUP

    def kernel(base_ref, offset_ref, picked_ref):
        local = lax.broadcasted_iota(jnp.int32, (sub, sub_groups), 0) - GROUP * lax.broadcasted_iota(
            jnp.int32, (sub, sub_groups), 1
        )
        for s in range(block // sub):
            to = slice(s * sub_groups, (s + 1) * sub_groups)
            chosen = (local == offset_ref[:, to]).astype(F32).astype(BF)
            picked_ref[to, :] = dot(chosen, base_ref[s * sub : (s + 1) * sub, :], TN).astype(BF)

    return pl.pallas_call(
        kernel,
        grid=(ways,),
        in_specs=[pl.BlockSpec((block, width), lambda i: (i, 0)), pl.BlockSpec((1, groups), lambda i: (0, i))],
        out_specs=pl.BlockSpec((groups, width), lambda i: (i, 0)),
        out_shape=jax.ShapeDtypeStruct((rows // GROUP, width), BF),
        cost_estimate=small_cost(),
        name="pick_only",
    )(base, offsets)


def merge_rows(base, offsets, pieces, mine, which, held_out=None):
    rows, width = base.shape
    ways, depth, _ = pieces.shape
    count = rows // ways
    groups = count // GROUP
    kept = [] if held_out is None else [held_out]
    sub = 256
    sub_groups = sub // GROUP

    first = which.start

    def kernel(part_ref, base_ref, offset_ref, piece_ref, *rest):
        out_ref = rest[-1]
        local = lax.broadcasted_iota(jnp.int32, (sub, sub_groups), 0) - GROUP * lax.broadcasted_iota(
            jnp.int32, (sub, sub_groups), 1
        )
        for s in range(count // sub):
            here = slice(s * sub, (s + 1) * sub)
            to = slice(s * sub_groups, (s + 1) * sub_groups)
            chosen = (local == offset_ref[:, to]).astype(F32)
            hit = jnp.sum(chosen, axis=1, keepdims=True) > 0.5
            spread = dot(chosen.astype(BF), piece_ref[0, to, :], NN)
            out_ref[here, :] = jnp.where(hit, spread, base_ref[here, :].astype(F32)).astype(BF)

    grid_spec = pltpu.PrefetchScalarGridSpec(
        num_scalar_prefetch=1,
        grid=(len(which),),
        in_specs=[
            pl.BlockSpec((count, width), lambda i, m: (m[0] ^ (i + first), 0)),
            pl.BlockSpec((1, groups), lambda i, m: (0, m[0] ^ (i + first))),
            pl.BlockSpec((1, depth, width), lambda i, m: (m[0] ^ (i + first), 0, 0)),
        ]
        + [pl.BlockSpec(memory_space=pl.ANY)] * len(kept),
        out_specs=pl.BlockSpec((count, width), lambda i, m: (m[0] ^ (i + first), 0)),
    )
    return pl.pallas_call(
        kernel,
        grid_spec=grid_spec,
        out_shape=jax.ShapeDtypeStruct((rows, width), BF),
        input_output_aliases={4: 0} if kept else {},
        cost_estimate=small_cost(),
        name="merge_rows",
    )(mine, base, offsets, pieces, *kept)


def attend(picked, gain, weight, seq_row, ways):
    rows, width = picked.shape
    heads_width = weight.shape[2]
    heads = heads_width // HEAD_DIM
    block = min(256, rows)

    def body(load, store, outs, scalars, scratch):
        low_ref, qkv_ref, out_ref, *probs_refs = outs
        values = load(0)[...].astype(F32)
        low_ref[...] = (values * inverse_rms(values) * load(1)[...].astype(F32)).astype(BF)
        store(0)
        weight_ref = load(2)
        for n in range(3):
            qkv_ref[n] = dot(low_ref[...], weight_ref[n], NN).astype(BF)
        store(1)
        sequence = load(3)[...].astype(F32)
        column = jnp.broadcast_to(sequence, (128, rows)).T[:, :1]
        lane_head = lax.broadcasted_iota(jnp.int32, (1, heads_width), 1) // HEAD_DIM
        for n in reversed(range(rows // block)):
            start, stop = n * block, (n + 1) * block
            query = qkv_ref[0, start:stop, :] * BF(HEAD_DIM ** (-0.5))
            order = lax.broadcasted_iota(jnp.int32, (block, stop), 0) + start
            keys = lax.broadcasted_iota(jnp.int32, (block, stop), 1)
            allowed = (column[start:stop, :] == sequence[:, :stop]) & (order >= keys)
            total = jnp.zeros((block, heads_width), F32)
            for head in range(heads):
                here = lane_head == head
                key = jnp.where(here, qkv_ref[1, :stop, :], BF(0))
                logits = jnp.where(allowed, dot(query, key, NT), mask_fill)
                raised = jnp.exp(logits - jnp.max(logits, axis=-1, keepdims=True))
                probs = (raised * (1.0 / jnp.sum(raised, axis=-1, keepdims=True))).astype(BF)
                probs_refs[n][head] = probs
                value = jnp.where(here, qkv_ref[2, :stop, :], BF(0))
                total = total + dot(probs, value, NN)
            for k in range(ways):
                out_ref[k, start:stop, :] = total.astype(BF)
            store(3 + n)

    return staged(
        "attend",
        body,
        [],
        [picked, gain, weight, seq_row],
        [
            ((rows, width), BF),
            ((3, rows, heads_width), BF),
            ((ways, rows, heads_width), BF),
        ]
        + [((heads, block, (n + 1) * block), BF) for n in range(rows // block)],
        [],
        60,
        small_cost(),
    )


def feed_forward(heads, own_weight, quarters, picked, gain, up, grad_act, grad_mixer, part, mine, ways):
    rows, width = picked.shape
    hidden = up.shape[1]
    sub = min(512, hidden)
    count, _, heads_width = heads.shape
    piece = heads_width // 4
    own = rows // ways
    slope = 0.7978845608028654
    cubic = 0.044715

    def body(load, store, outs, scalars, scratch):
        part_ref, mine_ref = scalars
        attended_ref, low_ref, act_ref, pre_ref, hidden_ref, part_out_ref, gain_part_ref, sent_ref = outs
        total, state, weights = scratch
        quarter = part_ref[0] & 3
        heads_ref = load(0)
        weights[0] = load(1)[...]
        for n in range(4):
            start = pl.multiple_of((quarter ^ n) * piece, piece)
            source = load(2 + n)
            for k in range(1, count):
                weights[k, pl.ds(start, piece), :] = source[k - 1]
        attended = dot(heads_ref[mine_ref[0]], weights[0], NN)
        for k in range(1, count):
            attended = attended + dot(heads_ref[mine_ref[0] ^ k], weights[k], NN)
        total[...] = attended
        attended_ref[...] = total[pl.ds(pl.multiple_of(mine_ref[0] * own, own), own), :]
        state_in = load(6)[...].astype(F32) + attended
        state[...] = state_in
        gain_row = load(7)[...].astype(F32)
        low_ref[...] = (state_in * inverse_rms(state_in) * gain_row).astype(BF)
        store(0, 1)
        up_ref, act_grad_ref = load(8), load(9)
        for s in range(hidden // sub):
            lanes = slice(s * sub, (s + 1) * sub)
            value = dot(low_ref[...], up_ref[:, lanes], NN)
            square = value * value
            bent = jnp.tanh(value * (slope + (slope * cubic) * square))
            half = 0.5 * (1.0 + bent)
            act_ref[:, lanes] = (value * half).astype(BF)
            rise = half + (0.5 * value) * (1.0 - bent * bent) * (slope + (3.0 * slope * cubic) * square)
            pre = (act_grad_ref[:, lanes] * rise).astype(BF)
            pre_ref[:, lanes] = pre
            term = dot(pre, up_ref[:, lanes], NT)
            if s == 0:
                total[...] = term
            else:
                total[...] += term
        store(2, 3)
        state_in = state[...]
        grad = total[...]
        inverse = inverse_rms(state_in)
        normal = state_in * inverse
        gain_part_ref[...] = jnp.sum(grad * normal, axis=0, keepdims=True)
        scaled = grad * gain_row
        along = jnp.mean(scaled * normal, axis=-1, keepdims=True)
        back = inverse * (scaled - normal * along)
        hidden_ref[...] = back.astype(BF)
        part_out_ref[...] = (back + load(10)[...].astype(F32) * (1.0 / count)).astype(BF)
        store(4, 5, 6)
        for k in range(count):
            sent_ref[mine_ref[0] ^ k] = dot(part_out_ref[...], weights[k], NT).astype(BF)

    return staged(
        "feed_forward",
        body,
        [part, mine],
        [heads, own_weight, *quarters, picked, gain, up, grad_act, grad_mixer],
        [
            ((own, width), F32),
            ((rows, width), BF),
            ((rows, hidden), BF),
            ((rows, hidden), BF),
            ((rows, width), BF),
            ((rows, width), BF),
            ((1, width), F32),
            (heads.shape, BF),
        ],
        [
            pltpu.VMEM((rows, width), F32),
            pltpu.VMEM((rows, width), F32),
            pltpu.VMEM((count, heads_width, width), BF),
        ],
        60,
        small_cost(),
    )


def act_grads(picked, router, grad_rows, down):
    rows, width = grad_rows.shape

    def kernel(picked_ref, router_ref, rows_ref, down_ref, gating_ref, square_ref, mixer_ref, grad_ref):
        score = jnp.sum(picked_ref[...].astype(F32) * router_ref[...].astype(F32), axis=-1, keepdims=True)
        gating = jax.nn.sigmoid(score)
        gating_ref[...] = gating
        square_ref[...] = jnp.broadcast_to(jnp.sum(score * score, axis=0, keepdims=True), square_ref.shape)
        mixer_ref[...] = (gating * rows_ref[...].astype(F32)).astype(BF)
        grad_ref[...] = dot(mixer_ref[...], down_ref[...], NT)

    whole = pl.BlockSpec(memory_space=pltpu.VMEM)
    return pl.pallas_call(
        kernel,
        in_specs=[whole] * 4,
        out_specs=[whole] * 4,
        out_shape=[
            jax.ShapeDtypeStruct((rows, 1), F32),
            jax.ShapeDtypeStruct((1, 128), F32),
            jax.ShapeDtypeStruct((rows, width), BF),
            jax.ShapeDtypeStruct((rows, down.shape[0]), F32),
        ],
        cost_estimate=small_cost(),
        name="act_grads",
    )(picked, router, grad_rows, down)


def attend_back(head_terms, qkv, probs, weight, picked, gain, hidden_part):
    rows, width = picked.shape
    heads_width = weight.shape[2]
    heads = heads_width // HEAD_DIM
    block = min(256, rows)
    scale = HEAD_DIM ** (-0.5)

    def kernel(
        head_ref,
        qkv_ref,
        weight_ref,
        picked_ref,
        gain_ref,
        hidden_ref,
        *rest,
    ):
        probs_refs, (grads_ref, gain_part_ref, result, grad_key, grad_value) = rest[: len(probs)], rest[len(probs) :]
        lane_head = lax.broadcasted_iota(jnp.int32, (1, heads_width), 1) // HEAD_DIM
        for start in reversed(range(0, rows, block)):
            stop = start + block
            here_rows = slice(start, stop)
            grad_head = head_ref[0, here_rows, :].astype(F32)
            for k in range(1, head_ref.shape[0]):
                grad_head = grad_head + head_ref[k, here_rows, :].astype(F32)
            grad_head = grad_head.astype(BF)
            query = qkv_ref[0, here_rows, :] * BF(scale)
            grad_query = jnp.zeros((block, heads_width), F32)
            add_key = jnp.zeros((stop, heads_width), F32)
            add_value = jnp.zeros((stop, heads_width), F32)
            for head in range(heads):
                here = lane_head == head
                value = jnp.where(here, qkv_ref[2, :stop, :], BF(0))
                key = jnp.where(here, qkv_ref[1, :stop, :], BF(0))
                low = probs_refs[start // block][head]
                weighted = low.astype(F32) * dot(grad_head, value, NT)
                row_sum = jnp.sum(weighted, axis=-1, keepdims=True)
                slopes = (weighted - low.astype(F32) * row_sum).astype(BF)
                grad_query = grad_query + dot(slopes, key, NN)
                add_key = add_key + dot(slopes, jnp.where(here, query, BF(0)), TN)
                add_value = add_value + dot(low, jnp.where(here, grad_head, BF(0)), TN)
            grads_ref[0, here_rows, :] = (grad_query * scale).astype(BF)
            if stop == rows:
                grad_key[...] = add_key
                grad_value[...] = add_value
            else:
                grad_key[:stop, :] += add_key
                grad_value[:stop, :] += add_value
        grads_ref[1] = grad_key[...].astype(BF)
        grads_ref[2] = grad_value[...].astype(BF)
        first = dot(grads_ref[0], weight_ref[0], NT)
        for n in range(1, 3):
            first = first + dot(grads_ref[n], weight_ref[n], NT)
        values = picked_ref[...].astype(F32)
        inverse = inverse_rms(values)
        normal = values * inverse
        gain_part_ref[...] = jnp.sum(first * normal, axis=0, keepdims=True)
        scaled = first * gain_ref[...].astype(F32)
        along = jnp.mean(scaled * normal, axis=-1, keepdims=True)
        result[...] = (hidden_ref[...].astype(F32) + inverse * (scaled - normal * along)).astype(BF)

    whole = pl.BlockSpec(memory_space=pltpu.VMEM)
    return pl.pallas_call(
        kernel,
        in_specs=[whole] * (6 + len(probs)),
        out_specs=[whole] * 3,
        out_shape=[
            jax.ShapeDtypeStruct((3, rows, heads_width), BF),
            jax.ShapeDtypeStruct((1, width), F32),
            jax.ShapeDtypeStruct((rows, width), BF),
        ],
        scratch_shapes=[
            pltpu.VMEM((rows, heads_width), F32),
            pltpu.VMEM((rows, heads_width), F32),
        ],
        cost_estimate=small_cost(),
        compiler_params=pltpu.CompilerParams(vmem_limit_bytes=20 << 20),
        name="attend_back",
    )(head_terms, qkv, weight, picked, gain, hidden_part, *probs)


def spread_rows(down, up, order_down, order_up, part):
    count = len(down)
    wide, width = down[0].shape
    rows = wide // (2 ** len(order_down) // count)
    each = wide // rows

    def kernel(part_ref, *refs):
        down_out, up_out = refs[2 * count :]
        for n in range(count):

            @pl.when(pl.program_id(0) // each == n)
            def _():
                down_out[...] = refs[n][...].astype(F32)
                up_out[...] = refs[count + n][...].astype(F32)

    def source(n):
        return pl.BlockSpec((rows, width), lambda i, p: (jnp.clip(i - n * each, 0, each - 1), 0))

    def target(order):
        def place(i, p):
            key = sum((i >> n & 1) * bit for n, bit in enumerate(order))
            return p[0] ^ key, 0

        return pl.BlockSpec((rows, width), place)

    return pl.pallas_call(
        kernel,
        grid_spec=pltpu.PrefetchScalarGridSpec(
            num_scalar_prefetch=1,
            grid=(count * each,),
            in_specs=[source(n) for n in range(count)] * 2,
            out_specs=[target(order_down), target(order_up)],
        ),
        out_shape=[jax.ShapeDtypeStruct((count * wide, width), F32)] * 2,
        cost_estimate=small_cost(),
        name="spread_rows",
    )(part, *down, *up)


def qkv_part_of(first_low, grads):
    rows, width = first_low.shape
    part_width = grads.shape[2]

    def kernel(low_ref, grads_ref, out_ref):
        for n in range(3):
            product = dot(grads_ref[n], low_ref[...], TN)
            out_ref[n * part_width : (n + 1) * part_width, :] = product.astype(BF)

    whole = pl.BlockSpec(memory_space=pltpu.VMEM)
    return pl.pallas_call(
        kernel,
        in_specs=[whole] * 2,
        out_specs=whole,
        out_shape=jax.ShapeDtypeStruct((3 * part_width, width), BF),
        cost_estimate=small_cost(),
        compiler_params=pltpu.CompilerParams(vmem_limit_bytes=12 << 20),
        name="qkv_part",
    )(first_low, grads)


def spread_qkv(lane_a, got_a, lane_b, got_b, part_width):
    rows, width = lane_a.shape
    tile = 128

    def kernel(a_ref, a_got, b_ref, b_got, out_ref):
        for n in range(2 * rows // tile):
            start = n * tile % rows
            ref, got = (a_ref, a_got) if n * tile < rows else (b_ref, b_got)
            lane, column = divmod(n * tile, part_width)
            piece = ref[start : start + tile, :].astype(F32) + got[start : start + tile, :].astype(F32)
            out_ref[lane, :, column : column + tile] = piece.T

    whole = pl.BlockSpec(memory_space=pltpu.VMEM)
    return pl.pallas_call(
        kernel,
        in_specs=[whole] * 4,
        out_specs=whole,
        out_shape=jax.ShapeDtypeStruct((2 * rows // part_width, width, part_width), F32),
        cost_estimate=small_cost(),
        compiler_params=pltpu.CompilerParams(vmem_limit_bytes=16 << 20),
        name="spread_qkv",
    )(lane_a, got_a, lane_b, got_b)


def core_grads(activated, grad_mixer, second_low, grad_pre, heads, attended_part, part, keys_a, keys_b):
    rows, hidden = activated.shape
    width = grad_mixer.shape[1]
    copies = len(keys_a)
    half = copies // 2
    count, _, heads_width = heads.shape
    block = hidden // copies
    small = heads_width // copies
    many = count // 2
    depth = half * (block + many * small)

    def kernel(part_ref, act_ref, mixer_ref, low_ref, pre_ref, heads_ref, term_ref, keep_ref, *rest):
        wide_refs, narrow_refs, (full, narrow) = rest[0:2], rest[2:4], rest[4:]

        def place(source, each, lane, keys, first, stride):
            for n, key in enumerate(keys):
                start = pl.multiple_of((part_ref[0] ^ key) * each, each)
                at = first + (n % half) * stride
                piece = source[pl.ds(start, each), :]
                if n < half:
                    keep_ref[lane, at : at + each, :] = piece
                elif first == 0:
                    wide_refs[lane][at : at + each, :] = piece
                else:
                    narrow_refs[lane][at - half * block : at - half * block + each, :] = piece

        full[...] = dot(act_ref[...], mixer_ref[...], TN).astype(BF)
        place(full, block, 0, keys_a, 0, block)
        full[...] = dot(low_ref[...], pre_ref[...], TN).astype(BF)
        place(full, block, 1, keys_b, 0, block)
        for k in range(count):
            narrow[...] = dot(heads_ref[k], term_ref[...], TN).astype(BF)
            lane, spot = divmod(k, many)
            place(narrow, small, lane, keys_b if lane else keys_a, half * block + spot * small, many * small)

    whole = pl.BlockSpec(memory_space=pltpu.VMEM)
    wide_shape = jax.ShapeDtypeStruct((half * block, width), BF)
    narrow_shape = jax.ShapeDtypeStruct((half * many * small, width), BF)
    return pl.pallas_call(
        kernel,
        in_specs=[pl.BlockSpec(memory_space=pltpu.SMEM)] + [whole] * 6,
        out_specs=[whole] * 5,
        out_shape=[jax.ShapeDtypeStruct((2, depth, width), BF)] + [wide_shape] * 2 + [narrow_shape] * 2,
        scratch_shapes=[pltpu.VMEM((hidden, width), BF), pltpu.VMEM((heads_width, width), BF)],
        cost_estimate=small_cost(),
        compiler_params=pltpu.CompilerParams(vmem_limit_bytes=14 << 20),
        name="core_grads",
    )(part, activated, grad_mixer, second_low, grad_pre, heads, attended_part)


def plus(left, right):
    return (left.astype(F32) + right.astype(F32)).astype(BF)


def halving_sums(keep, got_a, got_b, wide, narrow):
    width = keep.shape[2]
    count = len(got_a)

    def kernel(keep_ref, *refs):
        a_got, b_got, (stay_ref, a_out, b_out) = refs[:count], refs[count : 2 * count], refs[2 * count :]
        for lane, got, out in ((0, a_got, a_out), (1, b_got, b_out)):
            for first, size, at in ((0, wide // 2, 0), (wide, narrow // 2, wide // 2)):
                source, shift = (got[1], wide) if count == 2 and first else (got[0], 0)
                to = slice(at, at + size)
                for start, target in ((first, stay_ref.at[lane]), (first + size, out)):
                    here = slice(start - shift, start - shift + size)
                    target[to, :] = plus(keep_ref[lane, start : start + size, :], source[here, :])

    whole = pl.BlockSpec(memory_space=pltpu.VMEM)
    depth = (wide + narrow) // 2
    lane_shape = jax.ShapeDtypeStruct((depth, width), BF)
    return pl.pallas_call(
        kernel,
        in_specs=[whole] * (1 + 2 * count),
        out_specs=[whole] * 3,
        out_shape=[jax.ShapeDtypeStruct((2, depth, width), BF), lane_shape, lane_shape],
        cost_estimate=small_cost(),
        compiler_params=pltpu.CompilerParams(vmem_limit_bytes=14 << 20),
        name="halving_sums",
    )(keep, *got_a, *got_b)


def owned_sums(keep, got_a, got_b, fresh, small, wide, ways):
    width = keep.shape[2]
    narrow = keep.shape[1] - wide
    own = fresh.shape[0]
    many = ways // 2
    each = narrow // many
    depth = own + GAP + each

    def kernel(keep_ref, a_got, b_got, fresh_ref, small_ref, a_out, b_out, sent_ref):
        sums = split_sums(small_ref[...])
        for lane, got, out in ((0, a_got, a_out), (1, b_got, b_out)):
            out[...] = plus(keep_ref[lane, :wide, :], got[:wide, :])
            done = plus(keep_ref[lane, wide:, :], got[wide:, :])
            for spot in range(many):
                k = lane * many + spot
                sent_ref[k, :own, :] = fresh_ref[...]
                sent_ref[k, own : own + GAP, :] = sums
                sent_ref[k, own + GAP :, :] = done[spot * each : (spot + 1) * each, :]

    whole = pl.BlockSpec(memory_space=pltpu.VMEM)
    lane_shape = jax.ShapeDtypeStruct((wide, width), BF)
    return pl.pallas_call(
        kernel,
        in_specs=[whole] * 5,
        out_specs=[whole] * 3,
        out_shape=[lane_shape, lane_shape, jax.ShapeDtypeStruct((ways, depth, width), BF)],
        cost_estimate=small_cost(),
        compiler_params=pltpu.CompilerParams(vmem_limit_bytes=10 << 20),
        name="owned_sums",
    )(keep, got_a, got_b, fresh, small)


def core_sums(rows, other):
    depth, width = rows.shape
    third = depth // 2

    def kernel(rows_ref, other_ref, a_out, b_out):
        a_out[...] = plus(rows_ref[:third, :], other_ref[:third, :])
        b_out[...] = plus(rows_ref[third:, :], other_ref[third:, :])

    whole = pl.BlockSpec(memory_space=pltpu.VMEM)
    return pl.pallas_call(
        kernel,
        in_specs=[whole] * 2,
        out_specs=[whole] * 2,
        out_shape=[jax.ShapeDtypeStruct((third, width), BF)] * 2,
        cost_estimate=small_cost(),
        compiler_params=pltpu.CompilerParams(vmem_limit_bytes=10 << 20),
        name="core_sums",
    )(rows, other)


def lane_sums(lane_a, got_a, lane_b, got_b):
    def kernel(a_ref, a_got, b_ref, b_got, a_out, b_out):
        a_out[...] = plus(a_ref[...], a_got[...])
        b_out[...] = plus(b_ref[...], b_got[...])

    whole = pl.BlockSpec(memory_space=pltpu.VMEM)
    return pl.pallas_call(
        kernel,
        in_specs=[whole] * 4,
        out_specs=[whole] * 2,
        out_shape=[jax.ShapeDtypeStruct(lane_a.shape, BF)] * 2,
        cost_estimate=small_cost(),
        compiler_params=pltpu.CompilerParams(vmem_limit_bytes=12 << 20),
        name="lane_sums",
    )(lane_a, got_a, lane_b, got_b)


def gather_blocks(blocks_a, blocks_b):
    wide, width = blocks_a[0].shape
    count = len(blocks_a)

    def kernel(*refs):
        for lane in range(2):
            for n in range(count):
                refs[2 * count + lane][n * wide : (n + 1) * wide, :] = refs[lane * count + n][...]

    whole = pl.BlockSpec(memory_space=pltpu.VMEM)
    return pl.pallas_call(
        kernel,
        in_specs=[whole] * (2 * count),
        out_specs=[whole] * 2,
        out_shape=[jax.ShapeDtypeStruct((count * wide, width), BF)] * 2,
        cost_estimate=small_cost(),
        compiler_params=pltpu.CompilerParams(vmem_limit_bytes=10 << 20),
        name="gather_blocks",
    )(*blocks_a, *blocks_b)


def split_sums(values):
    high = values.astype(BF)
    low = (values - high.astype(F32)).astype(BF)
    return jnp.concatenate([high, low], axis=0)


def joined_sums(rows):
    return rows[:TERMS].astype(F32) + rows[TERMS : 2 * TERMS].astype(F32)


def first_small(received, own):
    ways, depth, width = received.shape
    each = depth - own - GAP

    def kernel(got_ref, out_ref):
        total = got_ref[0, own + GAP :, :].astype(F32)
        sums = joined_sums(got_ref[0, own : own + GAP, :])
        for k in range(1, ways):
            total = total + got_ref[k, own + GAP :, :].astype(F32)
            sums = sums + joined_sums(got_ref[k, own : own + GAP, :])
        out_ref[:each, :] = total.astype(BF)
        out_ref[each:, :] = split_sums(sums)

    whole = pl.BlockSpec(memory_space=pltpu.VMEM)
    return pl.pallas_call(
        kernel,
        in_specs=[whole],
        out_specs=whole,
        out_shape=jax.ShapeDtypeStruct((each + GAP, width), BF),
        cost_estimate=small_cost(),
        compiler_params=pltpu.CompilerParams(vmem_limit_bytes=8 << 20),
        name="first_small",
    )(received)


def last_small(blocks, keys, part, shares):
    depth, width = blocks[0].shape
    each = depth - GAP
    count = len(blocks)

    def kernel(part_ref, *refs):
        out_ref, small_refs = refs[count], refs[count + 1 :]
        total = joined_sums(refs[0][each:, :])
        for n in range(1, count):
            total = total + joined_sums(refs[n][each:, :])
        for n in range(TERMS - 1):
            small_refs[n][...] = total[n : n + 1, :]
        lane = lax.broadcasted_iota(jnp.int32, (1, 128), 1)
        small_refs[TERMS - 1][...] = total[TERMS - 1 :, :128] * jnp.where(lane == 0, shares[0], shares[1])
        for n in range(count):
            start = pl.multiple_of((part_ref[0] ^ keys[n]) * each, each)
            out_ref[pl.ds(start, each), :] = refs[n][:each, :].astype(F32)

    whole = pl.BlockSpec(memory_space=pltpu.VMEM)
    return pl.pallas_call(
        kernel,
        in_specs=[pl.BlockSpec(memory_space=pltpu.SMEM)] + [whole] * count,
        out_specs=[whole] * (1 + TERMS),
        out_shape=[jax.ShapeDtypeStruct((count * each, width), F32)] + [jax.ShapeDtypeStruct((1, width), F32)] * (TERMS - 1)
        + [jax.ShapeDtypeStruct((1, 128), F32)],
        cost_estimate=small_cost(),
        compiler_params=pltpu.CompilerParams(vmem_limit_bytes=10 << 20),
        name="last_small",
    )(part, *blocks)


def finish_rows(mixer_terms, picked, gating, attended, grad_rows, gain_one, gain_two, square, routed_square, mine, ways):
    rows, width = picked.shape
    own = rows // ways

    def kernel(
        mine_ref,
        terms_ref,
        picked_ref,
        gating_ref,
        attended_ref,
        rows_ref,
        one_ref,
        two_ref,
        square_ref,
        routed_ref,
        new_ref,
        score_ref,
        small_ref,
    ):
        branch = attended_ref[...]
        for k in range(ways):
            branch = branch + terms_ref[k].astype(F32)
        values = picked_ref[...].astype(F32)
        gate = gating_ref[...]
        new_ref[...] = (values + gate * branch).astype(BF)
        along = jnp.sum(rows_ref[...].astype(F32) * branch, axis=-1, keepdims=True)
        score = along * gate * (1.0 - gate)
        score_ref[...] = score
        small_ref[0:1, :] = jnp.sum(score * values, axis=0, keepdims=True)
        small_ref[1:2, :] = one_ref[...]
        small_ref[2:3, :] = two_ref[...]
        lane = lax.broadcasted_iota(jnp.int32, (1, width), 1)
        both = jnp.where(lane == 0, square_ref[:, 0:1], routed_ref[:, 0:1] * (1.0 / ways))
        small_ref[3:4, :] = jnp.where(lane < 2, both, 0.0)

    def block(shape):
        return pl.BlockSpec(shape, lambda i, m: (m[0], 0))

    def fixed(shape):
        return pl.BlockSpec(shape, lambda i, m: (0, 0))

    return pl.pallas_call(
        kernel,
        grid_spec=pltpu.PrefetchScalarGridSpec(
            num_scalar_prefetch=1,
            grid=(1,),
            in_specs=[pl.BlockSpec(mixer_terms.shape, lambda i, m: (0, 0, 0))]
            + [block((own, width)), block((own, 1)), fixed((own, width)), block((own, width))]
            + [fixed((1, width))] * 2
            + [fixed((1, 128))] * 2,
            out_specs=[fixed((own, width)), fixed((own, 1)), fixed((4, width))],
        ),
        out_shape=[
            jax.ShapeDtypeStruct((own, width), BF),
            jax.ShapeDtypeStruct((own, 1), F32),
            jax.ShapeDtypeStruct((4, width), F32),
        ],
        cost_estimate=cost_of(10),
        name="finish_rows",
    )(mine, mixer_terms, picked, gating, attended, grad_rows, gain_one, gain_two, square, routed_square)


def finish_input(terms, grad_rows, score, router, mine, ways):
    rows, width = grad_rows.shape
    own = rows // ways

    def kernel(mine_ref, terms_ref, rows_ref, score_ref, router_ref, out_ref):
        total = rows_ref[...].astype(F32) + score_ref[...] * router_ref[...].astype(F32)
        for k in range(ways):
            total = total + terms_ref[k].astype(F32)
        for k in range(ways):
            out_ref[k] = total.astype(BF)

    def fixed(shape):
        return pl.BlockSpec(shape, lambda i, m: (0,) * len(shape))

    return pl.pallas_call(
        kernel,
        grid_spec=pltpu.PrefetchScalarGridSpec(
            num_scalar_prefetch=1,
            grid=(1,),
            in_specs=[
                fixed((ways, own, width)),
                pl.BlockSpec((own, width), lambda i, m: (m[0], 0)),
                fixed((own, 1)),
                fixed((1, width)),
            ],
            out_specs=fixed((ways, own, width)),
        ),
        out_shape=jax.ShapeDtypeStruct((ways, own, width), BF),
        cost_estimate=small_cost(),
        compiler_params=pltpu.CompilerParams(vmem_limit_bytes=8 << 20),
        name="finish_input",
    )(mine, terms, grad_rows, score, router)


def split_kept(count, order):
    keys = [0]
    for bit in reversed(order):
        keys = keys + [k ^ bit for k in keys]
    return keys


def per_device(
    tokens,
    route_offset,
    unit_sequence,
    cotangent,
    router_weight,
    first_gain,
    second_gain,
    qkv_weight,
    out_weight,
    up_weight,
    down_weight,
):
    rows_local, width = tokens.shape
    routed = route_offset.shape[1]
    ways = lax.axis_size("tensor")
    copies = lax.axis_size("dp")
    mine = lax.axis_index("tensor")
    part = lax.axis_index("dp")
    mine_array = jnp.reshape(mine, (1,)).astype(jnp.int32)
    part_array = jnp.reshape(part, (1,)).astype(jnp.int32)
    ladder = [1 << b for b in range(1, copies.bit_length() - 1)]
    order_a = [1] + ladder
    order_b = [1] + ladder[::-1]
    keys_a = split_kept(copies, order_a)
    keys_b = split_kept(copies, order_b)

    tie = lax.optimization_barrier
    own_rows = routed // ways
    heads_width = out_weight.shape[0]
    hidden = up_weight.shape[1]
    by_swaps = copies == 8
    bit_x, bit_y = 2, 4
    shares = (1.0 / (rows_local * copies), 1.0 / (routed * copies))

    quarter = part & 3
    piece_rows = heads_width // 4
    piece = lax.dynamic_slice_in_dim(out_weight, quarter * piece_rows, piece_rows, 0)
    here = [swap(piece, "tensor", k) for k in range(1, ways)]

    picked = pick_rows(tokens, route_offset, ways)
    first_low, qkv, head_out, *probs = attend(picked, first_gain[None], qkv_weight, unit_sequence, ways)
    here, head_out = tie((here, head_out))

    heads = to_all(head_out)
    here = jnp.stack(here)
    beside, across = swap(here, "dp", bit_x), swap(here, "dp", 1)
    cotangent, router_weight, second_gain, here, head_out = tie(
        (cotangent, router_weight, second_gain, here, head_out)
    )
    weight_row = router_weight[None]
    grad_rows = pick_only(cotangent, route_offset, ways)
    beside, across, here, grad_rows = tie((beside, across, here, grad_rows))
    quarters = [here, across, beside, swap(beside, "dp", 1)]
    gating, routed_square, grad_mixer, grad_act = act_grads(picked, weight_row, grad_rows, down_weight)
    square = score_sums(tokens, weight_row, mine_array, ways)
    heads, quarters, grad_act, grad_mixer, square = tie((heads, quarters, grad_act, grad_mixer, square))
    attended, second_low, activated, grad_pre, hidden_part, attended_part, second_gain_part, head_sent = feed_forward(
        heads,
        out_weight,
        quarters,
        picked,
        second_gain[None],
        up_weight,
        grad_act,
        grad_mixer,
        part_array,
        mine_array,
        ways,
    )

    head_terms = to_all(head_sent)
    wide = hidden // 2
    narrow = heads_width * ways // 4
    if by_swaps:
        kept, *leaving = core_grads(
            activated, grad_mixer, second_low, grad_pre, heads, attended_part, part_array, keys_a, keys_b
        )
        wide_a, wide_b, narrow_a, narrow_b = (swap(array, "dp", 1) for array in leaving)
        activated, kept = tie((activated, kept))
    else:
        down_part = dot(activated, grad_mixer, TN).astype(BF)
        up_part = dot(second_low, grad_pre, TN).astype(BF)
        out_parts = jnp.stack([dot(heads[k], attended_part, TN).astype(BF) for k in range(ways)])
    mixer_part = dot(activated, down_weight, NN).astype(BF).reshape(ways, own_rows, width)
    if by_swaps:
        wide_a, wide_b, narrow_a, narrow_b, mixer_part = tie((wide_a, wide_b, narrow_a, narrow_b, mixer_part))
        kept, leave_a, leave_b = halving_sums(kept, (wide_a, narrow_a), (wide_b, narrow_b), wide, narrow)
        got_a, got_b = swap(leave_a, "dp", bit_x), swap(leave_b, "dp", bit_y)
        head_terms, mixer_part, kept = tie((head_terms, mixer_part, kept))
    else:
        head_terms, mixer_part = tie((head_terms, mixer_part))

    mixer_terms = to_all(mixer_part)
    grad_projected, first_gain_part, input_part = attend_back(
        head_terms, qkv, probs, qkv_weight, picked, first_gain[None], hidden_part
    )
    qkv_part = qkv_part_of(first_low, grad_projected)
    input_part = input_part.reshape(ways, own_rows, width)
    if by_swaps:
        got_a, got_b, qkv_part, input_part = tie((got_a, got_b, qkv_part, input_part))
        kept, leave_a, leave_b = halving_sums(kept, (got_a,), (got_b,), wide // 2, narrow // 2)
        mixer_terms, input_part, qkv_part, kept, leave_a, leave_b = tie(
            (mixer_terms, input_part, qkv_part, kept, leave_a, leave_b)
        )
    else:
        mixer_terms, input_part, qkv_part = tie((mixer_terms, input_part, qkv_part))

    input_terms = to_all(input_part)
    if by_swaps:
        got_a, got_b = swap(leave_a, "dp", bit_y), swap(leave_b, "dp", bit_x)
        qkv_got = swap(qkv_part, "dp", 1)
    new_own, grad_score, small = finish_rows(
        mixer_terms,
        picked,
        gating,
        attended,
        grad_rows,
        first_gain_part,
        second_gain_part,
        square,
        routed_square,
        mine_array,
        ways,
    )
    if by_swaps:
        got_a, got_b, new_own = tie((got_a, got_b, new_own))
        lane_a, lane_b, sent = owned_sums(kept, got_a, got_b, new_own, small, wide // 4, ways)
        got_a, got_b = swap(lane_a, "dp", bit_y), swap(lane_b, "dp", bit_x)
        qkv_part, qkv_got, lane_a, lane_b, sent = tie((qkv_part, qkv_got, lane_a, lane_b, sent))
        qkv_a, qkv_b = core_sums(qkv_part, qkv_got)
        input_terms, sent, got_a, got_b, qkv_a, qkv_b = tie((input_terms, sent, got_a, got_b, qkv_a, qkv_b))
    else:
        sent = jnp.concatenate([new_own, split_sums(small)])
        sent = jnp.broadcast_to(sent[None], (ways,) + sent.shape)
        input_terms, sent = tie((input_terms, sent))

    fresh = to_all(sent)
    if by_swaps:
        more_a = [swap(array, "dp", bit_x) for array in (lane_a, got_a)]
        more_b = [swap(array, "dp", bit_y) for array in (lane_b, got_b)]
    last = finish_input(input_terms, grad_rows, grad_score, weight_row, mine_array, ways)
    cotangent, last = tie((cotangent, last))
    early = merge_rows(cotangent, route_offset, last, mine_array, range(1))
    if by_swaps:
        more_a, more_b, early, qkv_a, qkv_b = tie((more_a, more_b, early, qkv_a, qkv_b))
        qkv_a_got, qkv_b_got = swap(qkv_a, "dp", bit_y), swap(qkv_b, "dp", bit_x)
        down_one, up_one = gather_blocks([lane_a, got_a], [lane_b, got_b])
        down_two, up_two = gather_blocks(more_a, more_b)
        down_near, up_near = [down_one, down_two], [up_one, up_two]
        down_far = [swap(array, "dp", 1) for array in down_near]
        up_far = [swap(array, "dp", 1) for array in up_near]

        def gathered(order):
            keys = [0]
            for bit in order:
                keys = keys + [k ^ bit for k in keys]
            return keys

        down_grad, up_grad = spread_rows(
            down_near + down_far, up_near + up_far, [bit_y, bit_x, 1], [bit_x, bit_y, 1], part_array
        )
        fresh, last, down_grad, up_grad = tie((fresh, last, down_grad, up_grad))
    else:
        fresh, last = tie((fresh, last))

    input_rows = to_all(last)
    if by_swaps:
        blocks = [first_small(fresh, own_rows)]
        more = [swap(array, "dp", bit_x) for array in blocks]
        qkv_a_got, qkv_b_got, blocks = tie((qkv_a_got, qkv_b_got, blocks))
        qkv_a, qkv_b = lane_sums(qkv_a, qkv_a_got, qkv_b, qkv_b_got)
        more, qkv_a, qkv_b = tie((more, qkv_a, qkv_b))
        blocks = blocks + more
        more = [swap(array, "dp", bit_y) for array in blocks]
        fresh, blocks = tie((fresh, blocks))
    output = merge_rows(tokens, route_offset, fresh, mine_array, range(ways // 2))
    if by_swaps:
        more, output, qkv_a, qkv_b = tie((more, output, qkv_a, qkv_b))
        qkv_a_got, qkv_b_got = swap(qkv_a, "dp", bit_x), swap(qkv_b, "dp", bit_y)
        blocks = blocks + more
        more = [swap(array, "dp", 1) for array in blocks]
        fresh, blocks, qkv_a = tie((fresh, blocks, qkv_a))
    output = merge_rows(tokens, route_offset, fresh, mine_array, range(ways // 2, ways), output)
    if by_swaps:
        more, output = tie((more, output))
        out_grad, *small = last_small(blocks + more, gathered([bit_x, bit_y, 1]), part_array, shares)
        small[3] = small[3][:, :2]
        input_rows, early, output, out_grad, small = tie((input_rows, early, output, out_grad, small))
    input_grad = merge_rows(cotangent, route_offset, input_rows, mine_array, range(1, ways), early)
    if by_swaps:
        qkv_a_got, qkv_b_got, input_grad = tie((qkv_a_got, qkv_b_got, input_grad))
        qkv_grad = spread_qkv(qkv_a, qkv_a_got, qkv_b, qkv_b_got, qkv_weight.shape[2])
    if not by_swaps:
        small = sum(joined_sums(fresh[k, own_rows:]) for k in range(ways))
        small = lax.psum(small, "dp")
        small = [small[n : n + 1] for n in range(TERMS)]
        small[3] = small[3][:, :2] * jnp.array((shares,), F32)
        down_grad, up_grad, qkv_sum, out_sum = (
            lax.psum(v, "dp").astype(F32) for v in (down_part, up_part, qkv_part, out_parts)
        )
        out_grad = jnp.sum(to_all(out_sum.astype(BF)).astype(F32), axis=0)
        qkv_grad = qkv_sum.reshape(3, -1, width).transpose(0, 2, 1)
    router_grad, first_gain_grad, second_gain_grad = (small[n].reshape(width) for n in range(3))
    score_stats = small[3].reshape(2)
    return (
        output,
        input_grad,
        router_grad,
        first_gain_grad,
        second_gain_grad,
        qkv_grad,
        out_grad,
        up_grad,
        down_grad,
        score_stats,
    )


def solution(mesh):
    placed = (
        P("dp", None),
        P("dp", None),
        P("dp", None),
        P("dp", None),
        P(),
        P(),
        P(),
        P(None, None, "tensor"),
        P("tensor", None),
        P(None, "tensor"),
        P("tensor", None),
    )
    return jax.shard_map(
        per_device,
        mesh=mesh,
        in_specs=placed,
        out_specs=(
            P("dp", None),
            P("dp", None),
            P(),
            P(),
            P(),
            P(None, None, "tensor"),
            P("tensor", None),
            P(None, "tensor"),
            P("tensor", None),
            P(),
        ),
        check_vma=False,
    )
```

```python
import jax
import jax.numpy as jnp
from jax import lax
from jax.experimental import pallas as pl
from jax.experimental.pallas import tpu as pltpu
from jax.sharding import PartitionSpec as P

BF = jnp.bfloat16
F32 = jnp.float32

NN = ((1,), (0,))
NT = ((1,), (1,))
TN = ((0,), (0,))


def dot(left, right, dims):
    return lax.dot_general(left, right, (dims, ((), ())), preferred_element_type=F32)


def swap(values, axis, bits):
    size = lax.axis_size(axis)
    return lax.ppermute(values, axis, [(i, i ^ bits) for i in range(size)])


def to_all(blocks):
    return lax.all_to_all(blocks, "tensor", 0, 0, tiled=True)


def inverse_rms(rows):
    return lax.rsqrt(jnp.mean(rows * rows, axis=-1, keepdims=True) + eps)


HEAD_DIM = 64
GROUP = 8
TERMS = 4
GAP = 2 * TERMS
eps = 1e-06
mask_fill = -1000000000.0


def small_cost():
    return pl.CostEstimate(flops=1024, bytes_accessed=1024, transcendentals=0)


def cost_of(microseconds):
    return pl.CostEstimate(flops=1024, bytes_accessed=int(microseconds * 3.0e6), transcendentals=0)


def staged(name, body, scalars, arrays, out_shapes, scratch, limit, cost):
    count, outs, extra = len(arrays), len(out_shapes), len(scalars)

    def kernel(*refs):
        scalar_refs, refs = refs[:extra], refs[extra:]
        in_refs, refs = refs[:count], refs[count:]
        out_refs, refs = refs[:outs], refs[outs:]
        held, refs = refs[:count], refs[count:]
        made, refs = refs[:outs], refs[outs:]
        load_sems, store_sems = refs[:2]
        loads = [pltpu.make_async_copy(s, h, load_sems.at[n]) for n, (s, h) in enumerate(zip(in_refs, held))]
        stores = [pltpu.make_async_copy(m, o, store_sems.at[n]) for n, (m, o) in enumerate(zip(made, out_refs))]
        for copy in loads:
            copy.start()
        here, gone = set(), set()

        def load(n):
            if n not in here:
                here.add(n)
                loads[n].wait()
            return held[n]

        def store(*which):
            for n in which:
                gone.add(n)
                stores[n].start()

        body(load, store, made, scalar_refs, refs[2:])
        for n in range(count):
            load(n)
        for n in range(outs):
            if n not in gone:
                store(n)
        for copy in stores:
            copy.wait()

    anywhere = pl.BlockSpec(memory_space=pl.ANY)
    return pl.pallas_call(
        kernel,
        in_specs=[pl.BlockSpec(memory_space=pltpu.SMEM)] * extra + [anywhere] * count,
        out_specs=[anywhere] * outs,
        out_shape=[jax.ShapeDtypeStruct(shape, kind) for shape, kind in out_shapes],
        scratch_shapes=[pltpu.VMEM(a.shape, a.dtype) for a in arrays]
        + [pltpu.VMEM(shape, kind) for shape, kind in out_shapes]
        + [pltpu.SemaphoreType.DMA((count,)), pltpu.SemaphoreType.DMA((outs,))]
        + scratch,
        cost_estimate=cost,
        compiler_params=pltpu.CompilerParams(vmem_limit_bytes=limit << 20),
        name=name,
    )(*scalars, *arrays)


def pick_rows(base, offsets, ways):
    rows, width = base.shape
    chunks = ways
    block = rows // chunks
    groups = block // GROUP
    sub = 256
    sub_groups = sub // GROUP

    def kernel(base_ref, offset_ref, picked_ref, held, sems):
        def load(n):
            part = pl.ds(pl.multiple_of(n * block, block), block)
            return pltpu.make_async_copy(base_ref.at[part], held.at[part], sems.at[n])

        for n in range(chunks):
            load(n).start()
        local = lax.broadcasted_iota(jnp.int32, (sub, sub_groups), 0) - GROUP * lax.broadcasted_iota(
            jnp.int32, (sub, sub_groups), 1
        )

        def step(n, carry):
            load(n).wait()
            offsets = offset_ref[:, pl.ds(pl.multiple_of(n * groups, groups), groups)]
            for s in range(block // sub):
                chosen = (local == offsets[:, s * sub_groups : (s + 1) * sub_groups]).astype(F32).astype(BF)
                rows_in = held[pl.ds(pl.multiple_of(n * block + s * sub, sub), sub), :]
                to = pl.ds(pl.multiple_of(n * groups + s * sub_groups, sub_groups), sub_groups)
                picked_ref[to, :] = dot(chosen, rows_in, TN).astype(BF)
            return carry

        lax.fori_loop(0, chunks, step, 0)

    whole = pl.BlockSpec(memory_space=pltpu.VMEM)
    return pl.pallas_call(
        kernel,
        in_specs=[pl.BlockSpec(memory_space=pl.ANY), whole],
        out_specs=whole,
        out_shape=jax.ShapeDtypeStruct((rows // GROUP, width), BF),
        scratch_shapes=[pltpu.VMEM((rows, width), BF), pltpu.SemaphoreType.DMA((chunks,))],
        cost_estimate=small_cost(),
        compiler_params=pltpu.CompilerParams(vmem_limit_bytes=60 << 20),
        name="pick_rows",
    )(base, offsets)


def score_sums(base, router, mine, ways):
    rows, width = base.shape
    block = rows // ways

    def kernel(mine_ref, base_ref, router_ref, square_ref):
        score = jnp.sum(base_ref[...].astype(F32) * router_ref[...].astype(F32), axis=1, keepdims=True)
        square_ref[...] = jnp.broadcast_to(jnp.sum(score * score, axis=0, keepdims=True), square_ref.shape)

    return pl.pallas_call(
        kernel,
        grid_spec=pltpu.PrefetchScalarGridSpec(
            num_scalar_prefetch=1,
            grid=(1,),
            in_specs=[
                pl.BlockSpec((block, width), lambda i, m: (m[0], 0)),
                pl.BlockSpec((1, width), lambda i, m: (0, 0)),
            ],
            out_specs=pl.BlockSpec((1, 128), lambda i, m: (0, 0)),
        ),
        out_shape=jax.ShapeDtypeStruct((1, 128), F32),
        cost_estimate=small_cost(),
        name="score_sums",
    )(mine, base, router)


def pick_only(base, offsets, ways):
    rows, width = base.shape
    block = rows // ways
    groups = block // GROUP
    sub = 256
    sub_groups = sub // GROUP

    def kernel(base_ref, offset_ref, picked_ref):
        local = lax.broadcasted_iota(jnp.int32, (sub, sub_groups), 0) - GROUP * lax.broadcasted_iota(
            jnp.int32, (sub, sub_groups), 1
        )
        for s in range(block // sub):
            to = slice(s * sub_groups, (s + 1) * sub_groups)
            chosen = (local == offset_ref[:, to]).astype(F32).astype(BF)
            picked_ref[to, :] = dot(chosen, base_ref[s * sub : (s + 1) * sub, :], TN).astype(BF)

    return pl.pallas_call(
        kernel,
        grid=(ways,),
        in_specs=[pl.BlockSpec((block, width), lambda i: (i, 0)), pl.BlockSpec((1, groups), lambda i: (0, i))],
        out_specs=pl.BlockSpec((groups, width), lambda i: (i, 0)),
        out_shape=jax.ShapeDtypeStruct((rows // GROUP, width), BF),
        cost_estimate=small_cost(),
        name="pick_only",
    )(base, offsets)


def merge_rows(base, offsets, pieces, mine, which, held_out=None):
    rows, width = base.shape
    ways, depth, _ = pieces.shape
    count = rows // ways
    groups = count // GROUP
    kept = [] if held_out is None else [held_out]
    sub = 256
    sub_groups = sub // GROUP

    first = which.start

    def kernel(part_ref, base_ref, offset_ref, piece_ref, *rest):
        out_ref = rest[-1]
        local = lax.broadcasted_iota(jnp.int32, (sub, sub_groups), 0) - GROUP * lax.broadcasted_iota(
            jnp.int32, (sub, sub_groups), 1
        )
        for s in range(count // sub):
            here = slice(s * sub, (s + 1) * sub)
            to = slice(s * sub_groups, (s + 1) * sub_groups)
            chosen = (local == offset_ref[:, to]).astype(F32)
            hit = jnp.sum(chosen, axis=1, keepdims=True) > 0.5
            spread = dot(chosen.astype(BF), piece_ref[0, to, :], NN)
            out_ref[here, :] = jnp.where(hit, spread, base_ref[here, :].astype(F32)).astype(BF)

    grid_spec = pltpu.PrefetchScalarGridSpec(
        num_scalar_prefetch=1,
        grid=(len(which),),
        in_specs=[
            pl.BlockSpec((count, width), lambda i, m: (m[0] ^ (i + first), 0)),
            pl.BlockSpec((1, groups), lambda i, m: (0, m[0] ^ (i + first))),
            pl.BlockSpec((1, depth, width), lambda i, m: (m[0] ^ (i + first), 0, 0)),
        ]
        + [pl.BlockSpec(memory_space=pl.ANY)] * len(kept),
        out_specs=pl.BlockSpec((count, width), lambda i, m: (m[0] ^ (i + first), 0)),
    )
    return pl.pallas_call(
        kernel,
        grid_spec=grid_spec,
        out_shape=jax.ShapeDtypeStruct((rows, width), BF),
        input_output_aliases={4: 0} if kept else {},
        cost_estimate=small_cost(),
        name="merge_rows",
    )(mine, base, offsets, pieces, *kept)


def attend(picked, gain, weight, seq_row, ways):
    rows, width = picked.shape
    heads_width = weight.shape[2]
    heads = heads_width // HEAD_DIM
    block = min(256, rows)

    def body(load, store, outs, scalars, scratch):
        low_ref, qkv_ref, out_ref, *probs_refs = outs
        values = load(0)[...].astype(F32)
        low_ref[...] = (values * inverse_rms(values) * load(1)[...].astype(F32)).astype(BF)
        store(0)
        weight_ref = load(2)
        for n in range(3):
            qkv_ref[n] = dot(low_ref[...], weight_ref[n], NN).astype(BF)
        store(1)
        sequence = load(3)[...].astype(F32)
        column = jnp.broadcast_to(sequence, (128, rows)).T[:, :1]
        lane_head = lax.broadcasted_iota(jnp.int32, (1, heads_width), 1) // HEAD_DIM
        for n in reversed(range(rows // block)):
            start, stop = n * block, (n + 1) * block
            query = qkv_ref[0, start:stop, :] * BF(HEAD_DIM ** (-0.5))
            order = lax.broadcasted_iota(jnp.int32, (block, stop), 0) + start
            keys = lax.broadcasted_iota(jnp.int32, (block, stop), 1)
            allowed = (column[start:stop, :] == sequence[:, :stop]) & (order >= keys)
            total = jnp.zeros((block, heads_width), F32)
            for head in range(heads):
                here = lane_head == head
                key = jnp.where(here, qkv_ref[1, :stop, :], BF(0))
                logits = jnp.where(allowed, dot(query, key, NT), mask_fill)
                raised = jnp.exp(logits - jnp.max(logits, axis=-1, keepdims=True))
                probs = (raised * (1.0 / jnp.sum(raised, axis=-1, keepdims=True))).astype(BF)
                probs_refs[n][head] = probs
                value = jnp.where(here, qkv_ref[2, :stop, :], BF(0))
                total = total + dot(probs, value, NN)
            for k in range(ways):
                out_ref[k, start:stop, :] = total.astype(BF)
            store(3 + n)

    return staged(
        "attend",
        body,
        [],
        [picked, gain, weight, seq_row],
        [
            ((rows, width), BF),
            ((3, rows, heads_width), BF),
            ((ways, rows, heads_width), BF),
        ]
        + [((heads, block, (n + 1) * block), BF) for n in range(rows // block)],
        [],
        60,
        small_cost(),
    )


def feed_forward(heads, own_weight, quarters, picked, gain, up, grad_act, grad_mixer, part, mine, ways):
    rows, width = picked.shape
    hidden = up.shape[1]
    sub = min(512, hidden)
    count, _, heads_width = heads.shape
    piece = heads_width // 4
    own = rows // ways
    slope = 0.7978845608028654
    cubic = 0.044715

    def body(load, store, outs, scalars, scratch):
        part_ref, mine_ref = scalars
        attended_ref, low_ref, act_ref, pre_ref, hidden_ref, part_out_ref, gain_part_ref, sent_ref = outs
        total, state, weights = scratch
        quarter = part_ref[0] & 3
        heads_ref = load(0)
        weights[0] = load(1)[...]
        for n in range(4):
            start = pl.multiple_of((quarter ^ n) * piece, piece)
            source = load(2 + n)
            for k in range(1, count):
                weights[k, pl.ds(start, piece), :] = source[k - 1]
        attended = dot(heads_ref[mine_ref[0]], weights[0], NN)
        for k in range(1, count):
            attended = attended + dot(heads_ref[mine_ref[0] ^ k], weights[k], NN)
        total[...] = attended
        attended_ref[...] = total[pl.ds(pl.multiple_of(mine_ref[0] * own, own), own), :]
        state_in = load(6)[...].astype(F32) + attended
        state[...] = state_in
        gain_row = load(7)[...].astype(F32)
        low_ref[...] = (state_in * inverse_rms(state_in) * gain_row).astype(BF)
        store(0, 1)
        up_ref, act_grad_ref = load(8), load(9)
        for s in range(hidden // sub):
            lanes = slice(s * sub, (s + 1) * sub)
            value = dot(low_ref[...], up_ref[:, lanes], NN)
            square = value * value
            bent = jnp.tanh(value * (slope + (slope * cubic) * square))
            half = 0.5 * (1.0 + bent)
            act_ref[:, lanes] = (value * half).astype(BF)
            rise = half + (0.5 * value) * (1.0 - bent * bent) * (slope + (3.0 * slope * cubic) * square)
            pre = (act_grad_ref[:, lanes] * rise).astype(BF)
            pre_ref[:, lanes] = pre
            term = dot(pre, up_ref[:, lanes], NT)
            if s == 0:
                total[...] = term
            else:
                total[...] += term
        store(2, 3)
        state_in = state[...]
        grad = total[...]
        inverse = inverse_rms(state_in)
        normal = state_in * inverse
        gain_part_ref[...] = jnp.sum(grad * normal, axis=0, keepdims=True)
        scaled = grad * gain_row
        along = jnp.mean(scaled * normal, axis=-1, keepdims=True)
        back = inverse * (scaled - normal * along)
        hidden_ref[...] = back.astype(BF)
        part_out_ref[...] = (back + load(10)[...].astype(F32) * (1.0 / count)).astype(BF)
        store(4, 5, 6)
        for k in range(count):
            sent_ref[mine_ref[0] ^ k] = dot(part_out_ref[...], weights[k], NT).astype(BF)

    return staged(
        "feed_forward",
        body,
        [part, mine],
        [heads, own_weight, *quarters, picked, gain, up, grad_act, grad_mixer],
        [
            ((own, width), F32),
            ((rows, width), BF),
            ((rows, hidden), BF),
            ((rows, hidden), BF),
            ((rows, width), BF),
            ((rows, width), BF),
            ((1, width), F32),
            (heads.shape, BF),
        ],
        [
            pltpu.VMEM((rows, width), F32),
            pltpu.VMEM((rows, width), F32),
            pltpu.VMEM((count, heads_width, width), BF),
        ],
        60,
        small_cost(),
    )


def act_grads(picked, router, grad_rows, down):
    rows, width = grad_rows.shape

    def kernel(picked_ref, router_ref, rows_ref, down_ref, gating_ref, square_ref, mixer_ref, grad_ref):
        score = jnp.sum(picked_ref[...].astype(F32) * router_ref[...].astype(F32), axis=-1, keepdims=True)
        gating = jax.nn.sigmoid(score)
        gating_ref[...] = gating
        square_ref[...] = jnp.broadcast_to(jnp.sum(score * score, axis=0, keepdims=True), square_ref.shape)
        mixer_ref[...] = (gating * rows_ref[...].astype(F32)).astype(BF)
        grad_ref[...] = dot(mixer_ref[...], down_ref[...], NT)

    whole = pl.BlockSpec(memory_space=pltpu.VMEM)
    return pl.pallas_call(
        kernel,
        in_specs=[whole] * 4,
        out_specs=[whole] * 4,
        out_shape=[
            jax.ShapeDtypeStruct((rows, 1), F32),
            jax.ShapeDtypeStruct((1, 128), F32),
            jax.ShapeDtypeStruct((rows, width), BF),
            jax.ShapeDtypeStruct((rows, down.shape[0]), F32),
        ],
        cost_estimate=small_cost(),
        name="act_grads",
    )(picked, router, grad_rows, down)


def attend_back(head_terms, qkv, probs, weight, picked, gain, hidden_part):
    rows, width = picked.shape
    heads_width = weight.shape[2]
    heads = heads_width // HEAD_DIM
    block = min(256, rows)
    scale = HEAD_DIM ** (-0.5)

    def kernel(
        head_ref,
        qkv_ref,
        weight_ref,
        picked_ref,
        gain_ref,
        hidden_ref,
        *rest,
    ):
        probs_refs, (grads_ref, gain_part_ref, result, grad_key, grad_value) = rest[: len(probs)], rest[len(probs) :]
        lane_head = lax.broadcasted_iota(jnp.int32, (1, heads_width), 1) // HEAD_DIM
        for start in reversed(range(0, rows, block)):
            stop = start + block
            here_rows = slice(start, stop)
            grad_head = head_ref[0, here_rows, :].astype(F32)
            for k in range(1, head_ref.shape[0]):
                grad_head = grad_head + head_ref[k, here_rows, :].astype(F32)
            grad_head = grad_head.astype(BF)
            query = qkv_ref[0, here_rows, :] * BF(scale)
            grad_query = jnp.zeros((block, heads_width), F32)
            add_key = jnp.zeros((stop, heads_width), F32)
            add_value = jnp.zeros((stop, heads_width), F32)
            for head in range(heads):
                here = lane_head == head
                value = jnp.where(here, qkv_ref[2, :stop, :], BF(0))
                key = jnp.where(here, qkv_ref[1, :stop, :], BF(0))
                low = probs_refs[start // block][head]
                weighted = low.astype(F32) * dot(grad_head, value, NT)
                row_sum = jnp.sum(weighted, axis=-1, keepdims=True)
                slopes = (weighted - low.astype(F32) * row_sum).astype(BF)
                grad_query = grad_query + dot(slopes, key, NN)
                add_key = add_key + dot(slopes, jnp.where(here, query, BF(0)), TN)
                add_value = add_value + dot(low, jnp.where(here, grad_head, BF(0)), TN)
            grads_ref[0, here_rows, :] = (grad_query * scale).astype(BF)
            if stop == rows:
                grad_key[...] = add_key
                grad_value[...] = add_value
            else:
                grad_key[:stop, :] += add_key
                grad_value[:stop, :] += add_value
        grads_ref[1] = grad_key[...].astype(BF)
        grads_ref[2] = grad_value[...].astype(BF)
        first = dot(grads_ref[0], weight_ref[0], NT)
        for n in range(1, 3):
            first = first + dot(grads_ref[n], weight_ref[n], NT)
        values = picked_ref[...].astype(F32)
        inverse = inverse_rms(values)
        normal = values * inverse
        gain_part_ref[...] = jnp.sum(first * normal, axis=0, keepdims=True)
        scaled = first * gain_ref[...].astype(F32)
        along = jnp.mean(scaled * normal, axis=-1, keepdims=True)
        result[...] = (hidden_ref[...].astype(F32) + inverse * (scaled - normal * along)).astype(BF)

    whole = pl.BlockSpec(memory_space=pltpu.VMEM)
    return pl.pallas_call(
        kernel,
        in_specs=[whole] * (6 + len(probs)),
        out_specs=[whole] * 3,
        out_shape=[
            jax.ShapeDtypeStruct((3, rows, heads_width), BF),
            jax.ShapeDtypeStruct((1, width), F32),
            jax.ShapeDtypeStruct((rows, width), BF),
        ],
        scratch_shapes=[
            pltpu.VMEM((rows, heads_width), F32),
            pltpu.VMEM((rows, heads_width), F32),
        ],
        cost_estimate=small_cost(),
        compiler_params=pltpu.CompilerParams(vmem_limit_bytes=20 << 20),
        name="attend_back",
    )(head_terms, qkv, weight, picked, gain, hidden_part, *probs)


def spread_rows(down, up, order_down, order_up, part):
    count = len(down)
    wide, width = down[0].shape
    rows = wide // (2 ** len(order_down) // count)
    each = wide // rows

    def kernel(part_ref, *refs):
        down_out, up_out = refs[2 * count :]
        for n in range(count):

            @pl.when(pl.program_id(0) // each == n)
            def _():
                down_out[...] = refs[n][...].astype(F32)
                up_out[...] = refs[count + n][...].astype(F32)

    def source(n):
        return pl.BlockSpec((rows, width), lambda i, p: (jnp.clip(i - n * each, 0, each - 1), 0))

    def target(order):
        def place(i, p):
            key = sum((i >> n & 1) * bit for n, bit in enumerate(order))
            return p[0] ^ key, 0

        return pl.BlockSpec((rows, width), place)

    return pl.pallas_call(
        kernel,
        grid_spec=pltpu.PrefetchScalarGridSpec(
            num_scalar_prefetch=1,
            grid=(count * each,),
            in_specs=[source(n) for n in range(count)] * 2,
            out_specs=[target(order_down), target(order_up)],
        ),
        out_shape=[jax.ShapeDtypeStruct((count * wide, width), F32)] * 2,
        cost_estimate=small_cost(),
        name="spread_rows",
    )(part, *down, *up)


def qkv_part_of(first_low, grads, part):
    rows, width = first_low.shape
    part_width = grads.shape[2]
    half = 3 * part_width // 2

    def kernel(part_ref, low_ref, grads_ref, keep_ref, send_ref, full):
        for n in range(3):
            product = dot(grads_ref[n], low_ref[...], TN)
            full[n * part_width : (n + 1) * part_width, :] = product.astype(BF)
        core = part_ref[0] & 1
        for target, which in ((keep_ref, core), (send_ref, 1 - core)):
            target[...] = full[pl.ds(pl.multiple_of(which * half, half), half), :]

    whole = pl.BlockSpec(memory_space=pltpu.VMEM)
    return pl.pallas_call(
        kernel,
        in_specs=[pl.BlockSpec(memory_space=pltpu.SMEM)] + [whole] * 2,
        out_specs=[whole] * 2,
        out_shape=[jax.ShapeDtypeStruct((half, width), BF)] * 2,
        scratch_shapes=[pltpu.VMEM((2 * half, width), BF)],
        cost_estimate=small_cost(),
        compiler_params=pltpu.CompilerParams(vmem_limit_bytes=14 << 20),
        name="qkv_part",
    )(part, first_low, grads)


def spread_qkv(near, far, part, part_width):
    rows, width = near.shape
    tile = 128
    count = rows // tile
    many = part_width // tile

    def kernel(part_ref, near_ref, far_ref, out_ref):
        core = part_ref[0] & 1
        for ref, which in ((near_ref, core), (far_ref, 1 - core)):
            for n in range(count):
                spot = which * count + n
                column = pl.multiple_of(spot % many * tile, tile)
                piece = ref[n * tile : (n + 1) * tile, :].astype(F32)
                out_ref[spot // many, :, pl.ds(column, tile)] = piece.T

    whole = pl.BlockSpec(memory_space=pltpu.VMEM)
    return pl.pallas_call(
        kernel,
        in_specs=[pl.BlockSpec(memory_space=pltpu.SMEM)] + [whole] * 2,
        out_specs=whole,
        out_shape=jax.ShapeDtypeStruct((2 * rows // part_width, width, part_width), F32),
        cost_estimate=small_cost(),
        compiler_params=pltpu.CompilerParams(vmem_limit_bytes=14 << 20),
        name="spread_qkv",
    )(part, near, far)


def core_grads(activated, grad_mixer, second_low, grad_pre, heads, attended_part, part, keys_a, keys_b):
    rows, hidden = activated.shape
    width = grad_mixer.shape[1]
    copies = len(keys_a)
    half = copies // 2
    count, _, heads_width = heads.shape
    block = hidden // copies
    small = heads_width // copies
    many = count // 2
    depth = half * (block + many * small)

    def kernel(part_ref, act_ref, mixer_ref, low_ref, pre_ref, heads_ref, term_ref, keep_ref, *rest):
        wide_refs, narrow_refs, (full, narrow) = rest[0:2], rest[2:4], rest[4:]

        def place(source, each, lane, keys, first, stride):
            for n, key in enumerate(keys):
                start = pl.multiple_of((part_ref[0] ^ key) * each, each)
                at = first + (n % half) * stride
                piece = source[pl.ds(start, each), :]
                if n < half:
                    keep_ref[lane, at : at + each, :] = piece
                elif first == 0:
                    wide_refs[lane][at : at + each, :] = piece
                else:
                    narrow_refs[lane][at - half * block : at - half * block + each, :] = piece

        full[...] = dot(act_ref[...], mixer_ref[...], TN).astype(BF)
        place(full, block, 0, keys_a, 0, block)
        full[...] = dot(low_ref[...], pre_ref[...], TN).astype(BF)
        place(full, block, 1, keys_b, 0, block)
        for k in range(count):
            narrow[...] = dot(heads_ref[k], term_ref[...], TN).astype(BF)
            lane, spot = divmod(k, many)
            place(narrow, small, lane, keys_b if lane else keys_a, half * block + spot * small, many * small)

    whole = pl.BlockSpec(memory_space=pltpu.VMEM)
    wide_shape = jax.ShapeDtypeStruct((half * block, width), BF)
    narrow_shape = jax.ShapeDtypeStruct((half * many * small, width), BF)
    return pl.pallas_call(
        kernel,
        in_specs=[pl.BlockSpec(memory_space=pltpu.SMEM)] + [whole] * 6,
        out_specs=[whole] * 5,
        out_shape=[jax.ShapeDtypeStruct((2, depth, width), BF)] + [wide_shape] * 2 + [narrow_shape] * 2,
        scratch_shapes=[pltpu.VMEM((hidden, width), BF), pltpu.VMEM((heads_width, width), BF)],
        cost_estimate=small_cost(),
        compiler_params=pltpu.CompilerParams(vmem_limit_bytes=14 << 20),
        name="core_grads",
    )(part, activated, grad_mixer, second_low, grad_pre, heads, attended_part)


def plus(left, right):
    return (left.astype(F32) + right.astype(F32)).astype(BF)


def halving_sums(keep, got_a, got_b, wide, narrow):
    width = keep.shape[2]
    count = len(got_a)

    def kernel(keep_ref, *refs):
        a_got, b_got, (stay_ref, a_out, b_out) = refs[:count], refs[count : 2 * count], refs[2 * count :]
        for lane, got, out in ((0, a_got, a_out), (1, b_got, b_out)):
            for first, size, at in ((0, wide // 2, 0), (wide, narrow // 2, wide // 2)):
                source, shift = (got[1], wide) if count == 2 and first else (got[0], 0)
                to = slice(at, at + size)
                for start, target in ((first, stay_ref.at[lane]), (first + size, out)):
                    here = slice(start - shift, start - shift + size)
                    target[to, :] = plus(keep_ref[lane, start : start + size, :], source[here, :])

    whole = pl.BlockSpec(memory_space=pltpu.VMEM)
    depth = (wide + narrow) // 2
    lane_shape = jax.ShapeDtypeStruct((depth, width), BF)
    return pl.pallas_call(
        kernel,
        in_specs=[whole] * (1 + 2 * count),
        out_specs=[whole] * 3,
        out_shape=[jax.ShapeDtypeStruct((2, depth, width), BF), lane_shape, lane_shape],
        cost_estimate=small_cost(),
        compiler_params=pltpu.CompilerParams(vmem_limit_bytes=14 << 20),
        name="halving_sums",
    )(keep, *got_a, *got_b)


def owned_sums(keep, got_a, got_b, fresh, small, wide, ways):
    width = keep.shape[2]
    narrow = keep.shape[1] - wide
    own = fresh.shape[0]
    many = ways // 2
    each = narrow // many
    depth = own + GAP + each

    def kernel(keep_ref, a_got, b_got, fresh_ref, small_ref, a_out, b_out, sent_ref):
        sums = split_sums(small_ref[...])
        for lane, got, out in ((0, a_got, a_out), (1, b_got, b_out)):
            out[...] = plus(keep_ref[lane, :wide, :], got[:wide, :])
            done = plus(keep_ref[lane, wide:, :], got[wide:, :])
            for spot in range(many):
                k = lane * many + spot
                sent_ref[k, :own, :] = fresh_ref[...]
                sent_ref[k, own : own + GAP, :] = sums
                sent_ref[k, own + GAP :, :] = done[spot * each : (spot + 1) * each, :]

    whole = pl.BlockSpec(memory_space=pltpu.VMEM)
    lane_shape = jax.ShapeDtypeStruct((wide, width), BF)
    return pl.pallas_call(
        kernel,
        in_specs=[whole] * 5,
        out_specs=[whole] * 3,
        out_shape=[lane_shape, lane_shape, jax.ShapeDtypeStruct((ways, depth, width), BF)],
        cost_estimate=small_cost(),
        compiler_params=pltpu.CompilerParams(vmem_limit_bytes=10 << 20),
        name="owned_sums",
    )(keep, got_a, got_b, fresh, small)


def core_sums(rows, other):
    depth, width = rows.shape
    third = depth // 2

    def kernel(rows_ref, other_ref, a_out, b_out):
        a_out[...] = plus(rows_ref[:third, :], other_ref[:third, :])
        b_out[...] = plus(rows_ref[third:, :], other_ref[third:, :])

    whole = pl.BlockSpec(memory_space=pltpu.VMEM)
    return pl.pallas_call(
        kernel,
        in_specs=[whole] * 2,
        out_specs=[whole] * 2,
        out_shape=[jax.ShapeDtypeStruct((third, width), BF)] * 2,
        cost_estimate=small_cost(),
        compiler_params=pltpu.CompilerParams(vmem_limit_bytes=10 << 20),
        name="core_sums",
    )(rows, other)


def lane_sums(lane_a, got_a, lane_b, got_b):
    def kernel(a_ref, a_got, b_ref, b_got, a_out, b_out):
        a_out[...] = plus(a_ref[...], a_got[...])
        b_out[...] = plus(b_ref[...], b_got[...])

    whole = pl.BlockSpec(memory_space=pltpu.VMEM)
    return pl.pallas_call(
        kernel,
        in_specs=[whole] * 4,
        out_specs=[whole] * 2,
        out_shape=[jax.ShapeDtypeStruct(lane_a.shape, BF)] * 2,
        cost_estimate=small_cost(),
        compiler_params=pltpu.CompilerParams(vmem_limit_bytes=12 << 20),
        name="lane_sums",
    )(lane_a, got_a, lane_b, got_b)


def joined_lanes(lane_a, got_a, lane_b, got_b):
    rows, width = lane_a.shape

    def kernel(a_ref, a_got, b_ref, b_got, out_ref):
        out_ref[:rows, :] = plus(a_ref[...], a_got[...])
        out_ref[rows:, :] = plus(b_ref[...], b_got[...])

    whole = pl.BlockSpec(memory_space=pltpu.VMEM)
    return pl.pallas_call(
        kernel,
        in_specs=[whole] * 4,
        out_specs=whole,
        out_shape=jax.ShapeDtypeStruct((2 * rows, width), BF),
        cost_estimate=small_cost(),
        compiler_params=pltpu.CompilerParams(vmem_limit_bytes=10 << 20),
        name="joined_lanes",
    )(lane_a, got_a, lane_b, got_b)


def gather_blocks(blocks_a, blocks_b):
    wide, width = blocks_a[0].shape
    count = len(blocks_a)

    def kernel(*refs):
        for lane in range(2):
            for n in range(count):
                refs[2 * count + lane][n * wide : (n + 1) * wide, :] = refs[lane * count + n][...]

    whole = pl.BlockSpec(memory_space=pltpu.VMEM)
    return pl.pallas_call(
        kernel,
        in_specs=[whole] * (2 * count),
        out_specs=[whole] * 2,
        out_shape=[jax.ShapeDtypeStruct((count * wide, width), BF)] * 2,
        cost_estimate=small_cost(),
        compiler_params=pltpu.CompilerParams(vmem_limit_bytes=10 << 20),
        name="gather_blocks",
    )(*blocks_a, *blocks_b)


def split_sums(values):
    high = values.astype(BF)
    low = (values - high.astype(F32)).astype(BF)
    return jnp.concatenate([high, low], axis=0)


def joined_sums(rows):
    return rows[:TERMS].astype(F32) + rows[TERMS : 2 * TERMS].astype(F32)


def first_small(received, own):
    ways, depth, width = received.shape
    each = depth - own - GAP

    def kernel(got_ref, out_ref):
        total = got_ref[0, own + GAP :, :].astype(F32)
        sums = joined_sums(got_ref[0, own : own + GAP, :])
        for k in range(1, ways):
            total = total + got_ref[k, own + GAP :, :].astype(F32)
            sums = sums + joined_sums(got_ref[k, own : own + GAP, :])
        out_ref[:each, :] = total.astype(BF)
        out_ref[each:, :] = split_sums(sums)

    whole = pl.BlockSpec(memory_space=pltpu.VMEM)
    return pl.pallas_call(
        kernel,
        in_specs=[whole],
        out_specs=whole,
        out_shape=jax.ShapeDtypeStruct((each + GAP, width), BF),
        cost_estimate=small_cost(),
        compiler_params=pltpu.CompilerParams(vmem_limit_bytes=8 << 20),
        name="first_small",
    )(received)


def last_small(blocks, keys, part, shares):
    depth, width = blocks[0].shape
    each = depth - GAP
    count = len(blocks)

    def kernel(part_ref, *refs):
        out_ref, small_refs = refs[count], refs[count + 1 :]
        total = joined_sums(refs[0][each:, :])
        for n in range(1, count):
            total = total + joined_sums(refs[n][each:, :])
        for n in range(TERMS - 1):
            small_refs[n][...] = total[n : n + 1, :]
        lane = lax.broadcasted_iota(jnp.int32, (1, 128), 1)
        small_refs[TERMS - 1][...] = total[TERMS - 1 :, :128] * jnp.where(lane == 0, shares[0], shares[1])
        for n in range(count):
            start = pl.multiple_of((part_ref[0] ^ keys[n]) * each, each)
            out_ref[pl.ds(start, each), :] = refs[n][:each, :].astype(F32)

    whole = pl.BlockSpec(memory_space=pltpu.VMEM)
    return pl.pallas_call(
        kernel,
        in_specs=[pl.BlockSpec(memory_space=pltpu.SMEM)] + [whole] * count,
        out_specs=[whole] * (1 + TERMS),
        out_shape=[jax.ShapeDtypeStruct((count * each, width), F32)] + [jax.ShapeDtypeStruct((1, width), F32)] * (TERMS - 1)
        + [jax.ShapeDtypeStruct((1, 128), F32)],
        cost_estimate=small_cost(),
        compiler_params=pltpu.CompilerParams(vmem_limit_bytes=10 << 20),
        name="last_small",
    )(part, *blocks)


def finish_rows(mixer_terms, picked, gating, attended, grad_rows, gain_one, gain_two, square, routed_square, mine, ways):
    rows, width = picked.shape
    own = rows // ways

    def kernel(
        mine_ref,
        terms_ref,
        picked_ref,
        gating_ref,
        attended_ref,
        rows_ref,
        one_ref,
        two_ref,
        square_ref,
        routed_ref,
        new_ref,
        score_ref,
        small_ref,
    ):
        branch = attended_ref[...]
        for k in range(ways):
            branch = branch + terms_ref[k].astype(F32)
        values = picked_ref[...].astype(F32)
        gate = gating_ref[...]
        new_ref[...] = (values + gate * branch).astype(BF)
        along = jnp.sum(rows_ref[...].astype(F32) * branch, axis=-1, keepdims=True)
        score = along * gate * (1.0 - gate)
        score_ref[...] = score
        small_ref[0:1, :] = jnp.sum(score * values, axis=0, keepdims=True)
        small_ref[1:2, :] = one_ref[...]
        small_ref[2:3, :] = two_ref[...]
        lane = lax.broadcasted_iota(jnp.int32, (1, width), 1)
        both = jnp.where(lane == 0, square_ref[:, 0:1], routed_ref[:, 0:1] * (1.0 / ways))
        small_ref[3:4, :] = jnp.where(lane < 2, both, 0.0)

    def block(shape):
        return pl.BlockSpec(shape, lambda i, m: (m[0], 0))

    def fixed(shape):
        return pl.BlockSpec(shape, lambda i, m: (0, 0))

    return pl.pallas_call(
        kernel,
        grid_spec=pltpu.PrefetchScalarGridSpec(
            num_scalar_prefetch=1,
            grid=(1,),
            in_specs=[pl.BlockSpec(mixer_terms.shape, lambda i, m: (0, 0, 0))]
            + [block((own, width)), block((own, 1)), fixed((own, width)), block((own, width))]
            + [fixed((1, width))] * 2
            + [fixed((1, 128))] * 2,
            out_specs=[fixed((own, width)), fixed((own, 1)), fixed((4, width))],
        ),
        out_shape=[
            jax.ShapeDtypeStruct((own, width), BF),
            jax.ShapeDtypeStruct((own, 1), F32),
            jax.ShapeDtypeStruct((4, width), F32),
        ],
        cost_estimate=cost_of(10),
        name="finish_rows",
    )(mine, mixer_terms, picked, gating, attended, grad_rows, gain_one, gain_two, square, routed_square)


def finish_input(terms, grad_rows, score, router, mine, ways):
    rows, width = grad_rows.shape
    own = rows // ways

    def kernel(mine_ref, terms_ref, rows_ref, score_ref, router_ref, out_ref):
        total = rows_ref[...].astype(F32) + score_ref[...] * router_ref[...].astype(F32)
        for k in range(ways):
            total = total + terms_ref[k].astype(F32)
        for k in range(ways):
            out_ref[k] = total.astype(BF)

    def fixed(shape):
        return pl.BlockSpec(shape, lambda i, m: (0,) * len(shape))

    return pl.pallas_call(
        kernel,
        grid_spec=pltpu.PrefetchScalarGridSpec(
            num_scalar_prefetch=1,
            grid=(1,),
            in_specs=[
                fixed((ways, own, width)),
                pl.BlockSpec((own, width), lambda i, m: (m[0], 0)),
                fixed((own, 1)),
                fixed((1, width)),
            ],
            out_specs=fixed((ways, own, width)),
        ),
        out_shape=jax.ShapeDtypeStruct((ways, own, width), BF),
        cost_estimate=small_cost(),
        compiler_params=pltpu.CompilerParams(vmem_limit_bytes=8 << 20),
        name="finish_input",
    )(mine, terms, grad_rows, score, router)


def split_kept(count, order):
    keys = [0]
    for bit in reversed(order):
        keys = keys + [k ^ bit for k in keys]
    return keys


def per_device(
    tokens,
    route_offset,
    unit_sequence,
    cotangent,
    router_weight,
    first_gain,
    second_gain,
    qkv_weight,
    out_weight,
    up_weight,
    down_weight,
):
    rows_local, width = tokens.shape
    routed = route_offset.shape[1]
    ways = lax.axis_size("tensor")
    copies = lax.axis_size("dp")
    mine = lax.axis_index("tensor")
    part = lax.axis_index("dp")
    mine_array = jnp.reshape(mine, (1,)).astype(jnp.int32)
    part_array = jnp.reshape(part, (1,)).astype(jnp.int32)
    ladder = [1 << b for b in range(1, copies.bit_length() - 1)]
    order_a = [1] + ladder
    order_b = [1] + ladder[::-1]
    keys_a = split_kept(copies, order_a)
    keys_b = split_kept(copies, order_b)

    tie = lax.optimization_barrier
    own_rows = routed // ways
    heads_width = out_weight.shape[0]
    hidden = up_weight.shape[1]
    by_swaps = copies == 8
    bit_x, bit_y = 2, 4
    shares = (1.0 / (rows_local * copies), 1.0 / (routed * copies))

    quarter = part & 3
    piece_rows = heads_width // 4
    piece = lax.dynamic_slice_in_dim(out_weight, quarter * piece_rows, piece_rows, 0)
    here = [swap(piece, "tensor", k) for k in range(1, ways)]

    picked = pick_rows(tokens, route_offset, ways)
    first_low, qkv, head_out, *probs = attend(picked, first_gain[None], qkv_weight, unit_sequence, ways)
    here, head_out = tie((here, head_out))

    heads = to_all(head_out)
    here = jnp.stack(here)
    beside, across = swap(here, "dp", bit_x), swap(here, "dp", 1)
    cotangent, router_weight, second_gain, here, head_out = tie(
        (cotangent, router_weight, second_gain, here, head_out)
    )
    weight_row = router_weight[None]
    grad_rows = pick_only(cotangent, route_offset, ways)
    beside, across, here, grad_rows = tie((beside, across, here, grad_rows))
    quarters = [here, across, beside, swap(beside, "dp", 1)]
    gating, routed_square, grad_mixer, grad_act = act_grads(picked, weight_row, grad_rows, down_weight)
    square = score_sums(tokens, weight_row, mine_array, ways)
    heads, quarters, grad_act, grad_mixer, square = tie((heads, quarters, grad_act, grad_mixer, square))
    attended, second_low, activated, grad_pre, hidden_part, attended_part, second_gain_part, head_sent = feed_forward(
        heads,
        out_weight,
        quarters,
        picked,
        second_gain[None],
        up_weight,
        grad_act,
        grad_mixer,
        part_array,
        mine_array,
        ways,
    )

    head_terms = to_all(head_sent)
    wide = hidden // 2
    narrow = heads_width * ways // 4
    if by_swaps:
        kept, *leaving = core_grads(
            activated, grad_mixer, second_low, grad_pre, heads, attended_part, part_array, keys_a, keys_b
        )
        wide_a, wide_b, narrow_a, narrow_b = (swap(array, "dp", 1) for array in leaving)
        activated, kept = tie((activated, kept))
    else:
        down_part = dot(activated, grad_mixer, TN).astype(BF)
        up_part = dot(second_low, grad_pre, TN).astype(BF)
        out_parts = jnp.stack([dot(heads[k], attended_part, TN).astype(BF) for k in range(ways)])
    mixer_part = dot(activated, down_weight, NN).astype(BF).reshape(ways, own_rows, width)
    if by_swaps:
        wide_a, wide_b, narrow_a, narrow_b, mixer_part = tie((wide_a, wide_b, narrow_a, narrow_b, mixer_part))
        kept, leave_a, leave_b = halving_sums(kept, (wide_a, narrow_a), (wide_b, narrow_b), wide, narrow)
        got_a, got_b = swap(leave_a, "dp", bit_x), swap(leave_b, "dp", bit_y)
        head_terms, mixer_part, kept = tie((head_terms, mixer_part, kept))
    else:
        head_terms, mixer_part = tie((head_terms, mixer_part))

    mixer_terms = to_all(mixer_part)
    grad_projected, first_gain_part, input_part = attend_back(
        head_terms, qkv, probs, qkv_weight, picked, first_gain[None], hidden_part
    )
    qkv_part, qkv_leaving = qkv_part_of(first_low, grad_projected, part_array)
    input_part = input_part.reshape(ways, own_rows, width)
    if by_swaps:
        got_a, got_b, qkv_part, qkv_leaving, input_part = tie((got_a, got_b, qkv_part, qkv_leaving, input_part))
        kept, leave_a, leave_b = halving_sums(kept, (got_a,), (got_b,), wide // 2, narrow // 2)
        mixer_terms, input_part, qkv_part, kept, leave_a, leave_b = tie(
            (mixer_terms, input_part, qkv_part, kept, leave_a, leave_b)
        )
    else:
        mixer_terms, input_part, qkv_part = tie((mixer_terms, input_part, qkv_part))

    input_terms = to_all(input_part)
    if by_swaps:
        got_a, got_b = swap(leave_a, "dp", bit_y), swap(leave_b, "dp", bit_x)
        qkv_got = swap(qkv_leaving, "dp", 1)
    new_own, grad_score, small = finish_rows(
        mixer_terms,
        picked,
        gating,
        attended,
        grad_rows,
        first_gain_part,
        second_gain_part,
        square,
        routed_square,
        mine_array,
        ways,
    )
    if by_swaps:
        got_a, got_b, new_own = tie((got_a, got_b, new_own))
        lane_a, lane_b, sent = owned_sums(kept, got_a, got_b, new_own, small, wide // 4, ways)
        got_a, got_b = swap(lane_a, "dp", bit_y), swap(lane_b, "dp", bit_x)
        qkv_part, qkv_got, lane_a, lane_b, sent = tie((qkv_part, qkv_got, lane_a, lane_b, sent))
        qkv_a, qkv_b = core_sums(qkv_part, qkv_got)
        input_terms, sent, got_a, got_b, qkv_a, qkv_b = tie((input_terms, sent, got_a, got_b, qkv_a, qkv_b))
    else:
        sent = jnp.concatenate([new_own, split_sums(small)])
        sent = jnp.broadcast_to(sent[None], (ways,) + sent.shape)
        input_terms, sent = tie((input_terms, sent))

    fresh = to_all(sent)
    if by_swaps:
        more_a = [swap(array, "dp", bit_x) for array in (lane_a, got_a)]
        more_b = [swap(array, "dp", bit_y) for array in (lane_b, got_b)]
    last = finish_input(input_terms, grad_rows, grad_score, weight_row, mine_array, ways)
    cotangent, last = tie((cotangent, last))
    early = merge_rows(cotangent, route_offset, last, mine_array, range(1))
    if by_swaps:
        more_a, more_b, early, qkv_a, qkv_b = tie((more_a, more_b, early, qkv_a, qkv_b))
        qkv_a_got, qkv_b_got = swap(qkv_a, "dp", bit_y), swap(qkv_b, "dp", bit_x)
        down_one, up_one = gather_blocks([lane_a, got_a], [lane_b, got_b])
        down_two, up_two = gather_blocks(more_a, more_b)
        down_near, up_near = [down_one, down_two], [up_one, up_two]
        down_far = [swap(array, "dp", 1) for array in down_near]
        up_far = [swap(array, "dp", 1) for array in up_near]

        def gathered(order):
            keys = [0]
            for bit in order:
                keys = keys + [k ^ bit for k in keys]
            return keys

        down_grad, up_grad = spread_rows(
            down_near + down_far, up_near + up_far, [bit_y, bit_x, 1], [bit_x, bit_y, 1], part_array
        )
        fresh, last, down_grad, up_grad = tie((fresh, last, down_grad, up_grad))
    else:
        fresh, last = tie((fresh, last))

    input_rows = to_all(last)
    if by_swaps:
        blocks = [first_small(fresh, own_rows)]
        more = [swap(array, "dp", bit_x) for array in blocks]
        qkv_a_got, qkv_b_got, blocks = tie((qkv_a_got, qkv_b_got, blocks))
        qkv_a, qkv_b = lane_sums(qkv_a, qkv_a_got, qkv_b, qkv_b_got)
        qkv_a_got, qkv_b_got = swap(qkv_a, "dp", bit_x), swap(qkv_b, "dp", bit_y)
        fresh, blocks, qkv_a, qkv_b = tie((fresh, blocks, qkv_a, qkv_b))
    output = merge_rows(tokens, route_offset, fresh, mine_array, range(ways // 2))
    if by_swaps:
        more, qkv_a_got, qkv_b_got, output = tie((more, qkv_a_got, qkv_b_got, output))
        qkv_near = joined_lanes(qkv_a, qkv_a_got, qkv_b, qkv_b_got)
        qkv_far = swap(qkv_near, "dp", 1)
        blocks = blocks + more
        more = [swap(array, "dp", bit_y) for array in blocks]
        fresh, blocks, qkv_near = tie((fresh, blocks, qkv_near))
    output = merge_rows(tokens, route_offset, fresh, mine_array, range(ways // 2, ways), output)
    if by_swaps:
        more, qkv_far, output = tie((more, qkv_far, output))
        blocks = blocks + more
        more = [swap(array, "dp", 1) for array in blocks]
        qkv_near, blocks = tie((qkv_near, blocks))
        qkv_grad = spread_qkv(qkv_near, qkv_far, part_array, qkv_weight.shape[2])
        more, qkv_grad = tie((more, qkv_grad))
        out_grad, *small = last_small(blocks + more, gathered([bit_x, bit_y, 1]), part_array, shares)
        small[3] = small[3][:, :2]
        input_rows, early, output, out_grad, small, qkv_grad = tie(
            (input_rows, early, output, out_grad, small, qkv_grad)
        )
    input_grad = merge_rows(cotangent, route_offset, input_rows, mine_array, range(1, ways), early)
    if not by_swaps:
        swapped = jnp.concatenate([qkv_leaving, qkv_part])
        qkv_whole = jnp.where(part & 1 == 0, jnp.concatenate([qkv_part, qkv_leaving]), swapped)
        small = sum(joined_sums(fresh[k, own_rows:]) for k in range(ways))
        small = lax.psum(small, "dp")
        small = [small[n : n + 1] for n in range(TERMS)]
        small[3] = small[3][:, :2] * jnp.array((shares,), F32)
        down_grad, up_grad, qkv_sum, out_sum = (
            lax.psum(v, "dp").astype(F32) for v in (down_part, up_part, qkv_whole, out_parts)
        )
        out_grad = jnp.sum(to_all(out_sum.astype(BF)).astype(F32), axis=0)
        qkv_grad = qkv_sum.reshape(3, -1, width).transpose(0, 2, 1)
    router_grad, first_gain_grad, second_gain_grad = (small[n].reshape(width) for n in range(3))
    score_stats = small[3].reshape(2)
    return (
        output,
        input_grad,
        router_grad,
        first_gain_grad,
        second_gain_grad,
        qkv_grad,
        out_grad,
        up_grad,
        down_grad,
        score_stats,
    )


def solution(mesh):
    placed = (
        P("dp", None),
        P("dp", None),
        P("dp", None),
        P("dp", None),
        P(),
        P(),
        P(),
        P(None, None, "tensor"),
        P("tensor", None),
        P(None, "tensor"),
        P("tensor", None),
    )
    return jax.shard_map(
        per_device,
        mesh=mesh,
        in_specs=placed,
        out_specs=(
            P("dp", None),
            P("dp", None),
            P(),
            P(),
            P(),
            P(None, None, "tensor"),
            P("tensor", None),
            P(None, "tensor"),
            P("tensor", None),
            P(),
        ),
        check_vma=False,
    )
```

```python
import jax
import jax.numpy as jnp
from jax import lax
from jax.experimental import pallas as pl
from jax.experimental.pallas import tpu as pltpu
from jax.sharding import PartitionSpec as P

BF = jnp.bfloat16
F32 = jnp.float32

NN = ((1,), (0,))
NT = ((1,), (1,))
TN = ((0,), (0,))


def dot(left, right, dims):
    return lax.dot_general(left, right, (dims, ((), ())), preferred_element_type=F32)


def swap(values, axis, bits):
    size = lax.axis_size(axis)
    return lax.ppermute(values, axis, [(i, i ^ bits) for i in range(size)])


def to_all(blocks):
    return lax.all_to_all(blocks, "tensor", 0, 0, tiled=True)


def inverse_rms(rows):
    return lax.rsqrt(jnp.mean(rows * rows, axis=-1, keepdims=True) + eps)


HEAD_DIM = 64
GROUP = 8
TERMS = 4
GAP = 2 * TERMS
eps = 1e-06
mask_fill = -1000000000.0


def small_cost():
    return pl.CostEstimate(flops=1024, bytes_accessed=1024, transcendentals=0)


def cost_of(microseconds):
    return pl.CostEstimate(flops=1024, bytes_accessed=int(microseconds * 3.0e6), transcendentals=0)


def staged(name, body, scalars, arrays, out_shapes, scratch, limit, cost):
    count, outs, extra = len(arrays), len(out_shapes), len(scalars)

    def kernel(*refs):
        scalar_refs, refs = refs[:extra], refs[extra:]
        in_refs, refs = refs[:count], refs[count:]
        out_refs, refs = refs[:outs], refs[outs:]
        held, refs = refs[:count], refs[count:]
        made, refs = refs[:outs], refs[outs:]
        load_sems, store_sems = refs[:2]
        loads = [pltpu.make_async_copy(s, h, load_sems.at[n]) for n, (s, h) in enumerate(zip(in_refs, held))]
        stores = [pltpu.make_async_copy(m, o, store_sems.at[n]) for n, (m, o) in enumerate(zip(made, out_refs))]
        for copy in loads:
            copy.start()
        here, gone = set(), set()

        def load(n):
            if n not in here:
                here.add(n)
                loads[n].wait()
            return held[n]

        def store(*which):
            for n in which:
                gone.add(n)
                stores[n].start()

        body(load, store, made, scalar_refs, refs[2:])
        for n in range(count):
            load(n)
        for n in range(outs):
            if n not in gone:
                store(n)
        for copy in stores:
            copy.wait()

    anywhere = pl.BlockSpec(memory_space=pl.ANY)
    return pl.pallas_call(
        kernel,
        in_specs=[pl.BlockSpec(memory_space=pltpu.SMEM)] * extra + [anywhere] * count,
        out_specs=[anywhere] * outs,
        out_shape=[jax.ShapeDtypeStruct(shape, kind) for shape, kind in out_shapes],
        scratch_shapes=[pltpu.VMEM(a.shape, a.dtype) for a in arrays]
        + [pltpu.VMEM(shape, kind) for shape, kind in out_shapes]
        + [pltpu.SemaphoreType.DMA((count,)), pltpu.SemaphoreType.DMA((outs,))]
        + scratch,
        cost_estimate=cost,
        compiler_params=pltpu.CompilerParams(vmem_limit_bytes=limit << 20),
        name=name,
    )(*scalars, *arrays)


def pick_rows(base, offsets, ways):
    rows, width = base.shape
    chunks = ways
    block = rows // chunks
    groups = block // GROUP
    sub = 256
    sub_groups = sub // GROUP

    def kernel(base_ref, offset_ref, picked_ref, held, sems):
        def load(n):
            part = pl.ds(pl.multiple_of(n * block, block), block)
            return pltpu.make_async_copy(base_ref.at[part], held.at[part], sems.at[n])

        for n in range(chunks):
            load(n).start()
        local = lax.broadcasted_iota(jnp.int32, (sub, sub_groups), 0) - GROUP * lax.broadcasted_iota(
            jnp.int32, (sub, sub_groups), 1
        )

        def step(n, carry):
            load(n).wait()
            offsets = offset_ref[:, pl.ds(pl.multiple_of(n * groups, groups), groups)]
            for s in range(block // sub):
                chosen = (local == offsets[:, s * sub_groups : (s + 1) * sub_groups]).astype(F32).astype(BF)
                rows_in = held[pl.ds(pl.multiple_of(n * block + s * sub, sub), sub), :]
                to = pl.ds(pl.multiple_of(n * groups + s * sub_groups, sub_groups), sub_groups)
                picked_ref[to, :] = dot(chosen, rows_in, TN).astype(BF)
            return carry

        lax.fori_loop(0, chunks, step, 0)

    whole = pl.BlockSpec(memory_space=pltpu.VMEM)
    return pl.pallas_call(
        kernel,
        in_specs=[pl.BlockSpec(memory_space=pl.ANY), whole],
        out_specs=whole,
        out_shape=jax.ShapeDtypeStruct((rows // GROUP, width), BF),
        scratch_shapes=[pltpu.VMEM((rows, width), BF), pltpu.SemaphoreType.DMA((chunks,))],
        cost_estimate=small_cost(),
        compiler_params=pltpu.CompilerParams(vmem_limit_bytes=60 << 20),
        name="pick_rows",
    )(base, offsets)


def score_sums(base, router, mine, ways):
    rows, width = base.shape
    block = rows // ways

    def kernel(mine_ref, base_ref, router_ref, square_ref):
        score = jnp.sum(base_ref[...].astype(F32) * router_ref[...].astype(F32), axis=1, keepdims=True)
        square_ref[...] = jnp.broadcast_to(jnp.sum(score * score, axis=0, keepdims=True), square_ref.shape)

    return pl.pallas_call(
        kernel,
        grid_spec=pltpu.PrefetchScalarGridSpec(
            num_scalar_prefetch=1,
            grid=(1,),
            in_specs=[
                pl.BlockSpec((block, width), lambda i, m: (m[0], 0)),
                pl.BlockSpec((1, width), lambda i, m: (0, 0)),
            ],
            out_specs=pl.BlockSpec((1, 128), lambda i, m: (0, 0)),
        ),
        out_shape=jax.ShapeDtypeStruct((1, 128), F32),
        cost_estimate=small_cost(),
        name="score_sums",
    )(mine, base, router)


def pick_only(base, offsets, ways):
    rows, width = base.shape
    block = rows // ways
    groups = block // GROUP
    sub = 256
    sub_groups = sub // GROUP

    def kernel(base_ref, offset_ref, picked_ref):
        local = lax.broadcasted_iota(jnp.int32, (sub, sub_groups), 0) - GROUP * lax.broadcasted_iota(
            jnp.int32, (sub, sub_groups), 1
        )
        for s in range(block // sub):
            to = slice(s * sub_groups, (s + 1) * sub_groups)
            chosen = (local == offset_ref[:, to]).astype(F32).astype(BF)
            picked_ref[to, :] = dot(chosen, base_ref[s * sub : (s + 1) * sub, :], TN).astype(BF)

    return pl.pallas_call(
        kernel,
        grid=(ways,),
        in_specs=[pl.BlockSpec((block, width), lambda i: (i, 0)), pl.BlockSpec((1, groups), lambda i: (0, i))],
        out_specs=pl.BlockSpec((groups, width), lambda i: (i, 0)),
        out_shape=jax.ShapeDtypeStruct((rows // GROUP, width), BF),
        cost_estimate=small_cost(),
        name="pick_only",
    )(base, offsets)


def merge_rows(base, offsets, pieces, mine, which, held_out=None):
    rows, width = base.shape
    ways, depth, _ = pieces.shape
    count = rows // ways
    groups = count // GROUP
    kept = [] if held_out is None else [held_out]
    sub = 256
    sub_groups = sub // GROUP

    first = which.start

    def kernel(part_ref, base_ref, offset_ref, piece_ref, *rest):
        out_ref = rest[-1]
        local = lax.broadcasted_iota(jnp.int32, (sub, sub_groups), 0) - GROUP * lax.broadcasted_iota(
            jnp.int32, (sub, sub_groups), 1
        )
        for s in range(count // sub):
            here = slice(s * sub, (s + 1) * sub)
            to = slice(s * sub_groups, (s + 1) * sub_groups)
            chosen = (local == offset_ref[:, to]).astype(F32)
            hit = jnp.sum(chosen, axis=1, keepdims=True) > 0.5
            spread = dot(chosen.astype(BF), piece_ref[0, to, :], NN)
            out_ref[here, :] = jnp.where(hit, spread, base_ref[here, :].astype(F32)).astype(BF)

    grid_spec = pltpu.PrefetchScalarGridSpec(
        num_scalar_prefetch=1,
        grid=(len(which),),
        in_specs=[
            pl.BlockSpec((count, width), lambda i, m: (m[0] ^ (i + first), 0)),
            pl.BlockSpec((1, groups), lambda i, m: (0, m[0] ^ (i + first))),
            pl.BlockSpec((1, depth, width), lambda i, m: (m[0] ^ (i + first), 0, 0)),
        ]
        + [pl.BlockSpec(memory_space=pl.ANY)] * len(kept),
        out_specs=pl.BlockSpec((count, width), lambda i, m: (m[0] ^ (i + first), 0)),
    )
    return pl.pallas_call(
        kernel,
        grid_spec=grid_spec,
        out_shape=jax.ShapeDtypeStruct((rows, width), BF),
        input_output_aliases={4: 0} if kept else {},
        cost_estimate=small_cost(),
        compiler_params=pltpu.CompilerParams(vmem_limit_bytes=52 << 20),
        name="merge_rows",
    )(mine, base, offsets, pieces, *kept)


def hold_rows(base, mine, which, ways):
    rows, width = base.shape
    count = rows // ways
    first = which.start

    def kernel(mine_ref, base_ref, out_ref):
        out_ref[0] = base_ref[...]

    return pl.pallas_call(
        kernel,
        grid_spec=pltpu.PrefetchScalarGridSpec(
            num_scalar_prefetch=1,
            grid=(len(which),),
            in_specs=[pl.BlockSpec((count, width), lambda i, m: (m[0] ^ (i + first), 0))],
            out_specs=pl.BlockSpec((1, count, width), lambda i, m: (i, 0, 0)),
        ),
        out_shape=jax.ShapeDtypeStruct((len(which), count, width), BF),
        cost_estimate=small_cost(),
        compiler_params=pltpu.CompilerParams(vmem_limit_bytes=52 << 20),
        name="hold_rows",
    )(mine, base)


def merge_held(held, offsets, pieces, mine, which, out):
    rows, width = out.shape
    ways, depth, _ = pieces.shape
    count = rows // ways
    groups = count // GROUP
    sub = 256
    sub_groups = sub // GROUP

    first = which.start

    def kernel(part_ref, base_ref, offset_ref, piece_ref, old_ref, out_ref):
        local = lax.broadcasted_iota(jnp.int32, (sub, sub_groups), 0) - GROUP * lax.broadcasted_iota(
            jnp.int32, (sub, sub_groups), 1
        )
        for s in range(count // sub):
            here = slice(s * sub, (s + 1) * sub)
            to = slice(s * sub_groups, (s + 1) * sub_groups)
            chosen = (local == offset_ref[:, to]).astype(F32)
            hit = jnp.sum(chosen, axis=1, keepdims=True) > 0.5
            spread = dot(chosen.astype(BF), piece_ref[0, to, :], NN)
            out_ref[here, :] = jnp.where(hit, spread, base_ref[pl.program_id(0), here, :].astype(F32)).astype(BF)

    grid_spec = pltpu.PrefetchScalarGridSpec(
        num_scalar_prefetch=1,
        grid=(len(which),),
        in_specs=[
            pl.BlockSpec(memory_space=pltpu.VMEM),
            pl.BlockSpec((1, groups), lambda i, m: (0, m[0] ^ (i + first))),
            pl.BlockSpec((1, depth, width), lambda i, m: (m[0] ^ (i + first), 0, 0)),
            pl.BlockSpec(memory_space=pl.ANY),
        ],
        out_specs=pl.BlockSpec((count, width), lambda i, m: (m[0] ^ (i + first), 0)),
    )
    return pl.pallas_call(
        kernel,
        grid_spec=grid_spec,
        out_shape=jax.ShapeDtypeStruct((rows, width), BF),
        input_output_aliases={4: 0},
        cost_estimate=small_cost(),
        compiler_params=pltpu.CompilerParams(vmem_limit_bytes=24 << 20),
        name="merge_held",
    )(mine, held, offsets, pieces, out)


def attend(picked, gain, weight, seq_row, ways):
    rows, width = picked.shape
    heads_width = weight.shape[2]
    heads = heads_width // HEAD_DIM
    block = min(256, rows)

    def body(load, store, outs, scalars, scratch):
        low_ref, qkv_ref, out_ref, *probs_refs = outs
        values = load(0)[...].astype(F32)
        low_ref[...] = (values * inverse_rms(values) * load(1)[...].astype(F32)).astype(BF)
        store(0)
        weight_ref = load(2)
        for n in range(3):
            qkv_ref[n] = dot(low_ref[...], weight_ref[n], NN).astype(BF)
        store(1)
        sequence = load(3)[...].astype(F32)
        column = jnp.broadcast_to(sequence, (128, rows)).T[:, :1]
        lane_head = lax.broadcasted_iota(jnp.int32, (1, heads_width), 1) // HEAD_DIM
        for n in reversed(range(rows // block)):
            start, stop = n * block, (n + 1) * block
            query = qkv_ref[0, start:stop, :] * BF(HEAD_DIM ** (-0.5))
            order = lax.broadcasted_iota(jnp.int32, (block, stop), 0) + start
            keys = lax.broadcasted_iota(jnp.int32, (block, stop), 1)
            allowed = (column[start:stop, :] == sequence[:, :stop]) & (order >= keys)
            total = jnp.zeros((block, heads_width), F32)
            for head in range(heads):
                here = lane_head == head
                key = jnp.where(here, qkv_ref[1, :stop, :], BF(0))
                logits = jnp.where(allowed, dot(query, key, NT), mask_fill)
                raised = jnp.exp(logits - jnp.max(logits, axis=-1, keepdims=True))
                probs = (raised * (1.0 / jnp.sum(raised, axis=-1, keepdims=True))).astype(BF)
                probs_refs[n][head] = probs
                value = jnp.where(here, qkv_ref[2, :stop, :], BF(0))
                total = total + dot(probs, value, NN)
            for k in range(ways):
                out_ref[k, start:stop, :] = total.astype(BF)
            store(3 + n)

    return staged(
        "attend",
        body,
        [],
        [picked, gain, weight, seq_row],
        [
            ((rows, width), BF),
            ((3, rows, heads_width), BF),
            ((ways, rows, heads_width), BF),
        ]
        + [((heads, block, (n + 1) * block), BF) for n in range(rows // block)],
        [],
        60,
        small_cost(),
    )


def feed_forward(heads, own_weight, quarters, picked, gain, up, grad_act, grad_mixer, part, mine, ways):
    rows, width = picked.shape
    hidden = up.shape[1]
    sub = min(1024, hidden)
    count, _, heads_width = heads.shape
    piece = heads_width // 4
    own = rows // ways
    slope = 0.7978845608028654
    cubic = 0.044715

    def body(load, store, outs, scalars, scratch):
        part_ref, mine_ref = scalars
        attended_ref, low_ref, act_ref, pre_ref, hidden_ref, part_out_ref, gain_part_ref, sent_ref = outs
        total, state, weights = scratch
        quarter = part_ref[0] & 3
        heads_ref = load(0)
        weights[0] = load(1)[...]
        for n in range(4):
            start = pl.multiple_of((quarter ^ n) * piece, piece)
            source = load(2 + n)
            for k in range(1, count):
                weights[k, pl.ds(start, piece), :] = source[k - 1]
        attended = dot(heads_ref[mine_ref[0]], weights[0], NN)
        for k in range(1, count):
            attended = attended + dot(heads_ref[mine_ref[0] ^ k], weights[k], NN)
        total[...] = attended
        attended_ref[...] = total[pl.ds(pl.multiple_of(mine_ref[0] * own, own), own), :]
        state_in = load(6)[...].astype(F32) + attended
        state[...] = state_in
        gain_row = load(7)[...].astype(F32)
        low_ref[...] = (state_in * inverse_rms(state_in) * gain_row).astype(BF)
        store(0, 1)
        up_ref, act_grad_ref = load(8), load(9)
        for s in range(hidden // sub):
            lanes = slice(s * sub, (s + 1) * sub)
            value = dot(low_ref[...], up_ref[:, lanes], NN)
            square = value * value
            bent = jnp.tanh(value * (slope + (slope * cubic) * square))
            half = 0.5 * (1.0 + bent)
            act_ref[:, lanes] = (value * half).astype(BF)
            rise = half + (0.5 * value) * (1.0 - bent * bent) * (slope + (3.0 * slope * cubic) * square)
            pre = (act_grad_ref[:, lanes] * rise).astype(BF)
            pre_ref[:, lanes] = pre
            term = dot(pre, up_ref[:, lanes], NT)
            if s == 0:
                total[...] = term
            else:
                total[...] += term
        store(2, 3)
        state_in = state[...]
        grad = total[...]
        inverse = inverse_rms(state_in)
        normal = state_in * inverse
        gain_part_ref[...] = jnp.sum(grad * normal, axis=0, keepdims=True)
        scaled = grad * gain_row
        along = jnp.mean(scaled * normal, axis=-1, keepdims=True)
        back = inverse * (scaled - normal * along)
        hidden_ref[...] = back.astype(BF)
        part_out_ref[...] = (back + load(10)[...].astype(F32) * (1.0 / count)).astype(BF)
        store(4, 5, 6)
        for k in range(count):
            sent_ref[mine_ref[0] ^ k] = dot(part_out_ref[...], weights[k], NT).astype(BF)

    return staged(
        "feed_forward",
        body,
        [part, mine],
        [heads, own_weight, *quarters, picked, gain, up, grad_act, grad_mixer],
        [
            ((own, width), F32),
            ((rows, width), BF),
            ((rows, hidden), BF),
            ((rows, hidden), BF),
            ((rows, width), BF),
            ((rows, width), BF),
            ((1, width), F32),
            (heads.shape, BF),
        ],
        [
            pltpu.VMEM((rows, width), F32),
            pltpu.VMEM((rows, width), F32),
            pltpu.VMEM((count, heads_width, width), BF),
        ],
        60,
        small_cost(),
    )


def act_grads(picked, router, grad_rows, down):
    rows, width = grad_rows.shape

    def kernel(picked_ref, router_ref, rows_ref, down_ref, gating_ref, square_ref, mixer_ref, grad_ref):
        score = jnp.sum(picked_ref[...].astype(F32) * router_ref[...].astype(F32), axis=-1, keepdims=True)
        gating = jax.nn.sigmoid(score)
        gating_ref[...] = gating
        square_ref[...] = jnp.broadcast_to(jnp.sum(score * score, axis=0, keepdims=True), square_ref.shape)
        mixer_ref[...] = (gating * rows_ref[...].astype(F32)).astype(BF)
        grad_ref[...] = dot(mixer_ref[...], down_ref[...], NT)

    whole = pl.BlockSpec(memory_space=pltpu.VMEM)
    return pl.pallas_call(
        kernel,
        in_specs=[whole] * 4,
        out_specs=[whole] * 4,
        out_shape=[
            jax.ShapeDtypeStruct((rows, 1), F32),
            jax.ShapeDtypeStruct((1, 128), F32),
            jax.ShapeDtypeStruct((rows, width), BF),
            jax.ShapeDtypeStruct((rows, down.shape[0]), F32),
        ],
        cost_estimate=small_cost(),
        name="act_grads",
    )(picked, router, grad_rows, down)


def attend_back(head_terms, qkv, probs, weight, picked, gain, hidden_part):
    rows, width = picked.shape
    heads_width = weight.shape[2]
    heads = heads_width // HEAD_DIM
    block = min(256, rows)
    scale = HEAD_DIM ** (-0.5)

    def kernel(
        head_ref,
        qkv_ref,
        weight_ref,
        picked_ref,
        gain_ref,
        hidden_ref,
        *rest,
    ):
        probs_refs, (grads_ref, gain_part_ref, result, grad_key, grad_value) = rest[: len(probs)], rest[len(probs) :]
        lane_head = lax.broadcasted_iota(jnp.int32, (1, heads_width), 1) // HEAD_DIM
        for start in reversed(range(0, rows, block)):
            stop = start + block
            here_rows = slice(start, stop)
            grad_head = head_ref[0, here_rows, :].astype(F32)
            for k in range(1, head_ref.shape[0]):
                grad_head = grad_head + head_ref[k, here_rows, :].astype(F32)
            grad_head = grad_head.astype(BF)
            query = qkv_ref[0, here_rows, :] * BF(scale)
            grad_query = jnp.zeros((block, heads_width), F32)
            add_key = jnp.zeros((stop, heads_width), F32)
            add_value = jnp.zeros((stop, heads_width), F32)
            for head in range(heads):
                here = lane_head == head
                value = jnp.where(here, qkv_ref[2, :stop, :], BF(0))
                key = jnp.where(here, qkv_ref[1, :stop, :], BF(0))
                low = probs_refs[start // block][head]
                weighted = low.astype(F32) * dot(grad_head, value, NT)
                row_sum = jnp.sum(weighted, axis=-1, keepdims=True)
                slopes = (weighted - low.astype(F32) * row_sum).astype(BF)
                grad_query = grad_query + dot(slopes, key, NN)
                add_key = add_key + dot(slopes, jnp.where(here, query, BF(0)), TN)
                add_value = add_value + dot(low, jnp.where(here, grad_head, BF(0)), TN)
            grads_ref[0, here_rows, :] = (grad_query * scale).astype(BF)
            if stop == rows:
                grad_key[...] = add_key
                grad_value[...] = add_value
            else:
                grad_key[:stop, :] += add_key
                grad_value[:stop, :] += add_value
        grads_ref[1] = grad_key[...].astype(BF)
        grads_ref[2] = grad_value[...].astype(BF)
        first = dot(grads_ref[0], weight_ref[0], NT)
        for n in range(1, 3):
            first = first + dot(grads_ref[n], weight_ref[n], NT)
        values = picked_ref[...].astype(F32)
        inverse = inverse_rms(values)
        normal = values * inverse
        gain_part_ref[...] = jnp.sum(first * normal, axis=0, keepdims=True)
        scaled = first * gain_ref[...].astype(F32)
        along = jnp.mean(scaled * normal, axis=-1, keepdims=True)
        result[...] = (hidden_ref[...].astype(F32) + inverse * (scaled - normal * along)).astype(BF)

    whole = pl.BlockSpec(memory_space=pltpu.VMEM)
    return pl.pallas_call(
        kernel,
        in_specs=[whole] * (6 + len(probs)),
        out_specs=[whole] * 3,
        out_shape=[
            jax.ShapeDtypeStruct((3, rows, heads_width), BF),
            jax.ShapeDtypeStruct((1, width), F32),
            jax.ShapeDtypeStruct((rows, width), BF),
        ],
        scratch_shapes=[
            pltpu.VMEM((rows, heads_width), F32),
            pltpu.VMEM((rows, heads_width), F32),
        ],
        cost_estimate=small_cost(),
        compiler_params=pltpu.CompilerParams(vmem_limit_bytes=20 << 20),
        name="attend_back",
    )(head_terms, qkv, weight, picked, gain, hidden_part, *probs)


def spread_rows(down, up, order_down, order_up, part):
    count = len(down)
    wide, width = down[0].shape
    rows = wide // (2 ** len(order_down) // count)
    each = wide // rows

    def kernel(part_ref, *refs):
        down_out, up_out = refs[2 * count :]
        for n in range(count):

            @pl.when(pl.program_id(0) // each == n)
            def _():
                down_out[...] = refs[n][...].astype(F32)
                up_out[...] = refs[count + n][...].astype(F32)

    def source(n):
        return pl.BlockSpec((rows, width), lambda i, p: (jnp.clip(i - n * each, 0, each - 1), 0))

    def target(order):
        def place(i, p):
            key = sum((i >> n & 1) * bit for n, bit in enumerate(order))
            return p[0] ^ key, 0

        return pl.BlockSpec((rows, width), place)

    return pl.pallas_call(
        kernel,
        grid_spec=pltpu.PrefetchScalarGridSpec(
            num_scalar_prefetch=1,
            grid=(count * each,),
            in_specs=[source(n) for n in range(count)] * 2,
            out_specs=[target(order_down), target(order_up)],
        ),
        out_shape=[jax.ShapeDtypeStruct((count * wide, width), F32)] * 2,
        cost_estimate=small_cost(),
        name="spread_rows",
    )(part, *down, *up)


def qkv_part_of(first_low, grads, part):
    rows, width = first_low.shape
    part_width = grads.shape[2]
    half = 3 * part_width // 2

    def kernel(part_ref, low_ref, grads_ref, keep_ref, send_ref, full):
        for n in range(3):
            product = dot(grads_ref[n], low_ref[...], TN)
            full[n * part_width : (n + 1) * part_width, :] = product.astype(BF)
        core = part_ref[0] & 1
        for target, which in ((keep_ref, core), (send_ref, 1 - core)):
            target[...] = full[pl.ds(pl.multiple_of(which * half, half), half), :]

    whole = pl.BlockSpec(memory_space=pltpu.VMEM)
    return pl.pallas_call(
        kernel,
        in_specs=[pl.BlockSpec(memory_space=pltpu.SMEM)] + [whole] * 2,
        out_specs=[whole] * 2,
        out_shape=[jax.ShapeDtypeStruct((half, width), BF)] * 2,
        scratch_shapes=[pltpu.VMEM((2 * half, width), BF)],
        cost_estimate=small_cost(),
        compiler_params=pltpu.CompilerParams(vmem_limit_bytes=14 << 20),
        name="qkv_part",
    )(part, first_low, grads)


def spread_qkv(near, far, part, part_width):
    rows, width = near.shape
    tile = 128
    count = rows // tile
    many = part_width // tile

    def kernel(part_ref, near_ref, far_ref, out_ref):
        core = part_ref[0] & 1
        for ref, which in ((near_ref, core), (far_ref, 1 - core)):
            for n in range(count):
                spot = which * count + n
                column = pl.multiple_of(spot % many * tile, tile)
                piece = ref[n * tile : (n + 1) * tile, :].astype(F32)
                out_ref[spot // many, :, pl.ds(column, tile)] = piece.T

    whole = pl.BlockSpec(memory_space=pltpu.VMEM)
    return pl.pallas_call(
        kernel,
        in_specs=[pl.BlockSpec(memory_space=pltpu.SMEM)] + [whole] * 2,
        out_specs=whole,
        out_shape=jax.ShapeDtypeStruct((2 * rows // part_width, width, part_width), F32),
        cost_estimate=small_cost(),
        compiler_params=pltpu.CompilerParams(vmem_limit_bytes=14 << 20),
        name="spread_qkv",
    )(part, near, far)


def core_grads(activated, grad_mixer, second_low, grad_pre, heads, attended_part, part, keys_a, keys_b):
    rows, hidden = activated.shape
    width = grad_mixer.shape[1]
    copies = len(keys_a)
    half = copies // 2
    count, _, heads_width = heads.shape
    block = hidden // copies
    small = heads_width // copies
    many = count // 2
    depth = half * (block + many * small)

    def kernel(part_ref, act_ref, mixer_ref, low_ref, pre_ref, heads_ref, term_ref, keep_ref, *rest):
        wide_refs, narrow_refs, (full, narrow) = rest[0:2], rest[2:4], rest[4:]

        def place(source, each, lane, keys, first, stride):
            for n, key in enumerate(keys):
                start = pl.multiple_of((part_ref[0] ^ key) * each, each)
                at = first + (n % half) * stride
                piece = source[pl.ds(start, each), :]
                if n < half:
                    keep_ref[lane, at : at + each, :] = piece
                elif first == 0:
                    wide_refs[lane][at : at + each, :] = piece
                else:
                    narrow_refs[lane][at - half * block : at - half * block + each, :] = piece

        full[...] = dot(act_ref[...], mixer_ref[...], TN).astype(BF)
        place(full, block, 0, keys_a, 0, block)
        full[...] = dot(low_ref[...], pre_ref[...], TN).astype(BF)
        place(full, block, 1, keys_b, 0, block)
        for k in range(count):
            narrow[...] = dot(heads_ref[k], term_ref[...], TN).astype(BF)
            lane, spot = divmod(k, many)
            place(narrow, small, lane, keys_b if lane else keys_a, half * block + spot * small, many * small)

    whole = pl.BlockSpec(memory_space=pltpu.VMEM)
    wide_shape = jax.ShapeDtypeStruct((half * block, width), BF)
    narrow_shape = jax.ShapeDtypeStruct((half * many * small, width), BF)
    return pl.pallas_call(
        kernel,
        in_specs=[pl.BlockSpec(memory_space=pltpu.SMEM)] + [whole] * 6,
        out_specs=[whole] * 5,
        out_shape=[jax.ShapeDtypeStruct((2, depth, width), BF)] + [wide_shape] * 2 + [narrow_shape] * 2,
        scratch_shapes=[pltpu.VMEM((hidden, width), BF), pltpu.VMEM((heads_width, width), BF)],
        cost_estimate=small_cost(),
        compiler_params=pltpu.CompilerParams(vmem_limit_bytes=14 << 20),
        name="core_grads",
    )(part, activated, grad_mixer, second_low, grad_pre, heads, attended_part)


def plus(left, right):
    return (left.astype(F32) + right.astype(F32)).astype(BF)


def halving_sums(keep, got_a, got_b, wide, narrow):
    width = keep.shape[2]
    count = len(got_a)

    def kernel(keep_ref, *refs):
        a_got, b_got, (stay_ref, a_out, b_out) = refs[:count], refs[count : 2 * count], refs[2 * count :]
        for lane, got, out in ((0, a_got, a_out), (1, b_got, b_out)):
            for first, size, at in ((0, wide // 2, 0), (wide, narrow // 2, wide // 2)):
                source, shift = (got[1], wide) if count == 2 and first else (got[0], 0)
                to = slice(at, at + size)
                for start, target in ((first, stay_ref.at[lane]), (first + size, out)):
                    here = slice(start - shift, start - shift + size)
                    target[to, :] = plus(keep_ref[lane, start : start + size, :], source[here, :])

    whole = pl.BlockSpec(memory_space=pltpu.VMEM)
    depth = (wide + narrow) // 2
    lane_shape = jax.ShapeDtypeStruct((depth, width), BF)
    return pl.pallas_call(
        kernel,
        in_specs=[whole] * (1 + 2 * count),
        out_specs=[whole] * 3,
        out_shape=[jax.ShapeDtypeStruct((2, depth, width), BF), lane_shape, lane_shape],
        cost_estimate=small_cost(),
        compiler_params=pltpu.CompilerParams(vmem_limit_bytes=14 << 20),
        name="halving_sums",
    )(keep, *got_a, *got_b)


def owned_sums(keep, got_a, got_b, fresh, small, wide, ways):
    width = keep.shape[2]
    narrow = keep.shape[1] - wide
    own = fresh.shape[0]
    many = ways // 2
    each = narrow // many
    depth = own + GAP + each

    def kernel(keep_ref, a_got, b_got, fresh_ref, small_ref, a_out, b_out, sent_ref):
        sums = split_sums(small_ref[...])
        for lane, got, out in ((0, a_got, a_out), (1, b_got, b_out)):
            out[...] = plus(keep_ref[lane, :wide, :], got[:wide, :])
            done = plus(keep_ref[lane, wide:, :], got[wide:, :])
            for spot in range(many):
                k = lane * many + spot
                sent_ref[k, :own, :] = fresh_ref[...]
                sent_ref[k, own : own + GAP, :] = sums
                sent_ref[k, own + GAP :, :] = done[spot * each : (spot + 1) * each, :]

    whole = pl.BlockSpec(memory_space=pltpu.VMEM)
    lane_shape = jax.ShapeDtypeStruct((wide, width), BF)
    return pl.pallas_call(
        kernel,
        in_specs=[whole] * 5,
        out_specs=[whole] * 3,
        out_shape=[lane_shape, lane_shape, jax.ShapeDtypeStruct((ways, depth, width), BF)],
        cost_estimate=small_cost(),
        compiler_params=pltpu.CompilerParams(vmem_limit_bytes=10 << 20),
        name="owned_sums",
    )(keep, got_a, got_b, fresh, small)


def core_sums(rows, other):
    depth, width = rows.shape
    third = depth // 2

    def kernel(rows_ref, other_ref, a_out, b_out):
        a_out[...] = plus(rows_ref[:third, :], other_ref[:third, :])
        b_out[...] = plus(rows_ref[third:, :], other_ref[third:, :])

    whole = pl.BlockSpec(memory_space=pltpu.VMEM)
    return pl.pallas_call(
        kernel,
        in_specs=[whole] * 2,
        out_specs=[whole] * 2,
        out_shape=[jax.ShapeDtypeStruct((third, width), BF)] * 2,
        cost_estimate=small_cost(),
        compiler_params=pltpu.CompilerParams(vmem_limit_bytes=10 << 20),
        name="core_sums",
    )(rows, other)


def lane_sums(lane_a, got_a, lane_b, got_b):
    def kernel(a_ref, a_got, b_ref, b_got, a_out, b_out):
        a_out[...] = plus(a_ref[...], a_got[...])
        b_out[...] = plus(b_ref[...], b_got[...])

    whole = pl.BlockSpec(memory_space=pltpu.VMEM)
    return pl.pallas_call(
        kernel,
        in_specs=[whole] * 4,
        out_specs=[whole] * 2,
        out_shape=[jax.ShapeDtypeStruct(lane_a.shape, BF)] * 2,
        cost_estimate=small_cost(),
        compiler_params=pltpu.CompilerParams(vmem_limit_bytes=12 << 20),
        name="lane_sums",
    )(lane_a, got_a, lane_b, got_b)


def joined_lanes(lane_a, got_a, lane_b, got_b):
    rows, width = lane_a.shape

    def kernel(a_ref, a_got, b_ref, b_got, out_ref):
        out_ref[:rows, :] = plus(a_ref[...], a_got[...])
        out_ref[rows:, :] = plus(b_ref[...], b_got[...])

    whole = pl.BlockSpec(memory_space=pltpu.VMEM)
    return pl.pallas_call(
        kernel,
        in_specs=[whole] * 4,
        out_specs=whole,
        out_shape=jax.ShapeDtypeStruct((2 * rows, width), BF),
        cost_estimate=small_cost(),
        compiler_params=pltpu.CompilerParams(vmem_limit_bytes=10 << 20),
        name="joined_lanes",
    )(lane_a, got_a, lane_b, got_b)


def gather_blocks(blocks_a, blocks_b):
    wide, width = blocks_a[0].shape
    count = len(blocks_a)

    def kernel(*refs):
        for lane in range(2):
            for n in range(count):
                refs[2 * count + lane][n * wide : (n + 1) * wide, :] = refs[lane * count + n][...]

    whole = pl.BlockSpec(memory_space=pltpu.VMEM)
    return pl.pallas_call(
        kernel,
        in_specs=[whole] * (2 * count),
        out_specs=[whole] * 2,
        out_shape=[jax.ShapeDtypeStruct((count * wide, width), BF)] * 2,
        cost_estimate=small_cost(),
        compiler_params=pltpu.CompilerParams(vmem_limit_bytes=10 << 20),
        name="gather_blocks",
    )(*blocks_a, *blocks_b)


def split_sums(values):
    high = values.astype(BF)
    low = (values - high.astype(F32)).astype(BF)
    return jnp.concatenate([high, low], axis=0)


def joined_sums(rows):
    return rows[:TERMS].astype(F32) + rows[TERMS : 2 * TERMS].astype(F32)


def first_small(received, own):
    ways, depth, width = received.shape
    each = depth - own - GAP

    def kernel(got_ref, out_ref):
        total = got_ref[0, own + GAP :, :].astype(F32)
        sums = joined_sums(got_ref[0, own : own + GAP, :])
        for k in range(1, ways):
            total = total + got_ref[k, own + GAP :, :].astype(F32)
            sums = sums + joined_sums(got_ref[k, own : own + GAP, :])
        out_ref[:each, :] = total.astype(BF)
        out_ref[each:, :] = split_sums(sums)

    whole = pl.BlockSpec(memory_space=pltpu.VMEM)
    return pl.pallas_call(
        kernel,
        in_specs=[whole],
        out_specs=whole,
        out_shape=jax.ShapeDtypeStruct((each + GAP, width), BF),
        cost_estimate=small_cost(),
        compiler_params=pltpu.CompilerParams(vmem_limit_bytes=8 << 20),
        name="first_small",
    )(received)


def last_small(blocks, keys, part, shares):
    depth, width = blocks[0].shape
    each = depth - GAP
    count = len(blocks)

    def kernel(part_ref, *refs):
        out_ref, small_refs = refs[count], refs[count + 1 :]
        total = joined_sums(refs[0][each:, :])
        for n in range(1, count):
            total = total + joined_sums(refs[n][each:, :])
        for n in range(TERMS - 1):
            small_refs[n][...] = total[n : n + 1, :]
        lane = lax.broadcasted_iota(jnp.int32, (1, 128), 1)
        small_refs[TERMS - 1][...] = total[TERMS - 1 :, :128] * jnp.where(lane == 0, shares[0], shares[1])
        for n in range(count):
            start = pl.multiple_of((part_ref[0] ^ keys[n]) * each, each)
            out_ref[pl.ds(start, each), :] = refs[n][:each, :].astype(F32)

    whole = pl.BlockSpec(memory_space=pltpu.VMEM)
    return pl.pallas_call(
        kernel,
        in_specs=[pl.BlockSpec(memory_space=pltpu.SMEM)] + [whole] * count,
        out_specs=[whole] * (1 + TERMS),
        out_shape=[jax.ShapeDtypeStruct((count * each, width), F32)] + [jax.ShapeDtypeStruct((1, width), F32)] * (TERMS - 1)
        + [jax.ShapeDtypeStruct((1, 128), F32)],
        cost_estimate=small_cost(),
        compiler_params=pltpu.CompilerParams(vmem_limit_bytes=10 << 20),
        name="last_small",
    )(part, *blocks)


def finish_rows(mixer_terms, picked, gating, attended, grad_rows, gain_one, gain_two, square, routed_square, mine, ways):
    rows, width = picked.shape
    own = rows // ways

    def kernel(
        mine_ref,
        terms_ref,
        picked_ref,
        gating_ref,
        attended_ref,
        rows_ref,
        one_ref,
        two_ref,
        square_ref,
        routed_ref,
        new_ref,
        score_ref,
        small_ref,
    ):
        branch = attended_ref[...]
        for k in range(ways):
            branch = branch + terms_ref[k].astype(F32)
        values = picked_ref[...].astype(F32)
        gate = gating_ref[...]
        new_ref[...] = (values + gate * branch).astype(BF)
        along = jnp.sum(rows_ref[...].astype(F32) * branch, axis=-1, keepdims=True)
        score = along * gate * (1.0 - gate)
        score_ref[...] = score
        small_ref[0:1, :] = jnp.sum(score * values, axis=0, keepdims=True)
        small_ref[1:2, :] = one_ref[...]
        small_ref[2:3, :] = two_ref[...]
        lane = lax.broadcasted_iota(jnp.int32, (1, width), 1)
        both = jnp.where(lane == 0, square_ref[:, 0:1], routed_ref[:, 0:1] * (1.0 / ways))
        small_ref[3:4, :] = jnp.where(lane < 2, both, 0.0)

    def block(shape):
        return pl.BlockSpec(shape, lambda i, m: (m[0], 0))

    def fixed(shape):
        return pl.BlockSpec(shape, lambda i, m: (0, 0))

    return pl.pallas_call(
        kernel,
        grid_spec=pltpu.PrefetchScalarGridSpec(
            num_scalar_prefetch=1,
            grid=(1,),
            in_specs=[pl.BlockSpec(mixer_terms.shape, lambda i, m: (0, 0, 0))]
            + [block((own, width)), block((own, 1)), fixed((own, width)), block((own, width))]
            + [fixed((1, width))] * 2
            + [fixed((1, 128))] * 2,
            out_specs=[fixed((own, width)), fixed((own, 1)), fixed((4, width))],
        ),
        out_shape=[
            jax.ShapeDtypeStruct((own, width), BF),
            jax.ShapeDtypeStruct((own, 1), F32),
            jax.ShapeDtypeStruct((4, width), F32),
        ],
        cost_estimate=cost_of(10),
        name="finish_rows",
    )(mine, mixer_terms, picked, gating, attended, grad_rows, gain_one, gain_two, square, routed_square)


def finish_input(terms, grad_rows, score, router, mine, ways):
    rows, width = grad_rows.shape
    own = rows // ways

    def kernel(mine_ref, terms_ref, rows_ref, score_ref, router_ref, out_ref):
        total = rows_ref[...].astype(F32) + score_ref[...] * router_ref[...].astype(F32)
        for k in range(ways):
            total = total + terms_ref[k].astype(F32)
        for k in range(ways):
            out_ref[k] = total.astype(BF)

    def fixed(shape):
        return pl.BlockSpec(shape, lambda i, m: (0,) * len(shape))

    return pl.pallas_call(
        kernel,
        grid_spec=pltpu.PrefetchScalarGridSpec(
            num_scalar_prefetch=1,
            grid=(1,),
            in_specs=[
                fixed((ways, own, width)),
                pl.BlockSpec((own, width), lambda i, m: (m[0], 0)),
                fixed((own, 1)),
                fixed((1, width)),
            ],
            out_specs=fixed((ways, own, width)),
        ),
        out_shape=jax.ShapeDtypeStruct((ways, own, width), BF),
        cost_estimate=small_cost(),
        compiler_params=pltpu.CompilerParams(vmem_limit_bytes=8 << 20),
        name="finish_input",
    )(mine, terms, grad_rows, score, router)


def split_kept(count, order):
    keys = [0]
    for bit in reversed(order):
        keys = keys + [k ^ bit for k in keys]
    return keys


def per_device(
    tokens,
    route_offset,
    unit_sequence,
    cotangent,
    router_weight,
    first_gain,
    second_gain,
    qkv_weight,
    out_weight,
    up_weight,
    down_weight,
):
    rows_local, width = tokens.shape
    routed = route_offset.shape[1]
    ways = lax.axis_size("tensor")
    copies = lax.axis_size("dp")
    mine = lax.axis_index("tensor")
    part = lax.axis_index("dp")
    mine_array = jnp.reshape(mine, (1,)).astype(jnp.int32)
    part_array = jnp.reshape(part, (1,)).astype(jnp.int32)
    ladder = [1 << b for b in range(1, copies.bit_length() - 1)]
    order_a = [1] + ladder
    order_b = [1] + ladder[::-1]
    keys_a = split_kept(copies, order_a)
    keys_b = split_kept(copies, order_b)

    tie = lax.optimization_barrier
    own_rows = routed // ways
    heads_width = out_weight.shape[0]
    hidden = up_weight.shape[1]
    by_swaps = copies == 8
    bit_x, bit_y = 2, 4
    shares = (1.0 / (rows_local * copies), 1.0 / (routed * copies))

    quarter = part & 3
    piece_rows = heads_width // 4
    piece = lax.dynamic_slice_in_dim(out_weight, quarter * piece_rows, piece_rows, 0)
    here = [swap(piece, "tensor", k) for k in range(1, ways)]

    picked = pick_rows(tokens, route_offset, ways)
    first_low, qkv, head_out, *probs = attend(picked, first_gain[None], qkv_weight, unit_sequence, ways)
    here, head_out = tie((here, head_out))

    heads = to_all(head_out)
    here = jnp.stack(here)
    beside, across = swap(here, "dp", bit_x), swap(here, "dp", 1)
    cotangent, router_weight, second_gain, here, head_out = tie(
        (cotangent, router_weight, second_gain, here, head_out)
    )
    weight_row = router_weight[None]
    grad_rows = pick_only(cotangent, route_offset, ways)
    beside, across, here, grad_rows = tie((beside, across, here, grad_rows))
    quarters = [here, across, beside, swap(beside, "dp", 1)]
    gating, routed_square, grad_mixer, grad_act = act_grads(picked, weight_row, grad_rows, down_weight)
    square = score_sums(tokens, weight_row, mine_array, ways)
    heads, quarters, grad_act, grad_mixer, square = tie((heads, quarters, grad_act, grad_mixer, square))
    attended, second_low, activated, grad_pre, hidden_part, attended_part, second_gain_part, head_sent = feed_forward(
        heads,
        out_weight,
        quarters,
        picked,
        second_gain[None],
        up_weight,
        grad_act,
        grad_mixer,
        part_array,
        mine_array,
        ways,
    )

    head_terms = to_all(head_sent)
    wide = hidden // 2
    narrow = heads_width * ways // 4
    if by_swaps:
        kept, *leaving = core_grads(
            activated, grad_mixer, second_low, grad_pre, heads, attended_part, part_array, keys_a, keys_b
        )
        wide_a, wide_b, narrow_a, narrow_b = (swap(array, "dp", 1) for array in leaving)
        activated, kept = tie((activated, kept))
    else:
        down_part = dot(activated, grad_mixer, TN).astype(BF)
        up_part = dot(second_low, grad_pre, TN).astype(BF)
        out_parts = jnp.stack([dot(heads[k], attended_part, TN).astype(BF) for k in range(ways)])
    mixer_part = dot(activated, down_weight, NN).astype(BF).reshape(ways, own_rows, width)
    if by_swaps:
        wide_a, wide_b, narrow_a, narrow_b, mixer_part = tie((wide_a, wide_b, narrow_a, narrow_b, mixer_part))
        kept, leave_a, leave_b = halving_sums(kept, (wide_a, narrow_a), (wide_b, narrow_b), wide, narrow)
        got_a, got_b = swap(leave_a, "dp", bit_x), swap(leave_b, "dp", bit_y)
        head_terms, mixer_part, kept = tie((head_terms, mixer_part, kept))
    else:
        head_terms, mixer_part = tie((head_terms, mixer_part))

    mixer_terms = to_all(mixer_part)
    grad_projected, first_gain_part, input_part = attend_back(
        head_terms, qkv, probs, qkv_weight, picked, first_gain[None], hidden_part
    )
    qkv_part, qkv_leaving = qkv_part_of(first_low, grad_projected, part_array)
    input_part = input_part.reshape(ways, own_rows, width)
    if by_swaps:
        got_a, got_b, qkv_part, qkv_leaving, input_part = tie((got_a, got_b, qkv_part, qkv_leaving, input_part))
        kept, leave_a, leave_b = halving_sums(kept, (got_a,), (got_b,), wide // 2, narrow // 2)
        mixer_terms, input_part, qkv_part, kept, leave_a, leave_b = tie(
            (mixer_terms, input_part, qkv_part, kept, leave_a, leave_b)
        )
    else:
        mixer_terms, input_part, qkv_part = tie((mixer_terms, input_part, qkv_part))

    input_terms = to_all(input_part)
    if by_swaps:
        got_a, got_b = swap(leave_a, "dp", bit_y), swap(leave_b, "dp", bit_x)
        qkv_got = swap(qkv_leaving, "dp", 1)
    new_own, grad_score, small = finish_rows(
        mixer_terms,
        picked,
        gating,
        attended,
        grad_rows,
        first_gain_part,
        second_gain_part,
        square,
        routed_square,
        mine_array,
        ways,
    )
    if by_swaps:
        got_a, got_b, new_own = tie((got_a, got_b, new_own))
        lane_a, lane_b, sent = owned_sums(kept, got_a, got_b, new_own, small, wide // 4, ways)
        got_a, got_b = swap(lane_a, "dp", bit_y), swap(lane_b, "dp", bit_x)
        qkv_part, qkv_got, lane_a, lane_b, sent = tie((qkv_part, qkv_got, lane_a, lane_b, sent))
        qkv_a, qkv_b = core_sums(qkv_part, qkv_got)
        input_terms, sent, got_a, got_b, qkv_a, qkv_b = tie((input_terms, sent, got_a, got_b, qkv_a, qkv_b))
    else:
        sent = jnp.concatenate([new_own, split_sums(small)])
        sent = jnp.broadcast_to(sent[None], (ways,) + sent.shape)
        input_terms, sent = tie((input_terms, sent))

    fresh = to_all(sent)
    if by_swaps:
        more_a = [swap(array, "dp", bit_x) for array in (lane_a, got_a)]
        more_b = [swap(array, "dp", bit_y) for array in (lane_b, got_b)]
    last = finish_input(input_terms, grad_rows, grad_score, weight_row, mine_array, ways)
    cotangent, last = tie((cotangent, last))
    early = merge_rows(cotangent, route_offset, last, mine_array, range(1))
    if by_swaps:
        more_a, more_b, early, qkv_a, qkv_b = tie((more_a, more_b, early, qkv_a, qkv_b))
        qkv_a_got, qkv_b_got = swap(qkv_a, "dp", bit_y), swap(qkv_b, "dp", bit_x)
        down_one, up_one = gather_blocks([lane_a, got_a], [lane_b, got_b])
        down_two, up_two = gather_blocks(more_a, more_b)
        down_near, up_near = [down_one, down_two], [up_one, up_two]
        down_far = [swap(array, "dp", 1) for array in down_near]
        up_far = [swap(array, "dp", 1) for array in up_near]

        def gathered(order):
            keys = [0]
            for bit in order:
                keys = keys + [k ^ bit for k in keys]
            return keys

        down_grad, up_grad = spread_rows(
            down_near + down_far, up_near + up_far, [bit_y, bit_x, 1], [bit_x, bit_y, 1], part_array
        )
        fresh, last, down_grad, up_grad = tie((fresh, last, down_grad, up_grad))
    else:
        fresh, last = tie((fresh, last))

    input_rows = to_all(last)
    if by_swaps:
        blocks = [first_small(fresh, own_rows)]
        more = [swap(array, "dp", bit_x) for array in blocks]
        qkv_a_got, qkv_b_got, blocks = tie((qkv_a_got, qkv_b_got, blocks))
        qkv_a, qkv_b = lane_sums(qkv_a, qkv_a_got, qkv_b, qkv_b_got)
        qkv_a_got, qkv_b_got = swap(qkv_a, "dp", bit_x), swap(qkv_b, "dp", bit_y)
        fresh, blocks, qkv_a, qkv_b = tie((fresh, blocks, qkv_a, qkv_b))
    output = merge_rows(tokens, route_offset, fresh, mine_array, range(ways // 2))
    cotangent, output = tie((cotangent, output))
    held = hold_rows(cotangent, mine_array, range(1, ways), ways)
    held = pltpu.with_memory_space_constraint(held, pltpu.VMEM)
    if by_swaps:
        more, qkv_a_got, qkv_b_got, output, held = tie((more, qkv_a_got, qkv_b_got, output, held))
        qkv_near = joined_lanes(qkv_a, qkv_a_got, qkv_b, qkv_b_got)
        qkv_far = swap(qkv_near, "dp", 1)
        blocks = blocks + more
        more = [swap(array, "dp", bit_y) for array in blocks]
        fresh, blocks, qkv_near = tie((fresh, blocks, qkv_near))
    output = merge_rows(tokens, route_offset, fresh, mine_array, range(ways // 2, ways), output)
    if by_swaps:
        more, qkv_far, output = tie((more, qkv_far, output))
        blocks = blocks + more
        more = [swap(array, "dp", 1) for array in blocks]
        qkv_near, blocks = tie((qkv_near, blocks))
        qkv_grad = spread_qkv(qkv_near, qkv_far, part_array, qkv_weight.shape[2])
        more, qkv_grad = tie((more, qkv_grad))
        out_grad, *small = last_small(blocks + more, gathered([bit_x, bit_y, 1]), part_array, shares)
        small[3] = small[3][:, :2]
        input_rows, early, output, held, out_grad, small, qkv_grad = tie(
            (input_rows, early, output, held, out_grad, small, qkv_grad)
        )
    input_grad = merge_held(held, route_offset, input_rows, mine_array, range(1, ways), early)
    if not by_swaps:
        swapped = jnp.concatenate([qkv_leaving, qkv_part])
        qkv_whole = jnp.where(part & 1 == 0, jnp.concatenate([qkv_part, qkv_leaving]), swapped)
        small = sum(joined_sums(fresh[k, own_rows:]) for k in range(ways))
        small = lax.psum(small, "dp")
        small = [small[n : n + 1] for n in range(TERMS)]
        small[3] = small[3][:, :2] * jnp.array((shares,), F32)
        down_grad, up_grad, qkv_sum, out_sum = (
            lax.psum(v, "dp").astype(F32) for v in (down_part, up_part, qkv_whole, out_parts)
        )
        out_grad = jnp.sum(to_all(out_sum.astype(BF)).astype(F32), axis=0)
        qkv_grad = qkv_sum.reshape(3, -1, width).transpose(0, 2, 1)
    router_grad, first_gain_grad, second_gain_grad = (small[n].reshape(width) for n in range(3))
    score_stats = small[3].reshape(2)
    return (
        output,
        input_grad,
        router_grad,
        first_gain_grad,
        second_gain_grad,
        qkv_grad,
        out_grad,
        up_grad,
        down_grad,
        score_stats,
    )


def solution(mesh):
    placed = (
        P("dp", None),
        P("dp", None),
        P("dp", None),
        P("dp", None),
        P(),
        P(),
        P(),
        P(None, None, "tensor"),
        P("tensor", None),
        P(None, "tensor"),
        P("tensor", None),
    )
    return jax.shard_map(
        per_device,
        mesh=mesh,
        in_specs=placed,
        out_specs=(
            P("dp", None),
            P("dp", None),
            P(),
            P(),
            P(),
            P(None, None, "tensor"),
            P("tensor", None),
            P(None, "tensor"),
            P("tensor", None),
            P(),
        ),
        check_vma=False,
    )
```

```python
import jax
import jax.numpy as jnp
from jax import lax
from jax.experimental import pallas as pl
from jax.experimental.pallas import tpu as pltpu
from jax.sharding import PartitionSpec as P

BF = jnp.bfloat16
F32 = jnp.float32

NN = ((1,), (0,))
NT = ((1,), (1,))
TN = ((0,), (0,))


def dot(left, right, dims):
    return lax.dot_general(left, right, (dims, ((), ())), preferred_element_type=F32)


def swap(values, axis, bits):
    size = lax.axis_size(axis)
    return lax.ppermute(values, axis, [(i, i ^ bits) for i in range(size)])


def to_all(blocks):
    return lax.all_to_all(blocks, "tensor", 0, 0, tiled=True)


def inverse_rms(rows):
    return lax.rsqrt(jnp.mean(rows * rows, axis=-1, keepdims=True) + eps)


HEAD_DIM = 64
GROUP = 8
TERMS = 4
GAP = 2 * TERMS
eps = 1e-06
mask_fill = -1000000000.0


def small_cost():
    return pl.CostEstimate(flops=1024, bytes_accessed=1024, transcendentals=0)


def cost_of(microseconds):
    return pl.CostEstimate(flops=1024, bytes_accessed=int(microseconds * 3.0e6), transcendentals=0)


def staged(name, body, scalars, arrays, out_shapes, scratch, limit, cost):
    count, outs, extra = len(arrays), len(out_shapes), len(scalars)

    def kernel(*refs):
        scalar_refs, refs = refs[:extra], refs[extra:]
        in_refs, refs = refs[:count], refs[count:]
        out_refs, refs = refs[:outs], refs[outs:]
        held, refs = refs[:count], refs[count:]
        made, refs = refs[:outs], refs[outs:]
        load_sems, store_sems = refs[:2]
        loads = [pltpu.make_async_copy(s, h, load_sems.at[n]) for n, (s, h) in enumerate(zip(in_refs, held))]
        stores = [pltpu.make_async_copy(m, o, store_sems.at[n]) for n, (m, o) in enumerate(zip(made, out_refs))]
        for copy in loads:
            copy.start()
        here, gone = set(), set()

        def load(n):
            if n not in here:
                here.add(n)
                loads[n].wait()
            return held[n]

        def store(*which):
            for n in which:
                gone.add(n)
                stores[n].start()

        body(load, store, made, scalar_refs, refs[2:])
        for n in range(count):
            load(n)
        for n in range(outs):
            if n not in gone:
                store(n)
        for copy in stores:
            copy.wait()

    anywhere = pl.BlockSpec(memory_space=pl.ANY)
    return pl.pallas_call(
        kernel,
        in_specs=[pl.BlockSpec(memory_space=pltpu.SMEM)] * extra + [anywhere] * count,
        out_specs=[anywhere] * outs,
        out_shape=[jax.ShapeDtypeStruct(shape, kind) for shape, kind in out_shapes],
        scratch_shapes=[pltpu.VMEM(a.shape, a.dtype) for a in arrays]
        + [pltpu.VMEM(shape, kind) for shape, kind in out_shapes]
        + [pltpu.SemaphoreType.DMA((count,)), pltpu.SemaphoreType.DMA((outs,))]
        + scratch,
        cost_estimate=cost,
        compiler_params=pltpu.CompilerParams(vmem_limit_bytes=limit << 20),
        name=name,
    )(*scalars, *arrays)


def pick_rows(base, offsets, ways):
    rows, width = base.shape
    chunks = ways
    block = rows // chunks
    groups = block // GROUP
    sub = 256
    sub_groups = sub // GROUP

    def kernel(base_ref, offset_ref, picked_ref, held, sems):
        def load(n):
            part = pl.ds(pl.multiple_of(n * block, block), block)
            return pltpu.make_async_copy(base_ref.at[part], held.at[part], sems.at[n])

        for n in range(chunks):
            load(n).start()
        local = lax.broadcasted_iota(jnp.int32, (sub, sub_groups), 0) - GROUP * lax.broadcasted_iota(
            jnp.int32, (sub, sub_groups), 1
        )

        def step(n, carry):
            load(n).wait()
            offsets = offset_ref[:, pl.ds(pl.multiple_of(n * groups, groups), groups)]
            for s in range(block // sub):
                chosen = (local == offsets[:, s * sub_groups : (s + 1) * sub_groups]).astype(F32).astype(BF)
                rows_in = held[pl.ds(pl.multiple_of(n * block + s * sub, sub), sub), :]
                to = pl.ds(pl.multiple_of(n * groups + s * sub_groups, sub_groups), sub_groups)
                picked_ref[to, :] = dot(chosen, rows_in, TN).astype(BF)
            return carry

        lax.fori_loop(0, chunks, step, 0)

    whole = pl.BlockSpec(memory_space=pltpu.VMEM)
    return pl.pallas_call(
        kernel,
        in_specs=[pl.BlockSpec(memory_space=pl.ANY), whole],
        out_specs=whole,
        out_shape=jax.ShapeDtypeStruct((rows // GROUP, width), BF),
        scratch_shapes=[pltpu.VMEM((rows, width), BF), pltpu.SemaphoreType.DMA((chunks,))],
        cost_estimate=small_cost(),
        compiler_params=pltpu.CompilerParams(vmem_limit_bytes=60 << 20),
        name="pick_rows",
    )(base, offsets)


def score_sums(base, router, mine, ways):
    rows, width = base.shape
    block = rows // ways

    def kernel(mine_ref, base_ref, router_ref, square_ref):
        score = jnp.sum(base_ref[...].astype(F32) * router_ref[...].astype(F32), axis=1, keepdims=True)
        square_ref[...] = jnp.broadcast_to(jnp.sum(score * score, axis=0, keepdims=True), square_ref.shape)

    return pl.pallas_call(
        kernel,
        grid_spec=pltpu.PrefetchScalarGridSpec(
            num_scalar_prefetch=1,
            grid=(1,),
            in_specs=[
                pl.BlockSpec((block, width), lambda i, m: (m[0], 0)),
                pl.BlockSpec((1, width), lambda i, m: (0, 0)),
            ],
            out_specs=pl.BlockSpec((1, 128), lambda i, m: (0, 0)),
        ),
        out_shape=jax.ShapeDtypeStruct((1, 128), F32),
        cost_estimate=small_cost(),
        name="score_sums",
    )(mine, base, router)


def pick_only(base, offsets, ways):
    rows, width = base.shape
    block = rows // ways
    groups = block // GROUP
    sub = 256
    sub_groups = sub // GROUP

    def kernel(base_ref, offset_ref, picked_ref):
        local = lax.broadcasted_iota(jnp.int32, (sub, sub_groups), 0) - GROUP * lax.broadcasted_iota(
            jnp.int32, (sub, sub_groups), 1
        )
        for s in range(block // sub):
            to = slice(s * sub_groups, (s + 1) * sub_groups)
            chosen = (local == offset_ref[:, to]).astype(F32).astype(BF)
            picked_ref[to, :] = dot(chosen, base_ref[s * sub : (s + 1) * sub, :], TN).astype(BF)

    return pl.pallas_call(
        kernel,
        grid=(ways,),
        in_specs=[pl.BlockSpec((block, width), lambda i: (i, 0)), pl.BlockSpec((1, groups), lambda i: (0, i))],
        out_specs=pl.BlockSpec((groups, width), lambda i: (i, 0)),
        out_shape=jax.ShapeDtypeStruct((rows // GROUP, width), BF),
        cost_estimate=small_cost(),
        name="pick_only",
    )(base, offsets)


def merge_rows(base, offsets, pieces, mine, which, held_out=None):
    rows, width = base.shape
    ways, depth, _ = pieces.shape
    count = rows // ways
    groups = count // GROUP
    kept = [] if held_out is None else [held_out]
    sub = 256
    sub_groups = sub // GROUP

    first = which.start

    def kernel(part_ref, base_ref, offset_ref, piece_ref, *rest):
        out_ref = rest[-1]
        local = lax.broadcasted_iota(jnp.int32, (sub, sub_groups), 0) - GROUP * lax.broadcasted_iota(
            jnp.int32, (sub, sub_groups), 1
        )
        for s in range(count // sub):
            here = slice(s * sub, (s + 1) * sub)
            to = slice(s * sub_groups, (s + 1) * sub_groups)
            chosen = (local == offset_ref[:, to]).astype(F32)
            hit = jnp.sum(chosen, axis=1, keepdims=True) > 0.5
            spread = dot(chosen.astype(BF), piece_ref[0, to, :], NN)
            out_ref[here, :] = jnp.where(hit, spread, base_ref[here, :].astype(F32)).astype(BF)

    grid_spec = pltpu.PrefetchScalarGridSpec(
        num_scalar_prefetch=1,
        grid=(len(which),),
        in_specs=[
            pl.BlockSpec((count, width), lambda i, m: (m[0] ^ (i + first), 0)),
            pl.BlockSpec((1, groups), lambda i, m: (0, m[0] ^ (i + first))),
            pl.BlockSpec((1, depth, width), lambda i, m: (m[0] ^ (i + first), 0, 0)),
        ]
        + [pl.BlockSpec(memory_space=pl.ANY)] * len(kept),
        out_specs=pl.BlockSpec((count, width), lambda i, m: (m[0] ^ (i + first), 0)),
    )
    return pl.pallas_call(
        kernel,
        grid_spec=grid_spec,
        out_shape=jax.ShapeDtypeStruct((rows, width), BF),
        input_output_aliases={4: 0} if kept else {},
        cost_estimate=small_cost(),
        name="merge_rows",
    )(mine, base, offsets, pieces, *kept)


def attend(picked, gain, weight, seq_row, ways):
    rows, width = picked.shape
    heads_width = weight.shape[2]
    heads = heads_width // HEAD_DIM
    block = min(256, rows)

    def body(load, store, outs, scalars, scratch):
        low_ref, qkv_ref, out_ref, *probs_refs = outs
        values = load(0)[...].astype(F32)
        low_ref[...] = (values * inverse_rms(values) * load(1)[...].astype(F32)).astype(BF)
        store(0)
        weight_ref = load(2)
        for n in range(3):
            qkv_ref[n] = dot(low_ref[...], weight_ref[n], NN).astype(BF)
        store(1)
        sequence = load(3)[...].astype(F32)
        column = jnp.broadcast_to(sequence, (128, rows)).T[:, :1]
        lane_head = lax.broadcasted_iota(jnp.int32, (1, heads_width), 1) // HEAD_DIM
        for n in reversed(range(rows // block)):
            start, stop = n * block, (n + 1) * block
            query = qkv_ref[0, start:stop, :] * BF(HEAD_DIM ** (-0.5))
            order = lax.broadcasted_iota(jnp.int32, (block, stop), 0) + start
            keys = lax.broadcasted_iota(jnp.int32, (block, stop), 1)
            allowed = (column[start:stop, :] == sequence[:, :stop]) & (order >= keys)
            total = jnp.zeros((block, heads_width), F32)
            for head in range(heads):
                here = lane_head == head
                key = jnp.where(here, qkv_ref[1, :stop, :], BF(0))
                logits = jnp.where(allowed, dot(query, key, NT), mask_fill)
                raised = jnp.exp(logits - jnp.max(logits, axis=-1, keepdims=True))
                probs = (raised * (1.0 / jnp.sum(raised, axis=-1, keepdims=True))).astype(BF)
                probs_refs[n][head] = probs
                value = jnp.where(here, qkv_ref[2, :stop, :], BF(0))
                total = total + dot(probs, value, NN)
            for k in range(ways):
                out_ref[k, start:stop, :] = total.astype(BF)
            store(3 + n)

    return staged(
        "attend",
        body,
        [],
        [picked, gain, weight, seq_row],
        [
            ((rows, width), BF),
            ((3, rows, heads_width), BF),
            ((ways, rows, heads_width), BF),
        ]
        + [((heads, block, (n + 1) * block), BF) for n in range(rows // block)],
        [],
        60,
        small_cost(),
    )


def feed_forward(heads, own_weight, quarters, picked, gain, up, grad_act, grad_mixer, part, mine, ways):
    rows, width = picked.shape
    hidden = up.shape[1]
    sub = min(1024, hidden)
    count, _, heads_width = heads.shape
    piece = heads_width // 4
    own = rows // ways
    slope = 0.7978845608028654
    cubic = 0.044715

    def body(load, store, outs, scalars, scratch):
        part_ref, mine_ref = scalars
        attended_ref, low_ref, act_ref, pre_ref, hidden_ref, part_out_ref, gain_part_ref, sent_ref = outs
        total, state, weights = scratch
        quarter = part_ref[0] & 3
        heads_ref = load(0)
        weights[0] = load(1)[...]
        for n in range(4):
            start = pl.multiple_of((quarter ^ n) * piece, piece)
            source = load(2 + n)
            for k in range(1, count):
                weights[k, pl.ds(start, piece), :] = source[k - 1]
        attended = dot(heads_ref[mine_ref[0]], weights[0], NN)
        for k in range(1, count):
            attended = attended + dot(heads_ref[mine_ref[0] ^ k], weights[k], NN)
        total[...] = attended
        attended_ref[...] = total[pl.ds(pl.multiple_of(mine_ref[0] * own, own), own), :]
        state_in = load(6)[...].astype(F32) + attended
        state[...] = state_in
        gain_row = load(7)[...].astype(F32)
        low_ref[...] = (state_in * inverse_rms(state_in) * gain_row).astype(BF)
        store(0, 1)
        up_ref, act_grad_ref = load(8), load(9)
        for s in range(hidden // sub):
            lanes = slice(s * sub, (s + 1) * sub)
            value = dot(low_ref[...], up_ref[:, lanes], NN)
            square = value * value
            bent = jnp.tanh(value * (slope + (slope * cubic) * square))
            half = 0.5 * (1.0 + bent)
            act_ref[:, lanes] = (value * half).astype(BF)
            rise = half + (0.5 * value) * (1.0 - bent * bent) * (slope + (3.0 * slope * cubic) * square)
            pre = (act_grad_ref[:, lanes] * rise).astype(BF)
            pre_ref[:, lanes] = pre
            term = dot(pre, up_ref[:, lanes], NT)
            if s == 0:
                total[...] = term
            else:
                total[...] += term
        store(2, 3)
        state_in = state[...]
        grad = total[...]
        inverse = inverse_rms(state_in)
        normal = state_in * inverse
        gain_part_ref[...] = jnp.sum(grad * normal, axis=0, keepdims=True)
        scaled = grad * gain_row
        along = jnp.mean(scaled * normal, axis=-1, keepdims=True)
        back = inverse * (scaled - normal * along)
        hidden_ref[...] = back.astype(BF)
        part_out_ref[...] = (back + load(10)[...].astype(F32) * (1.0 / count)).astype(BF)
        store(4, 5, 6)
        for k in range(count):
            sent_ref[mine_ref[0] ^ k] = dot(part_out_ref[...], weights[k], NT).astype(BF)

    return staged(
        "feed_forward",
        body,
        [part, mine],
        [heads, own_weight, *quarters, picked, gain, up, grad_act, grad_mixer],
        [
            ((own, width), F32),
            ((rows, width), BF),
            ((rows, hidden), BF),
            ((rows, hidden), BF),
            ((rows, width), BF),
            ((rows, width), BF),
            ((1, width), F32),
            (heads.shape, BF),
        ],
        [
            pltpu.VMEM((rows, width), F32),
            pltpu.VMEM((rows, width), F32),
            pltpu.VMEM((count, heads_width, width), BF),
        ],
        60,
        small_cost(),
    )


def act_grads(picked, router, grad_rows, down):
    rows, width = grad_rows.shape

    def kernel(picked_ref, router_ref, rows_ref, down_ref, gating_ref, square_ref, mixer_ref, grad_ref):
        score = jnp.sum(picked_ref[...].astype(F32) * router_ref[...].astype(F32), axis=-1, keepdims=True)
        gating = jax.nn.sigmoid(score)
        gating_ref[...] = gating
        square_ref[...] = jnp.broadcast_to(jnp.sum(score * score, axis=0, keepdims=True), square_ref.shape)
        mixer_ref[...] = (gating * rows_ref[...].astype(F32)).astype(BF)
        grad_ref[...] = dot(mixer_ref[...], down_ref[...], NT)

    whole = pl.BlockSpec(memory_space=pltpu.VMEM)
    return pl.pallas_call(
        kernel,
        in_specs=[whole] * 4,
        out_specs=[whole] * 4,
        out_shape=[
            jax.ShapeDtypeStruct((rows, 1), F32),
            jax.ShapeDtypeStruct((1, 128), F32),
            jax.ShapeDtypeStruct((rows, width), BF),
            jax.ShapeDtypeStruct((rows, down.shape[0]), F32),
        ],
        cost_estimate=small_cost(),
        name="act_grads",
    )(picked, router, grad_rows, down)


def attend_back(head_terms, qkv, probs, weight, picked, gain, hidden_part):
    rows, width = picked.shape
    heads_width = weight.shape[2]
    heads = heads_width // HEAD_DIM
    block = min(256, rows)
    scale = HEAD_DIM ** (-0.5)

    def kernel(
        head_ref,
        qkv_ref,
        weight_ref,
        picked_ref,
        gain_ref,
        hidden_ref,
        *rest,
    ):
        probs_refs, (grads_ref, gain_part_ref, result, grad_key, grad_value) = rest[: len(probs)], rest[len(probs) :]
        lane_head = lax.broadcasted_iota(jnp.int32, (1, heads_width), 1) // HEAD_DIM
        for start in reversed(range(0, rows, block)):
            stop = start + block
            here_rows = slice(start, stop)
            grad_head = head_ref[0, here_rows, :].astype(F32)
            for k in range(1, head_ref.shape[0]):
                grad_head = grad_head + head_ref[k, here_rows, :].astype(F32)
            grad_head = grad_head.astype(BF)
            query = qkv_ref[0, here_rows, :] * BF(scale)
            grad_query = jnp.zeros((block, heads_width), F32)
            add_key = jnp.zeros((stop, heads_width), F32)
            add_value = jnp.zeros((stop, heads_width), F32)
            for head in range(heads):
                here = lane_head == head
                value = jnp.where(here, qkv_ref[2, :stop, :], BF(0))
                key = jnp.where(here, qkv_ref[1, :stop, :], BF(0))
                low = probs_refs[start // block][head]
                weighted = low.astype(F32) * dot(grad_head, value, NT)
                row_sum = jnp.sum(weighted, axis=-1, keepdims=True)
                slopes = (weighted - low.astype(F32) * row_sum).astype(BF)
                grad_query = grad_query + dot(slopes, key, NN)
                add_key = add_key + dot(slopes, jnp.where(here, query, BF(0)), TN)
                add_value = add_value + dot(low, jnp.where(here, grad_head, BF(0)), TN)
            grads_ref[0, here_rows, :] = (grad_query * scale).astype(BF)
            if stop == rows:
                grad_key[...] = add_key
                grad_value[...] = add_value
            else:
                grad_key[:stop, :] += add_key
                grad_value[:stop, :] += add_value
        grads_ref[1] = grad_key[...].astype(BF)
        grads_ref[2] = grad_value[...].astype(BF)
        first = dot(grads_ref[0], weight_ref[0], NT)
        for n in range(1, 3):
            first = first + dot(grads_ref[n], weight_ref[n], NT)
        values = picked_ref[...].astype(F32)
        inverse = inverse_rms(values)
        normal = values * inverse
        gain_part_ref[...] = jnp.sum(first * normal, axis=0, keepdims=True)
        scaled = first * gain_ref[...].astype(F32)
        along = jnp.mean(scaled * normal, axis=-1, keepdims=True)
        result[...] = (hidden_ref[...].astype(F32) + inverse * (scaled - normal * along)).astype(BF)

    whole = pl.BlockSpec(memory_space=pltpu.VMEM)
    return pl.pallas_call(
        kernel,
        in_specs=[whole] * (6 + len(probs)),
        out_specs=[whole] * 3,
        out_shape=[
            jax.ShapeDtypeStruct((3, rows, heads_width), BF),
            jax.ShapeDtypeStruct((1, width), F32),
            jax.ShapeDtypeStruct((rows, width), BF),
        ],
        scratch_shapes=[
            pltpu.VMEM((rows, heads_width), F32),
            pltpu.VMEM((rows, heads_width), F32),
        ],
        cost_estimate=small_cost(),
        compiler_params=pltpu.CompilerParams(vmem_limit_bytes=20 << 20),
        name="attend_back",
    )(head_terms, qkv, weight, picked, gain, hidden_part, *probs)


def spread_rows(down, up, order_down, order_up, part):
    count = len(down)
    wide, width = down[0].shape
    rows = wide // (2 ** len(order_down) // count)
    each = wide // rows

    def kernel(part_ref, *refs):
        down_out, up_out = refs[2 * count :]
        for n in range(count):

            @pl.when(pl.program_id(0) // each == n)
            def _():
                down_out[...] = refs[n][...].astype(F32)
                up_out[...] = refs[count + n][...].astype(F32)

    def source(n):
        return pl.BlockSpec((rows, width), lambda i, p: (jnp.clip(i - n * each, 0, each - 1), 0))

    def target(order):
        def place(i, p):
            key = sum((i >> n & 1) * bit for n, bit in enumerate(order))
            return p[0] ^ key, 0

        return pl.BlockSpec((rows, width), place)

    return pl.pallas_call(
        kernel,
        grid_spec=pltpu.PrefetchScalarGridSpec(
            num_scalar_prefetch=1,
            grid=(count * each,),
            in_specs=[source(n) for n in range(count)] * 2,
            out_specs=[target(order_down), target(order_up)],
        ),
        out_shape=[jax.ShapeDtypeStruct((count * wide, width), F32)] * 2,
        cost_estimate=small_cost(),
        name="spread_rows",
    )(part, *down, *up)


def qkv_part_of(first_low, grads, part):
    rows, width = first_low.shape
    part_width = grads.shape[2]
    half = 3 * part_width // 2

    def kernel(part_ref, low_ref, grads_ref, keep_ref, send_ref, full):
        for n in range(3):
            product = dot(grads_ref[n], low_ref[...], TN)
            full[n * part_width : (n + 1) * part_width, :] = product.astype(BF)
        core = part_ref[0] & 1
        for target, which in ((keep_ref, core), (send_ref, 1 - core)):
            target[...] = full[pl.ds(pl.multiple_of(which * half, half), half), :]

    whole = pl.BlockSpec(memory_space=pltpu.VMEM)
    return pl.pallas_call(
        kernel,
        in_specs=[pl.BlockSpec(memory_space=pltpu.SMEM)] + [whole] * 2,
        out_specs=[whole] * 2,
        out_shape=[jax.ShapeDtypeStruct((half, width), BF)] * 2,
        scratch_shapes=[pltpu.VMEM((2 * half, width), BF)],
        cost_estimate=small_cost(),
        compiler_params=pltpu.CompilerParams(vmem_limit_bytes=14 << 20),
        name="qkv_part",
    )(part, first_low, grads)


def spread_qkv(near, far, part, part_width):
    rows, width = near.shape
    tile = 128
    count = rows // tile
    many = part_width // tile

    def kernel(part_ref, near_ref, far_ref, out_ref):
        core = part_ref[0] & 1
        for ref, which in ((near_ref, core), (far_ref, 1 - core)):
            for n in range(count):
                spot = which * count + n
                column = pl.multiple_of(spot % many * tile, tile)
                piece = ref[n * tile : (n + 1) * tile, :].astype(F32)
                out_ref[spot // many, :, pl.ds(column, tile)] = piece.T

    whole = pl.BlockSpec(memory_space=pltpu.VMEM)
    return pl.pallas_call(
        kernel,
        in_specs=[pl.BlockSpec(memory_space=pltpu.SMEM)] + [whole] * 2,
        out_specs=whole,
        out_shape=jax.ShapeDtypeStruct((2 * rows // part_width, width, part_width), F32),
        cost_estimate=small_cost(),
        compiler_params=pltpu.CompilerParams(vmem_limit_bytes=14 << 20),
        name="spread_qkv",
    )(part, near, far)


def core_grads(activated, grad_mixer, second_low, grad_pre, heads, attended_part, part, keys_a, keys_b):
    rows, hidden = activated.shape
    width = grad_mixer.shape[1]
    copies = len(keys_a)
    half = copies // 2
    count, _, heads_width = heads.shape
    block = hidden // copies
    small = heads_width // copies
    many = count // 2
    depth = half * (block + many * small)

    def kernel(part_ref, act_ref, mixer_ref, low_ref, pre_ref, heads_ref, term_ref, keep_ref, *rest):
        wide_refs, narrow_refs, (full, narrow) = rest[0:2], rest[2:4], rest[4:]

        def place(source, each, lane, keys, first, stride):
            for n, key in enumerate(keys):
                start = pl.multiple_of((part_ref[0] ^ key) * each, each)
                at = first + (n % half) * stride
                piece = source[pl.ds(start, each), :]
                if n < half:
                    keep_ref[lane, at : at + each, :] = piece
                elif first == 0:
                    wide_refs[lane][at : at + each, :] = piece
                else:
                    narrow_refs[lane][at - half * block : at - half * block + each, :] = piece

        full[...] = dot(act_ref[...], mixer_ref[...], TN).astype(BF)
        place(full, block, 0, keys_a, 0, block)
        full[...] = dot(low_ref[...], pre_ref[...], TN).astype(BF)
        place(full, block, 1, keys_b, 0, block)
        for k in range(count):
            narrow[...] = dot(heads_ref[k], term_ref[...], TN).astype(BF)
            lane, spot = divmod(k, many)
            place(narrow, small, lane, keys_b if lane else keys_a, half * block + spot * small, many * small)

    whole = pl.BlockSpec(memory_space=pltpu.VMEM)
    wide_shape = jax.ShapeDtypeStruct((half * block, width), BF)
    narrow_shape = jax.ShapeDtypeStruct((half * many * small, width), BF)
    return pl.pallas_call(
        kernel,
        in_specs=[pl.BlockSpec(memory_space=pltpu.SMEM)] + [whole] * 6,
        out_specs=[whole] * 5,
        out_shape=[jax.ShapeDtypeStruct((2, depth, width), BF)] + [wide_shape] * 2 + [narrow_shape] * 2,
        scratch_shapes=[pltpu.VMEM((hidden, width), BF), pltpu.VMEM((heads_width, width), BF)],
        cost_estimate=small_cost(),
        compiler_params=pltpu.CompilerParams(vmem_limit_bytes=14 << 20),
        name="core_grads",
    )(part, activated, grad_mixer, second_low, grad_pre, heads, attended_part)


def plus(left, right):
    return (left.astype(F32) + right.astype(F32)).astype(BF)


def halving_sums(keep, got_a, got_b, wide, narrow):
    width = keep.shape[2]
    count = len(got_a)

    def kernel(keep_ref, *refs):
        a_got, b_got, (stay_ref, a_out, b_out) = refs[:count], refs[count : 2 * count], refs[2 * count :]
        for lane, got, out in ((0, a_got, a_out), (1, b_got, b_out)):
            for first, size, at in ((0, wide // 2, 0), (wide, narrow // 2, wide // 2)):
                source, shift = (got[1], wide) if count == 2 and first else (got[0], 0)
                to = slice(at, at + size)
                for start, target in ((first, stay_ref.at[lane]), (first + size, out)):
                    here = slice(start - shift, start - shift + size)
                    target[to, :] = plus(keep_ref[lane, start : start + size, :], source[here, :])

    whole = pl.BlockSpec(memory_space=pltpu.VMEM)
    depth = (wide + narrow) // 2
    lane_shape = jax.ShapeDtypeStruct((depth, width), BF)
    return pl.pallas_call(
        kernel,
        in_specs=[whole] * (1 + 2 * count),
        out_specs=[whole] * 3,
        out_shape=[jax.ShapeDtypeStruct((2, depth, width), BF), lane_shape, lane_shape],
        cost_estimate=small_cost(),
        compiler_params=pltpu.CompilerParams(vmem_limit_bytes=14 << 20),
        name="halving_sums",
    )(keep, *got_a, *got_b)


def owned_sums(keep, got_a, got_b, fresh, small, wide, ways):
    width = keep.shape[2]
    narrow = keep.shape[1] - wide
    own = fresh.shape[0]
    many = ways // 2
    each = narrow // many
    depth = own + GAP + each

    def kernel(keep_ref, a_got, b_got, fresh_ref, small_ref, a_out, b_out, sent_ref):
        sums = split_sums(small_ref[...])
        for lane, got, out in ((0, a_got, a_out), (1, b_got, b_out)):
            out[...] = plus(keep_ref[lane, :wide, :], got[:wide, :])
            done = plus(keep_ref[lane, wide:, :], got[wide:, :])
            for spot in range(many):
                k = lane * many + spot
                sent_ref[k, :own, :] = fresh_ref[...]
                sent_ref[k, own : own + GAP, :] = sums
                sent_ref[k, own + GAP :, :] = done[spot * each : (spot + 1) * each, :]

    whole = pl.BlockSpec(memory_space=pltpu.VMEM)
    lane_shape = jax.ShapeDtypeStruct((wide, width), BF)
    return pl.pallas_call(
        kernel,
        in_specs=[whole] * 5,
        out_specs=[whole] * 3,
        out_shape=[lane_shape, lane_shape, jax.ShapeDtypeStruct((ways, depth, width), BF)],
        cost_estimate=small_cost(),
        compiler_params=pltpu.CompilerParams(vmem_limit_bytes=10 << 20),
        name="owned_sums",
    )(keep, got_a, got_b, fresh, small)


def core_sums(rows, other):
    depth, width = rows.shape
    third = depth // 2

    def kernel(rows_ref, other_ref, a_out, b_out):
        a_out[...] = plus(rows_ref[:third, :], other_ref[:third, :])
        b_out[...] = plus(rows_ref[third:, :], other_ref[third:, :])

    whole = pl.BlockSpec(memory_space=pltpu.VMEM)
    return pl.pallas_call(
        kernel,
        in_specs=[whole] * 2,
        out_specs=[whole] * 2,
        out_shape=[jax.ShapeDtypeStruct((third, width), BF)] * 2,
        cost_estimate=small_cost(),
        compiler_params=pltpu.CompilerParams(vmem_limit_bytes=10 << 20),
        name="core_sums",
    )(rows, other)


def lane_sums(lane_a, got_a, lane_b, got_b):
    def kernel(a_ref, a_got, b_ref, b_got, a_out, b_out):
        a_out[...] = plus(a_ref[...], a_got[...])
        b_out[...] = plus(b_ref[...], b_got[...])

    whole = pl.BlockSpec(memory_space=pltpu.VMEM)
    return pl.pallas_call(
        kernel,
        in_specs=[whole] * 4,
        out_specs=[whole] * 2,
        out_shape=[jax.ShapeDtypeStruct(lane_a.shape, BF)] * 2,
        cost_estimate=small_cost(),
        compiler_params=pltpu.CompilerParams(vmem_limit_bytes=12 << 20),
        name="lane_sums",
    )(lane_a, got_a, lane_b, got_b)


def joined_lanes(lane_a, got_a, lane_b, got_b):
    rows, width = lane_a.shape

    def kernel(a_ref, a_got, b_ref, b_got, out_ref):
        out_ref[:rows, :] = plus(a_ref[...], a_got[...])
        out_ref[rows:, :] = plus(b_ref[...], b_got[...])

    whole = pl.BlockSpec(memory_space=pltpu.VMEM)
    return pl.pallas_call(
        kernel,
        in_specs=[whole] * 4,
        out_specs=whole,
        out_shape=jax.ShapeDtypeStruct((2 * rows, width), BF),
        cost_estimate=small_cost(),
        compiler_params=pltpu.CompilerParams(vmem_limit_bytes=10 << 20),
        name="joined_lanes",
    )(lane_a, got_a, lane_b, got_b)


def gather_blocks(blocks_a, blocks_b):
    wide, width = blocks_a[0].shape
    count = len(blocks_a)

    def kernel(*refs):
        for lane in range(2):
            for n in range(count):
                refs[2 * count + lane][n * wide : (n + 1) * wide, :] = refs[lane * count + n][...]

    whole = pl.BlockSpec(memory_space=pltpu.VMEM)
    return pl.pallas_call(
        kernel,
        in_specs=[whole] * (2 * count),
        out_specs=[whole] * 2,
        out_shape=[jax.ShapeDtypeStruct((count * wide, width), BF)] * 2,
        cost_estimate=small_cost(),
        compiler_params=pltpu.CompilerParams(vmem_limit_bytes=10 << 20),
        name="gather_blocks",
    )(*blocks_a, *blocks_b)


def split_sums(values):
    high = values.astype(BF)
    low = (values - high.astype(F32)).astype(BF)
    return jnp.concatenate([high, low], axis=0)


def joined_sums(rows):
    return rows[:TERMS].astype(F32) + rows[TERMS : 2 * TERMS].astype(F32)


def first_small(received, own):
    ways, depth, width = received.shape
    each = depth - own - GAP

    def kernel(got_ref, out_ref):
        total = got_ref[0, own + GAP :, :].astype(F32)
        sums = joined_sums(got_ref[0, own : own + GAP, :])
        for k in range(1, ways):
            total = total + got_ref[k, own + GAP :, :].astype(F32)
            sums = sums + joined_sums(got_ref[k, own : own + GAP, :])
        out_ref[:each, :] = total.astype(BF)
        out_ref[each:, :] = split_sums(sums)

    whole = pl.BlockSpec(memory_space=pltpu.VMEM)
    return pl.pallas_call(
        kernel,
        in_specs=[whole],
        out_specs=whole,
        out_shape=jax.ShapeDtypeStruct((each + GAP, width), BF),
        cost_estimate=small_cost(),
        compiler_params=pltpu.CompilerParams(vmem_limit_bytes=8 << 20),
        name="first_small",
    )(received)


def last_small(blocks, keys, part, shares):
    depth, width = blocks[0].shape
    each = depth - GAP
    count = len(blocks)

    def kernel(part_ref, *refs):
        out_ref, small_refs = refs[count], refs[count + 1 :]
        total = joined_sums(refs[0][each:, :])
        for n in range(1, count):
            total = total + joined_sums(refs[n][each:, :])
        for n in range(TERMS - 1):
            small_refs[n][...] = total[n : n + 1, :]
        lane = lax.broadcasted_iota(jnp.int32, (1, 128), 1)
        small_refs[TERMS - 1][...] = total[TERMS - 1 :, :128] * jnp.where(lane == 0, shares[0], shares[1])
        for n in range(count):
            start = pl.multiple_of((part_ref[0] ^ keys[n]) * each, each)
            out_ref[pl.ds(start, each), :] = refs[n][:each, :].astype(F32)

    whole = pl.BlockSpec(memory_space=pltpu.VMEM)
    return pl.pallas_call(
        kernel,
        in_specs=[pl.BlockSpec(memory_space=pltpu.SMEM)] + [whole] * count,
        out_specs=[whole] * (1 + TERMS),
        out_shape=[jax.ShapeDtypeStruct((count * each, width), F32)] + [jax.ShapeDtypeStruct((1, width), F32)] * (TERMS - 1)
        + [jax.ShapeDtypeStruct((1, 128), F32)],
        cost_estimate=small_cost(),
        compiler_params=pltpu.CompilerParams(vmem_limit_bytes=10 << 20),
        name="last_small",
    )(part, *blocks)


def finish_rows(mixer_terms, picked, gating, attended, grad_rows, gain_one, gain_two, square, routed_square, mine, ways):
    rows, width = picked.shape
    own = rows // ways

    def kernel(
        mine_ref,
        terms_ref,
        picked_ref,
        gating_ref,
        attended_ref,
        rows_ref,
        one_ref,
        two_ref,
        square_ref,
        routed_ref,
        new_ref,
        score_ref,
        small_ref,
    ):
        branch = attended_ref[...]
        for k in range(ways):
            branch = branch + terms_ref[k].astype(F32)
        values = picked_ref[...].astype(F32)
        gate = gating_ref[...]
        new_ref[...] = (values + gate * branch).astype(BF)
        along = jnp.sum(rows_ref[...].astype(F32) * branch, axis=-1, keepdims=True)
        score = along * gate * (1.0 - gate)
        score_ref[...] = score
        small_ref[0:1, :] = jnp.sum(score * values, axis=0, keepdims=True)
        small_ref[1:2, :] = one_ref[...]
        small_ref[2:3, :] = two_ref[...]
        lane = lax.broadcasted_iota(jnp.int32, (1, width), 1)
        both = jnp.where(lane == 0, square_ref[:, 0:1], routed_ref[:, 0:1] * (1.0 / ways))
        small_ref[3:4, :] = jnp.where(lane < 2, both, 0.0)

    def block(shape):
        return pl.BlockSpec(shape, lambda i, m: (m[0], 0))

    def fixed(shape):
        return pl.BlockSpec(shape, lambda i, m: (0, 0))

    return pl.pallas_call(
        kernel,
        grid_spec=pltpu.PrefetchScalarGridSpec(
            num_scalar_prefetch=1,
            grid=(1,),
            in_specs=[pl.BlockSpec(mixer_terms.shape, lambda i, m: (0, 0, 0))]
            + [block((own, width)), block((own, 1)), fixed((own, width)), block((own, width))]
            + [fixed((1, width))] * 2
            + [fixed((1, 128))] * 2,
            out_specs=[fixed((own, width)), fixed((own, 1)), fixed((4, width))],
        ),
        out_shape=[
            jax.ShapeDtypeStruct((own, width), BF),
            jax.ShapeDtypeStruct((own, 1), F32),
            jax.ShapeDtypeStruct((4, width), F32),
        ],
        cost_estimate=cost_of(10),
        name="finish_rows",
    )(mine, mixer_terms, picked, gating, attended, grad_rows, gain_one, gain_two, square, routed_square)


def finish_input(terms, grad_rows, score, router, mine, ways):
    rows, width = grad_rows.shape
    own = rows // ways

    def kernel(mine_ref, terms_ref, rows_ref, score_ref, router_ref, out_ref):
        total = rows_ref[...].astype(F32) + score_ref[...] * router_ref[...].astype(F32)
        for k in range(ways):
            total = total + terms_ref[k].astype(F32)
        for k in range(ways):
            out_ref[k] = total.astype(BF)

    def fixed(shape):
        return pl.BlockSpec(shape, lambda i, m: (0,) * len(shape))

    return pl.pallas_call(
        kernel,
        grid_spec=pltpu.PrefetchScalarGridSpec(
            num_scalar_prefetch=1,
            grid=(1,),
            in_specs=[
                fixed((ways, own, width)),
                pl.BlockSpec((own, width), lambda i, m: (m[0], 0)),
                fixed((own, 1)),
                fixed((1, width)),
            ],
            out_specs=fixed((ways, own, width)),
        ),
        out_shape=jax.ShapeDtypeStruct((ways, own, width), BF),
        cost_estimate=small_cost(),
        compiler_params=pltpu.CompilerParams(vmem_limit_bytes=8 << 20),
        name="finish_input",
    )(mine, terms, grad_rows, score, router)


def split_kept(count, order):
    keys = [0]
    for bit in reversed(order):
        keys = keys + [k ^ bit for k in keys]
    return keys


def per_device(
    tokens,
    route_offset,
    unit_sequence,
    cotangent,
    router_weight,
    first_gain,
    second_gain,
    qkv_weight,
    out_weight,
    up_weight,
    down_weight,
):
    rows_local, width = tokens.shape
    routed = route_offset.shape[1]
    ways = lax.axis_size("tensor")
    copies = lax.axis_size("dp")
    mine = lax.axis_index("tensor")
    part = lax.axis_index("dp")
    mine_array = jnp.reshape(mine, (1,)).astype(jnp.int32)
    part_array = jnp.reshape(part, (1,)).astype(jnp.int32)
    ladder = [1 << b for b in range(1, copies.bit_length() - 1)]
    order_a = [1] + ladder
    order_b = [1] + ladder[::-1]
    keys_a = split_kept(copies, order_a)
    keys_b = split_kept(copies, order_b)

    tie = lax.optimization_barrier
    own_rows = routed // ways
    heads_width = out_weight.shape[0]
    hidden = up_weight.shape[1]
    by_swaps = copies == 8
    bit_x, bit_y = 2, 4
    shares = (1.0 / (rows_local * copies), 1.0 / (routed * copies))

    quarter = part & 3
    piece_rows = heads_width // 4
    piece = lax.dynamic_slice_in_dim(out_weight, quarter * piece_rows, piece_rows, 0)
    here = [swap(piece, "tensor", k) for k in range(1, ways)]

    picked = pick_rows(tokens, route_offset, ways)
    first_low, qkv, head_out, *probs = attend(picked, first_gain[None], qkv_weight, unit_sequence, ways)
    here, head_out = tie((here, head_out))

    heads = to_all(head_out)
    here = jnp.stack(here)
    beside, across = swap(here, "dp", bit_x), swap(here, "dp", 1)
    cotangent, router_weight, second_gain, here, head_out = tie(
        (cotangent, router_weight, second_gain, here, head_out)
    )
    weight_row = router_weight[None]
    grad_rows = pick_only(cotangent, route_offset, ways)
    beside, across, here, grad_rows = tie((beside, across, here, grad_rows))
    quarters = [here, across, beside, swap(beside, "dp", 1)]
    gating, routed_square, grad_mixer, grad_act = act_grads(picked, weight_row, grad_rows, down_weight)
    square = score_sums(tokens, weight_row, mine_array, ways)
    heads, quarters, grad_act, grad_mixer, square = tie((heads, quarters, grad_act, grad_mixer, square))
    attended, second_low, activated, grad_pre, hidden_part, attended_part, second_gain_part, head_sent = feed_forward(
        heads,
        out_weight,
        quarters,
        picked,
        second_gain[None],
        up_weight,
        grad_act,
        grad_mixer,
        part_array,
        mine_array,
        ways,
    )

    head_terms = to_all(head_sent)
    wide = hidden // 2
    narrow = heads_width * ways // 4
    if by_swaps:
        kept, *leaving = core_grads(
            activated, grad_mixer, second_low, grad_pre, heads, attended_part, part_array, keys_a, keys_b
        )
        wide_a, wide_b, narrow_a, narrow_b = (swap(array, "dp", 1) for array in leaving)
        activated, kept = tie((activated, kept))
    else:
        down_part = dot(activated, grad_mixer, TN).astype(BF)
        up_part = dot(second_low, grad_pre, TN).astype(BF)
        out_parts = jnp.stack([dot(heads[k], attended_part, TN).astype(BF) for k in range(ways)])
    mixer_part = dot(activated, down_weight, NN).astype(BF).reshape(ways, own_rows, width)
    if by_swaps:
        wide_a, wide_b, narrow_a, narrow_b, mixer_part = tie((wide_a, wide_b, narrow_a, narrow_b, mixer_part))
        kept, leave_a, leave_b = halving_sums(kept, (wide_a, narrow_a), (wide_b, narrow_b), wide, narrow)
        got_a, got_b = swap(leave_a, "dp", bit_x), swap(leave_b, "dp", bit_y)
        head_terms, mixer_part, kept = tie((head_terms, mixer_part, kept))
    else:
        head_terms, mixer_part = tie((head_terms, mixer_part))

    mixer_terms = to_all(mixer_part)
    grad_projected, first_gain_part, input_part = attend_back(
        head_terms, qkv, probs, qkv_weight, picked, first_gain[None], hidden_part
    )
    qkv_part, qkv_leaving = qkv_part_of(first_low, grad_projected, part_array)
    input_part = input_part.reshape(ways, own_rows, width)
    if by_swaps:
        got_a, got_b, qkv_part, qkv_leaving, input_part = tie((got_a, got_b, qkv_part, qkv_leaving, input_part))
        kept, leave_a, leave_b = halving_sums(kept, (got_a,), (got_b,), wide // 2, narrow // 2)
        mixer_terms, input_part, qkv_part, kept, leave_a, leave_b = tie(
            (mixer_terms, input_part, qkv_part, kept, leave_a, leave_b)
        )
    else:
        mixer_terms, input_part, qkv_part = tie((mixer_terms, input_part, qkv_part))

    input_terms = to_all(input_part)
    if by_swaps:
        got_a, got_b = swap(leave_a, "dp", bit_y), swap(leave_b, "dp", bit_x)
        qkv_got = swap(qkv_leaving, "dp", 1)
    new_own, grad_score, small = finish_rows(
        mixer_terms,
        picked,
        gating,
        attended,
        grad_rows,
        first_gain_part,
        second_gain_part,
        square,
        routed_square,
        mine_array,
        ways,
    )
    if by_swaps:
        got_a, got_b, new_own = tie((got_a, got_b, new_own))
        lane_a, lane_b, sent = owned_sums(kept, got_a, got_b, new_own, small, wide // 4, ways)
        got_a, got_b = swap(lane_a, "dp", bit_y), swap(lane_b, "dp", bit_x)
        qkv_part, qkv_got, lane_a, lane_b, sent = tie((qkv_part, qkv_got, lane_a, lane_b, sent))
        qkv_a, qkv_b = core_sums(qkv_part, qkv_got)
        input_terms, sent, got_a, got_b, qkv_a, qkv_b = tie((input_terms, sent, got_a, got_b, qkv_a, qkv_b))
    else:
        sent = jnp.concatenate([new_own, split_sums(small)])
        sent = jnp.broadcast_to(sent[None], (ways,) + sent.shape)
        input_terms, sent = tie((input_terms, sent))

    fresh = to_all(sent)
    if by_swaps:
        more_a = [swap(array, "dp", bit_x) for array in (lane_a, got_a)]
        more_b = [swap(array, "dp", bit_y) for array in (lane_b, got_b)]
    last = finish_input(input_terms, grad_rows, grad_score, weight_row, mine_array, ways)
    cotangent, last = tie((cotangent, last))
    early = merge_rows(cotangent, route_offset, last, mine_array, range(1))
    if by_swaps:
        more_a, more_b, early, qkv_a, qkv_b = tie((more_a, more_b, early, qkv_a, qkv_b))
        qkv_a_got, qkv_b_got = swap(qkv_a, "dp", bit_y), swap(qkv_b, "dp", bit_x)
        down_one, up_one = gather_blocks([lane_a, got_a], [lane_b, got_b])
        down_two, up_two = gather_blocks(more_a, more_b)
        down_near, up_near = [down_one, down_two], [up_one, up_two]
        down_far = [swap(array, "dp", 1) for array in down_near]
        up_far = [swap(array, "dp", 1) for array in up_near]

        def gathered(order):
            keys = [0]
            for bit in order:
                keys = keys + [k ^ bit for k in keys]
            return keys

        down_grad, up_grad = spread_rows(
            down_near + down_far, up_near + up_far, [bit_y, bit_x, 1], [bit_x, bit_y, 1], part_array
        )
        fresh, last, down_grad, up_grad = tie((fresh, last, down_grad, up_grad))
    else:
        fresh, last = tie((fresh, last))

    input_rows = to_all(last)
    if by_swaps:
        blocks = [first_small(fresh, own_rows)]
        more = [swap(array, "dp", bit_x) for array in blocks]
        qkv_a_got, qkv_b_got, blocks = tie((qkv_a_got, qkv_b_got, blocks))
        qkv_a, qkv_b = lane_sums(qkv_a, qkv_a_got, qkv_b, qkv_b_got)
        qkv_a_got, qkv_b_got = swap(qkv_a, "dp", bit_x), swap(qkv_b, "dp", bit_y)
        fresh, blocks, qkv_a, qkv_b = tie((fresh, blocks, qkv_a, qkv_b))
    output = merge_rows(tokens, route_offset, fresh, mine_array, range(ways // 2))
    if by_swaps:
        more, qkv_a_got, qkv_b_got, output = tie((more, qkv_a_got, qkv_b_got, output))
        qkv_near = joined_lanes(qkv_a, qkv_a_got, qkv_b, qkv_b_got)
        qkv_far = swap(qkv_near, "dp", 1)
        blocks = blocks + more
        more = [swap(array, "dp", bit_y) for array in blocks]
        fresh, blocks, qkv_near = tie((fresh, blocks, qkv_near))
    output = merge_rows(tokens, route_offset, fresh, mine_array, range(ways // 2, ways), output)
    if by_swaps:
        more, qkv_far, output = tie((more, qkv_far, output))
        blocks = blocks + more
        more = [swap(array, "dp", 1) for array in blocks]
        qkv_near, blocks = tie((qkv_near, blocks))
        qkv_grad = spread_qkv(qkv_near, qkv_far, part_array, qkv_weight.shape[2])
        more, qkv_grad = tie((more, qkv_grad))
        out_grad, *small = last_small(blocks + more, gathered([bit_x, bit_y, 1]), part_array, shares)
        small[3] = small[3][:, :2]
        input_rows, early, output, out_grad, small, qkv_grad = tie(
            (input_rows, early, output, out_grad, small, qkv_grad)
        )
    input_grad = merge_rows(cotangent, route_offset, input_rows, mine_array, range(1, ways), early)
    if not by_swaps:
        swapped = jnp.concatenate([qkv_leaving, qkv_part])
        qkv_whole = jnp.where(part & 1 == 0, jnp.concatenate([qkv_part, qkv_leaving]), swapped)
        small = sum(joined_sums(fresh[k, own_rows:]) for k in range(ways))
        small = lax.psum(small, "dp")
        small = [small[n : n + 1] for n in range(TERMS)]
        small[3] = small[3][:, :2] * jnp.array((shares,), F32)
        down_grad, up_grad, qkv_sum, out_sum = (
            lax.psum(v, "dp").astype(F32) for v in (down_part, up_part, qkv_whole, out_parts)
        )
        out_grad = jnp.sum(to_all(out_sum.astype(BF)).astype(F32), axis=0)
        qkv_grad = qkv_sum.reshape(3, -1, width).transpose(0, 2, 1)
    router_grad, first_gain_grad, second_gain_grad = (small[n].reshape(width) for n in range(3))
    score_stats = small[3].reshape(2)
    return (
        output,
        input_grad,
        router_grad,
        first_gain_grad,
        second_gain_grad,
        qkv_grad,
        out_grad,
        up_grad,
        down_grad,
        score_stats,
    )


def solution(mesh):
    placed = (
        P("dp", None),
        P("dp", None),
        P("dp", None),
        P("dp", None),
        P(),
        P(),
        P(),
        P(None, None, "tensor"),
        P("tensor", None),
        P(None, "tensor"),
        P("tensor", None),
    )
    return jax.shard_map(
        per_device,
        mesh=mesh,
        in_specs=placed,
        out_specs=(
            P("dp", None),
            P("dp", None),
            P(),
            P(),
            P(),
            P(None, None, "tensor"),
            P("tensor", None),
            P(None, "tensor"),
            P("tensor", None),
            P(),
        ),
        check_vma=False,
    )
```

```python
import jax
import jax.numpy as jnp
from jax import lax
from jax.experimental import pallas as pl
from jax.experimental.pallas import tpu as pltpu
from jax.sharding import PartitionSpec as P

BF = jnp.bfloat16
F32 = jnp.float32

NN = ((1,), (0,))
NT = ((1,), (1,))
TN = ((0,), (0,))


def dot(left, right, dims):
    return lax.dot_general(left, right, (dims, ((), ())), preferred_element_type=F32)


def swap(values, axis, bits):
    size = lax.axis_size(axis)
    return lax.ppermute(values, axis, [(i, i ^ bits) for i in range(size)])


def to_all(blocks):
    return lax.all_to_all(blocks, "tensor", 0, 0, tiled=True)


def inverse_rms(rows):
    return lax.rsqrt(jnp.mean(rows * rows, axis=-1, keepdims=True) + eps)


HEAD_DIM = 64
GROUP = 8
TERMS = 4
GAP = 2 * TERMS
eps = 1e-06
mask_fill = -1000000000.0


def small_cost():
    return pl.CostEstimate(flops=1024, bytes_accessed=1024, transcendentals=0)


def cost_of(microseconds):
    return pl.CostEstimate(flops=1024, bytes_accessed=int(microseconds * 3.0e6), transcendentals=0)


def staged(name, body, scalars, arrays, out_shapes, scratch, limit, cost):
    count, outs, extra = len(arrays), len(out_shapes), len(scalars)

    def kernel(*refs):
        scalar_refs, refs = refs[:extra], refs[extra:]
        in_refs, refs = refs[:count], refs[count:]
        out_refs, refs = refs[:outs], refs[outs:]
        held, refs = refs[:count], refs[count:]
        made, refs = refs[:outs], refs[outs:]
        load_sems, store_sems = refs[:2]
        loads = [pltpu.make_async_copy(s, h, load_sems.at[n]) for n, (s, h) in enumerate(zip(in_refs, held))]
        stores = [pltpu.make_async_copy(m, o, store_sems.at[n]) for n, (m, o) in enumerate(zip(made, out_refs))]
        for copy in loads:
            copy.start()
        here, gone = set(), set()

        def load(n):
            if n not in here:
                here.add(n)
                loads[n].wait()
            return held[n]

        def store(*which):
            for n in which:
                gone.add(n)
                stores[n].start()

        body(load, store, made, scalar_refs, refs[2:])
        for n in range(count):
            load(n)
        for n in range(outs):
            if n not in gone:
                store(n)
        for copy in stores:
            copy.wait()

    anywhere = pl.BlockSpec(memory_space=pl.ANY)
    return pl.pallas_call(
        kernel,
        in_specs=[pl.BlockSpec(memory_space=pltpu.SMEM)] * extra + [anywhere] * count,
        out_specs=[anywhere] * outs,
        out_shape=[jax.ShapeDtypeStruct(shape, kind) for shape, kind in out_shapes],
        scratch_shapes=[pltpu.VMEM(a.shape, a.dtype) for a in arrays]
        + [pltpu.VMEM(shape, kind) for shape, kind in out_shapes]
        + [pltpu.SemaphoreType.DMA((count,)), pltpu.SemaphoreType.DMA((outs,))]
        + scratch,
        cost_estimate=cost,
        compiler_params=pltpu.CompilerParams(vmem_limit_bytes=limit << 20),
        name=name,
    )(*scalars, *arrays)


def pick_rows(base, offsets, ways):
    rows, width = base.shape
    chunks = ways
    block = rows // chunks
    groups = block // GROUP
    sub = 256
    sub_groups = sub // GROUP

    def kernel(base_ref, offset_ref, picked_ref, held, sems):
        def load(n):
            part = pl.ds(pl.multiple_of(n * block, block), block)
            return pltpu.make_async_copy(base_ref.at[part], held.at[part], sems.at[n])

        for n in range(chunks):
            load(n).start()
        local = lax.broadcasted_iota(jnp.int32, (sub, sub_groups), 0) - GROUP * lax.broadcasted_iota(
            jnp.int32, (sub, sub_groups), 1
        )

        def step(n, carry):
            load(n).wait()
            offsets = offset_ref[:, pl.ds(pl.multiple_of(n * groups, groups), groups)]
            for s in range(block // sub):
                chosen = (local == offsets[:, s * sub_groups : (s + 1) * sub_groups]).astype(F32).astype(BF)
                rows_in = held[pl.ds(pl.multiple_of(n * block + s * sub, sub), sub), :]
                to = pl.ds(pl.multiple_of(n * groups + s * sub_groups, sub_groups), sub_groups)
                picked_ref[to, :] = dot(chosen, rows_in, TN).astype(BF)
            return carry

        lax.fori_loop(0, chunks, step, 0)

    whole = pl.BlockSpec(memory_space=pltpu.VMEM)
    return pl.pallas_call(
        kernel,
        in_specs=[pl.BlockSpec(memory_space=pl.ANY), whole],
        out_specs=whole,
        out_shape=jax.ShapeDtypeStruct((rows // GROUP, width), BF),
        scratch_shapes=[pltpu.VMEM((rows, width), BF), pltpu.SemaphoreType.DMA((chunks,))],
        cost_estimate=small_cost(),
        compiler_params=pltpu.CompilerParams(vmem_limit_bytes=60 << 20),
        name="pick_rows",
    )(base, offsets)


def score_sums(base, router, mine, ways):
    rows, width = base.shape
    block = rows // ways

    def kernel(mine_ref, base_ref, router_ref, square_ref):
        score = jnp.sum(base_ref[...].astype(F32) * router_ref[...].astype(F32), axis=1, keepdims=True)
        square_ref[...] = jnp.broadcast_to(jnp.sum(score * score, axis=0, keepdims=True), square_ref.shape)

    return pl.pallas_call(
        kernel,
        grid_spec=pltpu.PrefetchScalarGridSpec(
            num_scalar_prefetch=1,
            grid=(1,),
            in_specs=[
                pl.BlockSpec((block, width), lambda i, m: (m[0], 0)),
                pl.BlockSpec((1, width), lambda i, m: (0, 0)),
            ],
            out_specs=pl.BlockSpec((1, 128), lambda i, m: (0, 0)),
        ),
        out_shape=jax.ShapeDtypeStruct((1, 128), F32),
        cost_estimate=small_cost(),
        name="score_sums",
    )(mine, base, router)


def pick_only(base, offsets, ways):
    rows, width = base.shape
    block = rows // ways
    groups = block // GROUP
    sub = 256
    sub_groups = sub // GROUP

    def kernel(base_ref, offset_ref, picked_ref):
        local = lax.broadcasted_iota(jnp.int32, (sub, sub_groups), 0) - GROUP * lax.broadcasted_iota(
            jnp.int32, (sub, sub_groups), 1
        )
        for s in range(block // sub):
            to = slice(s * sub_groups, (s + 1) * sub_groups)
            chosen = (local == offset_ref[:, to]).astype(F32).astype(BF)
            picked_ref[to, :] = dot(chosen, base_ref[s * sub : (s + 1) * sub, :], TN).astype(BF)

    return pl.pallas_call(
        kernel,
        grid=(ways,),
        in_specs=[pl.BlockSpec((block, width), lambda i: (i, 0)), pl.BlockSpec((1, groups), lambda i: (0, i))],
        out_specs=pl.BlockSpec((groups, width), lambda i: (i, 0)),
        out_shape=jax.ShapeDtypeStruct((rows // GROUP, width), BF),
        cost_estimate=small_cost(),
        name="pick_only",
    )(base, offsets)


def merge_rows(base, offsets, pieces, mine, which, held_out=None):
    rows, width = base.shape
    ways, depth, _ = pieces.shape
    count = rows // ways
    groups = count // GROUP
    kept = [] if held_out is None else [held_out]
    sub = 256
    sub_groups = sub // GROUP

    first = which.start

    def kernel(part_ref, base_ref, offset_ref, piece_ref, *rest):
        out_ref = rest[-1]
        local = lax.broadcasted_iota(jnp.int32, (sub, sub_groups), 0) - GROUP * lax.broadcasted_iota(
            jnp.int32, (sub, sub_groups), 1
        )
        for s in range(count // sub):
            here = slice(s * sub, (s + 1) * sub)
            to = slice(s * sub_groups, (s + 1) * sub_groups)
            chosen = (local == offset_ref[:, to]).astype(F32)
            hit = jnp.sum(chosen, axis=1, keepdims=True) > 0.5
            spread = dot(chosen.astype(BF), piece_ref[0, to, :], NN)
            out_ref[here, :] = jnp.where(hit, spread, base_ref[here, :].astype(F32)).astype(BF)

    grid_spec = pltpu.PrefetchScalarGridSpec(
        num_scalar_prefetch=1,
        grid=(len(which),),
        in_specs=[
            pl.BlockSpec((count, width), lambda i, m: (m[0] ^ (i + first), 0)),
            pl.BlockSpec((1, groups), lambda i, m: (0, m[0] ^ (i + first))),
            pl.BlockSpec((1, depth, width), lambda i, m: (m[0] ^ (i + first), 0, 0)),
        ]
        + [pl.BlockSpec(memory_space=pl.ANY)] * len(kept),
        out_specs=pl.BlockSpec((count, width), lambda i, m: (m[0] ^ (i + first), 0)),
    )
    return pl.pallas_call(
        kernel,
        grid_spec=grid_spec,
        out_shape=jax.ShapeDtypeStruct((rows, width), BF),
        input_output_aliases={4: 0} if kept else {},
        cost_estimate=small_cost(),
        name="merge_rows",
    )(mine, base, offsets, pieces, *kept)


def attend(picked, gain, weight, seq_row, ways):
    rows, width = picked.shape
    heads_width = weight.shape[2]
    heads = heads_width // HEAD_DIM
    block = min(256, rows)

    def body(load, store, outs, scalars, scratch):
        low_ref, qkv_ref, out_ref, *probs_refs = outs
        values = load(0)[...].astype(F32)
        low_ref[...] = (values * inverse_rms(values) * load(1)[...].astype(F32).reshape(1, width)).astype(BF)
        store(0)
        weight_ref = load(2)
        for n in range(3):
            qkv_ref[n] = dot(low_ref[...], weight_ref[n], NN).astype(BF)
        store(1)
        sequence = load(3)[...].astype(F32)
        column = jnp.broadcast_to(sequence, (128, rows)).T[:, :1]
        lane_head = lax.broadcasted_iota(jnp.int32, (1, heads_width), 1) // HEAD_DIM
        for n in reversed(range(rows // block)):
            start, stop = n * block, (n + 1) * block
            query = qkv_ref[0, start:stop, :] * BF(HEAD_DIM ** (-0.5))
            order = lax.broadcasted_iota(jnp.int32, (block, stop), 0) + start
            keys = lax.broadcasted_iota(jnp.int32, (block, stop), 1)
            allowed = (column[start:stop, :] == sequence[:, :stop]) & (order >= keys)
            total = jnp.zeros((block, heads_width), F32)
            for head in range(heads):
                here = lane_head == head
                key = jnp.where(here, qkv_ref[1, :stop, :], BF(0))
                logits = jnp.where(allowed, dot(query, key, NT), mask_fill)
                raised = jnp.exp(logits - jnp.max(logits, axis=-1, keepdims=True))
                probs = (raised * (1.0 / jnp.sum(raised, axis=-1, keepdims=True))).astype(BF)
                probs_refs[n][head] = probs
                value = jnp.where(here, qkv_ref[2, :stop, :], BF(0))
                total = total + dot(probs, value, NN)
            for k in range(ways):
                out_ref[k, start:stop, :] = total.astype(BF)
            store(3 + n)

    return staged(
        "attend",
        body,
        [],
        [picked, gain, weight, seq_row],
        [
            ((rows, width), BF),
            ((3, rows, heads_width), BF),
            ((ways, rows, heads_width), BF),
        ]
        + [((heads, block, (n + 1) * block), BF) for n in range(rows // block)],
        [],
        60,
        small_cost(),
    )


def feed_forward(heads, own_weight, quarters, picked, gain, up, grad_act, grad_mixer, part, mine, ways):
    rows, width = picked.shape
    hidden = up.shape[1]
    sub = min(1024, hidden)
    count, _, heads_width = heads.shape
    piece = heads_width // 4
    own = rows // ways
    slope = 0.7978845608028654
    cubic = 0.044715

    def body(load, store, outs, scalars, scratch):
        part_ref, mine_ref = scalars
        attended_ref, low_ref, act_ref, pre_ref, hidden_ref, part_out_ref, gain_part_ref, sent_ref = outs
        total, state, weights = scratch
        quarter = part_ref[0] & 3
        heads_ref = load(0)
        weights[0] = load(1)[...]
        for n in range(4):
            start = pl.multiple_of((quarter ^ n) * piece, piece)
            source = load(2 + n)
            for k in range(1, count):
                weights[k, pl.ds(start, piece), :] = source[k - 1]
        attended = dot(heads_ref[mine_ref[0]], weights[0], NN)
        for k in range(1, count):
            attended = attended + dot(heads_ref[mine_ref[0] ^ k], weights[k], NN)
        total[...] = attended
        attended_ref[...] = total[pl.ds(pl.multiple_of(mine_ref[0] * own, own), own), :]
        state_in = load(6)[...].astype(F32) + attended
        state[...] = state_in
        gain_row = load(7)[...].astype(F32)
        low_ref[...] = (state_in * inverse_rms(state_in) * gain_row).astype(BF)
        store(0, 1)
        up_ref, act_grad_ref = load(8), load(9)
        for s in range(hidden // sub):
            lanes = slice(s * sub, (s + 1) * sub)
            value = dot(low_ref[...], up_ref[:, lanes], NN)
            square = value * value
            bent = jnp.tanh(value * (slope + (slope * cubic) * square))
            half = 0.5 * (1.0 + bent)
            act_ref[:, lanes] = (value * half).astype(BF)
            rise = half + (0.5 * value) * (1.0 - bent * bent) * (slope + (3.0 * slope * cubic) * square)
            pre = (act_grad_ref[:, lanes] * rise).astype(BF)
            pre_ref[:, lanes] = pre
            term = dot(pre, up_ref[:, lanes], NT)
            if s == 0:
                total[...] = term
            else:
                total[...] += term
        store(2, 3)
        state_in = state[...]
        grad = total[...]
        inverse = inverse_rms(state_in)
        normal = state_in * inverse
        gain_part_ref[...] = jnp.sum(grad * normal, axis=0, keepdims=True)
        scaled = grad * gain_row
        along = jnp.mean(scaled * normal, axis=-1, keepdims=True)
        back = inverse * (scaled - normal * along)
        hidden_ref[...] = back.astype(BF)
        part_out_ref[...] = (back + load(10)[...].astype(F32) * (1.0 / count)).astype(BF)
        store(4, 5, 6)
        for k in range(count):
            sent_ref[mine_ref[0] ^ k] = dot(part_out_ref[...], weights[k], NT).astype(BF)

    return staged(
        "feed_forward",
        body,
        [part, mine],
        [heads, own_weight, *quarters, picked, gain, up, grad_act, grad_mixer],
        [
            ((own, width), F32),
            ((rows, width), BF),
            ((rows, hidden), BF),
            ((rows, hidden), BF),
            ((rows, width), BF),
            ((rows, width), BF),
            ((1, width), F32),
            (heads.shape, BF),
        ],
        [
            pltpu.VMEM((rows, width), F32),
            pltpu.VMEM((rows, width), F32),
            pltpu.VMEM((count, heads_width, width), BF),
        ],
        60,
        small_cost(),
    )


def act_grads(picked, router, grad_rows, down):
    rows, width = grad_rows.shape

    def kernel(picked_ref, router_ref, rows_ref, down_ref, gating_ref, square_ref, mixer_ref, grad_ref):
        score = jnp.sum(picked_ref[...].astype(F32) * router_ref[...].astype(F32), axis=-1, keepdims=True)
        gating = jax.nn.sigmoid(score)
        gating_ref[...] = gating
        square_ref[...] = jnp.broadcast_to(jnp.sum(score * score, axis=0, keepdims=True), square_ref.shape)
        mixer_ref[...] = (gating * rows_ref[...].astype(F32)).astype(BF)
        grad_ref[...] = dot(mixer_ref[...], down_ref[...], NT)

    whole = pl.BlockSpec(memory_space=pltpu.VMEM)
    return pl.pallas_call(
        kernel,
        in_specs=[whole] * 4,
        out_specs=[whole] * 4,
        out_shape=[
            jax.ShapeDtypeStruct((rows, 1), F32),
            jax.ShapeDtypeStruct((1, 128), F32),
            jax.ShapeDtypeStruct((rows, width), BF),
            jax.ShapeDtypeStruct((rows, down.shape[0]), F32),
        ],
        cost_estimate=small_cost(),
        name="act_grads",
    )(picked, router, grad_rows, down)


def attend_back(head_terms, qkv, probs, weight, picked, gain, hidden_part):
    rows, width = picked.shape
    heads_width = weight.shape[2]
    heads = heads_width // HEAD_DIM
    block = min(256, rows)
    scale = HEAD_DIM ** (-0.5)

    def kernel(
        head_ref,
        qkv_ref,
        weight_ref,
        picked_ref,
        gain_ref,
        hidden_ref,
        *rest,
    ):
        probs_refs, (grads_ref, gain_part_ref, result, grad_key, grad_value) = rest[: len(probs)], rest[len(probs) :]
        lane_head = lax.broadcasted_iota(jnp.int32, (1, heads_width), 1) // HEAD_DIM
        for start in reversed(range(0, rows, block)):
            stop = start + block
            here_rows = slice(start, stop)
            grad_head = head_ref[0, here_rows, :].astype(F32)
            for k in range(1, head_ref.shape[0]):
                grad_head = grad_head + head_ref[k, here_rows, :].astype(F32)
            grad_head = grad_head.astype(BF)
            query = qkv_ref[0, here_rows, :] * BF(scale)
            grad_query = jnp.zeros((block, heads_width), F32)
            add_key = jnp.zeros((stop, heads_width), F32)
            add_value = jnp.zeros((stop, heads_width), F32)
            for head in range(heads):
                here = lane_head == head
                value = jnp.where(here, qkv_ref[2, :stop, :], BF(0))
                key = jnp.where(here, qkv_ref[1, :stop, :], BF(0))
                low = probs_refs[start // block][head]
                weighted = low.astype(F32) * dot(grad_head, value, NT)
                row_sum = jnp.sum(weighted, axis=-1, keepdims=True)
                slopes = (weighted - low.astype(F32) * row_sum).astype(BF)
                grad_query = grad_query + dot(slopes, key, NN)
                add_key = add_key + dot(slopes, jnp.where(here, query, BF(0)), TN)
                add_value = add_value + dot(low, jnp.where(here, grad_head, BF(0)), TN)
            grads_ref[0, here_rows, :] = (grad_query * scale).astype(BF)
            if stop == rows:
                grad_key[...] = add_key
                grad_value[...] = add_value
            else:
                grad_key[:stop, :] += add_key
                grad_value[:stop, :] += add_value
        grads_ref[1] = grad_key[...].astype(BF)
        grads_ref[2] = grad_value[...].astype(BF)
        first = dot(grads_ref[0], weight_ref[0], NT)
        for n in range(1, 3):
            first = first + dot(grads_ref[n], weight_ref[n], NT)
        values = picked_ref[...].astype(F32)
        inverse = inverse_rms(values)
        normal = values * inverse
        gain_part_ref[...] = jnp.sum(first * normal, axis=0, keepdims=True)
        scaled = first * gain_ref[...].astype(F32)
        along = jnp.mean(scaled * normal, axis=-1, keepdims=True)
        result[...] = (hidden_ref[...].astype(F32) + inverse * (scaled - normal * along)).astype(BF)

    whole = pl.BlockSpec(memory_space=pltpu.VMEM)
    return pl.pallas_call(
        kernel,
        in_specs=[whole] * (6 + len(probs)),
        out_specs=[whole] * 3,
        out_shape=[
            jax.ShapeDtypeStruct((3, rows, heads_width), BF),
            jax.ShapeDtypeStruct((1, width), F32),
            jax.ShapeDtypeStruct((rows, width), BF),
        ],
        scratch_shapes=[
            pltpu.VMEM((rows, heads_width), F32),
            pltpu.VMEM((rows, heads_width), F32),
        ],
        cost_estimate=small_cost(),
        compiler_params=pltpu.CompilerParams(vmem_limit_bytes=20 << 20),
        name="attend_back",
    )(head_terms, qkv, weight, picked, gain, hidden_part, *probs)


def spread_rows(down, up, order_down, order_up, part):
    count = len(down)
    wide, width = down[0].shape
    rows = wide // (2 ** len(order_down) // count)
    each = wide // rows

    def kernel(part_ref, *refs):
        down_out, up_out = refs[2 * count :]
        for n in range(count):

            @pl.when(pl.program_id(0) // each == n)
            def _():
                down_out[...] = refs[n][...].astype(F32)
                up_out[...] = refs[count + n][...].astype(F32)

    def source(n):
        return pl.BlockSpec((rows, width), lambda i, p: (jnp.clip(i - n * each, 0, each - 1), 0))

    def target(order):
        def place(i, p):
            key = sum((i >> n & 1) * bit for n, bit in enumerate(order))
            return p[0] ^ key, 0

        return pl.BlockSpec((rows, width), place)

    return pl.pallas_call(
        kernel,
        grid_spec=pltpu.PrefetchScalarGridSpec(
            num_scalar_prefetch=1,
            grid=(count * each,),
            in_specs=[source(n) for n in range(count)] * 2,
            out_specs=[target(order_down), target(order_up)],
        ),
        out_shape=[jax.ShapeDtypeStruct((count * wide, width), F32)] * 2,
        cost_estimate=small_cost(),
        name="spread_rows",
    )(part, *down, *up)


def qkv_part_of(first_low, grads, part):
    rows, width = first_low.shape
    part_width = grads.shape[2]
    half = 3 * part_width // 2

    def kernel(part_ref, low_ref, grads_ref, keep_ref, send_ref, full):
        for n in range(3):
            product = dot(grads_ref[n], low_ref[...], TN)
            full[n * part_width : (n + 1) * part_width, :] = product.astype(BF)
        core = part_ref[0] & 1
        for target, which in ((keep_ref, core), (send_ref, 1 - core)):
            target[...] = full[pl.ds(pl.multiple_of(which * half, half), half), :]

    whole = pl.BlockSpec(memory_space=pltpu.VMEM)
    return pl.pallas_call(
        kernel,
        in_specs=[pl.BlockSpec(memory_space=pltpu.SMEM)] + [whole] * 2,
        out_specs=[whole] * 2,
        out_shape=[jax.ShapeDtypeStruct((half, width), BF)] * 2,
        scratch_shapes=[pltpu.VMEM((2 * half, width), BF)],
        cost_estimate=small_cost(),
        compiler_params=pltpu.CompilerParams(vmem_limit_bytes=14 << 20),
        name="qkv_part",
    )(part, first_low, grads)


def spread_qkv(near, far, part, part_width):
    rows, width = near.shape
    tile = 128
    count = rows // tile
    many = part_width // tile

    def kernel(part_ref, near_ref, far_ref, out_ref):
        core = part_ref[0] & 1
        for ref, which in ((near_ref, core), (far_ref, 1 - core)):
            for n in range(count):
                spot = which * count + n
                column = pl.multiple_of(spot % many * tile, tile)
                piece = ref[n * tile : (n + 1) * tile, :].astype(F32)
                out_ref[spot // many, :, pl.ds(column, tile)] = piece.T

    whole = pl.BlockSpec(memory_space=pltpu.VMEM)
    return pl.pallas_call(
        kernel,
        in_specs=[pl.BlockSpec(memory_space=pltpu.SMEM)] + [whole] * 2,
        out_specs=whole,
        out_shape=jax.ShapeDtypeStruct((2 * rows // part_width, width, part_width), F32),
        cost_estimate=small_cost(),
        compiler_params=pltpu.CompilerParams(vmem_limit_bytes=14 << 20),
        name="spread_qkv",
    )(part, near, far)


def core_grads(activated, grad_mixer, second_low, grad_pre, heads, attended_part, part, keys_a, keys_b):
    rows, hidden = activated.shape
    width = grad_mixer.shape[1]
    copies = len(keys_a)
    half = copies // 2
    count, _, heads_width = heads.shape
    block = hidden // copies
    small = heads_width // copies
    many = count // 2
    depth = half * (block + many * small)

    def kernel(part_ref, act_ref, mixer_ref, low_ref, pre_ref, heads_ref, term_ref, keep_ref, *rest):
        wide_refs, narrow_refs, (full, narrow) = rest[0:2], rest[2:4], rest[4:]

        def place(source, each, lane, keys, first, stride):
            for n, key in enumerate(keys):
                start = pl.multiple_of((part_ref[0] ^ key) * each, each)
                at = first + (n % half) * stride
                piece = source[pl.ds(start, each), :]
                if n < half:
                    keep_ref[lane, at : at + each, :] = piece
                elif first == 0:
                    wide_refs[lane][at : at + each, :] = piece
                else:
                    narrow_refs[lane][at - half * block : at - half * block + each, :] = piece

        full[...] = dot(act_ref[...], mixer_ref[...], TN).astype(BF)
        place(full, block, 0, keys_a, 0, block)
        full[...] = dot(low_ref[...], pre_ref[...], TN).astype(BF)
        place(full, block, 1, keys_b, 0, block)
        for k in range(count):
            narrow[...] = dot(heads_ref[k], term_ref[...], TN).astype(BF)
            lane, spot = divmod(k, many)
            place(narrow, small, lane, keys_b if lane else keys_a, half * block + spot * small, many * small)

    whole = pl.BlockSpec(memory_space=pltpu.VMEM)
    wide_shape = jax.ShapeDtypeStruct((half * block, width), BF)
    narrow_shape = jax.ShapeDtypeStruct((half * many * small, width), BF)
    return pl.pallas_call(
        kernel,
        in_specs=[pl.BlockSpec(memory_space=pltpu.SMEM)] + [whole] * 6,
        out_specs=[whole] * 5,
        out_shape=[jax.ShapeDtypeStruct((2, depth, width), BF)] + [wide_shape] * 2 + [narrow_shape] * 2,
        scratch_shapes=[pltpu.VMEM((hidden, width), BF), pltpu.VMEM((heads_width, width), BF)],
        cost_estimate=small_cost(),
        compiler_params=pltpu.CompilerParams(vmem_limit_bytes=14 << 20),
        name="core_grads",
    )(part, activated, grad_mixer, second_low, grad_pre, heads, attended_part)


def plus(left, right):
    return (left.astype(F32) + right.astype(F32)).astype(BF)


def halving_sums(keep, got_a, got_b, wide, narrow):
    width = keep.shape[2]
    count = len(got_a)

    def kernel(keep_ref, *refs):
        a_got, b_got, (stay_ref, a_out, b_out) = refs[:count], refs[count : 2 * count], refs[2 * count :]
        for lane, got, out in ((0, a_got, a_out), (1, b_got, b_out)):
            for first, size, at in ((0, wide // 2, 0), (wide, narrow // 2, wide // 2)):
                source, shift = (got[1], wide) if count == 2 and first else (got[0], 0)
                to = slice(at, at + size)
                for start, target in ((first, stay_ref.at[lane]), (first + size, out)):
                    here = slice(start - shift, start - shift + size)
                    target[to, :] = plus(keep_ref[lane, start : start + size, :], source[here, :])

    whole = pl.BlockSpec(memory_space=pltpu.VMEM)
    depth = (wide + narrow) // 2
    lane_shape = jax.ShapeDtypeStruct((depth, width), BF)
    return pl.pallas_call(
        kernel,
        in_specs=[whole] * (1 + 2 * count),
        out_specs=[whole] * 3,
        out_shape=[jax.ShapeDtypeStruct((2, depth, width), BF), lane_shape, lane_shape],
        cost_estimate=small_cost(),
        compiler_params=pltpu.CompilerParams(vmem_limit_bytes=14 << 20),
        name="halving_sums",
    )(keep, *got_a, *got_b)


def owned_sums(keep, got_a, got_b, fresh, small, wide, ways):
    width = keep.shape[2]
    narrow = keep.shape[1] - wide
    own = fresh.shape[0]
    many = ways // 2
    each = narrow // many
    depth = own + GAP + each

    def kernel(keep_ref, a_got, b_got, fresh_ref, small_ref, a_out, b_out, sent_ref):
        sums = split_sums(small_ref[...])
        for lane, got, out in ((0, a_got, a_out), (1, b_got, b_out)):
            out[...] = plus(keep_ref[lane, :wide, :], got[:wide, :])
            done = plus(keep_ref[lane, wide:, :], got[wide:, :])
            for spot in range(many):
                k = lane * many + spot
                sent_ref[k, :own, :] = fresh_ref[...]
                sent_ref[k, own : own + GAP, :] = sums
                sent_ref[k, own + GAP :, :] = done[spot * each : (spot + 1) * each, :]

    whole = pl.BlockSpec(memory_space=pltpu.VMEM)
    lane_shape = jax.ShapeDtypeStruct((wide, width), BF)
    return pl.pallas_call(
        kernel,
        in_specs=[whole] * 5,
        out_specs=[whole] * 3,
        out_shape=[lane_shape, lane_shape, jax.ShapeDtypeStruct((ways, depth, width), BF)],
        cost_estimate=small_cost(),
        compiler_params=pltpu.CompilerParams(vmem_limit_bytes=10 << 20),
        name="owned_sums",
    )(keep, got_a, got_b, fresh, small)


def core_sums(rows, other):
    depth, width = rows.shape
    third = depth // 2

    def kernel(rows_ref, other_ref, a_out, b_out):
        a_out[...] = plus(rows_ref[:third, :], other_ref[:third, :])
        b_out[...] = plus(rows_ref[third:, :], other_ref[third:, :])

    whole = pl.BlockSpec(memory_space=pltpu.VMEM)
    return pl.pallas_call(
        kernel,
        in_specs=[whole] * 2,
        out_specs=[whole] * 2,
        out_shape=[jax.ShapeDtypeStruct((third, width), BF)] * 2,
        cost_estimate=small_cost(),
        compiler_params=pltpu.CompilerParams(vmem_limit_bytes=10 << 20),
        name="core_sums",
    )(rows, other)


def lane_sums(lane_a, got_a, lane_b, got_b):
    def kernel(a_ref, a_got, b_ref, b_got, a_out, b_out):
        a_out[...] = plus(a_ref[...], a_got[...])
        b_out[...] = plus(b_ref[...], b_got[...])

    whole = pl.BlockSpec(memory_space=pltpu.VMEM)
    return pl.pallas_call(
        kernel,
        in_specs=[whole] * 4,
        out_specs=[whole] * 2,
        out_shape=[jax.ShapeDtypeStruct(lane_a.shape, BF)] * 2,
        cost_estimate=small_cost(),
        compiler_params=pltpu.CompilerParams(vmem_limit_bytes=12 << 20),
        name="lane_sums",
    )(lane_a, got_a, lane_b, got_b)


def joined_lanes(lane_a, got_a, lane_b, got_b):
    rows, width = lane_a.shape

    def kernel(a_ref, a_got, b_ref, b_got, out_ref):
        out_ref[:rows, :] = plus(a_ref[...], a_got[...])
        out_ref[rows:, :] = plus(b_ref[...], b_got[...])

    whole = pl.BlockSpec(memory_space=pltpu.VMEM)
    return pl.pallas_call(
        kernel,
        in_specs=[whole] * 4,
        out_specs=whole,
        out_shape=jax.ShapeDtypeStruct((2 * rows, width), BF),
        cost_estimate=small_cost(),
        compiler_params=pltpu.CompilerParams(vmem_limit_bytes=10 << 20),
        name="joined_lanes",
    )(lane_a, got_a, lane_b, got_b)


def gather_blocks(blocks_a, blocks_b):
    wide, width = blocks_a[0].shape
    count = len(blocks_a)

    def kernel(*refs):
        for lane in range(2):
            for n in range(count):
                refs[2 * count + lane][n * wide : (n + 1) * wide, :] = refs[lane * count + n][...]

    whole = pl.BlockSpec(memory_space=pltpu.VMEM)
    return pl.pallas_call(
        kernel,
        in_specs=[whole] * (2 * count),
        out_specs=[whole] * 2,
        out_shape=[jax.ShapeDtypeStruct((count * wide, width), BF)] * 2,
        cost_estimate=small_cost(),
        compiler_params=pltpu.CompilerParams(vmem_limit_bytes=10 << 20),
        name="gather_blocks",
    )(*blocks_a, *blocks_b)


def split_sums(values):
    high = values.astype(BF)
    low = (values - high.astype(F32)).astype(BF)
    return jnp.concatenate([high, low], axis=0)


def joined_sums(rows):
    return rows[:TERMS].astype(F32) + rows[TERMS : 2 * TERMS].astype(F32)


def first_small(received, own):
    ways, depth, width = received.shape
    each = depth - own - GAP

    def kernel(got_ref, out_ref):
        total = got_ref[0, own + GAP :, :].astype(F32)
        sums = joined_sums(got_ref[0, own : own + GAP, :])
        for k in range(1, ways):
            total = total + got_ref[k, own + GAP :, :].astype(F32)
            sums = sums + joined_sums(got_ref[k, own : own + GAP, :])
        out_ref[:each, :] = total.astype(BF)
        out_ref[each:, :] = split_sums(sums)

    whole = pl.BlockSpec(memory_space=pltpu.VMEM)
    return pl.pallas_call(
        kernel,
        in_specs=[whole],
        out_specs=whole,
        out_shape=jax.ShapeDtypeStruct((each + GAP, width), BF),
        cost_estimate=small_cost(),
        compiler_params=pltpu.CompilerParams(vmem_limit_bytes=8 << 20),
        name="first_small",
    )(received)


def last_small(blocks, keys, part, shares):
    depth, width = blocks[0].shape
    each = depth - GAP
    count = len(blocks)

    def kernel(part_ref, *refs):
        out_ref, small_refs = refs[count], refs[count + 1 :]
        total = joined_sums(refs[0][each:, :])
        for n in range(1, count):
            total = total + joined_sums(refs[n][each:, :])
        for n in range(TERMS - 1):
            small_refs[n][...] = total[n : n + 1, :]
        lane = lax.broadcasted_iota(jnp.int32, (1, 128), 1)
        small_refs[TERMS - 1][...] = total[TERMS - 1 :, :128] * jnp.where(lane == 0, shares[0], shares[1])
        for n in range(count):
            start = pl.multiple_of((part_ref[0] ^ keys[n]) * each, each)
            out_ref[pl.ds(start, each), :] = refs[n][:each, :].astype(F32)

    whole = pl.BlockSpec(memory_space=pltpu.VMEM)
    return pl.pallas_call(
        kernel,
        in_specs=[pl.BlockSpec(memory_space=pltpu.SMEM)] + [whole] * count,
        out_specs=[whole] * (1 + TERMS),
        out_shape=[jax.ShapeDtypeStruct((count * each, width), F32)] + [jax.ShapeDtypeStruct((1, width), F32)] * (TERMS - 1)
        + [jax.ShapeDtypeStruct((1, 128), F32)],
        cost_estimate=small_cost(),
        compiler_params=pltpu.CompilerParams(vmem_limit_bytes=10 << 20),
        name="last_small",
    )(part, *blocks)


def finish_rows(mixer_terms, picked, gating, attended, grad_rows, gain_one, gain_two, square, routed_square, mine, ways):
    rows, width = picked.shape
    own = rows // ways

    def kernel(
        mine_ref,
        terms_ref,
        picked_ref,
        gating_ref,
        attended_ref,
        rows_ref,
        one_ref,
        two_ref,
        square_ref,
        routed_ref,
        new_ref,
        score_ref,
        small_ref,
    ):
        branch = attended_ref[...]
        for k in range(ways):
            branch = branch + terms_ref[k].astype(F32)
        values = picked_ref[...].astype(F32)
        gate = gating_ref[...]
        new_ref[...] = (values + gate * branch).astype(BF)
        along = jnp.sum(rows_ref[...].astype(F32) * branch, axis=-1, keepdims=True)
        score = along * gate * (1.0 - gate)
        score_ref[...] = score
        small_ref[0:1, :] = jnp.sum(score * values, axis=0, keepdims=True)
        small_ref[1:2, :] = one_ref[...]
        small_ref[2:3, :] = two_ref[...]
        lane = lax.broadcasted_iota(jnp.int32, (1, width), 1)
        both = jnp.where(lane == 0, square_ref[:, 0:1], routed_ref[:, 0:1] * (1.0 / ways))
        small_ref[3:4, :] = jnp.where(lane < 2, both, 0.0)

    def block(shape):
        return pl.BlockSpec(shape, lambda i, m: (m[0], 0))

    def fixed(shape):
        return pl.BlockSpec(shape, lambda i, m: (0, 0))

    return pl.pallas_call(
        kernel,
        grid_spec=pltpu.PrefetchScalarGridSpec(
            num_scalar_prefetch=1,
            grid=(1,),
            in_specs=[pl.BlockSpec(mixer_terms.shape, lambda i, m: (0, 0, 0))]
            + [block((own, width)), block((own, 1)), fixed((own, width)), block((own, width))]
            + [fixed((1, width))] * 2
            + [fixed((1, 128))] * 2,
            out_specs=[fixed((own, width)), fixed((own, 1)), fixed((4, width))],
        ),
        out_shape=[
            jax.ShapeDtypeStruct((own, width), BF),
            jax.ShapeDtypeStruct((own, 1), F32),
            jax.ShapeDtypeStruct((4, width), F32),
        ],
        cost_estimate=cost_of(10),
        name="finish_rows",
    )(mine, mixer_terms, picked, gating, attended, grad_rows, gain_one, gain_two, square, routed_square)


def finish_input(terms, grad_rows, score, router, mine, ways):
    rows, width = grad_rows.shape
    own = rows // ways

    def kernel(mine_ref, terms_ref, rows_ref, score_ref, router_ref, out_ref):
        total = rows_ref[...].astype(F32) + score_ref[...] * router_ref[...].astype(F32)
        for k in range(ways):
            total = total + terms_ref[k].astype(F32)
        for k in range(ways):
            out_ref[k] = total.astype(BF)

    def fixed(shape):
        return pl.BlockSpec(shape, lambda i, m: (0,) * len(shape))

    return pl.pallas_call(
        kernel,
        grid_spec=pltpu.PrefetchScalarGridSpec(
            num_scalar_prefetch=1,
            grid=(1,),
            in_specs=[
                fixed((ways, own, width)),
                pl.BlockSpec((own, width), lambda i, m: (m[0], 0)),
                fixed((own, 1)),
                fixed((1, width)),
            ],
            out_specs=fixed((ways, own, width)),
        ),
        out_shape=jax.ShapeDtypeStruct((ways, own, width), BF),
        cost_estimate=small_cost(),
        compiler_params=pltpu.CompilerParams(vmem_limit_bytes=8 << 20),
        name="finish_input",
    )(mine, terms, grad_rows, score, router)


def split_kept(count, order):
    keys = [0]
    for bit in reversed(order):
        keys = keys + [k ^ bit for k in keys]
    return keys


def per_device(
    tokens,
    route_offset,
    unit_sequence,
    cotangent,
    router_weight,
    first_gain,
    second_gain,
    qkv_weight,
    out_weight,
    up_weight,
    down_weight,
):
    rows_local, width = tokens.shape
    routed = route_offset.shape[1]
    ways = lax.axis_size("tensor")
    copies = lax.axis_size("dp")
    mine = lax.axis_index("tensor")
    part = lax.axis_index("dp")
    mine_array = jnp.reshape(mine, (1,)).astype(jnp.int32)
    part_array = jnp.reshape(part, (1,)).astype(jnp.int32)
    ladder = [1 << b for b in range(1, copies.bit_length() - 1)]
    order_a = [1] + ladder
    order_b = [1] + ladder[::-1]
    keys_a = split_kept(copies, order_a)
    keys_b = split_kept(copies, order_b)

    tie = lax.optimization_barrier
    own_rows = routed // ways
    heads_width = out_weight.shape[0]
    hidden = up_weight.shape[1]
    by_swaps = copies == 8
    bit_x, bit_y = 2, 4
    shares = (1.0 / (rows_local * copies), 1.0 / (routed * copies))

    quarter = part & 3
    piece_rows = heads_width // 4
    piece = lax.dynamic_slice_in_dim(out_weight, quarter * piece_rows, piece_rows, 0)
    here = [swap(piece, "tensor", k) for k in range(1, ways)]

    picked = pick_rows(tokens, route_offset, ways)
    first_low, qkv, head_out, *probs = attend(picked, first_gain, qkv_weight, unit_sequence, ways)
    here, head_out = tie((here, head_out))

    heads = to_all(head_out)
    here = jnp.stack(here)
    beside, across = swap(here, "dp", bit_x), swap(here, "dp", 1)
    cotangent, router_weight, second_gain, here, head_out = tie(
        (cotangent, router_weight, second_gain, here, head_out)
    )
    weight_row = router_weight[None]
    grad_rows = pick_only(cotangent, route_offset, ways)
    beside, across, here, grad_rows = tie((beside, across, here, grad_rows))
    quarters = [here, across, beside, swap(beside, "dp", 1)]
    gating, routed_square, grad_mixer, grad_act = act_grads(picked, weight_row, grad_rows, down_weight)
    square = score_sums(tokens, weight_row, mine_array, ways)
    heads, quarters, grad_act, grad_mixer, square = tie((heads, quarters, grad_act, grad_mixer, square))
    attended, second_low, activated, grad_pre, hidden_part, attended_part, second_gain_part, head_sent = feed_forward(
        heads,
        out_weight,
        quarters,
        picked,
        second_gain[None],
        up_weight,
        grad_act,
        grad_mixer,
        part_array,
        mine_array,
        ways,
    )

    head_terms = to_all(head_sent)
    wide = hidden // 2
    narrow = heads_width * ways // 4
    if by_swaps:
        kept, *leaving = core_grads(
            activated, grad_mixer, second_low, grad_pre, heads, attended_part, part_array, keys_a, keys_b
        )
        wide_a, wide_b, narrow_a, narrow_b = (swap(array, "dp", 1) for array in leaving)
        activated, kept = tie((activated, kept))
    else:
        down_part = dot(activated, grad_mixer, TN).astype(BF)
        up_part = dot(second_low, grad_pre, TN).astype(BF)
        out_parts = jnp.stack([dot(heads[k], attended_part, TN).astype(BF) for k in range(ways)])
    mixer_part = dot(activated, down_weight, NN).astype(BF).reshape(ways, own_rows, width)
    if by_swaps:
        wide_a, wide_b, narrow_a, narrow_b, mixer_part = tie((wide_a, wide_b, narrow_a, narrow_b, mixer_part))
        kept, leave_a, leave_b = halving_sums(kept, (wide_a, narrow_a), (wide_b, narrow_b), wide, narrow)
        got_a, got_b = swap(leave_a, "dp", bit_x), swap(leave_b, "dp", bit_y)
        head_terms, mixer_part, kept = tie((head_terms, mixer_part, kept))
    else:
        head_terms, mixer_part = tie((head_terms, mixer_part))

    mixer_terms = to_all(mixer_part)
    grad_projected, first_gain_part, input_part = attend_back(
        head_terms, qkv, probs, qkv_weight, picked, first_gain[None], hidden_part
    )
    qkv_part, qkv_leaving = qkv_part_of(first_low, grad_projected, part_array)
    input_part = input_part.reshape(ways, own_rows, width)
    if by_swaps:
        got_a, got_b, qkv_part, qkv_leaving, input_part = tie((got_a, got_b, qkv_part, qkv_leaving, input_part))
        kept, leave_a, leave_b = halving_sums(kept, (got_a,), (got_b,), wide // 2, narrow // 2)
        mixer_terms, input_part, qkv_part, kept, leave_a, leave_b = tie(
            (mixer_terms, input_part, qkv_part, kept, leave_a, leave_b)
        )
    else:
        mixer_terms, input_part, qkv_part = tie((mixer_terms, input_part, qkv_part))

    input_terms = to_all(input_part)
    if by_swaps:
        got_a, got_b = swap(leave_a, "dp", bit_y), swap(leave_b, "dp", bit_x)
        qkv_got = swap(qkv_leaving, "dp", 1)
    new_own, grad_score, small = finish_rows(
        mixer_terms,
        picked,
        gating,
        attended,
        grad_rows,
        first_gain_part,
        second_gain_part,
        square,
        routed_square,
        mine_array,
        ways,
    )
    if by_swaps:
        got_a, got_b, new_own = tie((got_a, got_b, new_own))
        lane_a, lane_b, sent = owned_sums(kept, got_a, got_b, new_own, small, wide // 4, ways)
        got_a, got_b = swap(lane_a, "dp", bit_y), swap(lane_b, "dp", bit_x)
        qkv_part, qkv_got, lane_a, lane_b, sent = tie((qkv_part, qkv_got, lane_a, lane_b, sent))
        qkv_a, qkv_b = core_sums(qkv_part, qkv_got)
        input_terms, sent, got_a, got_b, qkv_a, qkv_b = tie((input_terms, sent, got_a, got_b, qkv_a, qkv_b))
    else:
        sent = jnp.concatenate([new_own, split_sums(small)])
        sent = jnp.broadcast_to(sent[None], (ways,) + sent.shape)
        input_terms, sent = tie((input_terms, sent))

    fresh = to_all(sent)
    if by_swaps:
        more_a = [swap(array, "dp", bit_x) for array in (lane_a, got_a)]
        more_b = [swap(array, "dp", bit_y) for array in (lane_b, got_b)]
    last = finish_input(input_terms, grad_rows, grad_score, weight_row, mine_array, ways)
    cotangent, last = tie((cotangent, last))
    early = merge_rows(cotangent, route_offset, last, mine_array, range(1))
    if by_swaps:
        more_a, more_b, early, qkv_a, qkv_b = tie((more_a, more_b, early, qkv_a, qkv_b))
        qkv_a_got, qkv_b_got = swap(qkv_a, "dp", bit_y), swap(qkv_b, "dp", bit_x)
        down_one, up_one = gather_blocks([lane_a, got_a], [lane_b, got_b])
        down_two, up_two = gather_blocks(more_a, more_b)
        down_near, up_near = [down_one, down_two], [up_one, up_two]
        down_far = [swap(array, "dp", 1) for array in down_near]
        up_far = [swap(array, "dp", 1) for array in up_near]

        def gathered(order):
            keys = [0]
            for bit in order:
                keys = keys + [k ^ bit for k in keys]
            return keys

        down_grad, up_grad = spread_rows(
            down_near + down_far, up_near + up_far, [bit_y, bit_x, 1], [bit_x, bit_y, 1], part_array
        )
        fresh, last, down_grad, up_grad = tie((fresh, last, down_grad, up_grad))
    else:
        fresh, last = tie((fresh, last))

    input_rows = to_all(last)
    if by_swaps:
        blocks = [first_small(fresh, own_rows)]
        more = [swap(array, "dp", bit_x) for array in blocks]
        qkv_a_got, qkv_b_got, blocks = tie((qkv_a_got, qkv_b_got, blocks))
        qkv_a, qkv_b = lane_sums(qkv_a, qkv_a_got, qkv_b, qkv_b_got)
        qkv_a_got, qkv_b_got = swap(qkv_a, "dp", bit_x), swap(qkv_b, "dp", bit_y)
        fresh, blocks, qkv_a, qkv_b = tie((fresh, blocks, qkv_a, qkv_b))
    output = merge_rows(tokens, route_offset, fresh, mine_array, range(ways // 2))
    if by_swaps:
        more, qkv_a_got, qkv_b_got, output = tie((more, qkv_a_got, qkv_b_got, output))
        qkv_near = joined_lanes(qkv_a, qkv_a_got, qkv_b, qkv_b_got)
        qkv_far = swap(qkv_near, "dp", 1)
        blocks = blocks + more
        more = [swap(array, "dp", bit_y) for array in blocks]
        fresh, blocks, qkv_near = tie((fresh, blocks, qkv_near))
    output = merge_rows(tokens, route_offset, fresh, mine_array, range(ways // 2, ways), output)
    if by_swaps:
        more, qkv_far, output = tie((more, qkv_far, output))
        blocks = blocks + more
        more = [swap(array, "dp", 1) for array in blocks]
        qkv_near, blocks = tie((qkv_near, blocks))
        qkv_grad = spread_qkv(qkv_near, qkv_far, part_array, qkv_weight.shape[2])
        more, qkv_grad = tie((more, qkv_grad))
        out_grad, *small = last_small(blocks + more, gathered([bit_x, bit_y, 1]), part_array, shares)
        small[3] = small[3][:, :2]
        input_rows, early, output, out_grad, small, qkv_grad = tie(
            (input_rows, early, output, out_grad, small, qkv_grad)
        )
    input_grad = merge_rows(cotangent, route_offset, input_rows, mine_array, range(1, ways), early)
    if not by_swaps:
        swapped = jnp.concatenate([qkv_leaving, qkv_part])
        qkv_whole = jnp.where(part & 1 == 0, jnp.concatenate([qkv_part, qkv_leaving]), swapped)
        small = sum(joined_sums(fresh[k, own_rows:]) for k in range(ways))
        small = lax.psum(small, "dp")
        small = [small[n : n + 1] for n in range(TERMS)]
        small[3] = small[3][:, :2] * jnp.array((shares,), F32)
        down_grad, up_grad, qkv_sum, out_sum = (
            lax.psum(v, "dp").astype(F32) for v in (down_part, up_part, qkv_whole, out_parts)
        )
        out_grad = jnp.sum(to_all(out_sum.astype(BF)).astype(F32), axis=0)
        qkv_grad = qkv_sum.reshape(3, -1, width).transpose(0, 2, 1)
    router_grad, first_gain_grad, second_gain_grad = (small[n].reshape(width) for n in range(3))
    score_stats = small[3].reshape(2)
    return (
        output,
        input_grad,
        router_grad,
        first_gain_grad,
        second_gain_grad,
        qkv_grad,
        out_grad,
        up_grad,
        down_grad,
        score_stats,
    )


def solution(mesh):
    placed = (
        P("dp", None),
        P("dp", None),
        P("dp", None),
        P("dp", None),
        P(),
        P(),
        P(),
        P(None, None, "tensor"),
        P("tensor", None),
        P(None, "tensor"),
        P("tensor", None),
    )
    return jax.shard_map(
        per_device,
        mesh=mesh,
        in_specs=placed,
        out_specs=(
            P("dp", None),
            P("dp", None),
            P(),
            P(),
            P(),
            P(None, None, "tensor"),
            P("tensor", None),
            P(None, "tensor"),
            P("tensor", None),
            P(),
        ),
        check_vma=False,
    )
```
